32 devices in a mesh: grp: 2 (over core), wide: 8 (over z, x), narrow: 2 (over y).
Axes of the slice: x: 2, y: 2, z: 4, core: 2. Of those that a mesh axis runs over, the one named last changes fastest.
Arguments:
- tokens: bfloat16 [8192, 2048], P(('grp', 'wide', 'narrow')), parts along dimension 0, may hold values from -12 to 12
- cotangent: bfloat16 [8192, 2048], P(('grp', 'wide', 'narrow')), parts along dimension 0, may hold values from -6 to 6
- valid: int32 [8192], P(('grp', 'wide', 'narrow')), parts along dimension 0, may hold values from 0 to 1
- routes: int32 [8192, 8], P(('grp', 'wide', 'narrow')), parts along dimension 0, may hold values from 0 to 15, all different within a row; in each aligned block of 256 rows (0 to 255, 256 to 511, ...) at most 160 rows name the same one
- w_query: bfloat16 [2048, 2048], P(None, 'wide'), may hold values from -0.125 to 0.125
- w_key: bfloat16 [2048, 2048], P(None, 'wide'), may hold values from -0.125 to 0.125
- w_value: bfloat16 [2048, 2048], P(None, 'wide'), may hold values from -0.125 to 0.125
- w_out: bfloat16 [2048, 2048], P('wide'), may hold values from -2 to 2
- norm_attn: bfloat16 [2048], replicated, may hold values from 0.25 to 1.75
- norm_query: bfloat16 [2048], P('wide'), may hold values from 0.25 to 1.75
- norm_key: bfloat16 [2048], P('wide'), may hold values from 0.25 to 1.75
- norm_moe: bfloat16 [2048], replicated, may hold values from 0.25 to 1.75
- w_router: bfloat16 [2048, 16], replicated, may hold values from -0.0625 to 0.0625
- w_gate: bfloat16 [16, 2048, 1024], P(('wide', 'narrow')), may hold values from -0.125 to 0.125
- w_up: bfloat16 [16, 2048, 1024], P(('wide', 'narrow')), may hold values from -0.125 to 0.125
- w_down: bfloat16 [16, 1024, 2048], P(('wide', 'narrow')), may hold values from -1.5 to 1.5
Outputs:
- output: bfloat16 [8192, 2048], P(('grp', 'wide', 'narrow')), parts along dimension 0
- grad_input: float32 [8192, 2048], P(('grp', 'wide', 'narrow')), parts along dimension 0
- grad_query: float32 [4096, 2048], P('grp', 'wide'), parts along dimension 0
- grad_key: float32 [4096, 2048], P('grp', 'wide'), parts along dimension 0
- grad_value: float32 [4096, 2048], P('grp', 'wide'), parts along dimension 0
- grad_out: float32 [4096, 2048], P(('grp', 'wide')), parts along dimension 0
- grad_norm_attn: float32 [4096], P('grp'), parts along dimension 0
- grad_norm_query: float32 [4096], P(('grp', 'wide')), parts along dimension 0
- grad_norm_key: float32 [4096], P(('grp', 'wide')), parts along dimension 0
- grad_norm_moe: float32 [4096], P('grp'), parts along dimension 0
- grad_router: float32 [4096, 16], P('grp'), parts along dimension 0
- grad_gate: float32 [32, 2048, 1024], P(('grp', 'wide', 'narrow')), parts along dimension 0
- grad_up: float32 [32, 2048, 1024], P(('grp', 'wide', 'narrow')), parts along dimension 0
- grad_down: float32 [32, 1024, 2048], P(('grp', 'wide', 'narrow')), parts along dimension 0
- rms: float32 [10], P('grp'), parts along dimension 0
The draws below stay inside these ranges and needn't reach their ends.
There are 2 independent parts, one for each index of `grp`. The reference program is written for one: setup_inputs(seed, part) draws one part's arguments, and reference() takes and returns one part's arrays. A program takes and returns all parts, laid end to end along the dimension named above; an argument that names none is the same for every part. Nothing has to cross between parts.
Inputs may be any that keep to these rules, and one draw needn't show every extreme that they name: `routes`: in the rows of one device no expert is named by more than 160 rows, and in every draw some expert is named by exactly 160 rows of some device; each row names 8 different experts.
All inputs are finite; a program needn't handle non-finite values.
Results may differ from the reference program's by a relative error of at most 0.028.
Values may be sent and summed in bfloat16 or wider, within the bound.
A program may use at most 320 MiB of HBM per device.

```python
import math
import jax
import jax.numpy as jnp
import numpy as np
from jax import lax

D = 2048
HEADS = 16
HD = 128
FF = 1024
TOP = 8
PROMPT = 2048
CONT = 256
NCONT = 8
TOKENS = 4096
TOK_DEV = 256
EXPERTS = 16
CAP = 160


def draw_tokens(key, part):
    index = jnp.arange(TOKENS, dtype=jnp.float32) / max(TOKENS - 1, 1)
    scale = jnp.exp((index - 0.5) * math.log(3.0))
    values = jax.random.normal(key, (TOKENS, D), jnp.float32)
    return (values * scale[:, None]).astype(jnp.bfloat16)


def draw_valid(key, part):
    index = jnp.arange(TOKENS, dtype=jnp.int32)
    level = 25 + 50 * index // TOKENS
    return (jax.random.randint(key, (TOKENS,), 0, 100) < level).astype(jnp.int32)


def block_levels(stream_key, extent, shards, least, top_value):
    def one(dim, parts):
        steps = jax.random.uniform(jax.random.fold_in(jax.random.fold_in(stream_key, 6), dim), (parts,), jnp.float32, least / len(shards), top_value / len(shards))
        return jnp.repeat(jnp.exp(steps), extent[dim] // parts).reshape((-1,) + (1,) * (len(extent) - dim - 1))

    loudness = one(*shards[0])
    for cut in shards[1:]:
        loudness = loudness * one(*cut)
    return loudness


def deal_out(rng, own, number, rows, count, top, reach, slope):
    sequence = jax.random.permutation(rng, count)
    crowded, common = shares(count, rows * top, reach, slope, True), shares(count, rows * top, reach, slope, False)
    places = jnp.arange(count)

    def named(sizes, offset_by):
        used = int((sizes > 0).sum())
        fixed = max(1, used // 4)
        shifted = fixed + (places - fixed + offset_by * (used - fixed)) % max(1, count - fixed)
        return jnp.zeros((count,), jnp.int32).at[sequence[jnp.where(places < fixed, places, shifted)]].set(jnp.asarray(sizes, jnp.int32))

    sizes = jnp.where(number % 4 == 0, named(crowded, number // 4), named(common, number - number // 4 - 1))
    mixed = jax.random.permutation(jax.random.fold_in(own, 3), count)
    source_of, sink = mixed[0:count // 2 * 2:2], mixed[1:count // 2 * 2:2]
    margin = jnp.minimum(sizes[source_of] - 1, reach - sizes[sink]) // 2
    margin = jnp.where((source_of == sequence[0]) | (sink == sequence[0]) | (sizes[sink] == 0), 0, jnp.maximum(margin, 0))
    shifted = jax.random.randint(jax.random.fold_in(own, 4), (count // 2,), 0, 1 << 20) % (margin + 1)
    sizes = sizes.at[source_of].add(-shifted).at[sink].add(shifted)
    labels = jnp.searchsorted(jnp.cumsum(sizes), jnp.arange(rows * top), side="right").astype(jnp.int32)
    listing = labels.reshape(top, rows).T
    listing = listing[jax.random.permutation(jax.random.fold_in(own, 1), rows)]
    offset_by = jax.random.randint(jax.random.fold_in(own, 2), (rows, 1), 0, top)
    return jnp.take_along_axis(listing, (jnp.arange(top)[None, :] + offset_by) % top, axis=1)


def shares(number_of, total, bound, slope, full):
    weights = [(1 << 20) // math.isqrt(standing ** slope) + 1 for standing in range(1, number_of + 1)]
    largest = bound if full else min(bound, max(-(-total // number_of), total * weights[0] // sum(weights)))
    least = 1 if total - largest >= number_of - 1 else 0
    counts, spare = [largest] + [least] * (number_of - 1), total - largest - least * (number_of - 1)
    while spare > 0:
        free = [i for i in range(1, number_of) if counts[i] < largest] or [i for i in range(1, number_of) if counts[i] < bound]
        mass, remaining = sum([weights[i] for i in free]), spare
        for i in free:
            more = min(bound - counts[i], max(1, remaining * weights[i] // mass), spare)
            counts[i] = counts[i] + more
            spare = spare - more
    return np.array(counts)


def scatter_about(key, extent, deviation, reach, split=(), kind=jnp.bfloat16):
    result = deviation * jax.random.normal(key, extent, jnp.float32)
    if split:
        result = result * block_levels(key, extent, split, -0.22, 0.18)
    return jnp.clip(result, -reach, reach).astype(kind)


def setup_inputs(seed: int = 0, part: int = 0) -> dict:
    seeds = jax.random.split(jax.random.key(seed), 17)
    own_keys = jax.random.split(jax.random.fold_in(seeds[16], part), 17)
    tokens = draw_tokens(jax.random.fold_in(jax.random.fold_in(seeds[16], part), 71), part)
    cotangent = scatter_about(own_keys[1], (TOKENS, D), 1.0, 6.0, ((0, 16),))
    valid = draw_valid(jax.random.fold_in(jax.random.fold_in(seeds[16], part), 71), part)
    routes_keys = jax.random.split(jax.random.fold_in(own_keys[3], 1), TOKENS // TOK_DEV)
    routes_turns = jax.random.permutation(jax.random.fold_in(own_keys[3], 3), TOKENS // TOK_DEV)
    routes = jax.vmap(lambda own, number: deal_out(jax.random.fold_in(own_keys[3], 2), own, number, TOK_DEV, EXPERTS, TOP, CAP, 2))(routes_keys, routes_turns).reshape((TOKENS, TOP))
    w_query = scatter_about(seeds[4], (D, HEADS * HD), D ** -0.5, 0.125, ((1, 8),))
    w_key = scatter_about(seeds[5], (D, HEADS * HD), D ** -0.5, 0.125, ((1, 8),))
    w_value = scatter_about(seeds[6], (D, HEADS * HD), D ** -0.5, 0.125, ((1, 8),))
    w_out = scatter_about(seeds[7], (HEADS * HD, D), (HEADS * HD * 16 // (PROMPT + NCONT * CONT)) ** -0.5, 2.0, ((0, 8),))
    norm_attn = jnp.clip(1.0 + 0.15 * jax.random.normal(seeds[8], (D,), jnp.float32), 0.25, 1.75).astype(jnp.bfloat16)
    norm_query = jnp.clip(1.0 + 0.15 * jax.random.normal(seeds[9], (HEADS * HD,), jnp.float32), 0.25, 1.75).astype(jnp.bfloat16)
    norm_key = jnp.clip(1.0 + 0.15 * jax.random.normal(seeds[10], (HEADS * HD,), jnp.float32), 0.25, 1.75).astype(jnp.bfloat16)
    norm_moe = jnp.clip(1.0 + 0.15 * jax.random.normal(seeds[11], (D,), jnp.float32), 0.25, 1.75).astype(jnp.bfloat16)
    w_router = scatter_about(seeds[12], (D, EXPERTS), (4 * D) ** -0.5, 0.0625)
    w_gate = scatter_about(seeds[13], (EXPERTS, D, FF), D ** -0.5, 0.125, ((0, 16),))
    w_up = scatter_about(seeds[14], (EXPERTS, D, FF), D ** -0.5, 0.125, ((0, 16),))
    w_down = scatter_about(seeds[15], (EXPERTS, FF, D), (max(FF // 64, 1)) ** -0.5, 1.5, ((0, 16),))
    return {"tokens": tokens, "cotangent": cotangent, "valid": valid, "routes": routes, "w_query": w_query, "w_key": w_key, "w_value": w_value, "w_out": w_out, "norm_attn": norm_attn, "norm_query": norm_query, "norm_key": norm_key, "norm_moe": norm_moe, "w_router": w_router, "w_gate": w_gate, "w_up": w_up, "w_down": w_down}


@jax.custom_vjp
def low(v):
    return lax.optimization_barrier(v.astype(jnp.bfloat16)).astype(jnp.float32)

@jax.custom_vjp
def low_back(v):
    return v

def low_keep(v):
    return (low(v), None)

def low_pass(kept, grad):
    return (grad,)

def back_keep(v):
    return (v, None)

def back_low(kept, grad):
    return (low(grad),)
low.defvjp(low_keep, low_pass)
low_back.defvjp(back_keep, back_low)
EPSILON = 1e-05
THETA = 10000.0
NEGATIVE = -1e+30
HIGHEST = lax.Precision.HIGHEST

def token_info(token_ids):
    span = PROMPT + NCONT * CONT
    local = token_ids % span
    group = token_ids // span
    branch = jnp.where(local < PROMPT, -1, (local - PROMPT) // CONT)
    place = jnp.where(local < PROMPT, local, PROMPT + (local - PROMPT) % CONT)
    return (group, local, branch, place)

def allowed(query_ids, key_ids):
    query_group, query_local, query_branch, query_place = token_info(query_ids)
    key_group, key_local, key_branch, key_place = token_info(key_ids)
    same = query_group[:, None] == key_group[None, :]
    earlier = key_local[None, :] <= query_local[:, None]
    prompt_key = (key_branch[None, :] < 0) & ((query_branch[:, None] >= 0) | earlier)
    own_key = (key_branch[None, :] >= 0) & (key_branch[None, :] == query_branch[:, None]) & earlier
    return same & (prompt_key | own_key)

def rotation(place):
    frequency = THETA ** (-2.0 * jnp.arange(HD // 2, dtype=jnp.float32) / HD)
    angle = place.astype(jnp.float32)[:, None] * frequency[None, :]
    return (jnp.cos(angle), jnp.sin(angle))

def rotate(values, cosine, sine):
    first = values[..., :HD // 2]
    second = values[..., HD // 2:]
    cos_row = cosine[:, None, :]
    sin_row = sine[:, None, :]
    return jnp.concatenate([first * cos_row - second * sin_row, second * cos_row + first * sin_row], -1)

def slot_layout(routes):
    count = routes.shape[0]
    blocks = count // TOK_DEV
    flat = routes.reshape(-1)
    token = jnp.arange(count * TOP, dtype=jnp.int32) // TOP
    onehot = (flat[:, None] == jnp.arange(EXPERTS, dtype=jnp.int32)[None, :]).astype(jnp.int32)
    grouped = onehot.reshape(blocks, TOK_DEV * TOP, EXPERTS)
    before = jnp.cumsum(grouped, 1) - grouped
    rank = lax.optimization_barrier(jnp.sum(before * grouped, -1)).reshape(-1)
    width = blocks * CAP
    slot = (flat * width + token // TOK_DEV * CAP + rank).astype(jnp.int32)
    table = jnp.full((EXPERTS * width,), count, jnp.int32).at[slot].set(token)
    return (table.reshape(EXPERTS, width), slot)

def layer(stream, query_w, key_w, value_w, out_w, attn_gain, query_gain, key_gain, moe_gain, router_w, gate_w, up_w, down_w, routes, table, slot):
    count = stream.shape[0]
    inv_one = lax.rsqrt(lax.optimization_barrier(jnp.mean(stream * stream, -1, keepdims=True)) + EPSILON)
    normed = low(stream * inv_one * attn_gain)
    query = low_back(jnp.dot(normed, query_w, precision=HIGHEST))
    key = low_back(jnp.dot(normed, key_w, precision=HIGHEST))
    value = low_back(jnp.dot(normed, value_w, precision=HIGHEST))
    query = query * lax.rsqrt(lax.optimization_barrier(jnp.mean(query * query, -1, keepdims=True)) + EPSILON) * query_gain
    key = key * lax.rsqrt(lax.optimization_barrier(jnp.mean(key * key, -1, keepdims=True)) + EPSILON) * key_gain
    token_ids = jnp.arange(count, dtype=jnp.int32)
    place = token_info(token_ids)[3]
    cosine, sine = rotation(place)
    heads = query_w.shape[1] // HD
    query_rot = low(rotate(query.reshape(count, heads, HD), cosine, sine))
    key_rot = low(rotate(key.reshape(count, heads, HD), cosine, sine))
    value_b = low(value.reshape(count, heads, HD))
    mask = allowed(token_ids, token_ids)
    scale = 1.0 / math.sqrt(HD)

    def one_head(operands):
        query_head, key_head, value_head = operands
        scores = jnp.dot(query_head, key_head.T, precision=HIGHEST) * scale
        scores = low_back(jnp.where(mask, scores, NEGATIVE))
        weights = jax.nn.softmax(scores, -1)
        return jnp.dot(low(weights), value_head, precision=HIGHEST)
    attended = lax.map(jax.checkpoint(one_head), (jnp.transpose(query_rot, (1, 0, 2)), jnp.transpose(key_rot, (1, 0, 2)), jnp.transpose(value_b, (1, 0, 2))))
    attended = low_back(low(jnp.transpose(attended, (1, 0, 2)).reshape(count, heads * HD)))
    branch = low_back(jnp.dot(attended, out_w, precision=HIGHEST))
    hidden = stream + branch
    inv_two = lax.rsqrt(lax.optimization_barrier(jnp.mean(hidden * hidden, -1, keepdims=True)) + EPSILON)
    moe_in = low(hidden * inv_two * moe_gain)
    logits = low_back(jnp.dot(moe_in, router_w, precision=HIGHEST))
    router_probs = jax.nn.softmax(logits, -1)
    gates = jnp.take_along_axis(router_probs, routes, 1)
    padded = jnp.concatenate([moe_in, jnp.zeros((1, moe_in.shape[1]), moe_in.dtype)], 0)

    def one_expert(operands):
        index, expert_gate, expert_up, expert_down = operands
        inputs = low_back(jnp.take(padded, index, axis=0))
        gate_pre = low_back(jnp.dot(inputs, expert_gate, precision=HIGHEST))
        up_pre = low_back(jnp.dot(inputs, expert_up, precision=HIGHEST))
        inner = low(jax.nn.silu(gate_pre) * up_pre)
        return low_back(low(jnp.dot(inner, expert_down, precision=HIGHEST)))
    outputs = lax.map(one_expert, (table, gate_w, up_w, down_w))
    routed = jnp.take(outputs.reshape(-1, outputs.shape[2]), slot, axis=0).reshape(count, TOP, outputs.shape[2])
    moe = lax.optimization_barrier(jnp.sum(gates[:, :, None] * routed, 1))
    final = hidden + moe
    return (final, (branch, hidden, moe))

def reference(tokens, cotangent, valid, routes, w_query, w_key, w_value, w_out, norm_attn, norm_query, norm_key, norm_moe, w_router, w_gate, w_up, w_down):
    table, slot = slot_layout(routes)
    floats = tuple((array.astype(jnp.float32) for array in (tokens, w_query, w_key, w_value, w_out, norm_attn, norm_query, norm_key, norm_moe, w_router, w_gate, w_up, w_down)))

    def wrapped(*inputs):
        return layer(*inputs, routes, table, slot)
    final, pullback, extras = jax.vjp(wrapped, *floats, has_aux=True)
    mask = valid.astype(jnp.float32)
    grads = pullback(cotangent.astype(jnp.float32) * mask[:, None])
    branch, hidden, moe = extras
    count = jnp.maximum(jnp.sum(mask), 1.0)

    def measure(values):
        return jnp.sum(values * values * mask[:, None]) / (count * D)
    rms = jnp.sqrt(jnp.stack([measure(floats[0]), measure(branch), measure(hidden), measure(moe), measure(final)]))
    return (final.astype(jnp.bfloat16), grads[0], grads[1], grads[2], grads[3], grads[4], grads[5], grads[6], grads[7], grads[8], grads[9], grads[10], grads[11], grads[12], rms)
```

```python
import functools

import jax
import jax.numpy as jnp
from jax import lax
from jax.experimental import pallas as pl
from jax.experimental.pallas import tpu as pltpu
from jax.sharding import PartitionSpec as P

D = 2048
HD = 128
TOP = 8
PROMPT = 2048
CONT = 256
NCONT = 8

EPSILON = 1e-05
THETA = 10000.0
NEGATIVE = -1e30


LOG2E = 1.4426950408889634
NT = (((1,), (1,)), ((), ()))


def block_parts(w, rows, prompt_blocks, paired, limit):
    def cut(plane, count):
        return [
            (plane, first, min(limit, count - first), None) for first in range(0, count, limit)
        ]

    if w is None:
        parts = cut(0, prompt_blocks * rows) + cut(1, prompt_blocks * rows)
        own = None
        if paired:
            parts.append((1, None, rows, "side"))
    else:
        own = w * rows
        parts = cut(0, own) + cut(1, own) + [(1, own, rows, "side")]
    return parts + [(0, own, rows, "causal")]


def for_blocks(blocks, prompt_blocks, one):
    for w in range(prompt_blocks):
        one(w, w)

    def body(w, carry):
        one(None, w)
        return carry

    lax.fori_loop(prompt_blocks, blocks, body, 0)


def masked_scores(score, mask, side, rows):
    if mask == "causal":
        key = lax.broadcasted_iota(jnp.int32, (rows, rows), 0)
        query = lax.broadcasted_iota(jnp.int32, (rows, rows), 1)
        return jnp.where(key <= query, score, NEGATIVE)
    if mask == "side":
        return jnp.where(side == 1, score, NEGATIVE)
    return score


def attend_kernel(rows, prompt_blocks, paired, side_ref, q_ref, k_ref, v_ref, ko_ref, vo_ref, o_ref, lse_ref, vt_ref):
    half, columns = q_ref.shape
    side = side_ref[0]
    for h in range(columns // HD):
        hs = slice(h * HD, (h + 1) * HD)
        for plane, ref in enumerate((v_ref, vo_ref)):
            vt_ref[plane, hs, :] = ref[:, hs].T

    def one(w, w_index):
        start = w_index * rows if w is not None else pl.multiple_of(w_index * rows, rows)
        for h in range(columns // HD):
            hs = slice(h * HD, (h + 1) * HD)
            query = q_ref[pl.ds(start, rows), hs]
            scores = []
            for plane, first, count, mask in block_parts(w, rows, prompt_blocks, paired, 512):
                at = pl.ds(start if first is None else first, count)
                key = (k_ref, ko_ref)[plane][at, hs]
                score = lax.dot_general(key, query, NT, preferred_element_type=jnp.float32)
                score = score * (HD**-0.5 * LOG2E)
                scores.append((plane, at, masked_scores(score, mask, side, rows)))
            largest = functools.reduce(
                jnp.maximum, [jnp.max(score, 0, keepdims=True) for _, _, score in scores]
            )
            total = jnp.zeros((1, rows), jnp.float32)
            mixed = jnp.zeros((HD, rows), jnp.float32)
            for plane, at, score in scores:
                weight = jnp.exp2(score - largest)
                total = total + jnp.sum(weight, 0, keepdims=True)
                mixed = mixed + jnp.dot(
                    vt_ref[plane, hs, at], weight.astype(jnp.bfloat16), preferred_element_type=jnp.float32
                )
            o_ref[pl.ds(start, rows), hs] = (mixed / total).T.astype(jnp.bfloat16)
            lse_ref[h : h + 1, pl.ds(start, rows)] = largest + jnp.log(total) * LOG2E

    for_blocks(half // rows, prompt_blocks, one)


def attend_back_kernel(
    rows, prompt_blocks, paired, side_ref, q_ref, k_ref, v_ref, ko_ref, vo_ref, do_ref, o_ref, lse_ref,
    dq_ref, dk_ref, dv_ref, dko_ref, dvo_ref, kt_ref,
):
    half, columns = q_ref.shape
    side = side_ref[0]
    for ref in (dk_ref, dv_ref, dko_ref, dvo_ref):
        ref[...] = jnp.zeros_like(ref)
    for h in range(columns // HD):
        hs = slice(h * HD, (h + 1) * HD)
        for plane, ref in enumerate((k_ref, ko_ref)):
            kt_ref[plane, hs, :] = ref[:, hs].T

    def one(w, w_index):
        start = w_index * rows if w is not None else pl.multiple_of(w_index * rows, rows)
        for h in range(columns // HD):
            hs = slice(h * HD, (h + 1) * HD)
            query = q_ref[pl.ds(start, rows), hs]
            grad = do_ref[pl.ds(start, rows), hs]
            product = grad.astype(jnp.float32) * o_ref[pl.ds(start, rows), hs].astype(jnp.float32)
            delta = jnp.sum(product.T, 0, keepdims=True)
            lse = lse_ref[h : h + 1, pl.ds(start, rows)]
            back = jnp.zeros((HD, rows), jnp.float32)
            for plane, first, count, mask in block_parts(w, rows, prompt_blocks, paired, 512):
                at = pl.ds(start if first is None else first, count)
                key = (k_ref, ko_ref)[plane][at, hs]
                value = (v_ref, vo_ref)[plane][at, hs]
                score = lax.dot_general(key, query, NT, preferred_element_type=jnp.float32)
                score = masked_scores(score * (HD**-0.5 * LOG2E), mask, side, rows)
                weight = jnp.exp2(score - lse)
                grad_weight = lax.dot_general(value, grad, NT, preferred_element_type=jnp.float32)
                grad_score = (weight * (grad_weight - delta)).astype(jnp.bfloat16)
                dv = (dv_ref, dvo_ref)[plane]
                dv[at, hs] += jnp.dot(weight.astype(jnp.bfloat16), grad, preferred_element_type=jnp.float32)
                dk = (dk_ref, dko_ref)[plane]
                dk[at, hs] += jnp.dot(grad_score, query, preferred_element_type=jnp.float32) * HD**-0.5
                back = back + jnp.dot(kt_ref[plane, hs, at], grad_score, preferred_element_type=jnp.float32)
            dq_ref[pl.ds(start, rows), hs] = back.T * HD**-0.5

    for_blocks(half // rows, prompt_blocks, one)


def attention_calls(rows, half, columns, prompt_blocks, paired):
    smem = pl.BlockSpec(memory_space=pltpu.SMEM)
    vmem = pl.BlockSpec(memory_space=pltpu.VMEM)
    heads = columns // HD
    params = pltpu.CompilerParams(vmem_limit_bytes=60 * 2**20)
    wide16 = jax.ShapeDtypeStruct((half, columns), jnp.bfloat16)
    wide32 = jax.ShapeDtypeStruct((half, columns), jnp.float32)
    work = half * half * columns * 2
    forward = pl.pallas_call(
        functools.partial(attend_kernel, rows, prompt_blocks, paired),
        out_shape=(wide16, jax.ShapeDtypeStruct((heads, half), jnp.float32)),
        in_specs=[smem] + [vmem] * 5,
        out_specs=(vmem, vmem),
        scratch_shapes=[pltpu.VMEM((2, columns, half), jnp.bfloat16)],
        compiler_params=params,
        cost_estimate=pl.CostEstimate(flops=2 * work, bytes_accessed=half * columns * 12, transcendentals=0),
    )
    backward = pl.pallas_call(
        functools.partial(attend_back_kernel, rows, prompt_blocks, paired),
        out_shape=(wide32,) * 5,
        in_specs=[smem] + [vmem] * 8,
        out_specs=(vmem,) * 5,
        scratch_shapes=[pltpu.VMEM((2, columns, half), jnp.bfloat16)],
        compiler_params=params,
        cost_estimate=pl.CostEstimate(flops=5 * work, bytes_accessed=half * columns * 40, transcendentals=0),
    )
    return forward, backward


def positions(token_ids):
    local = token_ids % (PROMPT + NCONT * CONT)
    return jnp.where(local < PROMPT, local, PROMPT + (local - PROMPT) % CONT)


def rotation(place):
    frequency = THETA ** (-2.0 * jnp.arange(HD // 2, dtype=jnp.float32) / HD)
    angle = place.astype(jnp.float32)[:, None] * frequency[None, :]
    cosine, sine = jnp.cos(angle), jnp.sin(angle)
    return jnp.concatenate([cosine, cosine], 1), jnp.concatenate([-sine, sine], 1)


def swap_halves(values):
    return jnp.concatenate([values[..., HD // 2 :], values[..., : HD // 2]], -1)


def rotate(values, cosine, sine):
    rows, columns = values.shape
    heads = values.reshape(rows, columns // HD, HD)
    turned = heads * cosine[:, None, :] + swap_halves(heads) * sine[:, None, :]
    return turned.reshape(rows, columns)


def dot(a, b):
    return jnp.dot(a, b, preferred_element_type=jnp.float32)


def dot_nt(a, b):
    return lax.dot_general(a, b, (((1,), (1,)), ((), ())), preferred_element_type=jnp.float32)


def dot_tn(a, b):
    return lax.dot_general(a, b, (((0,), (0,)), ((), ())), preferred_element_type=jnp.float32)


def shards(
    tokens,
    cotangent,
    valid,
    routes,
    w_query,
    w_key,
    w_value,
    w_out,
    norm_attn,
    norm_query,
    norm_key,
    norm_moe,
    w_router,
    w_gate,
    w_up,
    w_down,
):
    bf16, f32 = jnp.bfloat16, jnp.float32
    wide_count = lax.axis_size("wide")
    narrow_count = lax.axis_size("narrow")
    rows = tokens.shape[0]
    half = rows * wide_count
    columns = w_query.shape[1]
    experts = w_router.shape[1]
    capacity = min(max(rows * TOP * 5 // (4 * experts), 2), rows)
    assert narrow_count == 2 and CONT in (rows, 2 * rows)
    side = lax.axis_index("narrow")
    place = lax.axis_index("wide")
    swap = [(0, 1), (1, 0)]
    prompt_blocks = PROMPT // (rows * narrow_count)
    attend, attend_back = attention_calls(rows, half, columns, prompt_blocks, CONT == 2 * rows)
    side_array = side.astype(jnp.int32).reshape(1)

    stream = tokens.astype(f32)
    inv_one = lax.rsqrt(jnp.mean(stream * stream, -1, keepdims=True) + EPSILON)
    gain_one = norm_attn.astype(f32)
    normed = (stream * inv_one * gain_one).astype(bf16)
    normed_plane = lax.all_gather(normed, "wide", axis=0, tiled=True)
    mask = valid.astype(f32)[:, None]
    grad_final = cotangent.astype(f32) * mask
    routes_plane = lax.all_gather(routes, "wide", axis=0, tiled=True)
    w_out_all = lax.all_gather(w_out, "wide", axis=0, tiled=True)
    grad_plane = lax.all_gather(grad_final.astype(bf16), "wide", axis=0, tiled=True)
    other_weights = [lax.ppermute(w, "narrow", swap) for w in (w_gate[0], w_up[0], w_down[0])]

    joined = jnp.concatenate([w_query, w_key, w_value], 1)
    raw = dot(normed_plane, joined)
    query_raw, key_raw, value_raw = (raw[:, i * columns : (i + 1) * columns] for i in range(3))
    sums = lax.psum(jnp.stack([jnp.sum(query_raw * query_raw, -1), jnp.sum(key_raw * key_raw, -1)]), "wide")
    inv_query, inv_key = lax.rsqrt(sums / D + EPSILON)[:, :, None]
    gain_query = norm_query.astype(f32)
    gain_key = norm_key.astype(f32)
    plane_ids = (
        (jnp.arange(wide_count, dtype=jnp.int32)[:, None] * narrow_count + side) * rows
        + jnp.arange(rows, dtype=jnp.int32)[None, :]
    ).reshape(half)
    cosine, sine = rotation(positions(plane_ids))
    query_rot = rotate(query_raw * inv_query * gain_query, cosine, sine).astype(bf16)
    key_rot = rotate(key_raw * inv_key * gain_key, cosine, sine).astype(bf16)
    value_b = value_raw.astype(bf16)
    key_other = lax.ppermute(key_rot, "narrow", swap)
    value_other = lax.ppermute(value_b, "narrow", swap)
    attended, lse = attend(side_array, query_rot, key_rot, value_b, key_other, value_other)

    attended_own = lax.all_to_all(attended, "wide", split_axis=0, concat_axis=1, tiled=True)
    branch = dot(attended_own, w_out_all)
    hidden = stream + branch
    inv_two = lax.rsqrt(jnp.mean(hidden * hidden, -1, keepdims=True) + EPSILON)
    gain_two = norm_moe.astype(f32)
    moe_in = (hidden * inv_two * gain_two).astype(bf16)
    moe_plane = lax.all_gather(moe_in, "wide", axis=0, tiled=True)

    probs = jax.nn.softmax(dot(moe_plane, w_router), -1)
    named = jnp.any(routes_plane[:, :, None] == jnp.arange(experts, dtype=jnp.int32), 1)
    gates_dense = jnp.where(named, probs, 0.0)
    blocks = lambda a: a.reshape(wide_count, rows, -1)
    earlier = (jnp.arange(rows)[:, None] < jnp.arange(rows)[None, :]).astype(bf16)

    def pick(expert):
        chosen = jnp.take(named, expert, axis=1).reshape(wide_count, rows)
        rank = dot(chosen.astype(bf16), earlier).astype(jnp.int32)
        slot = jnp.where(chosen, rank, -1)
        onehot = (jnp.arange(capacity, dtype=jnp.int32)[None, :, None] == slot[:, None, :]).astype(bf16)
        return onehot

    def compact(onehot, values):
        return jnp.einsum(
            "wcr,wrd->wcd", onehot, blocks(values), preferred_element_type=f32
        ).astype(bf16).reshape(wide_count * capacity, -1)

    def spread(onehot, values):
        return jnp.einsum(
            "wcr,wcd->wrd", onehot, values.reshape(wide_count, capacity, -1), preferred_element_type=f32
        ).reshape(half, -1)

    moe_part = 0.0
    grad_part = 0.0
    mixing = 0.0
    expert_grads = []
    for expert, (gate_w, up_w, down_w) in (
        (place * narrow_count + side, (w_gate[0], w_up[0], w_down[0])),
        (place * narrow_count + 1 - side, other_weights),
    ):
        onehot = pick(expert)
        inputs = compact(onehot, moe_plane)
        grads = compact(onehot, grad_plane)
        gate_own = jnp.take(gates_dense, expert, axis=1)
        gate = jnp.sum(
            onehot.astype(f32) * gate_own.reshape(wide_count, 1, rows), -1
        ).reshape(wide_count * capacity, 1)
        gate_pre = dot(inputs, gate_w)
        up_pre = dot(inputs, up_w)
        back = dot_nt(grads, down_w)
        sigmoid = jax.nn.sigmoid(gate_pre)
        silu = gate_pre * sigmoid
        inner = silu * up_pre
        inner_gated = (gate * inner).astype(bf16)
        grad_gate_row = jnp.sum(inner * back, -1)
        grad_inner = gate * back
        grad_gate_pre = (grad_inner * up_pre * sigmoid * (1.0 + gate_pre * (1.0 - sigmoid))).astype(bf16)
        grad_up_pre = (grad_inner * silu).astype(bf16)
        route_in = (dot_nt(grad_gate_pre, gate_w) + dot_nt(grad_up_pre, up_w)).astype(bf16)
        grad_part = grad_part + spread(onehot, route_in)
        moe_part = moe_part + spread(onehot, dot(inner_gated, down_w).astype(bf16))
        grad_gates = jnp.sum(
            onehot.astype(f32) * grad_gate_row.reshape(wide_count, capacity, 1), 1
        ).reshape(half, 1)
        weight = gate_own[:, None] * grad_gates
        here = (jnp.arange(experts, dtype=jnp.int32) == expert).astype(f32)
        mixing = mixing + weight * (here[None, :] - probs)
        expert_grads.append(
            (dot_tn(inputs, grad_gate_pre), dot_tn(inputs, grad_up_pre), dot_tn(inner_gated, grads))
        )
    mixing = mixing.astype(bf16)
    grad_part = grad_part + dot_nt(mixing, w_router)
    grad_moe_in = lax.psum_scatter(
        grad_part.astype(bf16), "wide", scatter_dimension=0, tiled=True
    ).astype(f32)
    moe = lax.psum_scatter(moe_part.astype(bf16), "wide", scatter_dimension=0, tiled=True).astype(f32)
    grad_router = dot_tn(moe_plane, mixing)
    partner = [lax.ppermute(g.astype(bf16), "narrow", swap) for g in expert_grads[1]]
    grad_gate_w, grad_up_w, grad_down_w = (
        (own + other.astype(f32))[None] for own, other in zip(expert_grads[0], partner)
    )

    final = hidden + moe
    output = final.astype(bf16)
    grad_gain_two = jnp.sum(grad_moe_in * hidden * inv_two, 0)
    grad_hidden = (
        grad_final
        + inv_two * gain_two * grad_moe_in
        - hidden * inv_two**3 * jnp.sum(grad_moe_in * gain_two * hidden, -1, keepdims=True) / D
    )
    grad_branch = grad_hidden.astype(bf16)
    grad_attended_own = dot_nt(grad_branch, w_out_all).astype(bf16)
    grad_attended = lax.all_to_all(grad_attended_own, "wide", split_axis=1, concat_axis=0, tiled=True)
    branch_plane = lax.all_gather(grad_branch, "wide", axis=0, tiled=True)
    grad_out = dot_tn(attended, branch_plane)

    grad_query_rot, grad_key_rot, grad_value, grad_key_other, grad_value_other = attend_back(
        side_array, query_rot, key_rot, value_b, key_other, value_other, grad_attended, attended, lse
    )
    grad_key_rot = grad_key_rot + lax.ppermute(grad_key_other.astype(bf16), "narrow", swap).astype(f32)
    grad_value = grad_value + lax.ppermute(grad_value_other.astype(bf16), "narrow", swap).astype(f32)
    grad_query_normed = rotate(grad_query_rot, cosine, -sine)
    grad_key_normed = rotate(grad_key_rot, cosine, -sine)
    dots = lax.psum(
        jnp.stack(
            [
                jnp.sum(grad_query_normed * gain_query * query_raw, -1),
                jnp.sum(grad_key_normed * gain_key * key_raw, -1),
            ]
        ),
        "wide",
    )[:, :, None]
    grad_gain_query = jnp.sum(grad_query_normed * query_raw * inv_query, 0)
    grad_gain_key = jnp.sum(grad_key_normed * key_raw * inv_key, 0)
    grad_query_raw = inv_query * gain_query * grad_query_normed - query_raw * inv_query**3 * dots[0] / D
    grad_key_raw = inv_key * gain_key * grad_key_normed - key_raw * inv_key**3 * dots[1] / D
    grads_joined = jnp.concatenate([grad_query_raw, grad_key_raw, grad_value], 1).astype(bf16)
    grad_normed = lax.psum_scatter(
        dot_nt(grads_joined, joined).astype(bf16), "wide", scatter_dimension=0, tiled=True
    ).astype(f32)
    grad_weights = dot_tn(normed_plane, grads_joined)
    summed = lax.psum(
        (
            grad_weights.astype(bf16),
            grad_out.astype(bf16),
            grad_gain_query.astype(bf16),
            grad_gain_key.astype(bf16),
        ),
        "narrow",
    )
    grad_query_w, grad_key_w, grad_value_w = (
        summed[0][:, i * columns : (i + 1) * columns].astype(f32) for i in range(3)
    )
    grad_gain_one = jnp.sum(grad_normed * stream * inv_one, 0)
    grad_input = (
        grad_hidden
        + inv_one * gain_one * grad_normed
        - stream * inv_one**3 * jnp.sum(grad_normed * gain_one * stream, -1, keepdims=True) / D
    )
    stat_sums = jnp.stack([jnp.sum(v * v * mask) for v in (stream, branch, hidden, moe, final)])
    replicated = lax.psum(
        (
            grad_router.astype(bf16),
            grad_gain_one.astype(bf16),
            grad_gain_two.astype(bf16),
            stat_sums.astype(bf16),
            jnp.sum(mask).astype(bf16),
        ),
        ("wide", "narrow"),
    )
    grad_router, grad_gain_one, grad_gain_two, stat_sums, count = (v.astype(f32) for v in replicated)
    rms = jnp.sqrt(stat_sums / (jnp.maximum(count, 1.0) * D))
    return (
        output,
        grad_input,
        grad_query_w,
        grad_key_w,
        grad_value_w,
        summed[1].astype(f32),
        grad_gain_one,
        summed[2].astype(f32),
        summed[3].astype(f32),
        grad_gain_two,
        grad_router,
        grad_gate_w,
        grad_up_w,
        grad_down_w,
        rms,
    )


def solution(mesh):
    return jax.shard_map(
        shards,
        mesh=mesh,
        in_specs=(
            P(("grp", "wide", "narrow"), None),
            P(("grp", "wide", "narrow"), None),
            P(("grp", "wide", "narrow")),
            P(("grp", "wide", "narrow"), None),
            P(None, "wide"),
            P(None, "wide"),
            P(None, "wide"),
            P("wide", None),
            P(),
            P("wide"),
            P("wide"),
            P(),
            P(),
            P(("wide", "narrow"), None, None),
            P(("wide", "narrow"), None, None),
            P(("wide", "narrow"), None, None),
        ),
        out_specs=(
            P(("grp", "wide", "narrow"), None),
            P(("grp", "wide", "narrow"), None),
            P("grp", "wide"),
            P("grp", "wide"),
            P("grp", "wide"),
            P(("grp", "wide"), None),
            P("grp"),
            P(("grp", "wide")),
            P(("grp", "wide")),
            P("grp"),
            P("grp", None),
            P(("grp", "wide", "narrow"), None, None),
            P(("grp", "wide", "narrow"), None, None),
            P(("grp", "wide", "narrow"), None, None),
            P("grp"),
        ),
        check_vma=False,
    )
```

```python
import functools

import jax
import jax.numpy as jnp
from jax import lax
from jax.experimental import pallas as pl
from jax.experimental.pallas import tpu as pltpu
from jax.sharding import PartitionSpec as P

D = 2048
HD = 128
TOP = 8
PROMPT = 2048
CONT = 256
NCONT = 8

EPSILON = 1e-05
THETA = 10000.0
NEGATIVE = -1e30


LOG2E = 1.4426950408889634
NT = (((1,), (1,)), ((), ()))


def block_parts(w, rows, prompt_blocks, paired, limit):
    def cut(plane, count):
        return [
            (plane, first, min(limit, count - first), None) for first in range(0, count, limit)
        ]

    if w is None:
        parts = cut(0, prompt_blocks * rows) + cut(1, prompt_blocks * rows)
        own = None
        if paired:
            parts.append((1, None, rows, "side"))
    else:
        own = w * rows
        parts = cut(0, own) + cut(1, own) + [(1, own, rows, "side")]
    return parts + [(0, own, rows, "causal")]


def for_blocks(blocks, prompt_blocks, one):
    for w in range(prompt_blocks):
        one(w, w)

    def body(w, carry):
        one(None, w)
        return carry

    lax.fori_loop(prompt_blocks, blocks, body, 0)


def masked_scores(score, mask, side, rows):
    if mask == "causal":
        key = lax.broadcasted_iota(jnp.int32, (rows, rows), 0)
        query = lax.broadcasted_iota(jnp.int32, (rows, rows), 1)
        return jnp.where(key <= query, score, NEGATIVE)
    if mask == "side":
        return jnp.where(side == 1, score, NEGATIVE)
    return score


def attend_kernel(rows, prompt_blocks, paired, side_ref, q_ref, k_ref, v_ref, ko_ref, vo_ref, o_ref, lse_ref, vt_ref, vto_ref):
    half, columns = q_ref.shape
    side = side_ref[0]
    for h in range(columns // HD):
        hs = slice(h * HD, (h + 1) * HD)
        vt_ref[hs, :] = v_ref[:, hs].T
        vto_ref[hs, :] = vo_ref[:, hs].T

    def one(w, w_index):
        start = w_index * rows if w is not None else pl.multiple_of(w_index * rows, rows)
        for h in range(columns // HD):
            hs = slice(h * HD, (h + 1) * HD)
            query = q_ref[pl.ds(start, rows), hs]
            scores = []
            for plane, first, count, mask in block_parts(w, rows, prompt_blocks, paired, 512):
                at = pl.ds(start if first is None else first, count)
                key = (k_ref, ko_ref)[plane][at, hs]
                score = lax.dot_general(key, query, NT, preferred_element_type=jnp.float32)
                score = score * (HD**-0.5 * LOG2E)
                scores.append((plane, at, masked_scores(score, mask, side, rows)))
            largest = functools.reduce(
                jnp.maximum, [jnp.max(score, 0, keepdims=True) for _, _, score in scores]
            )
            total = jnp.zeros((1, rows), jnp.float32)
            mixed = jnp.zeros((HD, rows), jnp.float32)
            for plane, at, score in scores:
                weight = jnp.exp2(score - largest)
                total = total + jnp.sum(weight, 0, keepdims=True)
                mixed = mixed + jnp.dot(
                    (vt_ref, vto_ref)[plane][hs, at], weight.astype(jnp.bfloat16), preferred_element_type=jnp.float32
                )
            o_ref[pl.ds(start, rows), hs] = (mixed / total).T.astype(jnp.bfloat16)
            lse_ref[h : h + 1, pl.ds(start, rows)] = largest + jnp.log(total) * LOG2E

    for_blocks(half // rows, prompt_blocks, one)


def attend_back_kernel(
    rows, prompt_blocks, paired, side_ref, q_ref, k_ref, v_ref, ko_ref, vo_ref, do_ref, o_ref, lse_ref,
    dq_ref, dk_ref, dv_ref, dkb_ref, dvb_ref, kt_ref, kto_ref, dko_ref, dvo_ref,
):
    half, columns = q_ref.shape
    side = side_ref[0]
    for ref in (dk_ref, dv_ref, dko_ref, dvo_ref):
        ref[...] = jnp.zeros_like(ref)
    for h in range(columns // HD):
        hs = slice(h * HD, (h + 1) * HD)
        kt_ref[hs, :] = k_ref[:, hs].T
        kto_ref[hs, :] = ko_ref[:, hs].T

    def one(w, w_index):
        start = w_index * rows if w is not None else pl.multiple_of(w_index * rows, rows)
        for h in range(columns // HD):
            hs = slice(h * HD, (h + 1) * HD)
            query = q_ref[pl.ds(start, rows), hs]
            grad = do_ref[pl.ds(start, rows), hs]
            product = grad.astype(jnp.float32) * o_ref[pl.ds(start, rows), hs].astype(jnp.float32)
            delta = jnp.sum(product.T, 0, keepdims=True)
            lse = lse_ref[h : h + 1, pl.ds(start, rows)]
            back = jnp.zeros((HD, rows), jnp.float32)
            for plane, first, count, mask in block_parts(w, rows, prompt_blocks, paired, 512):
                at = pl.ds(start if first is None else first, count)
                key = (k_ref, ko_ref)[plane][at, hs]
                value = (v_ref, vo_ref)[plane][at, hs]
                score = lax.dot_general(key, query, NT, preferred_element_type=jnp.float32)
                score = masked_scores(score * (HD**-0.5 * LOG2E), mask, side, rows)
                weight = jnp.exp2(score - lse)
                grad_weight = lax.dot_general(value, grad, NT, preferred_element_type=jnp.float32)
                grad_score = (weight * (grad_weight - delta)).astype(jnp.bfloat16)
                dv = (dv_ref, dvo_ref)[plane]
                dv[at, hs] += jnp.dot(weight.astype(jnp.bfloat16), grad, preferred_element_type=jnp.float32)
                dk = (dk_ref, dko_ref)[plane]
                dk[at, hs] += jnp.dot(grad_score, query, preferred_element_type=jnp.float32) * HD**-0.5
                back = back + jnp.dot((kt_ref, kto_ref)[plane][hs, at], grad_score, preferred_element_type=jnp.float32)
            dq_ref[pl.ds(start, rows), hs] = back.T * HD**-0.5

    for_blocks(half // rows, prompt_blocks, one)
    dkb_ref[...] = dko_ref[...].astype(jnp.bfloat16)
    dvb_ref[...] = dvo_ref[...].astype(jnp.bfloat16)


def attention_calls(rows, half, shared, columns, prompt_blocks, paired):
    smem = pl.BlockSpec(memory_space=pltpu.SMEM)
    vmem = pl.BlockSpec(memory_space=pltpu.VMEM)
    heads = columns // HD
    params = pltpu.CompilerParams(vmem_limit_bytes=60 * 2**20)
    wide16 = jax.ShapeDtypeStruct((half, columns), jnp.bfloat16)
    wide32 = jax.ShapeDtypeStruct((half, columns), jnp.float32)
    work = half * half * columns * 2
    forward = pl.pallas_call(
        functools.partial(attend_kernel, rows, prompt_blocks, paired),
        out_shape=(wide16, jax.ShapeDtypeStruct((heads, half), jnp.float32)),
        in_specs=[smem] + [vmem] * 5,
        out_specs=(vmem, vmem),
        scratch_shapes=[pltpu.VMEM((columns, half), jnp.bfloat16), pltpu.VMEM((columns, shared), jnp.bfloat16)],
        compiler_params=params,
        cost_estimate=pl.CostEstimate(flops=2 * work, bytes_accessed=half * columns * 12, transcendentals=0),
    )
    backward = pl.pallas_call(
        functools.partial(attend_back_kernel, rows, prompt_blocks, paired),
        out_shape=(wide32,) * 3 + (jax.ShapeDtypeStruct((shared, columns), jnp.bfloat16),) * 2,
        in_specs=[smem] + [vmem] * 8,
        out_specs=(vmem,) * 5,
        scratch_shapes=[pltpu.VMEM((columns, half), jnp.bfloat16), pltpu.VMEM((columns, shared), jnp.bfloat16)]
        + [pltpu.VMEM((shared, columns), jnp.float32)] * 2,
        compiler_params=params,
        cost_estimate=pl.CostEstimate(flops=5 * work, bytes_accessed=half * columns * 40, transcendentals=0),
    )
    return forward, backward


MESH_ID = pl.DeviceIdType.MESH
ANY = pl.BlockSpec(memory_space=pl.ANY)
VMEM = pl.BlockSpec(memory_space=pltpu.VMEM)
LINE = 4


def position():
    grp, wide, narrow = (lax.axis_index(a) for a in ("grp", "wide", "narrow"))
    return grp, wide, narrow, wide // 2, lax.rem(wide, 2)


def greet(targets):
    barrier = pltpu.get_barrier_semaphore()
    for device, when in targets:
        def signal(device=device):
            pl.semaphore_signal(barrier, inc=1, device_id=device, device_id_type=MESH_ID)

        if when is None:
            signal()
        else:
            pl.when(when)(signal)
    peers = sum(1 if when is None else when.astype(jnp.int32) for _, when in targets)
    pl.semaphore_wait(barrier, peers)


def remote(src, dst, send, recv, device):
    return pltpu.make_async_remote_copy(
        src_ref=src, dst_ref=dst, send_sem=send, recv_sem=recv, device_id=device, device_id_type=MESH_ID
    )


def gather_kernel(count, *refs):
    ins, outs = refs[:count], refs[count : 2 * count]
    gather_body(count, ins, outs, *refs[2 * count :])


def gather_body(count, ins, outs, send, recv, local, more=(), begin=None, finish=None):
    grp, wide, narrow, line, cross = position()
    across = (grp, line * 2 + 1 - cross, narrow)
    above = (grp, wide + 2, narrow)
    below = (grp, wide - 2, narrow)
    has_above, has_below = line < LINE - 1, line > 0
    greet([(across, None), (above, has_above), (below, has_below), *more])

    def copy(i, source_line, way, device):
        slot = source_line * 2 + cross
        return remote(outs[i].at[slot], outs[i].at[slot], send.at[i, way, source_line], recv.at[i, slot], device)

    def own(i, way, device):
        return remote(ins[i], outs[i].at[wide], send.at[i, way, line], recv.at[i, wide], device)

    mine = [pltpu.make_async_copy(ins[i], outs[i].at[wide], local.at[i]) for i in range(count)]
    for i in range(count):
        pl.when(has_above)(own(i, 1, above).start)
        pl.when(has_below)(own(i, 2, below).start)
        own(i, 0, across).start()
        mine[i].start()
    if begin is not None:
        begin()
    for i in range(count):
        for distance in range(1, LINE):
            for sign in (-1, 1):
                source = line + sign * distance

                @pl.when((source >= 0) & (source < LINE))
                def _(i=i, source=source, sign=sign):
                    slot = source * 2 + cross
                    copy(i, source, 0, across).wait_recv()
                    onward = above if sign < 0 else below

                    @pl.when(has_above if sign < 0 else has_below)
                    def _():
                        copy(i, source, 1 if sign < 0 else 2, onward).start()

                    copy(i, source, 0, across).start()

    for i in range(count):
        for source in range(LINE):
            other = source * 2 + 1 - cross
            remote(ins[i], outs[i].at[other], send.at[i, 0, 0], recv.at[i, other], across).wait_recv()
        for source in range(LINE):
            remote(ins[i], outs[i].at[0], send.at[i, 0, source], recv.at[i, 0], across).wait_send()

            @pl.when(has_above & (source <= line))
            def _(i=i, source=source):
                remote(ins[i], outs[i].at[0], send.at[i, 1, source], recv.at[i, 0], above).wait_send()

            @pl.when(has_below & (source >= line))
            def _(i=i, source=source):
                remote(ins[i], outs[i].at[0], send.at[i, 2, source], recv.at[i, 0], below).wait_send()

        mine[i].wait()
    if finish is not None:
        finish()


def gather_wide(arrays, collective_id):
    count = len(arrays)
    size = lax.axis_size("wide")
    if size != 2 * LINE:
        return [lax.all_gather(a, "wide", axis=0) for a in arrays]
    return pl.pallas_call(
        functools.partial(gather_kernel, count),
        out_shape=[jax.ShapeDtypeStruct((size, *a.shape), a.dtype) for a in arrays],
        in_specs=[ANY] * count,
        out_specs=[ANY] * count,
        scratch_shapes=[
            pltpu.SemaphoreType.DMA((count, 3, LINE)),
            pltpu.SemaphoreType.DMA((count, size)),
            pltpu.SemaphoreType.DMA((count,)),
        ],
        compiler_params=pltpu.CompilerParams(collective_id=collective_id, has_side_effects=True),
    )(*arrays)


def scatter_kernel(part_ref, out_ref, held, from_across, from_line, load, send, recv_a, recv_l):
    grp, wide, narrow, line, cross = position()
    across = (grp, line * 2 + 1 - cross, narrow)
    above = (grp, wide + 2, narrow)
    below = (grp, wide - 2, narrow)
    has_above, has_below = line < LINE - 1, line > 0
    f32 = jnp.float32
    greet([(across, None), (above, has_above), (below, has_below)])

    order = []
    for distance in range(LINE - 1, 0, -1):
        for sign in (1, -1):
            order.append((distance, sign))

    def valid(owner):
        return (owner >= 0) & (owner < LINE)

    def across_copy(owner):
        return remote(
            part_ref.at[owner * 2 + 1 - cross], from_across.at[owner], send.at[0, owner], recv_a.at[owner], across
        )

    def load_copy(owner):
        return pltpu.make_async_copy(part_ref.at[owner * 2 + cross], held.at[owner], load.at[owner])

    def line_copy(owner, up):
        return remote(
            held.at[owner],
            from_line.at[0 if up else 1, owner],
            send.at[1, owner],
            recv_l.at[0 if up else 1, owner],
            above if up else below,
        )

    for distance, sign in order + [(0, 1)]:
        owner = line + sign * distance

        @pl.when(valid(owner))
        def _(owner=owner):
            across_copy(owner).start()
            load_copy(owner).start()

    for distance, sign in order:
        owner = line + sign * distance

        @pl.when(valid(owner))
        def _(owner=owner, sign=sign):
            load_copy(owner).wait()
            across_copy(owner).wait_recv()
            up = sign > 0
            came = has_below if up else has_above
            total = held[owner].astype(f32) + from_across[owner].astype(f32)

            @pl.when(came)
            def _():
                line_copy(owner, up).wait_recv()
                held[owner] = (total + from_line[0 if up else 1, owner].astype(f32)).astype(held.dtype)

            @pl.when(jnp.logical_not(came))
            def _():
                held[owner] = total.astype(held.dtype)

            line_copy(owner, up).start()

    load_copy(line).wait()
    across_copy(line).wait_recv()
    out_ref[...] = held[line].astype(f32) + from_across[line].astype(f32)

    @pl.when(has_below)
    def _():
        line_copy(line, True).wait_recv()
        out_ref[...] += from_line[0, line].astype(f32)

    @pl.when(has_above)
    def _():
        line_copy(line, False).wait_recv()
        out_ref[...] += from_line[1, line].astype(f32)

    for owner in range(LINE):
        across_copy(owner).wait_send()

        @pl.when(owner > line)
        def _(owner=owner):
            line_copy(owner, True).wait_send()

        @pl.when(owner < line)
        def _(owner=owner):
            line_copy(owner, False).wait_send()


def scatter_wide(part, collective_id):
    size, rows, columns = part.shape
    if size != 2 * LINE:
        return lax.psum_scatter(part, "wide", scatter_dimension=0, tiled=False).astype(jnp.float32)
    block = (LINE, rows, columns)
    return pl.pallas_call(
        scatter_kernel,
        out_shape=jax.ShapeDtypeStruct((rows, columns), jnp.float32),
        in_specs=[ANY],
        out_specs=VMEM,
        scratch_shapes=[
            pltpu.VMEM(block, part.dtype),
            pltpu.VMEM(block, part.dtype),
            pltpu.VMEM((2, *block), part.dtype),
            pltpu.SemaphoreType.DMA((LINE,)),
            pltpu.SemaphoreType.DMA((2, LINE)),
            pltpu.SemaphoreType.DMA((LINE,)),
            pltpu.SemaphoreType.DMA((2, LINE)),
        ],
        compiler_params=pltpu.CompilerParams(
            collective_id=collective_id, has_side_effects=True, vmem_limit_bytes=48 * 2**20
        ),
    )(part)


def sum_kernel(x_ref, o_ref, held, send, recv):
    grp, wide, narrow, _, _ = position()
    size = held.shape[0] + 1
    others = [(grp, lax.rem(wide + k, size), narrow) for k in range(1, size)]
    greet([(device, None) for device in others])
    copies = [
        remote(x_ref, held.at[k], send.at[k], recv.at[k], device) for k, device in enumerate(others)
    ]
    for copy in copies:
        copy.start()
    for copy in copies:
        copy.wait()
    total = x_ref[...]
    for k in range(size - 1):
        total = total + held[k]
    o_ref[...] = total


def sum_wide(x, collective_id):
    size = lax.axis_size("wide")
    if size != 2 * LINE:
        return lax.psum(x, "wide")
    return pl.pallas_call(
        sum_kernel,
        out_shape=jax.ShapeDtypeStruct(x.shape, x.dtype),
        in_specs=[VMEM],
        out_specs=VMEM,
        scratch_shapes=[
            pltpu.VMEM((size - 1, *x.shape), x.dtype),
            pltpu.SemaphoreType.DMA((size - 1,)),
            pltpu.SemaphoreType.DMA((size - 1,)),
        ],
        compiler_params=pltpu.CompilerParams(collective_id=collective_id, has_side_effects=True),
    )(x)


def start_kernel(count, swaps, *refs):
    ins, given = refs[:count], refs[count : count + swaps]
    outs = refs[count + swaps : 2 * count + swaps]
    got = refs[2 * count + swaps : 2 * (count + swaps)]
    send, recv, local, swap_send, swap_recv, twin_send, twin_recv = refs[2 * (count + swaps) :]
    grp, wide, narrow, line, cross = position()
    partner = (grp, wide, 1 - narrow)
    twin = (1 - grp, wide, narrow)

    def half(ref, which):
        size = ref.shape[0] // 2
        return ref.at[pl.ds(pl.multiple_of(which * size, size), size)]

    def swap(i):
        return remote(half(given[i], grp), half(got[i], grp), swap_send.at[i], swap_recv.at[i], partner)

    def share(i, which):
        return remote(half(got[i], which), half(got[i], which), twin_send.at[i], twin_recv.at[i], twin)

    def begin():
        for i in range(swaps):
            swap(i).start()

    def finish():
        for i in range(swaps):
            swap(i).wait_recv()
            share(i, grp).start()
        for i in range(swaps):
            swap(i).wait_send()
            share(i, grp).wait_send()
            share(i, 1 - grp).wait_recv()

    gather_body(count, ins, outs, send, recv, local, [(partner, None), (twin, None)], begin, finish)


def start_exchange(arrays, weights, collective_id):
    size = lax.axis_size("wide")
    if size != 2 * LINE or lax.axis_size("grp") != 2:
        swap = [(0, 1), (1, 0)]
        return [lax.all_gather(a, "wide", axis=0) for a in arrays], [lax.ppermute(w, "narrow", swap) for w in weights]
    count, swaps = len(arrays), len(weights)
    out = pl.pallas_call(
        functools.partial(start_kernel, count, swaps),
        out_shape=[jax.ShapeDtypeStruct((size, *a.shape), a.dtype) for a in arrays]
        + [jax.ShapeDtypeStruct(w.shape, w.dtype) for w in weights],
        in_specs=[ANY] * (count + swaps),
        out_specs=[ANY] * (count + swaps),
        scratch_shapes=[
            pltpu.SemaphoreType.DMA((count, 3, LINE)),
            pltpu.SemaphoreType.DMA((count, size)),
            pltpu.SemaphoreType.DMA((count,)),
        ]
        + [pltpu.SemaphoreType.DMA((swaps,))] * 4,
        compiler_params=pltpu.CompilerParams(collective_id=collective_id, has_side_effects=True),
    )(*arrays, *weights)
    return out[:count], out[count:]


def sum_all_kernel(x_ref, o_ref, parts, total, send, recv, send_back, recv_back):
    grp, wide, narrow, _, _ = position()
    size, _, width = parts.shape
    me = wide * 2 + narrow
    ranks = [lax.rem(me + k, size) for k in range(size)]
    devices = [(grp, rank // 2, lax.rem(rank, 2)) for rank in ranks]
    greet([(device, None) for device in devices[1:]])

    def columns(rank):
        return pl.ds(pl.multiple_of(rank * width, width), width)

    out = [
        remote(x_ref.at[:, columns(ranks[k])], parts.at[k], send.at[k], recv.at[k], devices[k])
        for k in range(1, size)
    ]
    for copy in out:
        copy.start()
    total[...] = x_ref[:, columns(me)]
    for k, copy in enumerate(out):
        copy.wait()
        total[...] += parts[k + 1]
    back = [
        remote(total, o_ref.at[:, columns(me)], send_back.at[k], recv_back.at[k], devices[k])
        for k in range(1, size)
    ]
    for copy in back:
        copy.start()
    o_ref[:, columns(me)] = total[...]
    for copy in back:
        copy.wait_send()
    for k in range(1, size):
        rank = lax.rem(me - k + size, size)
        remote(total, o_ref.at[:, columns(rank)], send_back.at[k], recv_back.at[k], devices[k]).wait_recv()


def sum_all(x, collective_id):
    size = lax.axis_size("wide") * lax.axis_size("narrow")
    rows, columns = x.shape
    if size != 4 * LINE:
        return lax.psum(x, ("wide", "narrow"))
    width = columns // size
    return pl.pallas_call(
        sum_all_kernel,
        out_shape=jax.ShapeDtypeStruct(x.shape, x.dtype),
        in_specs=[VMEM],
        out_specs=VMEM,
        scratch_shapes=[
            pltpu.VMEM((size, rows, width), x.dtype),
            pltpu.VMEM((rows, width), x.dtype),
        ]
        + [pltpu.SemaphoreType.DMA((size,))] * 4,
        compiler_params=pltpu.CompilerParams(collective_id=collective_id, has_side_effects=True),
    )(x)


def positions(token_ids):
    local = token_ids % (PROMPT + NCONT * CONT)
    return jnp.where(local < PROMPT, local, PROMPT + (local - PROMPT) % CONT)


def rotation(place):
    frequency = THETA ** (-2.0 * jnp.arange(HD // 2, dtype=jnp.float32) / HD)
    angle = place.astype(jnp.float32)[:, None] * frequency[None, :]
    cosine, sine = jnp.cos(angle), jnp.sin(angle)
    return jnp.concatenate([cosine, cosine], 1), jnp.concatenate([-sine, sine], 1)


def swap_halves(values):
    return jnp.concatenate([values[..., HD // 2 :], values[..., : HD // 2]], -1)


def rotate(values, cosine, sine):
    rows, columns = values.shape
    heads = values.reshape(rows, columns // HD, HD)
    turned = heads * cosine[:, None, :] + swap_halves(heads) * sine[:, None, :]
    return turned.reshape(rows, columns)


def dot(a, b):
    return jnp.dot(a, b, preferred_element_type=jnp.float32)


def dot_nt(a, b):
    return lax.dot_general(a, b, (((1,), (1,)), ((), ())), preferred_element_type=jnp.float32)


def dot_tn(a, b):
    return lax.dot_general(a, b, (((0,), (0,)), ((), ())), preferred_element_type=jnp.float32)


def shards(
    tokens,
    cotangent,
    valid,
    routes,
    w_query,
    w_key,
    w_value,
    w_out,
    norm_attn,
    norm_query,
    norm_key,
    norm_moe,
    w_router,
    w_gate,
    w_up,
    w_down,
):
    bf16, f32 = jnp.bfloat16, jnp.float32
    wide_count = lax.axis_size("wide")
    narrow_count = lax.axis_size("narrow")
    rows = tokens.shape[0]
    half = rows * wide_count
    columns = w_query.shape[1]
    experts = w_router.shape[1]
    hidden_units = w_gate.shape[2]
    capacity = min(max(rows * TOP * 5 // (4 * experts), 2), rows)
    assert narrow_count == 2 and CONT in (rows, 2 * rows)
    paired = CONT == 2 * rows
    side = lax.axis_index("narrow")
    place = lax.axis_index("wide")
    group = lax.axis_index("grp")
    swap = [(0, 1), (1, 0)]
    twins = lax.axis_size("grp") == 2
    prompt_blocks = PROMPT // (rows * narrow_count)
    shared = half if paired else prompt_blocks * rows
    attend, attend_back = attention_calls(rows, half, shared, columns, prompt_blocks, paired)
    side_array = side.astype(jnp.int32).reshape(1)
    barrier = lax.optimization_barrier

    def exchange(value):
        return lax.ppermute(value, "narrow", swap)

    stream = tokens.astype(f32)
    inv_one = lax.rsqrt(jnp.mean(stream * stream, -1, keepdims=True) + EPSILON)
    gain_one = norm_attn.astype(f32)
    normed = (stream * inv_one * gain_one).astype(bf16)
    mask = valid.astype(f32)[:, None]
    grad_final = cotangent.astype(f32) * mask
    pieces = 2 if twins else 1
    piece_width = D // pieces
    piece = lax.dynamic_slice_in_dim(w_out, group * piece_width, piece_width, 1) if twins else w_out
    (routes_plane, normed_plane, out_piece), (other_gate, other_up, other_down) = start_exchange(
        [routes.T, normed, piece], [w_gate[0], w_up[0], w_down[0]], 0
    )
    normed_plane = normed_plane.reshape(half, D)
    out_pieces = [out_piece.reshape(D, piece_width)]
    if twins:
        out_pieces.append(lax.ppermute(out_pieces[0], "grp", swap))

    def ordered(parts):
        if not twins:
            return parts
        return [jnp.where(group == 0, parts[k], parts[k ^ 1]) for k in range(2)]

    def unordered(whole):
        return ordered([whole[:, k * piece_width : (k + 1) * piece_width] for k in range(pieces)])

    grad_final_b, _ = barrier((grad_final.astype(bf16), normed_plane))
    grad_plane = lax.all_gather(grad_final_b, "wide", axis=0, tiled=True)

    joined = jnp.concatenate([w_query, w_key, w_value], 1)
    raw = dot(normed_plane, joined)
    query_raw, key_raw, value_raw = (raw[:, i * columns : (i + 1) * columns] for i in range(3))
    sums = sum_wide(
        jnp.stack([jnp.sum(query_raw * query_raw, -1), jnp.sum(key_raw * key_raw, -1)]), 1
    )
    inv_query, inv_key = lax.rsqrt(sums / D + EPSILON)[:, :, None]
    gain_query = norm_query.astype(f32)
    gain_key = norm_key.astype(f32)
    plane_ids = (
        (jnp.arange(wide_count, dtype=jnp.int32)[:, None] * narrow_count + side) * rows
        + jnp.arange(rows, dtype=jnp.int32)[None, :]
    ).reshape(half)
    cosine, sine = rotation(positions(plane_ids))
    value_b = value_raw.astype(bf16)
    value_other = exchange(value_b[:shared])
    key_rot = rotate(key_raw * inv_key * gain_key, cosine, sine).astype(bf16)
    key_other = exchange(key_rot[:shared])
    query_rot = rotate(query_raw * inv_query * gain_query, cosine, sine).astype(bf16)
    attended, lse = attend(side_array, query_rot, key_rot, value_b, key_other, value_other)

    attended_own = lax.all_to_all(attended, "wide", split_axis=0, concat_axis=1, tiled=True)
    branch = jnp.concatenate(ordered([dot(attended_own, p) for p in out_pieces]), 1)
    hidden = stream + branch
    inv_two = lax.rsqrt(jnp.mean(hidden * hidden, -1, keepdims=True) + EPSILON)
    gain_two = norm_moe.astype(f32)
    moe_in = (hidden * inv_two * gain_two).astype(bf16)
    moe_plane = lax.all_gather(moe_in, "wide", axis=0, tiled=True)

    kinds = jnp.arange(experts, dtype=jnp.int32)
    named = jnp.any(routes_plane[:, :, :, None] == kinds, 1).reshape(half, experts)
    earlier = (jnp.arange(rows)[:, None] < jnp.arange(rows)[None, :]).astype(bf16)
    blocks = lambda a: a.reshape(wide_count, rows, -1)

    def pick(expert):
        chosen = jnp.any(routes_plane == expert, 1)
        rank = dot(chosen.astype(bf16), earlier).astype(jnp.int32)
        slot = jnp.where(chosen, rank, -1)
        return (jnp.arange(capacity, dtype=jnp.int32)[None, :, None] == slot[:, None, :]).astype(bf16)

    def compact(onehot, values):
        return jnp.einsum(
            "wcr,wrd->wcd", onehot, blocks(values), preferred_element_type=f32
        ).astype(bf16).reshape(wide_count * capacity, -1)

    def spread(onehot, values):
        return jnp.einsum(
            "wcr,wcd->wrd", onehot, values.reshape(wide_count, capacity, -1), preferred_element_type=f32
        ).reshape(half, -1)

    ids = (place * narrow_count + 1 - side, place * narrow_count + side)
    weights = ((other_gate, other_up, other_down), (w_gate[0], w_up[0], w_down[0]))
    onehots = [pick(e) for e in ids]
    grads = [compact(o, grad_plane) for o in onehots]
    backs = [dot_nt(g, w[2]) for g, w in zip(grads, weights)]
    probs = jax.nn.softmax(dot(moe_plane, w_router), -1)
    gates_dense = jnp.where(named, probs, 0.0)
    inputs = [compact(o, moe_plane) for o in onehots]
    gates_own = [jnp.take(gates_dense, e, axis=1) for e in ids]
    gates = [
        jnp.sum(o.astype(f32) * g.reshape(wide_count, 1, rows), -1).reshape(wide_count * capacity, 1)
        for o, g in zip(onehots, gates_own)
    ]
    gate_pres = [dot(x, w[0]) for x, w in zip(inputs, weights)]
    up_pres = [dot(x, w[1]) for x, w in zip(inputs, weights)]
    inners = [g * jax.nn.sigmoid(g) * u for g, u in zip(gate_pres, up_pres)]
    inners_gated = [(g * i).astype(bf16) for g, i in zip(gates, inners)]
    moe_part = sum(spread(o, dot(i, w[2]).astype(bf16)) for o, i, w in zip(onehots, inners_gated, weights))
    moe_part = moe_part.astype(bf16)
    moe = lax.psum_scatter(moe_part, "wide", scatter_dimension=0, tiled=True).astype(f32)

    _, gate_pres = barrier((moe_part, gate_pres))
    grad_part = 0.0
    mixing = 0.0
    grad_pres = []
    for k in range(2):
        gate_pre, up_pre, back, gate = gate_pres[k], up_pres[k], backs[k], gates[k]
        sigmoid = jax.nn.sigmoid(gate_pre)
        silu = gate_pre * sigmoid
        grad_gate_row = jnp.sum(silu * up_pre * back, -1)
        grad_inner = gate * back
        grad_gate_pre = (grad_inner * up_pre * sigmoid * (1.0 + gate_pre * (1.0 - sigmoid))).astype(bf16)
        grad_up_pre = (grad_inner * silu).astype(bf16)
        grad_pres.append((grad_gate_pre, grad_up_pre))
        route_in = (dot_nt(grad_gate_pre, weights[k][0]) + dot_nt(grad_up_pre, weights[k][1])).astype(bf16)
        grad_part = grad_part + spread(onehots[k], route_in)
        grad_gates = jnp.sum(
            onehots[k].astype(f32) * grad_gate_row.reshape(wide_count, capacity, 1), 1
        ).reshape(half, 1)
        here = (kinds == ids[k]).astype(f32)
        mixing = mixing + gates_own[k][:, None] * grad_gates * (here[None, :] - probs)
    mixing = mixing.astype(bf16)
    grad_part = (grad_part + dot_nt(mixing, w_router)).astype(bf16)
    grad_router = dot_tn(mixing, moe_plane)
    partner_grads = [
        dot_tn(inputs[0], grad_pres[0][0]).astype(bf16),
        dot_tn(inputs[0], grad_pres[0][1]).astype(bf16),
        dot_tn(inners_gated[0], grads[0]).astype(bf16),
    ]
    came = [exchange(g) for g in partner_grads]
    grad_part, partner_grads = barrier((grad_part, partner_grads))
    grad_moe_in = scatter_wide(grad_part.reshape(wide_count, rows, D), 5)
    grad_moe_in, moe, inputs, grads = barrier((grad_moe_in, moe, inputs, grads))
    expert_grads = [
        dot_tn(inputs[1], grad_pres[1][0]), dot_tn(inputs[1], grad_pres[1][1]), dot_tn(inners_gated[1], grads[1])
    ]

    grad_gain_two = jnp.sum(grad_moe_in * hidden * inv_two, 0)
    grad_hidden = (
        grad_final
        + inv_two * gain_two * grad_moe_in
        - hidden * inv_two**3 * jnp.sum(grad_moe_in * gain_two * hidden, -1, keepdims=True) / D
    )
    grad_branch = grad_hidden.astype(bf16)
    grad_attended_own = sum(dot_nt(g, p) for g, p in zip(unordered(grad_branch), out_pieces)).astype(bf16)
    grad_attended = lax.all_to_all(grad_attended_own, "wide", split_axis=1, concat_axis=0, tiled=True)
    branch_plane = lax.all_gather(grad_branch, "wide", axis=0, tiled=True)

    grad_query_rot, grad_key_rot, grad_value, grad_key_other, grad_value_other = attend_back(
        side_array, query_rot, key_rot, value_b, key_other, value_other, grad_attended, attended, lse
    )

    def add_shared(own, other):
        return jnp.concatenate([own[:shared] + other.astype(f32), own[shared:]], 0)

    grad_key_rot = add_shared(grad_key_rot, exchange(grad_key_other))
    grad_value = add_shared(grad_value, exchange(grad_value_other))
    grad_query_normed = rotate(grad_query_rot, cosine, -sine)
    grad_key_normed = rotate(grad_key_rot, cosine, -sine)
    dots = sum_wide(
        jnp.stack(
            [
                jnp.sum(grad_query_normed * gain_query * query_raw, -1),
                jnp.sum(grad_key_normed * gain_key * key_raw, -1),
            ]
        ),
        2,
    )[:, :, None]
    grad_gain_query = jnp.sum(grad_query_normed * query_raw * inv_query, 0)
    grad_gain_key = jnp.sum(grad_key_normed * key_raw * inv_key, 0)
    grad_query_raw = inv_query * gain_query * grad_query_normed - query_raw * inv_query**3 * dots[0] / D
    grad_key_raw = inv_key * gain_key * grad_key_normed - key_raw * inv_key**3 * dots[1] / D
    grads_joined = jnp.concatenate([grad_query_raw, grad_key_raw, grad_value], 1).astype(bf16)
    grad_weights = barrier(dot_tn(normed_plane, grads_joined).astype(bf16))
    weights_came = exchange(grad_weights)
    normed_part, _ = barrier((dot_nt(grads_joined, joined).astype(bf16), grad_weights))
    grad_normed = scatter_wide(normed_part.reshape(wide_count, rows, D), 3)
    grad_out = barrier(dot_tn(attended, branch_plane).astype(bf16))
    out_came = exchange(grad_out)
    grad_weights = grad_weights.astype(f32) + weights_came.astype(f32)
    grad_out = grad_out.astype(f32) + out_came.astype(f32)
    grad_query_w, grad_key_w, grad_value_w = (
        grad_weights[:, i * columns : (i + 1) * columns] for i in range(3)
    )
    grad_gain_one = jnp.sum(grad_normed * stream * inv_one, 0)
    grad_input = (
        grad_hidden
        + inv_one * gain_one * grad_normed
        - stream * inv_one**3 * jnp.sum(grad_normed * gain_one * stream, -1, keepdims=True) / D
    )
    final = hidden + moe
    output = final.astype(bf16)
    grad_gate_w, grad_up_w, grad_down_w = (
        (own + other.astype(f32))[None] for own, other in zip(expert_grads, came)
    )

    stats = jnp.stack([jnp.sum(v * v * mask) for v in (stream, branch, hidden, moe, final)] + [jnp.sum(mask)])
    here = jnp.repeat(jnp.arange(wide_count) == place, columns)
    spots = [jnp.where(here, jnp.tile(g, wide_count), 0.0) for g in (grad_gain_query, grad_gain_key)]
    small = jnp.stack([grad_gain_one, grad_gain_two, *spots, jnp.pad(stats, (0, D - stats.shape[0]))])
    small = jnp.concatenate([grad_router, small, jnp.zeros((-(experts + 5) % 8, D), f32)], 0)
    small = sum_all(small, 4)
    spots = lax.dynamic_slice_in_dim(small[experts + 2 : experts + 4], place * columns, columns, 1)
    stats = small[experts + 4, :6]
    rms = jnp.sqrt(stats[:5] / (jnp.maximum(stats[5], 1.0) * D))
    return (
        output,
        grad_input,
        grad_query_w,
        grad_key_w,
        grad_value_w,
        grad_out,
        small[experts],
        spots[0],
        spots[1],
        small[experts + 1],
        small[:experts].T,
        grad_gate_w,
        grad_up_w,
        grad_down_w,
        rms,
    )


def solution(mesh):
    return jax.shard_map(
        shards,
        mesh=mesh,
        in_specs=(
            P(("grp", "wide", "narrow"), None),
            P(("grp", "wide", "narrow"), None),
            P(("grp", "wide", "narrow")),
            P(("grp", "wide", "narrow"), None),
            P(None, "wide"),
            P(None, "wide"),
            P(None, "wide"),
            P("wide", None),
            P(),
            P("wide"),
            P("wide"),
            P(),
            P(),
            P(("wide", "narrow"), None, None),
            P(("wide", "narrow"), None, None),
            P(("wide", "narrow"), None, None),
        ),
        out_specs=(
            P(("grp", "wide", "narrow"), None),
            P(("grp", "wide", "narrow"), None),
            P("grp", "wide"),
            P("grp", "wide"),
            P("grp", "wide"),
            P(("grp", "wide"), None),
            P("grp"),
            P(("grp", "wide")),
            P(("grp", "wide")),
            P("grp"),
            P("grp", None),
            P(("grp", "wide", "narrow"), None, None),
            P(("grp", "wide", "narrow"), None, None),
            P(("grp", "wide", "narrow"), None, None),
            P("grp"),
        ),
        check_vma=False,
    )
```

```python
import functools

import jax
import jax.numpy as jnp
from jax import lax
from jax.experimental import pallas as pl
from jax.experimental.pallas import tpu as pltpu
from jax.sharding import PartitionSpec as P

D = 2048
HD = 128
TOP = 8
PROMPT = 2048
CONT = 256
NCONT = 8

EPSILON = 1e-05
THETA = 10000.0
NEGATIVE = -1e30


LOG2E = 1.4426950408889634
NT = (((1,), (1,)), ((), ()))


def key_parts(w, plane, rows, prompt_blocks, paired, limit=512):
    count = (prompt_blocks if w is None else w) * rows
    parts = [(first, min(limit, count - first), None) for first in range(0, count, limit)]
    own = None if w is None else w * rows
    if plane == 0:
        parts.append((own, rows, "causal"))
    elif w is not None or paired:
        parts.append((own, rows, "side"))
    return parts


def for_blocks(blocks, prompt_blocks, one):
    for w in range(prompt_blocks):
        one(w, w, w * one.rows)

    def body(w, carry):
        one(None, w, pl.multiple_of(w * one.rows, one.rows))
        return carry

    lax.fori_loop(prompt_blocks, blocks, body, 0)


def masked_scores(score, mask, side, rows):
    if mask == "causal":
        key = lax.broadcasted_iota(jnp.int32, (rows, rows), 0)
        query = lax.broadcasted_iota(jnp.int32, (rows, rows), 1)
        return jnp.where(key <= query, score, NEGATIVE)
    if mask == "side":
        return jnp.where(side == 1, score, NEGATIVE)
    return score


def row_sums(values):
    total = values[:, :HD]
    for first in range(HD, values.shape[1], HD):
        total = total + values[:, first : first + HD]
    return jnp.sum(total.T, 0, keepdims=True)


def turn(values, cosine, sine):
    return values * cosine + pltpu.roll(values, HD // 2, 1) * sine


def inverse_norms(sums_ref, at):
    inverse = lax.rsqrt(sums_ref[:, at].T / D + EPSILON)
    return inverse[:, 0:1], inverse[:, 1:2]


def peer_copies(size, src, dst, send, recv, grp, wide, narrow):
    return [
        remote(src, dst.at[k - 1], send.at[k - 1], recv.at[k - 1], (grp, lax.rem(wide + k, size), narrow))
        for k in range(1, size)
    ]


def attend_kernel(
    rows, prompt_blocks, paired, shared, raw_ref, gains_ref, cos_ref, sin_ref,
    q_ref, k_ref, v_ref, ko_ref, vo_ref, o_ref, own_ref, lse_ref, sums_ref,
    vt_ref, vto_ref, came_ref, sum_send, sum_recv, pair_send, pair_recv, out_send, out_recv,
):
    half, columns = q_ref.shape
    size = half // rows
    heads = columns // HD
    grp, wide, narrow = (lax.axis_index(a) for a in ("grp", "wide", "narrow"))
    partner = (grp, wide, 1 - narrow)
    greet([((grp, lax.rem(wide + k, size), narrow), None) for k in range(1, size)] + [(partner, None)])
    pairs = [
        remote(src.at[pl.ds(0, shared)], dst, pair_send.at[i], pair_recv.at[i], partner)
        for i, (src, dst) in enumerate(((k_ref, ko_ref), (v_ref, vo_ref)))
    ]
    v_ref[...] = raw_ref[:, 2 * columns :].astype(jnp.bfloat16)
    pairs[1].start()
    sums_ref[...] = jnp.zeros_like(sums_ref)

    def squares(b, carry):
        at = pl.ds(pl.multiple_of(b * rows, rows), rows)
        for i in range(2):
            part = raw_ref[at, i * columns : (i + 1) * columns]
            sums_ref[i : i + 1, at] = row_sums(part * part)
        return carry

    lax.fori_loop(0, size, squares, 0)
    copies = peer_copies(size, sums_ref, came_ref, sum_send, sum_recv, grp, wide, narrow)
    for copy in copies:
        copy.start()
    for h in range(heads):
        hs = slice(h * HD, (h + 1) * HD)
        vt_ref[hs, :] = v_ref[:, hs].T
    for copy in copies:
        copy.wait()
    total = sums_ref[...]
    for k in range(size - 1):
        total = total + came_ref[k]
    sums_ref[...] = total

    def prepare(i, ref):
        def body(b, carry):
            at = pl.ds(pl.multiple_of(b * rows, rows), rows)
            inverse = inverse_norms(sums_ref, at)[i]
            for h in range(heads):
                hs = slice(h * HD, (h + 1) * HD)
                values = raw_ref[at, i * columns + h * HD : i * columns + (h + 1) * HD]
                values = values * inverse * gains_ref[i : i + 1, hs]
                ref[at, hs] = turn(values, cos_ref[at], sin_ref[at]).astype(jnp.bfloat16)
            return carry

        return body

    lax.fori_loop(0, shared // rows, prepare(1, k_ref), 0)
    pairs[0].start()
    lax.fori_loop(shared // rows, size, prepare(1, k_ref), 0)
    lax.fori_loop(0, size, prepare(0, q_ref), 0)
    pairs[1].wait()
    for h in range(heads):
        hs = slice(h * HD, (h + 1) * HD)
        vto_ref[hs, :] = vo_ref[:, hs].T
    pairs[0].wait()

    def mine():
        return pl.ds(pl.multiple_of(wide * columns, columns), columns)

    def hand_out(w):
        return remote(
            o_ref.at[pl.ds(pl.multiple_of(w * rows, rows), rows)],
            own_ref.at[:, mine()],
            out_send.at[w],
            out_recv.at[wide],
            (grp, w, narrow),
        )

    def one(w, w_index, start):
        block = pl.ds(start, rows)
        for h in range(heads):
            hs = slice(h * HD, (h + 1) * HD)
            query = q_ref[block, hs]
            scores = []
            for plane in range(2):
                for first, count, mask in key_parts(w, plane, rows, prompt_blocks, paired):
                    at = pl.ds(start if first is None else first, count)
                    key = (k_ref, ko_ref)[plane][at, hs]
                    score = lax.dot_general(key, query, NT, preferred_element_type=jnp.float32)
                    score = score * (HD**-0.5 * LOG2E)
                    scores.append((plane, at, masked_scores(score, mask, narrow, rows)))
            largest = functools.reduce(
                jnp.maximum, [jnp.max(score, 0, keepdims=True) for _, _, score in scores]
            )
            total = jnp.zeros((1, rows), jnp.float32)
            mixed = jnp.zeros((HD, rows), jnp.float32)
            for plane, at, score in scores:
                weight = jnp.exp2(score - largest)
                total = total + jnp.sum(weight, 0, keepdims=True)
                mixed = mixed + dot((vt_ref, vto_ref)[plane][hs, at], weight.astype(jnp.bfloat16))
            o_ref[block, hs] = (mixed / total).T.astype(jnp.bfloat16)
            lse_ref[h : h + 1, block] = largest + jnp.log(total) * LOG2E

        @pl.when(w_index != wide)
        def _():
            hand_out(w_index).start()

    one.rows = rows
    for_blocks(size, prompt_blocks, one)
    own_ref[:, mine()] = o_ref[pl.ds(pl.multiple_of(wide * rows, rows), rows)]

    def finish(w, carry):
        @pl.when(w != wide)
        def _():
            hand_out(w).wait_send()
            remote(
                o_ref.at[pl.ds(0, rows)], own_ref.at[:, mine()], out_send.at[w], out_recv.at[w], (grp, w, narrow)
            ).wait_recv()

        return carry

    lax.fori_loop(0, size, finish, 0)


def attend_back_kernel(
    rows, prompt_blocks, paired, shared, raw_ref, gains_ref, cos_ref, sin_ref, sums_ref,
    q_ref, k_ref, v_ref, ko_ref, vo_ref, grad_ref, o_ref, lse_ref,
    joined_ref, gain_ref,
    do_ref, dq_ref, dk_ref, dv_ref, dko_ref, dvo_ref, dkb_ref, dvb_ref, dkr_ref, dvr_ref, kt_ref, kto_ref,
    dots_ref, came_ref, sum_send, sum_recv, pair_send, pair_recv, in_send, in_recv,
):
    half, columns = q_ref.shape
    size = half // rows
    heads = columns // HD
    grp, wide, narrow = (lax.axis_index(a) for a in ("grp", "wide", "narrow"))
    partner = (grp, wide, 1 - narrow)
    greet([((grp, lax.rem(wide + k, size), narrow), None) for k in range(1, size)] + [(partner, None)])
    my_rows = pl.ds(pl.multiple_of(wide * rows, rows), rows)

    def part_of(w):
        return pl.ds(pl.multiple_of(w * columns, columns), columns)

    def hand_in(w):
        return remote(
            grad_ref.at[:, part_of(w)], do_ref.at[my_rows], in_send.at[w], in_recv.at[wide], (grp, w, narrow)
        )

    def each_peer(act):
        def body(w, carry):
            pl.when(w != wide)(lambda: act(w))
            return carry

        lax.fori_loop(0, size, body, 0)

    each_peer(lambda w: hand_in(w).start())
    do_ref[my_rows, :] = grad_ref[:, part_of(wide)]
    for ref in (dk_ref, dv_ref, dko_ref, dvo_ref, dots_ref, gain_ref):
        ref[...] = jnp.zeros_like(ref)
    for h in range(heads):
        hs = slice(h * HD, (h + 1) * HD)
        kt_ref[hs, :] = k_ref[:, hs].T
        kto_ref[hs, :] = ko_ref[:, hs].T
    each_peer(
        lambda w: remote(
            grad_ref.at[:, part_of(w)], do_ref.at[my_rows], in_send.at[w], in_recv.at[w], (grp, w, narrow)
        ).wait_recv()
    )

    def sweep(plane):
        keys, values = ((k_ref, v_ref), (ko_ref, vo_ref))[plane]
        dk, dv = ((dk_ref, dv_ref), (dko_ref, dvo_ref))[plane]
        flipped = (kt_ref, kto_ref)[plane]

        def one(w, w_index, start):
            block = pl.ds(start, rows)
            for h in range(heads):
                hs = slice(h * HD, (h + 1) * HD)
                query = q_ref[block, hs]
                grad = do_ref[block, hs]
                delta = row_sums(grad.astype(jnp.float32) * o_ref[block, hs].astype(jnp.float32))
                lse = lse_ref[h : h + 1, block]
                back = jnp.zeros((HD, rows), jnp.float32)
                for first, count, mask in key_parts(w, plane, rows, prompt_blocks, paired):
                    at = pl.ds(start if first is None else first, count)
                    score = lax.dot_general(keys[at, hs], query, NT, preferred_element_type=jnp.float32)
                    score = masked_scores(score * (HD**-0.5 * LOG2E), mask, narrow, rows)
                    weight = jnp.exp2(score - lse)
                    grad_weight = lax.dot_general(values[at, hs], grad, NT, preferred_element_type=jnp.float32)
                    grad_score = (weight * (grad_weight - delta)).astype(jnp.bfloat16)
                    dv[at, hs] += dot(weight.astype(jnp.bfloat16), grad)
                    dk[at, hs] += dot(grad_score, query) * HD**-0.5
                    back = back + dot(flipped[hs, at], grad_score)
                back = back.T * HD**-0.5
                dq_ref[block, hs] = back if plane == 1 else dq_ref[block, hs] + back

        one.rows = rows
        for_blocks(size, prompt_blocks, one)

    sweep(1)
    dkb_ref[...] = dko_ref[...].astype(jnp.bfloat16)
    dvb_ref[...] = dvo_ref[...].astype(jnp.bfloat16)
    pairs = [
        remote(src, dst, pair_send.at[i], pair_recv.at[i], partner)
        for i, (src, dst) in enumerate(((dkb_ref, dkr_ref), (dvb_ref, dvr_ref)))
    ]
    for copy in pairs:
        copy.start()
    sweep(0)

    def turn_back(i, ref):
        def body(b, carry):
            at = pl.ds(pl.multiple_of(b * rows, rows), rows)
            inverse = inverse_norms(sums_ref, at)[i]
            products = []
            for h in range(heads):
                hs = slice(h * HD, (h + 1) * HD)
                grad = turn(ref[at, hs], cos_ref[at], -sin_ref[at])
                ref[at, hs] = grad
                product = grad * raw_ref[at, i * columns + h * HD : i * columns + (h + 1) * HD]
                gain_ref[i : i + 1, hs] += jnp.sum(product * inverse, 0, keepdims=True)
                products.append(product * gains_ref[i : i + 1, hs])
            dots_ref[i : i + 1, at] = row_sums(sum(products[1:], products[0]))
            return carry

        lax.fori_loop(0, size, body, 0)

    turn_back(0, dq_ref)
    for copy in pairs:
        copy.wait()
    dk_ref[0:shared, :] += dkr_ref[...].astype(jnp.float32)
    turn_back(1, dk_ref)
    copies = peer_copies(size, dots_ref, came_ref, sum_send, sum_recv, grp, wide, narrow)
    for copy in copies:
        copy.start()
    joined_ref[0:shared, 2 * columns :] = (dv_ref[0:shared] + dvr_ref[...].astype(jnp.float32)).astype(jnp.bfloat16)
    if shared < half:
        joined_ref[shared:, 2 * columns :] = dv_ref[shared:].astype(jnp.bfloat16)
    for copy in copies:
        copy.wait()
    total = dots_ref[...]
    for k in range(size - 1):
        total = total + came_ref[k]
    dots_ref[...] = total

    def finish(b, carry):
        at = pl.ds(pl.multiple_of(b * rows, rows), rows)
        inverses = inverse_norms(sums_ref, at)
        products = dots_ref[:, at].T / D
        for i, ref in enumerate((dq_ref, dk_ref)):
            inverse = inverses[i]
            cubed = inverse * inverse * inverse * products[:, i : i + 1]
            for h in range(heads):
                hs = slice(h * HD, (h + 1) * HD)
                there = slice(i * columns + h * HD, i * columns + (h + 1) * HD)
                value = inverse * gains_ref[i : i + 1, hs] * ref[at, hs] - raw_ref[at, there] * cubed
                joined_ref[at, there] = value.astype(jnp.bfloat16)
        return carry

    lax.fori_loop(0, size, finish, 0)
    each_peer(lambda w: hand_in(w).wait_send())


def attention_calls(rows, half, shared, columns, prompt_blocks, paired, ids):
    heads = columns // HD
    size = half // rows
    bf16, f32 = jnp.bfloat16, jnp.float32
    shape = lambda dtype, *dims: jax.ShapeDtypeStruct(dims, dtype)
    sems = pltpu.SemaphoreType.DMA
    work = half * half * columns * 2
    peers = [sems((size - 1,)), sems((size - 1,)), sems((2,)), sems((2,)), sems((size,)), sems((size,))]

    def params(k):
        return pltpu.CompilerParams(vmem_limit_bytes=60 * 2**20, collective_id=ids[k], has_side_effects=True)

    forward = pl.pallas_call(
        functools.partial(attend_kernel, rows, prompt_blocks, paired, shared),
        out_shape=[shape(bf16, half, columns)] * 3
        + [shape(bf16, shared, columns)] * 2
        + [shape(bf16, half, columns), shape(bf16, rows, size * columns), shape(f32, heads, half), shape(f32, 8, half)],
        in_specs=[VMEM] * 4,
        out_specs=[VMEM] * 9,
        scratch_shapes=[
            pltpu.VMEM((columns, half), bf16),
            pltpu.VMEM((columns, shared), bf16),
            pltpu.VMEM((size - 1, 8, half), f32),
        ]
        + peers,
        compiler_params=params(0),
        cost_estimate=pl.CostEstimate(flops=2 * work, bytes_accessed=120_000_000, transcendentals=0),
    )
    backward = pl.pallas_call(
        functools.partial(attend_back_kernel, rows, prompt_blocks, paired, shared),
        out_shape=[shape(bf16, half, 3 * columns), shape(f32, 8, columns)],
        in_specs=[VMEM] * 13,
        out_specs=[VMEM] * 2,
        scratch_shapes=[pltpu.VMEM((half, columns), bf16)]
        + [pltpu.VMEM((half, columns), f32)] * 3
        + [pltpu.VMEM((shared, columns), f32)] * 2
        + [pltpu.VMEM((shared, columns), bf16)] * 4
        + [
            pltpu.VMEM((columns, half), bf16),
            pltpu.VMEM((columns, shared), bf16),
            pltpu.VMEM((8, half), f32),
            pltpu.VMEM((size - 1, 8, half), f32),
        ]
        + peers,
        compiler_params=params(1),
        cost_estimate=pl.CostEstimate(flops=5 * work, bytes_accessed=200_000_000, transcendentals=0),
    )
    return forward, backward


def dot(a, b):
    return jnp.dot(a, b, preferred_element_type=jnp.float32)


def dot_nt(a, b):
    return lax.dot_general(a, b, NT, preferred_element_type=jnp.float32)


def dot_tn(a, b):
    return lax.dot_general(a, b, (((0,), (0,)), ((), ())), preferred_element_type=jnp.float32)


MESH_ID = pl.DeviceIdType.MESH
ANY = pl.BlockSpec(memory_space=pl.ANY)
VMEM = pl.BlockSpec(memory_space=pltpu.VMEM)
LINE = 4


def lasts(microseconds):
    return pl.CostEstimate(flops=0, bytes_accessed=microseconds * 3_000_000, transcendentals=0)


def position():
    grp, wide, narrow = (lax.axis_index(a) for a in ("grp", "wide", "narrow"))
    return grp, wide, narrow, wide // 2, lax.rem(wide, 2)


def greet(targets):
    barrier = pltpu.get_barrier_semaphore()
    for device, when in targets:
        def signal(device=device):
            pl.semaphore_signal(barrier, inc=1, device_id=device, device_id_type=MESH_ID)

        if when is None:
            signal()
        else:
            pl.when(when)(signal)
    peers = sum(1 if when is None else when.astype(jnp.int32) for _, when in targets)
    pl.semaphore_wait(barrier, peers)


def remote(src, dst, send, recv, device):
    return pltpu.make_async_remote_copy(
        src_ref=src, dst_ref=dst, send_sem=send, recv_sem=recv, device_id=device, device_id_type=MESH_ID
    )


def gather_kernel(count, *refs):
    ins, outs = refs[:count], refs[count : 2 * count]
    gather_body(count, ins, outs, *refs[2 * count :])


def gather_body(count, ins, outs, send, recv, local, more=(), begin=None, finish=None):
    grp, wide, narrow, line, cross = position()
    across = (grp, line * 2 + 1 - cross, narrow)
    above = (grp, wide + 2, narrow)
    below = (grp, wide - 2, narrow)
    has_above, has_below = line < LINE - 1, line > 0
    greet([(across, None), (above, has_above), (below, has_below), *more])

    def copy(i, source_line, way, device):
        slot = source_line * 2 + cross
        return remote(outs[i].at[slot], outs[i].at[slot], send.at[i, way, source_line], recv.at[i, slot], device)

    def own(i, way, device):
        return remote(ins[i], outs[i].at[wide], send.at[i, way, line], recv.at[i, wide], device)

    mine = [pltpu.make_async_copy(ins[i], outs[i].at[wide], local.at[i]) for i in range(count)]
    for i in range(count):
        pl.when(has_above)(own(i, 1, above).start)
        pl.when(has_below)(own(i, 2, below).start)
        own(i, 0, across).start()
        mine[i].start()
    if begin is not None:
        begin()
    for i in range(count):
        for distance in range(1, LINE):
            for sign in (-1, 1):
                source = line + sign * distance

                @pl.when((source >= 0) & (source < LINE))
                def _(i=i, source=source, sign=sign):
                    slot = source * 2 + cross
                    copy(i, source, 0, across).wait_recv()
                    onward = above if sign < 0 else below

                    @pl.when(has_above if sign < 0 else has_below)
                    def _():
                        copy(i, source, 1 if sign < 0 else 2, onward).start()

                    copy(i, source, 0, across).start()

    for i in range(count):
        for source in range(LINE):
            other = source * 2 + 1 - cross
            remote(ins[i], outs[i].at[other], send.at[i, 0, 0], recv.at[i, other], across).wait_recv()
        for source in range(LINE):
            remote(ins[i], outs[i].at[0], send.at[i, 0, source], recv.at[i, 0], across).wait_send()

            @pl.when(has_above & (source <= line))
            def _(i=i, source=source):
                remote(ins[i], outs[i].at[0], send.at[i, 1, source], recv.at[i, 0], above).wait_send()

            @pl.when(has_below & (source >= line))
            def _(i=i, source=source):
                remote(ins[i], outs[i].at[0], send.at[i, 2, source], recv.at[i, 0], below).wait_send()

        mine[i].wait()
    if finish is not None:
        finish()


def gather_wide(arrays, collective_id):
    count = len(arrays)
    size = lax.axis_size("wide")
    if size != 2 * LINE:
        return [lax.all_gather(a, "wide", axis=0) for a in arrays]
    return pl.pallas_call(
        functools.partial(gather_kernel, count),
        out_shape=[jax.ShapeDtypeStruct((size, *a.shape), a.dtype) for a in arrays],
        in_specs=[ANY] * count,
        out_specs=[ANY] * count,
        scratch_shapes=[
            pltpu.SemaphoreType.DMA((count, 3, LINE)),
            pltpu.SemaphoreType.DMA((count, size)),
            pltpu.SemaphoreType.DMA((count,)),
        ],
        compiler_params=pltpu.CompilerParams(collective_id=collective_id, has_side_effects=True),
        cost_estimate=lasts(100),
    )(*arrays)


def scatter_kernel(part_ref, out_ref, held, from_across, from_line, load, send, recv_a, recv_l):
    grp, wide, narrow, line, cross = position()
    across = (grp, line * 2 + 1 - cross, narrow)
    above = (grp, wide + 2, narrow)
    below = (grp, wide - 2, narrow)
    has_above, has_below = line < LINE - 1, line > 0
    f32 = jnp.float32
    greet([(across, None), (above, has_above), (below, has_below)])

    order = []
    for distance in range(LINE - 1, 0, -1):
        for sign in (1, -1):
            order.append((distance, sign))

    def valid(owner):
        return (owner >= 0) & (owner < LINE)

    def across_copy(owner):
        return remote(
            part_ref.at[owner * 2 + 1 - cross], from_across.at[owner], send.at[0, owner], recv_a.at[owner], across
        )

    def load_copy(owner):
        return pltpu.make_async_copy(part_ref.at[owner * 2 + cross], held.at[owner], load.at[owner])

    def line_copy(owner, up):
        return remote(
            held.at[owner],
            from_line.at[0 if up else 1, owner],
            send.at[1, owner],
            recv_l.at[0 if up else 1, owner],
            above if up else below,
        )

    for distance, sign in order + [(0, 1)]:
        owner = line + sign * distance

        @pl.when(valid(owner))
        def _(owner=owner):
            across_copy(owner).start()
            load_copy(owner).start()

    for distance, sign in order:
        owner = line + sign * distance

        @pl.when(valid(owner))
        def _(owner=owner, sign=sign):
            load_copy(owner).wait()
            across_copy(owner).wait_recv()
            up = sign > 0
            came = has_below if up else has_above
            total = held[owner].astype(f32) + from_across[owner].astype(f32)

            @pl.when(came)
            def _():
                line_copy(owner, up).wait_recv()
                held[owner] = (total + from_line[0 if up else 1, owner].astype(f32)).astype(held.dtype)

            @pl.when(jnp.logical_not(came))
            def _():
                held[owner] = total.astype(held.dtype)

            line_copy(owner, up).start()

    load_copy(line).wait()
    across_copy(line).wait_recv()
    out_ref[...] = held[line].astype(f32) + from_across[line].astype(f32)

    @pl.when(has_below)
    def _():
        line_copy(line, True).wait_recv()
        out_ref[...] += from_line[0, line].astype(f32)

    @pl.when(has_above)
    def _():
        line_copy(line, False).wait_recv()
        out_ref[...] += from_line[1, line].astype(f32)

    for owner in range(LINE):
        across_copy(owner).wait_send()

        @pl.when(owner > line)
        def _(owner=owner):
            line_copy(owner, True).wait_send()

        @pl.when(owner < line)
        def _(owner=owner):
            line_copy(owner, False).wait_send()


def scatter_wide(part, collective_id):
    size, rows, columns = part.shape
    if size != 2 * LINE:
        return lax.psum_scatter(part, "wide", scatter_dimension=0, tiled=False).astype(jnp.float32)
    block = (LINE, rows, columns)
    return pl.pallas_call(
        scatter_kernel,
        out_shape=jax.ShapeDtypeStruct((rows, columns), jnp.float32),
        in_specs=[ANY],
        out_specs=VMEM,
        scratch_shapes=[
            pltpu.VMEM(block, part.dtype),
            pltpu.VMEM(block, part.dtype),
            pltpu.VMEM((2, *block), part.dtype),
            pltpu.SemaphoreType.DMA((LINE,)),
            pltpu.SemaphoreType.DMA((2, LINE)),
            pltpu.SemaphoreType.DMA((LINE,)),
            pltpu.SemaphoreType.DMA((2, LINE)),
        ],
        compiler_params=pltpu.CompilerParams(
            collective_id=collective_id, has_side_effects=True, vmem_limit_bytes=48 * 2**20
        ),
        cost_estimate=lasts(95),
    )(part)


def sum_kernel(x_ref, o_ref, held, send, recv):
    grp, wide, narrow, _, _ = position()
    size = held.shape[0] + 1
    others = [(grp, lax.rem(wide + k, size), narrow) for k in range(1, size)]
    greet([(device, None) for device in others])
    copies = [
        remote(x_ref, held.at[k], send.at[k], recv.at[k], device) for k, device in enumerate(others)
    ]
    for copy in copies:
        copy.start()
    for copy in copies:
        copy.wait()
    total = x_ref[...]
    for k in range(size - 1):
        total = total + held[k]
    o_ref[...] = total


def sum_wide(x, collective_id):
    size = lax.axis_size("wide")
    if size != 2 * LINE:
        return lax.psum(x, "wide")
    return pl.pallas_call(
        sum_kernel,
        out_shape=jax.ShapeDtypeStruct(x.shape, x.dtype),
        in_specs=[VMEM],
        out_specs=VMEM,
        scratch_shapes=[
            pltpu.VMEM((size - 1, *x.shape), x.dtype),
            pltpu.SemaphoreType.DMA((size - 1,)),
            pltpu.SemaphoreType.DMA((size - 1,)),
        ],
        compiler_params=pltpu.CompilerParams(collective_id=collective_id, has_side_effects=True),
        cost_estimate=lasts(8),
    )(x)


def start_kernel(count, swaps, *refs):
    ins, given = refs[:count], refs[count : count + swaps]
    outs = refs[count + swaps : 2 * count + swaps]
    got = refs[2 * count + swaps : 2 * (count + swaps)]
    send, recv, local, swap_send, swap_recv, twin_send, twin_recv = refs[2 * (count + swaps) :]
    grp, wide, narrow, line, cross = position()
    partner = (grp, wide, 1 - narrow)
    twin = (1 - grp, wide, narrow)

    def half(ref, which):
        size = ref.shape[0] // 2
        return ref.at[pl.ds(pl.multiple_of(which * size, size), size)]

    def swap(i):
        return remote(half(given[i], grp), half(got[i], grp), swap_send.at[i], swap_recv.at[i], partner)

    def share(i, which):
        return remote(half(got[i], which), half(got[i], which), twin_send.at[i], twin_recv.at[i], twin)

    def begin():
        for i in range(swaps):
            swap(i).start()

    def finish():
        for i in range(swaps):
            swap(i).wait_recv()
            share(i, grp).start()
        for i in range(swaps):
            swap(i).wait_send()
            share(i, grp).wait_send()
            share(i, 1 - grp).wait_recv()

    gather_body(count, ins, outs, send, recv, local, [(partner, None), (twin, None)], begin, finish)


def start_exchange(arrays, weights, collective_id):
    size = lax.axis_size("wide")
    if size != 2 * LINE or lax.axis_size("grp") != 2:
        swap = [(0, 1), (1, 0)]
        return [lax.all_gather(a, "wide", axis=0) for a in arrays], [lax.ppermute(w, "narrow", swap) for w in weights]
    count, swaps = len(arrays), len(weights)
    out = pl.pallas_call(
        functools.partial(start_kernel, count, swaps),
        out_shape=[jax.ShapeDtypeStruct((size, *a.shape), a.dtype) for a in arrays]
        + [jax.ShapeDtypeStruct(w.shape, w.dtype) for w in weights],
        in_specs=[ANY] * (count + swaps),
        out_specs=[ANY] * (count + swaps),
        scratch_shapes=[
            pltpu.SemaphoreType.DMA((count, 3, LINE)),
            pltpu.SemaphoreType.DMA((count, size)),
            pltpu.SemaphoreType.DMA((count,)),
        ]
        + [pltpu.SemaphoreType.DMA((swaps,))] * 4,
        compiler_params=pltpu.CompilerParams(collective_id=collective_id, has_side_effects=True),
        cost_estimate=lasts(150),
    )(*arrays, *weights)
    return out[:count], out[count:]


def sum_all_kernel(x_ref, o_ref, parts, total, send, recv, send_back, recv_back):
    grp, wide, narrow, _, _ = position()
    size, _, width = parts.shape
    me = wide * 2 + narrow
    ranks = [lax.rem(me + k, size) for k in range(size)]
    devices = [(grp, rank // 2, lax.rem(rank, 2)) for rank in ranks]
    greet([(device, None) for device in devices[1:]])

    def columns(rank):
        return pl.ds(pl.multiple_of(rank * width, width), width)

    out = [
        remote(x_ref.at[:, columns(ranks[k])], parts.at[k], send.at[k], recv.at[k], devices[k])
        for k in range(1, size)
    ]
    for copy in out:
        copy.start()
    total[...] = x_ref[:, columns(me)]
    for k, copy in enumerate(out):
        copy.wait()
        total[...] += parts[k + 1]
    back = [
        remote(total, o_ref.at[:, columns(me)], send_back.at[k], recv_back.at[k], devices[k])
        for k in range(1, size)
    ]
    for copy in back:
        copy.start()
    o_ref[:, columns(me)] = total[...]
    for copy in back:
        copy.wait_send()
    for k in range(1, size):
        rank = lax.rem(me - k + size, size)
        remote(total, o_ref.at[:, columns(rank)], send_back.at[k], recv_back.at[k], devices[k]).wait_recv()


def sum_all(x, collective_id):
    size = lax.axis_size("wide") * lax.axis_size("narrow")
    rows, columns = x.shape
    if size != 4 * LINE:
        return lax.psum(x, ("wide", "narrow"))
    width = columns // size
    return pl.pallas_call(
        sum_all_kernel,
        out_shape=jax.ShapeDtypeStruct(x.shape, x.dtype),
        in_specs=[VMEM],
        out_specs=VMEM,
        scratch_shapes=[
            pltpu.VMEM((size, rows, width), x.dtype),
            pltpu.VMEM((rows, width), x.dtype),
        ]
        + [pltpu.SemaphoreType.DMA((size,))] * 4,
        compiler_params=pltpu.CompilerParams(collective_id=collective_id, has_side_effects=True),
        cost_estimate=lasts(15),
    )(x)


def expert_kernel(
    tiles, capacity, experts, first, id_ref, slot_ref, tokens_ref, grads_ref, router_ref, gate_ref, up_ref, down_ref, *refs
):
    if not first:
        moe_in_ref, part_in_ref, router_in_ref = refs[:3]
        refs = refs[3:]
    (
        moe_ref, part_ref, x_ref, g_ref, inner_ref, grad_gate_ref, grad_up_ref, router_grad_ref,
        x_all, g_all, picks, moe_all, part_all, probs_all, scores_all, router_sum,
    ) = refs
    f32, bf16 = jnp.float32, jnp.bfloat16
    group, step = pl.program_id(0), pl.program_id(1)
    blocks = picks.shape[0]
    expert = id_ref[0]
    lane = lax.broadcasted_iota(jnp.int32, (1, 128), 1)

    @pl.when(step < blocks)
    def _():
        rows = tokens_ref.shape[1]
        row = lax.broadcasted_iota(jnp.int32, (capacity, rows), 0)
        pick = jnp.where(row == slot_ref[0], 1.0, 0.0).astype(bf16)
        picks[step] = pick
        here = pl.ds(pl.multiple_of(step * capacity, capacity), capacity)
        x = dot(pick, tokens_ref[0]).astype(bf16)
        g = dot(pick, grads_ref[0]).astype(bf16)
        x_all[here], x_ref[...] = x, x
        g_all[here], g_ref[...] = g, g

    @pl.when(step == blocks)
    def _():
        logits = jnp.where(lane < experts, dot(x_all[...], router_ref[...]), NEGATIVE)
        weight = jnp.exp(logits - jnp.max(logits, -1, keepdims=True))
        probs_all[...] = weight / jnp.sum(weight, -1, keepdims=True)
        moe_all[...] = jnp.zeros_like(moe_all)
        part_all[...] = jnp.zeros_like(part_all)
        scores_all[...] = jnp.zeros_like(scores_all)

    @pl.when((step >= blocks) & (step < blocks + tiles))
    def _():
        x, g = x_all[...], g_all[...]
        gate = jnp.sum(jnp.where(lane == expert, probs_all[...], 0.0), -1, keepdims=True)
        gate_pre = dot(x, gate_ref[...])
        up_pre = dot(x, up_ref[...])
        back = dot_nt(g, down_ref[...])
        sigmoid = 1.0 / (1.0 + jnp.exp(-gate_pre))
        silu = gate_pre * sigmoid
        inner = silu * up_pre
        scores_all[...] += jnp.sum(inner * back, -1, keepdims=True)
        inner_gated = (gate * inner).astype(bf16)
        back = gate * back
        grad_gate_pre = (back * up_pre * sigmoid * (1.0 + gate_pre * (1.0 - sigmoid))).astype(bf16)
        grad_up_pre = (back * silu).astype(bf16)
        inner_ref[...] = inner_gated
        grad_gate_ref[...] = grad_gate_pre
        grad_up_ref[...] = grad_up_pre
        moe_all[...] += dot(inner_gated, down_ref[...])
        part_all[...] += dot_nt(grad_gate_pre, gate_ref[...]) + dot_nt(grad_up_pre, up_ref[...])

    @pl.when(step == blocks + tiles)
    def _():
        probs = probs_all[...]
        here = jnp.where(lane == expert, 1.0, 0.0)
        gate = jnp.sum(probs * here, -1, keepdims=True)
        mixing = (gate * scores_all[...] * (here - probs)).astype(bf16)
        part_all[...] += dot_nt(mixing, router_ref[...])
        grad = dot_tn(mixing, x_all[...])

        @pl.when(group == 0)
        def _():
            router_sum[...] = grad if first else grad + router_in_ref[...]

        @pl.when(group > 0)
        def _():
            router_sum[...] += grad

        router_grad_ref[...] = router_sum[...]

    @pl.when(step >= blocks + tiles)
    def _():
        block = step - blocks - tiles
        pick = picks[block]
        here = pl.ds(pl.multiple_of(block * capacity, capacity), capacity)
        moe = dot_tn(pick, moe_all[here].astype(bf16))
        part = dot_tn(pick, part_all[here].astype(bf16))
        if not first:
            moe = moe + moe_in_ref[0].astype(f32)
            part = part + part_in_ref[0].astype(f32)
        moe_ref[0] = moe.astype(bf16)
        part_ref[0] = part.astype(bf16)


def expert_call(expert, slots, tokens, grads, router, weights, capacity, experts, before=None):
    wide, rows, _ = tokens.shape
    units = weights[0].shape[1]
    groups = 2 if wide * capacity > 1024 else 1
    blocks, tile = wide // groups, 256
    tiles = units // tile
    last = blocks + tiles
    first = before is None
    bf16, f32 = jnp.bfloat16, jnp.float32

    def picked(g, i):
        return g * blocks + jnp.minimum(i, blocks - 1)

    def tiled(i):
        return jnp.clip(i - blocks, 0, tiles - 1)

    def spread(g, i):
        return g * blocks + jnp.clip(i - last, 0, blocks - 1)

    whole = pl.BlockSpec((1, rows, D), lambda g, i: (picked(g, i), 0, 0))
    back = pl.BlockSpec((1, rows, D), lambda g, i: (spread(g, i), 0, 0))
    row = pl.BlockSpec((capacity, D), lambda g, i: (picked(g, i), 0))
    column = pl.BlockSpec((D, tile), lambda g, i: (0, tiled(i)))
    unit = pl.BlockSpec((blocks * capacity, tile), lambda g, i: (g, tiled(i)))
    fixed = pl.BlockSpec((128, D), lambda g, i: (0, 0))
    in_specs = [
        pl.BlockSpec(memory_space=pltpu.SMEM),
        pl.BlockSpec((1, 1, rows), lambda g, i: (picked(g, i), 0, 0)),
        whole,
        whole,
        pl.BlockSpec((D, 128), lambda g, i: (0, 0)),
        column,
        column,
        pl.BlockSpec((tile, D), lambda g, i: (tiled(i), 0)),
    ] + ([] if first else [back, back, fixed])
    count = wide * capacity
    compact = jax.ShapeDtypeStruct((count, D), bf16)
    narrow = jax.ShapeDtypeStruct((count, units), bf16)
    held = blocks * capacity
    return pl.pallas_call(
        functools.partial(expert_kernel, tiles, capacity, experts, first),
        grid=(groups, last + blocks),
        in_specs=in_specs,
        out_specs=[back, back, row, row, unit, unit, unit, fixed],
        out_shape=[jax.ShapeDtypeStruct((wide, rows, D), bf16)] * 2
        + [compact] * 2
        + [narrow] * 3
        + [jax.ShapeDtypeStruct((128, D), f32)],
        scratch_shapes=[
            pltpu.VMEM((held, D), bf16),
            pltpu.VMEM((held, D), bf16),
            pltpu.VMEM((blocks, capacity, rows), bf16),
            pltpu.VMEM((held, D), f32),
            pltpu.VMEM((held, D), f32),
            pltpu.VMEM((held, 128), f32),
            pltpu.VMEM((held, 1), f32),
            pltpu.VMEM((128, D), f32),
        ],
        compiler_params=pltpu.CompilerParams(vmem_limit_bytes=60 * 2**20),
        cost_estimate=pl.CostEstimate(
            flops=12 * count * D * units, bytes_accessed=count * D * 12 + 6 * D * units, transcendentals=0
        ),
    )(expert.astype(jnp.int32).reshape(1), slots, tokens, grads, router, *weights, *(before or ()))


def positions(token_ids):
    local = token_ids % (PROMPT + NCONT * CONT)
    return jnp.where(local < PROMPT, local, PROMPT + (local - PROMPT) % CONT)


def rotation(place):
    frequency = THETA ** (-2.0 * jnp.arange(HD // 2, dtype=jnp.float32) / HD)
    angle = place.astype(jnp.float32)[:, None] * frequency[None, :]
    cosine, sine = jnp.cos(angle), jnp.sin(angle)
    return jnp.concatenate([cosine, cosine], 1), jnp.concatenate([-sine, sine], 1)


def shards(
    tokens,
    cotangent,
    valid,
    routes,
    w_query,
    w_key,
    w_value,
    w_out,
    norm_attn,
    norm_query,
    norm_key,
    norm_moe,
    w_router,
    w_gate,
    w_up,
    w_down,
):
    bf16, f32 = jnp.bfloat16, jnp.float32
    wide_count = lax.axis_size("wide")
    narrow_count = lax.axis_size("narrow")
    rows = tokens.shape[0]
    half = rows * wide_count
    columns = w_query.shape[1]
    experts = w_router.shape[1]
    hidden_units = w_gate.shape[2]
    capacity = min(max(rows * TOP * 5 // (4 * experts), 2), rows)
    assert narrow_count == 2 and CONT in (rows, 2 * rows)
    paired = CONT == 2 * rows
    side = lax.axis_index("narrow")
    place = lax.axis_index("wide")
    group = lax.axis_index("grp")
    swap = [(0, 1), (1, 0)]
    twins = lax.axis_size("grp") == 2
    prompt_blocks = PROMPT // (rows * narrow_count)
    shared = half if paired else prompt_blocks * rows
    attend, attend_back = attention_calls(rows, half, shared, columns, prompt_blocks, paired, (1, 2))
    barrier = lax.optimization_barrier

    def exchange(value):
        return lax.ppermute(value, "narrow", swap)

    stream = tokens.astype(f32)
    inv_one = lax.rsqrt(jnp.mean(stream * stream, -1, keepdims=True) + EPSILON)
    gain_one = norm_attn.astype(f32)
    normed = (stream * inv_one * gain_one).astype(bf16)
    mask = valid.astype(f32)[:, None]
    grad_final = cotangent.astype(f32) * mask
    pieces = 2 if twins else 1
    piece_width = D // pieces
    piece = lax.dynamic_slice_in_dim(w_out, group * piece_width, piece_width, 1) if twins else w_out
    (routes_plane, normed_plane, out_piece), (other_gate, other_up, other_down) = start_exchange(
        [routes.T, normed, piece], [w_gate[0], w_up[0], w_down[0]], 0
    )
    normed_plane = normed_plane.reshape(half, D)
    out_pieces = [out_piece.reshape(D, piece_width)]
    if twins:
        out_pieces.append(lax.ppermute(out_pieces[0], "grp", swap))

    def ordered(parts):
        if not twins:
            return parts
        return [jnp.where(group == 0, parts[k], parts[k ^ 1]) for k in range(2)]

    def unordered(whole):
        return ordered([whole[:, k * piece_width : (k + 1) * piece_width] for k in range(pieces)])

    grad_final_b, _ = barrier((grad_final.astype(bf16), normed_plane))
    grad_plane = lax.all_gather(grad_final_b, "wide", axis=0, tiled=True)

    joined = jnp.concatenate([w_query, w_key, w_value], 1)
    raw = dot(normed_plane, joined)
    gains = jnp.pad(jnp.stack([norm_query, norm_key]).astype(f32), ((0, 6), (0, 0)))
    plane_ids = (
        (jnp.arange(wide_count, dtype=jnp.int32)[:, None] * narrow_count + side) * rows
        + jnp.arange(rows, dtype=jnp.int32)[None, :]
    ).reshape(half)
    cosine, sine = rotation(positions(plane_ids))
    kept = attend(raw, gains, cosine, sine)
    attended, attended_own, lse, sums = kept[5:]

    branch = jnp.concatenate(ordered([dot(attended_own, p) for p in out_pieces]), 1)
    hidden = stream + branch
    inv_two = lax.rsqrt(jnp.mean(hidden * hidden, -1, keepdims=True) + EPSILON)
    gain_two = norm_moe.astype(f32)
    moe_in = (hidden * inv_two * gain_two).astype(bf16)
    moe_plane = lax.all_gather(moe_in, "wide", axis=0, tiled=True)

    earlier = (jnp.arange(rows)[:, None] < jnp.arange(rows)[None, :]).astype(bf16)

    def slots_of(expert):
        chosen = jnp.any(routes_plane == expert, 1)
        rank = dot(chosen.astype(bf16), earlier).astype(jnp.int32)
        return jnp.where(chosen, rank, -1).reshape(wide_count, 1, rows)

    router = jnp.pad(w_router, ((0, 0), (0, 128 - experts)))
    tokens_in = moe_plane.reshape(wide_count, rows, D)
    grads_in = grad_plane.reshape(wide_count, rows, D)

    def run_expert(expert, weights, before):
        return expert_call(
            expert, slots_of(expert), tokens_in, grads_in, router, weights, capacity, experts, before
        )

    own = run_expert(place * narrow_count + side, (w_gate[0], w_up[0], w_down[0]), None)
    other = run_expert(
        place * narrow_count + 1 - side, (other_gate, other_up, other_down), (own[0], own[1], own[7])
    )
    moe_part, grad_part, grad_router = other[0], other[1], other[7][:experts]
    inputs, grads, inners_gated = (own[2], other[2]), (own[3], other[3]), (own[4], other[4])
    grad_pres = ((own[5], own[6]), (other[5], other[6]))
    moe = lax.psum_scatter(moe_part.reshape(half, D), "wide", scatter_dimension=0, tiled=True).astype(f32)
    partner_grads = [
        dot_tn(inputs[1], grad_pres[1][0]).astype(bf16),
        dot_tn(inputs[1], grad_pres[1][1]).astype(bf16),
        dot_tn(inners_gated[1], grads[1]).astype(bf16),
    ]
    came = [exchange(g) for g in partner_grads[:2]]
    grad_part, partner_grads = barrier((grad_part, partner_grads))
    grad_moe_in = scatter_wide(grad_part, 5)
    grad_moe_in, moe, came[0] = barrier((grad_moe_in, moe, came[0]))

    grad_gain_two = jnp.sum(grad_moe_in * hidden * inv_two, 0)
    grad_hidden = (
        grad_final
        + inv_two * gain_two * grad_moe_in
        - hidden * inv_two**3 * jnp.sum(grad_moe_in * gain_two * hidden, -1, keepdims=True) / D
    )
    grad_branch = grad_hidden.astype(bf16)
    grad_attended_own = sum(dot_nt(g, p) for g, p in zip(unordered(grad_branch), out_pieces)).astype(bf16)
    branch_plane = lax.all_gather(grad_branch, "wide", axis=0, tiled=True)
    grad_out = barrier(dot_tn(attended, branch_plane).astype(bf16))

    grads_joined, gain_grads = attend_back(
        raw, gains, cosine, sine, sums, *kept[:5], grad_attended_own, attended, lse
    )
    grads_joined, came[1], down_partner = barrier((grads_joined, came[1], partner_grads[2]))
    came.append(exchange(down_partner))
    grad_weights = barrier(dot_tn(normed_plane, grads_joined).astype(bf16))
    weights_came = exchange(grad_weights)
    normed_part, _ = barrier((dot_nt(grads_joined, joined).astype(bf16), grad_weights))
    grad_normed = scatter_wide(normed_part.reshape(wide_count, rows, D), 3)
    grad_normed, came[2] = barrier((grad_normed, came[2]))
    expert_grads = [
        dot_tn(inputs[0], grad_pres[0][0]), dot_tn(inputs[0], grad_pres[0][1]), dot_tn(inners_gated[0], grads[0])
    ]
    out_came = exchange(grad_out)
    grad_weights = grad_weights.astype(f32) + weights_came.astype(f32)
    grad_out = grad_out.astype(f32) + out_came.astype(f32)
    grad_query_w, grad_key_w, grad_value_w = (
        grad_weights[:, i * columns : (i + 1) * columns] for i in range(3)
    )
    grad_gain_one = jnp.sum(grad_normed * stream * inv_one, 0)
    grad_input = (
        grad_hidden
        + inv_one * gain_one * grad_normed
        - stream * inv_one**3 * jnp.sum(grad_normed * gain_one * stream, -1, keepdims=True) / D
    )
    final = hidden + moe
    output = final.astype(bf16)
    grad_gate_w, grad_up_w, grad_down_w = (
        (own + other.astype(f32))[None] for own, other in zip(expert_grads, came)
    )

    stats = jnp.stack([jnp.sum(v * v * mask) for v in (stream, branch, hidden, moe, final)] + [jnp.sum(mask)])
    here = jnp.repeat(jnp.arange(wide_count) == place, columns)
    spots = [jnp.where(here, jnp.tile(g, wide_count), 0.0) for g in gain_grads[:2]]
    small = jnp.stack([grad_gain_one, grad_gain_two, *spots, jnp.pad(stats, (0, D - stats.shape[0]))])
    small = jnp.concatenate([grad_router, small, jnp.zeros((-(experts + 5) % 8, D), f32)], 0)
    small = sum_all(small, 4)
    spots = lax.dynamic_slice_in_dim(small[experts + 2 : experts + 4], place * columns, columns, 1)
    stats = small[experts + 4, :6]
    rms = jnp.sqrt(stats[:5] / (jnp.maximum(stats[5], 1.0) * D))
    return (
        output,
        grad_input,
        grad_query_w,
        grad_key_w,
        grad_value_w,
        grad_out,
        small[experts],
        spots[0],
        spots[1],
        small[experts + 1],
        small[:experts].T,
        grad_gate_w,
        grad_up_w,
        grad_down_w,
        rms,
    )


def solution(mesh):
    return jax.shard_map(
        shards,
        mesh=mesh,
        in_specs=(
            P(("grp", "wide", "narrow"), None),
            P(("grp", "wide", "narrow"), None),
            P(("grp", "wide", "narrow")),
            P(("grp", "wide", "narrow"), None),
            P(None, "wide"),
            P(None, "wide"),
            P(None, "wide"),
            P("wide", None),
            P(),
            P("wide"),
            P("wide"),
            P(),
            P(),
            P(("wide", "narrow"), None, None),
            P(("wide", "narrow"), None, None),
            P(("wide", "narrow"), None, None),
        ),
        out_specs=(
            P(("grp", "wide", "narrow"), None),
            P(("grp", "wide", "narrow"), None),
            P("grp", "wide"),
            P("grp", "wide"),
            P("grp", "wide"),
            P(("grp", "wide"), None),
            P("grp"),
            P(("grp", "wide")),
            P(("grp", "wide")),
            P("grp"),
            P("grp", None),
            P(("grp", "wide", "narrow"), None, None),
            P(("grp", "wide", "narrow"), None, None),
            P(("grp", "wide", "narrow"), None, None),
            P("grp"),
        ),
        check_vma=False,
    )
```

```python
import functools

import jax
import jax.numpy as jnp
from jax import lax
from jax.experimental import pallas as pl
from jax.experimental.pallas import tpu as pltpu
from jax.sharding import PartitionSpec as P

D = 2048
HD = 128
TOP = 8
PROMPT = 2048
CONT = 256
NCONT = 8

EPSILON = 1e-05
THETA = 10000.0
NEGATIVE = -1e30


MESH_ID = pl.DeviceIdType.MESH
ANY = pl.BlockSpec(memory_space=pl.ANY)
VMEM = pl.BlockSpec(memory_space=pltpu.VMEM)
LINE = 4


def lasts(microseconds):
    return pl.CostEstimate(flops=0, bytes_accessed=microseconds * 3_000_000, transcendentals=0)


def position():
    grp, wide, narrow = (lax.axis_index(a) for a in ("grp", "wide", "narrow"))
    return grp, wide, narrow, wide // 2, lax.rem(wide, 2)


def greet(targets):
    barrier = pltpu.get_barrier_semaphore()
    for device, when in targets:
        def signal(device=device):
            pl.semaphore_signal(barrier, inc=1, device_id=device, device_id_type=MESH_ID)

        if when is None:
            signal()
        else:
            pl.when(when)(signal)
    peers = sum(1 if when is None else when.astype(jnp.int32) for _, when in targets)
    pl.semaphore_wait(barrier, peers)


def remote(src, dst, send, recv, device):
    return pltpu.make_async_remote_copy(
        src_ref=src, dst_ref=dst, send_sem=send, recv_sem=recv, device_id=device, device_id_type=MESH_ID
    )


def gather_kernel(count, *refs):
    ins, outs = refs[:count], refs[count : 2 * count]
    gather_body(count, ins, outs, *refs[2 * count :])


class Gather:
    def __init__(self, ins, outs, send, recv, local):
        self.ins, self.outs, self.send, self.recv, self.local = ins, outs, send, recv, local
        grp, wide, narrow, self.line, self.cross = position()
        self.wide = wide
        self.across = (grp, self.line * 2 + 1 - self.cross, narrow)
        self.above = (grp, wide + 2, narrow)
        self.below = (grp, wide - 2, narrow)
        self.has_above, self.has_below = self.line < LINE - 1, self.line > 0
        self.targets = [(self.across, None), (self.above, self.has_above), (self.below, self.has_below)]

    def copy(self, i, source_line, way, device):
        slot = source_line * 2 + self.cross
        out = self.outs[i].at[slot]
        return remote(out, out, self.send.at[i, way, source_line], self.recv.at[i, slot], device)

    def own(self, i, way, device):
        return remote(
            self.ins[i], self.outs[i].at[self.wide], self.send.at[i, way, self.line], self.recv.at[i, self.wide], device
        )

    def mine(self, i):
        return pltpu.make_async_copy(self.ins[i], self.outs[i].at[self.wide], self.local.at[i])

    def start(self):
        for i in range(len(self.ins)):
            pl.when(self.has_above)(self.own(i, 1, self.above).start)
            pl.when(self.has_below)(self.own(i, 2, self.below).start)
            self.own(i, 0, self.across).start()
            self.mine(i).start()

    def forward(self, distance, only=None):
        for i in range(len(self.ins)) if only is None else (only,):
            for sign in (-1, 1):
                source = self.line + sign * distance

                @pl.when((source >= 0) & (source < LINE))
                def _(i=i, source=source, sign=sign):
                    self.copy(i, source, 0, self.across).wait_recv()
                    onward = self.above if sign < 0 else self.below

                    @pl.when(self.has_above if sign < 0 else self.has_below)
                    def _():
                        self.copy(i, source, 1 if sign < 0 else 2, onward).start()

                    self.copy(i, source, 0, self.across).start()

    def finish(self):
        for i in range(len(self.ins)):
            send, recv, src, out = self.send, self.recv, self.ins[i], self.outs[i]
            for source in range(LINE):
                other = source * 2 + 1 - self.cross
                remote(src, out.at[other], send.at[i, 0, 0], recv.at[i, other], self.across).wait_recv()
            for source in range(LINE):
                remote(src, out.at[0], send.at[i, 0, source], recv.at[i, 0], self.across).wait_send()

                @pl.when(self.has_above & (source <= self.line))
                def _(source=source):
                    remote(src, out.at[0], send.at[i, 1, source], recv.at[i, 0], self.above).wait_send()

                @pl.when(self.has_below & (source >= self.line))
                def _(source=source):
                    remote(src, out.at[0], send.at[i, 2, source], recv.at[i, 0], self.below).wait_send()

            self.mine(i).wait()


def gather_sems(count):
    return [
        pltpu.SemaphoreType.DMA((count, 3, LINE)),
        pltpu.SemaphoreType.DMA((count, 2 * LINE)),
        pltpu.SemaphoreType.DMA((count,)),
    ]


def gather_body(count, ins, outs, send, recv, local, more=(), begin=None, finish=None):
    gather = Gather(ins, outs, send, recv, local)
    greet([*gather.targets, *more])
    gather.start()
    if begin is not None:
        begin()
    for i in range(count):
        for distance in range(1, LINE):
            gather.forward(distance, i)
    gather.finish()
    if finish is not None:
        finish()


def gather_wide(arrays, collective_id):
    count = len(arrays)
    size = lax.axis_size("wide")
    if size != 2 * LINE:
        return [lax.all_gather(a, "wide", axis=0) for a in arrays]
    return pl.pallas_call(
        functools.partial(gather_kernel, count),
        out_shape=[jax.ShapeDtypeStruct((size, *a.shape), a.dtype) for a in arrays],
        in_specs=[ANY] * count,
        out_specs=[ANY] * count,
        scratch_shapes=[
            pltpu.SemaphoreType.DMA((count, 3, LINE)),
            pltpu.SemaphoreType.DMA((count, size)),
            pltpu.SemaphoreType.DMA((count,)),
        ],
        compiler_params=pltpu.CompilerParams(collective_id=collective_id, has_side_effects=True),
        cost_estimate=lasts(100),
    )(*arrays)


def scatter_kernel(part_ref, out_ref, held, from_across, from_line, load, send, recv_a, recv_l):
    grp, wide, narrow, line, cross = position()
    across = (grp, line * 2 + 1 - cross, narrow)
    above = (grp, wide + 2, narrow)
    below = (grp, wide - 2, narrow)
    has_above, has_below = line < LINE - 1, line > 0
    f32 = jnp.float32
    greet([(across, None), (above, has_above), (below, has_below)])

    order = []
    for distance in range(LINE - 1, 0, -1):
        for sign in (1, -1):
            order.append((distance, sign))

    def valid(owner):
        return (owner >= 0) & (owner < LINE)

    def across_copy(owner):
        return remote(
            part_ref.at[owner * 2 + 1 - cross], from_across.at[owner], send.at[0, owner], recv_a.at[owner], across
        )

    def load_copy(owner):
        return pltpu.make_async_copy(part_ref.at[owner * 2 + cross], held.at[owner], load.at[owner])

    def line_copy(owner, up):
        return remote(
            held.at[owner],
            from_line.at[0 if up else 1, owner],
            send.at[1, owner],
            recv_l.at[0 if up else 1, owner],
            above if up else below,
        )

    for distance, sign in order + [(0, 1)]:
        owner = line + sign * distance

        @pl.when(valid(owner))
        def _(owner=owner):
            across_copy(owner).start()
            load_copy(owner).start()

    for distance, sign in order:
        owner = line + sign * distance

        @pl.when(valid(owner))
        def _(owner=owner, sign=sign):
            load_copy(owner).wait()
            across_copy(owner).wait_recv()
            up = sign > 0
            came = has_below if up else has_above
            total = held[owner].astype(f32) + from_across[owner].astype(f32)

            @pl.when(came)
            def _():
                line_copy(owner, up).wait_recv()
                held[owner] = (total + from_line[0 if up else 1, owner].astype(f32)).astype(held.dtype)

            @pl.when(jnp.logical_not(came))
            def _():
                held[owner] = total.astype(held.dtype)

            line_copy(owner, up).start()

    load_copy(line).wait()
    across_copy(line).wait_recv()
    out_ref[...] = held[line].astype(f32) + from_across[line].astype(f32)

    @pl.when(has_below)
    def _():
        line_copy(line, True).wait_recv()
        out_ref[...] += from_line[0, line].astype(f32)

    @pl.when(has_above)
    def _():
        line_copy(line, False).wait_recv()
        out_ref[...] += from_line[1, line].astype(f32)

    for owner in range(LINE):
        across_copy(owner).wait_send()

        @pl.when(owner > line)
        def _(owner=owner):
            line_copy(owner, True).wait_send()

        @pl.when(owner < line)
        def _(owner=owner):
            line_copy(owner, False).wait_send()


def scatter_wide(part, collective_id):
    size, rows, columns = part.shape
    if size != 2 * LINE:
        return lax.psum_scatter(part, "wide", scatter_dimension=0, tiled=False).astype(jnp.float32)
    block = (LINE, rows, columns)
    return pl.pallas_call(
        scatter_kernel,
        out_shape=jax.ShapeDtypeStruct((rows, columns), jnp.float32),
        in_specs=[ANY],
        out_specs=VMEM,
        scratch_shapes=[
            pltpu.VMEM(block, part.dtype),
            pltpu.VMEM(block, part.dtype),
            pltpu.VMEM((2, *block), part.dtype),
            pltpu.SemaphoreType.DMA((LINE,)),
            pltpu.SemaphoreType.DMA((2, LINE)),
            pltpu.SemaphoreType.DMA((LINE,)),
            pltpu.SemaphoreType.DMA((2, LINE)),
        ],
        compiler_params=pltpu.CompilerParams(
            collective_id=collective_id, has_side_effects=True, vmem_limit_bytes=48 * 2**20
        ),
        cost_estimate=lasts(95),
    )(part)


def sum_kernel(x_ref, o_ref, held, send, recv):
    grp, wide, narrow, _, _ = position()
    size = held.shape[0] + 1
    others = [(grp, lax.rem(wide + k, size), narrow) for k in range(1, size)]
    greet([(device, None) for device in others])
    copies = [
        remote(x_ref, held.at[k], send.at[k], recv.at[k], device) for k, device in enumerate(others)
    ]
    for copy in copies:
        copy.start()
    for copy in copies:
        copy.wait()
    total = x_ref[...]
    for k in range(size - 1):
        total = total + held[k]
    o_ref[...] = total


def sum_wide(x, collective_id):
    size = lax.axis_size("wide")
    if size != 2 * LINE:
        return lax.psum(x, "wide")
    return pl.pallas_call(
        sum_kernel,
        out_shape=jax.ShapeDtypeStruct(x.shape, x.dtype),
        in_specs=[VMEM],
        out_specs=VMEM,
        scratch_shapes=[
            pltpu.VMEM((size - 1, *x.shape), x.dtype),
            pltpu.SemaphoreType.DMA((size - 1,)),
            pltpu.SemaphoreType.DMA((size - 1,)),
        ],
        compiler_params=pltpu.CompilerParams(collective_id=collective_id, has_side_effects=True),
        cost_estimate=lasts(8),
    )(x)


LOG2E = 1.4426950408889634
NT = (((1,), (1,)), ((), ()))


def key_parts(w, plane, rows, prompt_blocks, paired, limit=512):
    count = (prompt_blocks if w is None else w) * rows
    parts = [(first, min(limit, count - first), None) for first in range(0, count, limit)]
    own = None if w is None else w * rows
    if plane == 0:
        parts.append((own, rows, "causal"))
    elif w is not None or paired:
        parts.append((own, rows, "side"))
    return parts


def for_blocks(blocks, prompt_blocks, one):
    for w in range(prompt_blocks):
        one(w, w, w * one.rows)

    def body(w, carry):
        one(None, w, pl.multiple_of(w * one.rows, one.rows))
        return carry

    lax.fori_loop(prompt_blocks, blocks, body, 0)


def masked_scores(score, mask, side, rows):
    if mask == "causal":
        key = lax.broadcasted_iota(jnp.int32, (rows, rows), 0)
        query = lax.broadcasted_iota(jnp.int32, (rows, rows), 1)
        return jnp.where(key <= query, score, NEGATIVE)
    if mask == "side":
        return jnp.where(side == 1, score, NEGATIVE)
    return score


def row_sums(values):
    total = values[:, :HD]
    for first in range(HD, values.shape[1], HD):
        total = total + values[:, first : first + HD]
    return jnp.sum(total.T, 0, keepdims=True)


def turn(values, cosine, sine):
    return values * cosine + pltpu.roll(values, HD // 2, 1) * sine


def inverse_norms(sums_ref, at):
    inverse = lax.rsqrt(sums_ref[:, at].T / D + EPSILON)
    return inverse[:, 0:1], inverse[:, 1:2]


def peer_copies(size, src, dst, send, recv, grp, wide, narrow):
    return [
        remote(src, dst.at[k - 1], send.at[k - 1], recv.at[k - 1], (grp, lax.rem(wide + k, size), narrow))
        for k in range(1, size)
    ]


def attend_kernel(
    rows, prompt_blocks, paired, shared, carried, raw_ref, gains_ref, cos_ref, sin_ref, *refs
):
    carry_in, refs = refs[:carried], refs[carried:]
    q_ref, k_ref, v_ref, ko_ref, vo_ref, o_ref, own_ref, lse_ref, sums_ref = refs[:9]
    carry_out, refs = refs[9 : 9 + carried], refs[9 + carried :]
    vt_ref, vto_ref, came_ref, sum_send, sum_recv, pair_send, pair_recv, out_send, out_recv = refs[:9]
    gather = Gather(carry_in, carry_out, *refs[9:]) if carried else None
    half, columns = q_ref.shape
    size = half // rows
    heads = columns // HD
    grp, wide, narrow = (lax.axis_index(a) for a in ("grp", "wide", "narrow"))
    partner = (grp, wide, 1 - narrow)
    greet([((grp, lax.rem(wide + k, size), narrow), None) for k in range(1, size)] + [(partner, None)])
    if carried:
        gather.start()
    pairs = [
        remote(src.at[pl.ds(0, shared)], dst, pair_send.at[i], pair_recv.at[i], partner)
        for i, (src, dst) in enumerate(((k_ref, ko_ref), (v_ref, vo_ref)))
    ]
    v_ref[...] = raw_ref[:, 2 * columns :].astype(jnp.bfloat16)
    pairs[1].start()
    sums_ref[...] = jnp.zeros_like(sums_ref)

    def squares(b, carry):
        at = pl.ds(pl.multiple_of(b * rows, rows), rows)
        for i in range(2):
            part = raw_ref[at, i * columns : (i + 1) * columns]
            sums_ref[i : i + 1, at] = row_sums(part * part)
        return carry

    lax.fori_loop(0, size, squares, 0)
    copies = peer_copies(size, sums_ref, came_ref, sum_send, sum_recv, grp, wide, narrow)
    for copy in copies:
        copy.start()
    for h in range(heads):
        hs = slice(h * HD, (h + 1) * HD)
        vt_ref[hs, :] = v_ref[:, hs].T
    for copy in copies:
        copy.wait()
    total = sums_ref[...]
    for k in range(size - 1):
        total = total + came_ref[k]
    sums_ref[...] = total

    def prepare(i, ref):
        def body(b, carry):
            at = pl.ds(pl.multiple_of(b * rows, rows), rows)
            inverse = inverse_norms(sums_ref, at)[i]
            for h in range(heads):
                hs = slice(h * HD, (h + 1) * HD)
                values = raw_ref[at, i * columns + h * HD : i * columns + (h + 1) * HD]
                values = values * inverse * gains_ref[i : i + 1, hs]
                ref[at, hs] = turn(values, cos_ref[at], sin_ref[at]).astype(jnp.bfloat16)
            return carry

        return body

    lax.fori_loop(0, shared // rows, prepare(1, k_ref), 0)
    pairs[0].start()
    lax.fori_loop(shared // rows, size, prepare(1, k_ref), 0)
    lax.fori_loop(0, size, prepare(0, q_ref), 0)
    pairs[1].wait()
    for h in range(heads):
        hs = slice(h * HD, (h + 1) * HD)
        vto_ref[hs, :] = vo_ref[:, hs].T
    pairs[0].wait()
    if carried:
        gather.forward(1)

    def mine():
        return pl.ds(pl.multiple_of(wide * columns, columns), columns)

    def hand_out(w):
        return remote(
            o_ref.at[pl.ds(pl.multiple_of(w * rows, rows), rows)],
            own_ref.at[:, mine()],
            out_send.at[w],
            out_recv.at[wide],
            (grp, w, narrow),
        )

    def one(w, w_index, start):
        block = pl.ds(start, rows)
        for h in range(heads):
            hs = slice(h * HD, (h + 1) * HD)
            query = q_ref[block, hs]
            scores = []
            for plane in range(2):
                for first, count, mask in key_parts(w, plane, rows, prompt_blocks, paired):
                    at = pl.ds(start if first is None else first, count)
                    key = (k_ref, ko_ref)[plane][at, hs]
                    score = lax.dot_general(key, query, NT, preferred_element_type=jnp.float32)
                    score = score * (HD**-0.5 * LOG2E)
                    scores.append((plane, at, masked_scores(score, mask, narrow, rows)))
            largest = functools.reduce(
                jnp.maximum, [jnp.max(score, 0, keepdims=True) for _, _, score in scores]
            )
            total = jnp.zeros((1, rows), jnp.float32)
            mixed = jnp.zeros((HD, rows), jnp.float32)
            for plane, at, score in scores:
                weight = jnp.exp2(score - largest)
                total = total + jnp.sum(weight, 0, keepdims=True)
                mixed = mixed + dot((vt_ref, vto_ref)[plane][hs, at], weight.astype(jnp.bfloat16))
            o_ref[block, hs] = (mixed / total).T.astype(jnp.bfloat16)
            lse_ref[h : h + 1, block] = largest + jnp.log(total) * LOG2E

        @pl.when(w_index != wide)
        def _():
            hand_out(w_index).start()

    one.rows = rows
    for_blocks(size, prompt_blocks, one)
    if carried:
        for distance in range(2, LINE):
            gather.forward(distance)
    own_ref[:, mine()] = o_ref[pl.ds(pl.multiple_of(wide * rows, rows), rows)]

    def finish(w, carry):
        @pl.when(w != wide)
        def _():
            hand_out(w).wait_send()
            remote(
                o_ref.at[pl.ds(0, rows)], own_ref.at[:, mine()], out_send.at[w], out_recv.at[w], (grp, w, narrow)
            ).wait_recv()

        return carry

    lax.fori_loop(0, size, finish, 0)
    if carried:
        gather.finish()


def attend_back_kernel(
    rows, prompt_blocks, paired, shared, raw_ref, gains_ref, cos_ref, sin_ref, sums_ref,
    q_ref, k_ref, v_ref, ko_ref, vo_ref, grad_ref, o_ref, lse_ref,
    joined_ref, gain_ref,
    do_ref, dq_ref, dk_ref, dv_ref, dko_ref, dvo_ref, dkb_ref, dvb_ref, dkr_ref, dvr_ref, kt_ref, kto_ref,
    dots_ref, came_ref, sum_send, sum_recv, pair_send, pair_recv, in_send, in_recv,
):
    half, columns = q_ref.shape
    size = half // rows
    heads = columns // HD
    grp, wide, narrow = (lax.axis_index(a) for a in ("grp", "wide", "narrow"))
    partner = (grp, wide, 1 - narrow)
    greet([((grp, lax.rem(wide + k, size), narrow), None) for k in range(1, size)] + [(partner, None)])
    my_rows = pl.ds(pl.multiple_of(wide * rows, rows), rows)

    def part_of(w):
        return pl.ds(pl.multiple_of(w * columns, columns), columns)

    def hand_in(w):
        return remote(
            grad_ref.at[:, part_of(w)], do_ref.at[my_rows], in_send.at[w], in_recv.at[wide], (grp, w, narrow)
        )

    def each_peer(act):
        def body(w, carry):
            pl.when(w != wide)(lambda: act(w))
            return carry

        lax.fori_loop(0, size, body, 0)

    each_peer(lambda w: hand_in(w).start())
    do_ref[my_rows, :] = grad_ref[:, part_of(wide)]
    for ref in (dk_ref, dv_ref, dko_ref, dvo_ref, dots_ref, gain_ref):
        ref[...] = jnp.zeros_like(ref)
    for h in range(heads):
        hs = slice(h * HD, (h + 1) * HD)
        kt_ref[hs, :] = k_ref[:, hs].T
        kto_ref[hs, :] = ko_ref[:, hs].T
    each_peer(
        lambda w: remote(
            grad_ref.at[:, part_of(w)], do_ref.at[my_rows], in_send.at[w], in_recv.at[w], (grp, w, narrow)
        ).wait_recv()
    )

    def sweep(plane):
        keys, values = ((k_ref, v_ref), (ko_ref, vo_ref))[plane]
        dk, dv = ((dk_ref, dv_ref), (dko_ref, dvo_ref))[plane]
        flipped = (kt_ref, kto_ref)[plane]

        def one(w, w_index, start):
            block = pl.ds(start, rows)
            for h in range(heads):
                hs = slice(h * HD, (h + 1) * HD)
                query = q_ref[block, hs]
                grad = do_ref[block, hs]
                delta = row_sums(grad.astype(jnp.float32) * o_ref[block, hs].astype(jnp.float32))
                lse = lse_ref[h : h + 1, block]
                back = jnp.zeros((HD, rows), jnp.float32)
                for first, count, mask in key_parts(w, plane, rows, prompt_blocks, paired):
                    at = pl.ds(start if first is None else first, count)
                    score = lax.dot_general(keys[at, hs], query, NT, preferred_element_type=jnp.float32)
                    score = masked_scores(score * (HD**-0.5 * LOG2E), mask, narrow, rows)
                    weight = jnp.exp2(score - lse)
                    grad_weight = lax.dot_general(values[at, hs], grad, NT, preferred_element_type=jnp.float32)
                    grad_score = (weight * (grad_weight - delta)).astype(jnp.bfloat16)
                    dv[at, hs] += dot(weight.astype(jnp.bfloat16), grad)
                    dk[at, hs] += dot(grad_score, query) * HD**-0.5
                    back = back + dot(flipped[hs, at], grad_score)
                back = back.T * HD**-0.5
                dq_ref[block, hs] = back if plane == 1 else dq_ref[block, hs] + back

        one.rows = rows
        for_blocks(size, prompt_blocks, one)

    sweep(1)
    dkb_ref[...] = dko_ref[...].astype(jnp.bfloat16)
    dvb_ref[...] = dvo_ref[...].astype(jnp.bfloat16)
    pairs = [
        remote(src, dst, pair_send.at[i], pair_recv.at[i], partner)
        for i, (src, dst) in enumerate(((dkb_ref, dkr_ref), (dvb_ref, dvr_ref)))
    ]
    for copy in pairs:
        copy.start()
    sweep(0)

    def turn_back(i, ref):
        def body(b, carry):
            at = pl.ds(pl.multiple_of(b * rows, rows), rows)
            inverse = inverse_norms(sums_ref, at)[i]
            products = []
            for h in range(heads):
                hs = slice(h * HD, (h + 1) * HD)
                grad = turn(ref[at, hs], cos_ref[at], -sin_ref[at])
                ref[at, hs] = grad
                product = grad * raw_ref[at, i * columns + h * HD : i * columns + (h + 1) * HD]
                gain_ref[i : i + 1, hs] += jnp.sum(product * inverse, 0, keepdims=True)
                products.append(product * gains_ref[i : i + 1, hs])
            dots_ref[i : i + 1, at] = row_sums(sum(products[1:], products[0]))
            return carry

        lax.fori_loop(0, size, body, 0)

    turn_back(0, dq_ref)
    for copy in pairs:
        copy.wait()
    dk_ref[0:shared, :] += dkr_ref[...].astype(jnp.float32)
    turn_back(1, dk_ref)
    copies = peer_copies(size, dots_ref, came_ref, sum_send, sum_recv, grp, wide, narrow)
    for copy in copies:
        copy.start()
    joined_ref[0:shared, 2 * columns :] = (dv_ref[0:shared] + dvr_ref[...].astype(jnp.float32)).astype(jnp.bfloat16)
    if shared < half:
        joined_ref[shared:, 2 * columns :] = dv_ref[shared:].astype(jnp.bfloat16)
    for copy in copies:
        copy.wait()
    total = dots_ref[...]
    for k in range(size - 1):
        total = total + came_ref[k]
    dots_ref[...] = total

    def finish(b, carry):
        at = pl.ds(pl.multiple_of(b * rows, rows), rows)
        inverses = inverse_norms(sums_ref, at)
        products = dots_ref[:, at].T / D
        for i, ref in enumerate((dq_ref, dk_ref)):
            inverse = inverses[i]
            cubed = inverse * inverse * inverse * products[:, i : i + 1]
            for h in range(heads):
                hs = slice(h * HD, (h + 1) * HD)
                there = slice(i * columns + h * HD, i * columns + (h + 1) * HD)
                value = inverse * gains_ref[i : i + 1, hs] * ref[at, hs] - raw_ref[at, there] * cubed
                joined_ref[at, there] = value.astype(jnp.bfloat16)
        return carry

    lax.fori_loop(0, size, finish, 0)
    each_peer(lambda w: hand_in(w).wait_send())


def attention_calls(rows, half, shared, columns, prompt_blocks, paired, ids):
    heads = columns // HD
    size = half // rows
    bf16, f32 = jnp.bfloat16, jnp.float32
    shape = lambda dtype, *dims: jax.ShapeDtypeStruct(dims, dtype)
    sems = pltpu.SemaphoreType.DMA
    work = half * half * columns * 2
    peers = [sems((size - 1,)), sems((size - 1,)), sems((2,)), sems((2,)), sems((size,)), sems((size,))]

    def params(k):
        return pltpu.CompilerParams(vmem_limit_bytes=60 * 2**20, collective_id=ids[k], has_side_effects=True)

    carried = 1 if size == 2 * LINE else 0
    forward_call = pl.pallas_call(
        functools.partial(attend_kernel, rows, prompt_blocks, paired, shared, carried),
        out_shape=[shape(bf16, half, columns)] * 3
        + [shape(bf16, shared, columns)] * 2
        + [shape(bf16, half, columns), shape(bf16, rows, size * columns), shape(f32, heads, half), shape(f32, 8, half)]
        + [shape(bf16, size, rows, D)] * carried,
        in_specs=[VMEM] * 4 + [ANY] * carried,
        out_specs=[VMEM] * 9 + [ANY] * carried,
        scratch_shapes=[
            pltpu.VMEM((columns, half), bf16),
            pltpu.VMEM((columns, shared), bf16),
            pltpu.VMEM((size - 1, 8, half), f32),
        ]
        + peers
        + gather_sems(carried) * carried,
        compiler_params=params(0),
        cost_estimate=pl.CostEstimate(flops=2 * work, bytes_accessed=120_000_000, transcendentals=0),
    )

    def forward(raw, gains, cosine, sine, carry):
        if carried:
            return forward_call(raw, gains, cosine, sine, carry)
        return [*forward_call(raw, gains, cosine, sine), lax.all_gather(carry, "wide", axis=0)]

    backward = pl.pallas_call(
        functools.partial(attend_back_kernel, rows, prompt_blocks, paired, shared),
        out_shape=[shape(bf16, half, 3 * columns), shape(f32, 8, columns)],
        in_specs=[VMEM] * 13,
        out_specs=[VMEM] * 2,
        scratch_shapes=[pltpu.VMEM((half, columns), bf16)]
        + [pltpu.VMEM((half, columns), f32)] * 3
        + [pltpu.VMEM((shared, columns), f32)] * 2
        + [pltpu.VMEM((shared, columns), bf16)] * 4
        + [
            pltpu.VMEM((columns, half), bf16),
            pltpu.VMEM((columns, shared), bf16),
            pltpu.VMEM((8, half), f32),
            pltpu.VMEM((size - 1, 8, half), f32),
        ]
        + peers,
        compiler_params=params(1),
        cost_estimate=pl.CostEstimate(flops=5 * work, bytes_accessed=200_000_000, transcendentals=0),
    )
    return forward, backward


def dot(a, b):
    return jnp.dot(a, b, preferred_element_type=jnp.float32)


def dot_nt(a, b):
    return lax.dot_general(a, b, NT, preferred_element_type=jnp.float32)


def dot_tn(a, b):
    return lax.dot_general(a, b, (((0,), (0,)), ((), ())), preferred_element_type=jnp.float32)


def start_kernel(count, swaps, *refs):
    ins, given = refs[:count], refs[count : count + swaps]
    outs = refs[count + swaps : 2 * count + swaps]
    got = refs[2 * count + swaps : 2 * (count + swaps)]
    send, recv, local, swap_send, swap_recv, twin_send, twin_recv = refs[2 * (count + swaps) :]
    grp, wide, narrow, line, cross = position()
    partner = (grp, wide, 1 - narrow)
    twin = (1 - grp, wide, narrow)

    def half(ref, which):
        size = ref.shape[0] // 2
        return ref.at[pl.ds(pl.multiple_of(which * size, size), size)]

    def swap(i):
        return remote(half(given[i], grp), half(got[i], grp), swap_send.at[i], swap_recv.at[i], partner)

    def share(i, which):
        return remote(half(got[i], which), half(got[i], which), twin_send.at[i], twin_recv.at[i], twin)

    def begin():
        for i in range(swaps):
            swap(i).start()

    def finish():
        for i in range(swaps):
            swap(i).wait_recv()
            share(i, grp).start()
        for i in range(swaps):
            swap(i).wait_send()
            share(i, grp).wait_send()
            share(i, 1 - grp).wait_recv()

    gather_body(count, ins, outs, send, recv, local, [(partner, None), (twin, None)], begin, finish)


def start_exchange(arrays, weights, collective_id):
    size = lax.axis_size("wide")
    if size != 2 * LINE or lax.axis_size("grp") != 2:
        swap = [(0, 1), (1, 0)]
        return [lax.all_gather(a, "wide", axis=0) for a in arrays], [lax.ppermute(w, "narrow", swap) for w in weights]
    count, swaps = len(arrays), len(weights)
    out = pl.pallas_call(
        functools.partial(start_kernel, count, swaps),
        out_shape=[jax.ShapeDtypeStruct((size, *a.shape), a.dtype) for a in arrays]
        + [jax.ShapeDtypeStruct(w.shape, w.dtype) for w in weights],
        in_specs=[ANY] * (count + swaps),
        out_specs=[ANY] * (count + swaps),
        scratch_shapes=[
            pltpu.SemaphoreType.DMA((count, 3, LINE)),
            pltpu.SemaphoreType.DMA((count, size)),
            pltpu.SemaphoreType.DMA((count,)),
        ]
        + [pltpu.SemaphoreType.DMA((swaps,))] * 4,
        compiler_params=pltpu.CompilerParams(collective_id=collective_id, has_side_effects=True),
        cost_estimate=lasts(150),
    )(*arrays, *weights)
    return out[:count], out[count:]


class SmallSum:
    def __init__(self, x_ref, o_ref, parts, total, send, recv, send_back, recv_back):
        self.refs = x_ref, o_ref, parts, total, send, recv, send_back, recv_back
        grp, wide, narrow, _, _ = position()
        self.size, _, self.width = parts.shape
        self.me = wide * 2 + narrow
        self.ranks = [lax.rem(self.me + k, self.size) for k in range(self.size)]
        self.devices = [(grp, rank // 2, lax.rem(rank, 2)) for rank in self.ranks]
        self.targets = [(device, None) for device in self.devices[1:]]

    def columns(self, rank):
        return pl.ds(pl.multiple_of(rank * self.width, self.width), self.width)

    def run(self):
        x_ref, o_ref, parts, total, send, recv, send_back, recv_back = self.refs
        devices, size, mine = self.devices, self.size, self.columns(self.me)
        out = [
            remote(x_ref.at[:, self.columns(self.ranks[k])], parts.at[k], send.at[k], recv.at[k], devices[k])
            for k in range(1, size)
        ]
        for copy in out:
            copy.start()
        total[...] = x_ref[:, mine]
        for k, copy in enumerate(out):
            copy.wait()
            total[...] += parts[k + 1]
        back = [
            remote(total, o_ref.at[:, mine], send_back.at[k], recv_back.at[k], devices[k]) for k in range(1, size)
        ]
        for copy in back:
            copy.start()
        o_ref[:, mine] = total[...]
        for copy in back:
            copy.wait_send()
        for k in range(1, size):
            rank = lax.rem(self.me - k + size, size)
            remote(total, o_ref.at[:, self.columns(rank)], send_back.at[k], recv_back.at[k], devices[k]).wait_recv()


def input_grad_kernel(
    gain_row, joined_ref, weights_ref, tokens_ref, hidden_ref, gain_ref, small_ref, out_ref, sums_ref,
    held, from_across, from_line, x_ref, parts, total_ref, send, recv_a, recv_l, *small_sems
):
    rows = tokens_ref.shape[0]
    f32 = jnp.float32
    small = SmallSum(x_ref, sums_ref, parts, total_ref, *small_sems)
    grp, wide, narrow, line, cross = position()
    across = (grp, line * 2 + 1 - cross, narrow)
    above = (grp, wide + 2, narrow)
    below = (grp, wide - 2, narrow)
    has_above, has_below = line < LINE - 1, line > 0
    greet(small.targets)
    order = [(distance, sign) for distance in range(LINE - 1, 0, -1) for sign in (1, -1)] + [(0, 1)]

    def valid(owner):
        return (owner >= 0) & (owner < LINE)

    def part(owner, column):
        at = pl.ds(pl.multiple_of((owner * 2 + column) * rows, rows), rows)
        return dot_nt(joined_ref[at], weights_ref[...])

    def across_copy(owner):
        return remote(held.at[0, owner], from_across.at[owner], send.at[0, owner], recv_a.at[owner], across)

    def line_copy(owner, up):
        slot = 0 if up else 1
        return remote(
            held.at[1, owner], from_line.at[slot, owner], send.at[1, owner], recv_l.at[slot, owner], above if up else below
        )

    for distance, sign in order:
        owner = line + sign * distance

        @pl.when(valid(owner))
        def _(owner=owner):
            held[0, owner] = part(owner, 1 - cross).astype(held.dtype)
            across_copy(owner).start()

    for distance, sign in order[:-1]:
        owner = line + sign * distance

        @pl.when(valid(owner))
        def _(owner=owner, sign=sign):
            up = sign > 0
            came = has_below if up else has_above
            total = part(owner, cross)
            across_copy(owner).wait_recv()
            total = total + from_across[owner].astype(f32)

            @pl.when(came)
            def _():
                line_copy(owner, up).wait_recv()
                held[1, owner] = (total + from_line[0 if up else 1, owner].astype(f32)).astype(held.dtype)

            @pl.when(jnp.logical_not(came))
            def _():
                held[1, owner] = total.astype(held.dtype)

            line_copy(owner, up).start()

    out_ref[...] = part(line, cross)
    across_copy(line).wait_recv()
    out_ref[...] += from_across[line].astype(f32)

    @pl.when(has_below)
    def _():
        line_copy(line, True).wait_recv()
        out_ref[...] += from_line[0, line].astype(f32)

    @pl.when(has_above)
    def _():
        line_copy(line, False).wait_recv()
        out_ref[...] += from_line[1, line].astype(f32)

    x_ref[...] = small_ref[...]
    x_ref[gain_row : gain_row + 1, :] = jnp.zeros((1, D), f32)
    chunk = min(rows, 64)

    def finish(i, carry):
        at = pl.ds(pl.multiple_of(i * chunk, chunk), chunk)
        grad = out_ref[at]
        stream = tokens_ref[at].astype(f32)
        inverse = lax.rsqrt(jnp.mean(stream * stream, -1, keepdims=True) + EPSILON)
        product = grad * stream
        x_ref[gain_row : gain_row + 1, :] += jnp.sum(product * inverse, 0, keepdims=True)
        slope = inverse * inverse * inverse * jnp.sum(product * gain_ref[...], -1, keepdims=True) / D
        out_ref[at] = hidden_ref[at] + inverse * gain_ref[...] * grad - stream * slope
        return carry

    lax.fori_loop(0, rows // chunk, finish, 0)
    small.run()

    for owner in range(LINE):
        across_copy(owner).wait_send()

        @pl.when(owner > line)
        def _(owner=owner):
            line_copy(owner, True).wait_send()

        @pl.when(owner < line)
        def _(owner=owner):
            line_copy(owner, False).wait_send()


def input_grad(joined, weights, tokens, grad_hidden, gain, small, gain_row, ids):
    size = lax.axis_size("wide")
    rows = tokens.shape[0]
    f32, bf16 = jnp.float32, jnp.bfloat16
    if size != 2 * LINE:
        part = dot_nt(joined, weights).astype(bf16).reshape(size, rows, D)
        grad = lax.psum_scatter(part, "wide", scatter_dimension=0, tiled=False).astype(f32)
        stream = tokens.astype(f32)
        inverse = lax.rsqrt(jnp.mean(stream * stream, -1, keepdims=True) + EPSILON)
        small = small.at[gain_row].set(jnp.sum(grad * stream * inverse, 0))
        slope = inverse**3 * jnp.sum(grad * gain * stream, -1, keepdims=True) / D
        return grad_hidden + inverse * gain * grad - stream * slope, lax.psum(small, ("wide", "narrow"))
    devices = 4 * LINE
    block = (LINE, rows, D)
    dma = pltpu.SemaphoreType.DMA
    return pl.pallas_call(
        functools.partial(input_grad_kernel, gain_row),
        out_shape=[jax.ShapeDtypeStruct((rows, D), f32), jax.ShapeDtypeStruct(small.shape, f32)],
        in_specs=[VMEM] * 6,
        out_specs=[VMEM] * 2,
        scratch_shapes=[
            pltpu.VMEM((2, *block), bf16),
            pltpu.VMEM(block, bf16),
            pltpu.VMEM((2, *block), bf16),
            pltpu.VMEM(small.shape, f32),
            pltpu.VMEM((devices, small.shape[0], D // devices), f32),
            pltpu.VMEM((small.shape[0], D // devices), f32),
            dma((2, LINE)),
            dma((LINE,)),
            dma((2, LINE)),
        ]
        + [dma((devices,))] * 4,
        compiler_params=pltpu.CompilerParams(
            collective_id=ids, has_side_effects=True, vmem_limit_bytes=56 * 2**20
        ),
        cost_estimate=lasts(110),
    )(joined, weights, tokens, grad_hidden, gain, small)


def expert_kernel(
    tiles, capacity, experts, first, id_ref, slot_ref, tokens_ref, grads_ref, router_ref, gate_ref, up_ref, down_ref, *refs
):
    if not first:
        moe_in_ref, part_in_ref, router_in_ref = refs[:3]
        refs = refs[3:]
    (
        moe_ref, part_ref, x_ref, g_ref, inner_ref, grad_gate_ref, grad_up_ref, router_grad_ref,
        x_all, g_all, picks, moe_all, part_all, probs_all, scores_all, router_sum,
    ) = refs
    f32, bf16 = jnp.float32, jnp.bfloat16
    group, step = pl.program_id(0), pl.program_id(1)
    blocks = picks.shape[0]
    expert = id_ref[0]
    lane = lax.broadcasted_iota(jnp.int32, (1, 128), 1)

    @pl.when(step < blocks)
    def _():
        rows = tokens_ref.shape[1]
        row = lax.broadcasted_iota(jnp.int32, (capacity, rows), 0)
        pick = jnp.where(row == slot_ref[0], 1.0, 0.0).astype(bf16)
        picks[step] = pick
        here = pl.ds(pl.multiple_of(step * capacity, capacity), capacity)
        x = dot(pick, tokens_ref[0]).astype(bf16)
        g = dot(pick, grads_ref[0]).astype(bf16)
        x_all[here], x_ref[...] = x, x
        g_all[here], g_ref[...] = g, g

    @pl.when(step == blocks)
    def _():
        logits = jnp.where(lane < experts, dot(x_all[...], router_ref[...]), NEGATIVE)
        weight = jnp.exp(logits - jnp.max(logits, -1, keepdims=True))
        probs_all[...] = weight / jnp.sum(weight, -1, keepdims=True)
        moe_all[...] = jnp.zeros_like(moe_all)
        part_all[...] = jnp.zeros_like(part_all)
        scores_all[...] = jnp.zeros_like(scores_all)

    @pl.when((step >= blocks) & (step < blocks + tiles))
    def _():
        x, g = x_all[...], g_all[...]
        gate = jnp.sum(jnp.where(lane == expert, probs_all[...], 0.0), -1, keepdims=True)
        gate_pre = dot(x, gate_ref[...])
        up_pre = dot(x, up_ref[...])
        back = dot_nt(g, down_ref[...])
        sigmoid = 1.0 / (1.0 + jnp.exp(-gate_pre))
        silu = gate_pre * sigmoid
        inner = silu * up_pre
        scores_all[...] += jnp.sum(inner * back, -1, keepdims=True)
        inner_gated = (gate * inner).astype(bf16)
        back = gate * back
        grad_gate_pre = (back * up_pre * sigmoid * (1.0 + gate_pre * (1.0 - sigmoid))).astype(bf16)
        grad_up_pre = (back * silu).astype(bf16)
        inner_ref[...] = inner_gated
        grad_gate_ref[...] = grad_gate_pre
        grad_up_ref[...] = grad_up_pre
        moe_all[...] += dot(inner_gated, down_ref[...])
        part_all[...] += dot_nt(grad_gate_pre, gate_ref[...]) + dot_nt(grad_up_pre, up_ref[...])

    @pl.when(step == blocks + tiles)
    def _():
        probs = probs_all[...]
        here = jnp.where(lane == expert, 1.0, 0.0)
        gate = jnp.sum(probs * here, -1, keepdims=True)
        mixing = (gate * scores_all[...] * (here - probs)).astype(bf16)
        part_all[...] += dot_nt(mixing, router_ref[...])
        grad = dot_tn(mixing, x_all[...])

        @pl.when(group == 0)
        def _():
            router_sum[...] = grad if first else grad + router_in_ref[...]

        @pl.when(group > 0)
        def _():
            router_sum[...] += grad

        router_grad_ref[...] = router_sum[...]

    @pl.when(step >= blocks + tiles)
    def _():
        block = step - blocks - tiles
        pick = picks[block]
        here = pl.ds(pl.multiple_of(block * capacity, capacity), capacity)
        moe = dot_tn(pick, moe_all[here].astype(bf16))
        part = dot_tn(pick, part_all[here].astype(bf16))
        if not first:
            moe = moe + moe_in_ref[0].astype(f32)
            part = part + part_in_ref[0].astype(f32)
        moe_ref[0] = moe.astype(bf16)
        part_ref[0] = part.astype(bf16)


def expert_call(expert, slots, tokens, grads, router, weights, capacity, experts, before=None):
    wide, rows, _ = tokens.shape
    units = weights[0].shape[1]
    groups = 2 if wide * capacity > 1024 else 1
    blocks, tile = wide // groups, 256
    tiles = units // tile
    last = blocks + tiles
    first = before is None
    bf16, f32 = jnp.bfloat16, jnp.float32

    def picked(g, i):
        return g * blocks + jnp.minimum(i, blocks - 1)

    def tiled(i):
        return jnp.clip(i - blocks, 0, tiles - 1)

    def spread(g, i):
        return g * blocks + jnp.clip(i - last, 0, blocks - 1)

    whole = pl.BlockSpec((1, rows, D), lambda g, i: (picked(g, i), 0, 0))
    back = pl.BlockSpec((1, rows, D), lambda g, i: (spread(g, i), 0, 0))
    row = pl.BlockSpec((capacity, D), lambda g, i: (picked(g, i), 0))
    column = pl.BlockSpec((D, tile), lambda g, i: (0, tiled(i)))
    unit = pl.BlockSpec((blocks * capacity, tile), lambda g, i: (g, tiled(i)))
    fixed = pl.BlockSpec((128, D), lambda g, i: (0, 0))
    in_specs = [
        pl.BlockSpec(memory_space=pltpu.SMEM),
        pl.BlockSpec((1, 1, rows), lambda g, i: (picked(g, i), 0, 0)),
        whole,
        whole,
        pl.BlockSpec((D, 128), lambda g, i: (0, 0)),
        column,
        column,
        pl.BlockSpec((tile, D), lambda g, i: (tiled(i), 0)),
    ] + ([] if first else [back, back, fixed])
    count = wide * capacity
    compact = jax.ShapeDtypeStruct((count, D), bf16)
    narrow = jax.ShapeDtypeStruct((count, units), bf16)
    held = blocks * capacity
    return pl.pallas_call(
        functools.partial(expert_kernel, tiles, capacity, experts, first),
        grid=(groups, last + blocks),
        in_specs=in_specs,
        out_specs=[back, back, row, row, unit, unit, unit, fixed],
        out_shape=[jax.ShapeDtypeStruct((wide, rows, D), bf16)] * 2
        + [compact] * 2
        + [narrow] * 3
        + [jax.ShapeDtypeStruct((128, D), f32)],
        scratch_shapes=[
            pltpu.VMEM((held, D), bf16),
            pltpu.VMEM((held, D), bf16),
            pltpu.VMEM((blocks, capacity, rows), bf16),
            pltpu.VMEM((held, D), f32),
            pltpu.VMEM((held, D), f32),
            pltpu.VMEM((held, 128), f32),
            pltpu.VMEM((held, 1), f32),
            pltpu.VMEM((128, D), f32),
        ],
        compiler_params=pltpu.CompilerParams(vmem_limit_bytes=60 * 2**20),
        cost_estimate=pl.CostEstimate(
            flops=12 * count * D * units, bytes_accessed=count * D * 12 + 6 * D * units, transcendentals=0
        ),
    )(expert.astype(jnp.int32).reshape(1), slots, tokens, grads, router, *weights, *(before or ()))


def positions(token_ids):
    local = token_ids % (PROMPT + NCONT * CONT)
    return jnp.where(local < PROMPT, local, PROMPT + (local - PROMPT) % CONT)


def rotation(place):
    frequency = THETA ** (-2.0 * jnp.arange(HD // 2, dtype=jnp.float32) / HD)
    angle = place.astype(jnp.float32)[:, None] * frequency[None, :]
    cosine, sine = jnp.cos(angle), jnp.sin(angle)
    return jnp.concatenate([cosine, cosine], 1), jnp.concatenate([-sine, sine], 1)


def shards(
    tokens,
    cotangent,
    valid,
    routes,
    w_query,
    w_key,
    w_value,
    w_out,
    norm_attn,
    norm_query,
    norm_key,
    norm_moe,
    w_router,
    w_gate,
    w_up,
    w_down,
):
    bf16, f32 = jnp.bfloat16, jnp.float32
    wide_count = lax.axis_size("wide")
    narrow_count = lax.axis_size("narrow")
    rows = tokens.shape[0]
    half = rows * wide_count
    columns = w_query.shape[1]
    experts = w_router.shape[1]
    hidden_units = w_gate.shape[2]
    capacity = min(max(rows * TOP * 5 // (4 * experts), 2), rows)
    assert narrow_count == 2 and CONT in (rows, 2 * rows)
    paired = CONT == 2 * rows
    side = lax.axis_index("narrow")
    place = lax.axis_index("wide")
    group = lax.axis_index("grp")
    swap = [(0, 1), (1, 0)]
    twins = lax.axis_size("grp") == 2
    prompt_blocks = PROMPT // (rows * narrow_count)
    shared = half if paired else prompt_blocks * rows
    attend, attend_back = attention_calls(rows, half, shared, columns, prompt_blocks, paired, (1, 2))
    barrier = lax.optimization_barrier

    def exchange(value):
        return lax.ppermute(value, "narrow", swap)

    stream = tokens.astype(f32)
    inv_one = lax.rsqrt(jnp.mean(stream * stream, -1, keepdims=True) + EPSILON)
    gain_one = norm_attn.astype(f32)
    normed = (stream * inv_one * gain_one).astype(bf16)
    mask = valid.astype(f32)[:, None]
    grad_final = cotangent.astype(f32) * mask
    pieces = 2 if twins else 1
    piece_width = D // pieces
    piece = lax.dynamic_slice_in_dim(w_out, group * piece_width, piece_width, 1) if twins else w_out
    (routes_plane, normed_plane, out_piece), (other_gate, other_up, other_down) = start_exchange(
        [routes.T, normed, piece], [w_gate[0], w_up[0], w_down[0]], 0
    )
    normed_plane = normed_plane.reshape(half, D)
    out_pieces = [out_piece.reshape(D, piece_width)]
    if twins:
        out_pieces.append(lax.ppermute(out_pieces[0], "grp", swap))

    def ordered(parts):
        if not twins:
            return parts
        return [jnp.where(group == 0, parts[k], parts[k ^ 1]) for k in range(2)]

    def unordered(whole):
        return ordered([whole[:, k * piece_width : (k + 1) * piece_width] for k in range(pieces)])

    joined = jnp.concatenate([w_query, w_key, w_value], 1)
    raw = dot(normed_plane, joined)
    gains = jnp.pad(jnp.stack([norm_query, norm_key]).astype(f32), ((0, 6), (0, 0)))
    plane_ids = (
        (jnp.arange(wide_count, dtype=jnp.int32)[:, None] * narrow_count + side) * rows
        + jnp.arange(rows, dtype=jnp.int32)[None, :]
    ).reshape(half)
    cosine, sine = rotation(positions(plane_ids))
    kept = attend(raw, gains, cosine, sine, grad_final.astype(bf16))
    attended, attended_own, lse, sums, grads_in = kept[5:]

    branch = jnp.concatenate(ordered([dot(attended_own, p) for p in out_pieces]), 1)
    hidden = stream + branch
    inv_two = lax.rsqrt(jnp.mean(hidden * hidden, -1, keepdims=True) + EPSILON)
    gain_two = norm_moe.astype(f32)
    moe_in = (hidden * inv_two * gain_two).astype(bf16)
    (tokens_in,) = gather_wide([moe_in], 6)

    earlier = (jnp.arange(rows)[:, None] < jnp.arange(rows)[None, :]).astype(bf16)

    def slots_of(expert):
        chosen = jnp.any(routes_plane == expert, 1)
        rank = dot(chosen.astype(bf16), earlier).astype(jnp.int32)
        return jnp.where(chosen, rank, -1).reshape(wide_count, 1, rows)

    router = jnp.pad(w_router, ((0, 0), (0, 128 - experts)))

    def run_expert(expert, weights, before):
        return expert_call(
            expert, slots_of(expert), tokens_in, grads_in, router, weights, capacity, experts, before
        )

    own = run_expert(place * narrow_count + side, (w_gate[0], w_up[0], w_down[0]), None)
    other = run_expert(
        place * narrow_count + 1 - side, (other_gate, other_up, other_down), (own[0], own[1], own[7])
    )
    moe_part, grad_part, grad_router = other[0], other[1], other[7][:experts]
    inputs, grads, inners_gated = (own[2], other[2]), (own[3], other[3]), (own[4], other[4])
    grad_pres = ((own[5], own[6]), (other[5], other[6]))
    moe = lax.psum_scatter(moe_part.reshape(half, D), "wide", scatter_dimension=0, tiled=True).astype(f32)
    partner_grads = [
        dot_tn(inputs[1], grad_pres[1][0]).astype(bf16),
        dot_tn(inputs[1], grad_pres[1][1]).astype(bf16),
        dot_tn(inners_gated[1], grads[1]).astype(bf16),
    ]
    came = [exchange(g) for g in partner_grads[:2]]
    grad_part, partner_grads = barrier((grad_part, partner_grads))
    grad_moe_in = scatter_wide(grad_part, 5)
    grad_moe_in, moe, came[0] = barrier((grad_moe_in, moe, came[0]))

    grad_gain_two = jnp.sum(grad_moe_in * hidden * inv_two, 0)
    grad_hidden = (
        grad_final
        + inv_two * gain_two * grad_moe_in
        - hidden * inv_two**3 * jnp.sum(grad_moe_in * gain_two * hidden, -1, keepdims=True) / D
    )
    grad_branch = grad_hidden.astype(bf16)
    grad_attended_own = sum(dot_nt(g, p) for g, p in zip(unordered(grad_branch), out_pieces)).astype(bf16)
    branch_plane = lax.all_gather(grad_branch, "wide", axis=0, tiled=True)
    grad_out = barrier(dot_tn(attended, branch_plane).astype(bf16))

    grads_joined, gain_grads = attend_back(
        raw, gains, cosine, sine, sums, *kept[:5], grad_attended_own, attended, lse
    )
    grads_joined, came[1], down_partner = barrier((grads_joined, came[1], partner_grads[2]))
    came.append(exchange(down_partner))
    grad_weights = barrier(dot_tn(normed_plane, grads_joined).astype(bf16))
    weights_came = exchange(grad_weights)
    out_came = exchange(grad_out)
    stats = jnp.stack([jnp.sum(v * v * mask) for v in (stream, branch, hidden, moe, hidden + moe)] + [jnp.sum(mask)])
    here = jnp.repeat(jnp.arange(wide_count) == place, columns)
    spots = [jnp.where(here, jnp.tile(g, wide_count), 0.0) for g in gain_grads[:2]]
    zeros = jnp.zeros((D,), f32)
    small = jnp.stack([zeros, grad_gain_two, *spots, jnp.pad(stats, (0, D - stats.shape[0]))])
    small = jnp.concatenate([grad_router, small, jnp.zeros((-(experts + 5) % 8, D), f32)], 0)
    small, _ = barrier((small, grad_weights))
    grad_input, small = input_grad(
        grads_joined, joined, tokens, grad_hidden, gain_one.reshape(1, D), small, experts, 3
    )
    grad_input, came[2] = barrier((grad_input, came[2]))
    expert_grads = [
        dot_tn(inputs[0], grad_pres[0][0]), dot_tn(inputs[0], grad_pres[0][1]), dot_tn(inners_gated[0], grads[0])
    ]
    grad_weights = grad_weights.astype(f32) + weights_came.astype(f32)
    grad_out = grad_out.astype(f32) + out_came.astype(f32)
    grad_query_w, grad_key_w, grad_value_w = (
        grad_weights[:, i * columns : (i + 1) * columns] for i in range(3)
    )
    final = hidden + moe
    output = final.astype(bf16)
    grad_gate_w, grad_up_w, grad_down_w = (
        (own + other.astype(f32))[None] for own, other in zip(expert_grads, came)
    )

    spots = lax.dynamic_slice_in_dim(small[experts + 2 : experts + 4], place * columns, columns, 1)
    stats = small[experts + 4, :6]
    rms = jnp.sqrt(stats[:5] / (jnp.maximum(stats[5], 1.0) * D))
    return (
        output,
        grad_input,
        grad_query_w,
        grad_key_w,
        grad_value_w,
        grad_out,
        small[experts],
        spots[0],
        spots[1],
        small[experts + 1],
        small[:experts].T,
        grad_gate_w,
        grad_up_w,
        grad_down_w,
        rms,
    )


def solution(mesh):
    return jax.shard_map(
        shards,
        mesh=mesh,
        in_specs=(
            P(("grp", "wide", "narrow"), None),
            P(("grp", "wide", "narrow"), None),
            P(("grp", "wide", "narrow")),
            P(("grp", "wide", "narrow"), None),
            P(None, "wide"),
            P(None, "wide"),
            P(None, "wide"),
            P("wide", None),
            P(),
            P("wide"),
            P("wide"),
            P(),
            P(),
            P(("wide", "narrow"), None, None),
            P(("wide", "narrow"), None, None),
            P(("wide", "narrow"), None, None),
        ),
        out_specs=(
            P(("grp", "wide", "narrow"), None),
            P(("grp", "wide", "narrow"), None),
            P("grp", "wide"),
            P("grp", "wide"),
            P("grp", "wide"),
            P(("grp", "wide"), None),
            P("grp"),
            P(("grp", "wide")),
            P(("grp", "wide")),
            P("grp"),
            P("grp", None),
            P(("grp", "wide", "narrow"), None, None),
            P(("grp", "wide", "narrow"), None, None),
            P(("grp", "wide", "narrow"), None, None),
            P("grp"),
        ),
        check_vma=False,
    )
```

```python
import functools

import jax
import jax.numpy as jnp
from jax import lax
from jax.experimental import pallas as pl
from jax.experimental.pallas import tpu as pltpu
from jax.sharding import PartitionSpec as P

D = 2048
HD = 128
TOP = 8
PROMPT = 2048
CONT = 256
NCONT = 8

EPSILON = 1e-05
THETA = 10000.0
NEGATIVE = -1e30


MESH_ID = pl.DeviceIdType.MESH
ANY = pl.BlockSpec(memory_space=pl.ANY)
VMEM = pl.BlockSpec(memory_space=pltpu.VMEM)
LINE = 4


def lasts(microseconds):
    return pl.CostEstimate(flops=0, bytes_accessed=microseconds * 3_000_000, transcendentals=0)


def position():
    grp, wide, narrow = (lax.axis_index(a) for a in ("grp", "wide", "narrow"))
    return grp, wide, narrow, wide // 2, lax.rem(wide, 2)


def greet(targets):
    barrier = pltpu.get_barrier_semaphore()
    for device, when in targets:
        def signal(device=device):
            pl.semaphore_signal(barrier, inc=1, device_id=device, device_id_type=MESH_ID)

        if when is None:
            signal()
        else:
            pl.when(when)(signal)
    peers = sum(1 if when is None else when.astype(jnp.int32) for _, when in targets)
    pl.semaphore_wait(barrier, peers)


def remote(src, dst, send, recv, device):
    return pltpu.make_async_remote_copy(
        src_ref=src, dst_ref=dst, send_sem=send, recv_sem=recv, device_id=device, device_id_type=MESH_ID
    )


def gather_kernel(count, *refs):
    ins, outs = refs[:count], refs[count : 2 * count]
    gather_body(count, ins, outs, *refs[2 * count :])


class Gather:
    def __init__(self, ins, outs, send, recv, local):
        self.ins, self.outs, self.send, self.recv, self.local = ins, outs, send, recv, local
        grp, wide, narrow, self.line, self.cross = position()
        self.wide = wide
        self.across = (grp, self.line * 2 + 1 - self.cross, narrow)
        self.above = (grp, wide + 2, narrow)
        self.below = (grp, wide - 2, narrow)
        self.has_above, self.has_below = self.line < LINE - 1, self.line > 0
        self.targets = [(self.across, None), (self.above, self.has_above), (self.below, self.has_below)]

    def copy(self, i, source_line, way, device):
        slot = source_line * 2 + self.cross
        out = self.outs[i].at[slot]
        return remote(out, out, self.send.at[i, way, source_line], self.recv.at[i, slot], device)

    def own(self, i, way, device):
        return remote(
            self.ins[i], self.outs[i].at[self.wide], self.send.at[i, way, self.line], self.recv.at[i, self.wide], device
        )

    def mine(self, i):
        return pltpu.make_async_copy(self.ins[i], self.outs[i].at[self.wide], self.local.at[i])

    def start(self):
        for i in range(len(self.ins)):
            pl.when(self.has_above)(self.own(i, 1, self.above).start)
            pl.when(self.has_below)(self.own(i, 2, self.below).start)
            self.own(i, 0, self.across).start()
            self.mine(i).start()

    def forward(self, distance, only=None):
        for i in range(len(self.ins)) if only is None else (only,):
            for sign in (-1, 1):
                source = self.line + sign * distance

                @pl.when((source >= 0) & (source < LINE))
                def _(i=i, source=source, sign=sign):
                    self.copy(i, source, 0, self.across).wait_recv()
                    onward = self.above if sign < 0 else self.below

                    @pl.when(self.has_above if sign < 0 else self.has_below)
                    def _():
                        self.copy(i, source, 1 if sign < 0 else 2, onward).start()

                    self.copy(i, source, 0, self.across).start()

    def finish(self):
        for i in range(len(self.ins)):
            send, recv, src, out = self.send, self.recv, self.ins[i], self.outs[i]
            for source in range(LINE):
                other = source * 2 + 1 - self.cross
                remote(src, out.at[other], send.at[i, 0, 0], recv.at[i, other], self.across).wait_recv()
            for source in range(LINE):
                remote(src, out.at[0], send.at[i, 0, source], recv.at[i, 0], self.across).wait_send()

                @pl.when(self.has_above & (source <= self.line))
                def _(source=source):
                    remote(src, out.at[0], send.at[i, 1, source], recv.at[i, 0], self.above).wait_send()

                @pl.when(self.has_below & (source >= self.line))
                def _(source=source):
                    remote(src, out.at[0], send.at[i, 2, source], recv.at[i, 0], self.below).wait_send()

            self.mine(i).wait()


def gather_sems(count):
    return [
        pltpu.SemaphoreType.DMA((count, 3, LINE)),
        pltpu.SemaphoreType.DMA((count, 2 * LINE)),
        pltpu.SemaphoreType.DMA((count,)),
    ]


def gather_body(count, ins, outs, send, recv, local, more=(), begin=None, finish=None):
    gather = Gather(ins, outs, send, recv, local)
    greet([*gather.targets, *more])
    gather.start()
    if begin is not None:
        begin()
    for i in range(count):
        for distance in range(1, LINE):
            gather.forward(distance, i)
    gather.finish()
    if finish is not None:
        finish()


def gather_wide(arrays, collective_id):
    count = len(arrays)
    size = lax.axis_size("wide")
    if size != 2 * LINE:
        return [lax.all_gather(a, "wide", axis=0) for a in arrays]
    return pl.pallas_call(
        functools.partial(gather_kernel, count),
        out_shape=[jax.ShapeDtypeStruct((size, *a.shape), a.dtype) for a in arrays],
        in_specs=[ANY] * count,
        out_specs=[ANY] * count,
        scratch_shapes=[
            pltpu.SemaphoreType.DMA((count, 3, LINE)),
            pltpu.SemaphoreType.DMA((count, size)),
            pltpu.SemaphoreType.DMA((count,)),
        ],
        compiler_params=pltpu.CompilerParams(collective_id=collective_id, has_side_effects=True),
        cost_estimate=lasts(100),
    )(*arrays)


def scatter_kernel(part_ref, out_ref, held, from_across, from_line, load, send, recv_a, recv_l):
    grp, wide, narrow, line, cross = position()
    across = (grp, line * 2 + 1 - cross, narrow)
    above = (grp, wide + 2, narrow)
    below = (grp, wide - 2, narrow)
    has_above, has_below = line < LINE - 1, line > 0
    f32 = jnp.float32
    greet([(across, None), (above, has_above), (below, has_below)])

    order = []
    for distance in range(LINE - 1, 0, -1):
        for sign in (1, -1):
            order.append((distance, sign))

    def valid(owner):
        return (owner >= 0) & (owner < LINE)

    def across_copy(owner):
        return remote(
            part_ref.at[owner * 2 + 1 - cross], from_across.at[owner], send.at[0, owner], recv_a.at[owner], across
        )

    def load_copy(owner):
        return pltpu.make_async_copy(part_ref.at[owner * 2 + cross], held.at[owner], load.at[owner])

    def line_copy(owner, up):
        return remote(
            held.at[owner],
            from_line.at[0 if up else 1, owner],
            send.at[1, owner],
            recv_l.at[0 if up else 1, owner],
            above if up else below,
        )

    for distance, sign in order + [(0, 1)]:
        owner = line + sign * distance

        @pl.when(valid(owner))
        def _(owner=owner):
            across_copy(owner).start()
            load_copy(owner).start()

    for distance, sign in order:
        owner = line + sign * distance

        @pl.when(valid(owner))
        def _(owner=owner, sign=sign):
            load_copy(owner).wait()
            across_copy(owner).wait_recv()
            up = sign > 0
            came = has_below if up else has_above
            total = held[owner].astype(f32) + from_across[owner].astype(f32)

            @pl.when(came)
            def _():
                line_copy(owner, up).wait_recv()
                held[owner] = (total + from_line[0 if up else 1, owner].astype(f32)).astype(held.dtype)

            @pl.when(jnp.logical_not(came))
            def _():
                held[owner] = total.astype(held.dtype)

            line_copy(owner, up).start()

    load_copy(line).wait()
    across_copy(line).wait_recv()
    out_ref[...] = held[line].astype(f32) + from_across[line].astype(f32)

    @pl.when(has_below)
    def _():
        line_copy(line, True).wait_recv()
        out_ref[...] += from_line[0, line].astype(f32)

    @pl.when(has_above)
    def _():
        line_copy(line, False).wait_recv()
        out_ref[...] += from_line[1, line].astype(f32)

    for owner in range(LINE):
        across_copy(owner).wait_send()

        @pl.when(owner > line)
        def _(owner=owner):
            line_copy(owner, True).wait_send()

        @pl.when(owner < line)
        def _(owner=owner):
            line_copy(owner, False).wait_send()


def scatter_wide(part, collective_id):
    size, rows, columns = part.shape
    if size != 2 * LINE:
        return lax.psum_scatter(part, "wide", scatter_dimension=0, tiled=False).astype(jnp.float32)
    block = (LINE, rows, columns)
    return pl.pallas_call(
        scatter_kernel,
        out_shape=jax.ShapeDtypeStruct((rows, columns), jnp.float32),
        in_specs=[ANY],
        out_specs=VMEM,
        scratch_shapes=[
            pltpu.VMEM(block, part.dtype),
            pltpu.VMEM(block, part.dtype),
            pltpu.VMEM((2, *block), part.dtype),
            pltpu.SemaphoreType.DMA((LINE,)),
            pltpu.SemaphoreType.DMA((2, LINE)),
            pltpu.SemaphoreType.DMA((LINE,)),
            pltpu.SemaphoreType.DMA((2, LINE)),
        ],
        compiler_params=pltpu.CompilerParams(
            collective_id=collective_id, has_side_effects=True, vmem_limit_bytes=48 * 2**20
        ),
        cost_estimate=lasts(95),
    )(part)


def sum_kernel(x_ref, o_ref, held, send, recv):
    grp, wide, narrow, _, _ = position()
    size = held.shape[0] + 1
    others = [(grp, lax.rem(wide + k, size), narrow) for k in range(1, size)]
    greet([(device, None) for device in others])
    copies = [
        remote(x_ref, held.at[k], send.at[k], recv.at[k], device) for k, device in enumerate(others)
    ]
    for copy in copies:
        copy.start()
    for copy in copies:
        copy.wait()
    total = x_ref[...]
    for k in range(size - 1):
        total = total + held[k]
    o_ref[...] = total


def sum_wide(x, collective_id):
    size = lax.axis_size("wide")
    if size != 2 * LINE:
        return lax.psum(x, "wide")
    return pl.pallas_call(
        sum_kernel,
        out_shape=jax.ShapeDtypeStruct(x.shape, x.dtype),
        in_specs=[VMEM],
        out_specs=VMEM,
        scratch_shapes=[
            pltpu.VMEM((size - 1, *x.shape), x.dtype),
            pltpu.SemaphoreType.DMA((size - 1,)),
            pltpu.SemaphoreType.DMA((size - 1,)),
        ],
        compiler_params=pltpu.CompilerParams(collective_id=collective_id, has_side_effects=True),
        cost_estimate=lasts(8),
    )(x)


LOG2E = 1.4426950408889634
NT = (((1,), (1,)), ((), ()))


def key_parts(w, plane, rows, prompt_blocks, paired, limit=512):
    count = (prompt_blocks if w is None else w) * rows
    parts = [(first, min(limit, count - first), None) for first in range(0, count, limit)]
    own = None if w is None else w * rows
    if plane == 0:
        parts.append((own, rows, "causal"))
    elif w is not None or paired:
        parts.append((own, rows, "side"))
    return parts


def for_blocks(blocks, prompt_blocks, one, between=None):
    for w in range(prompt_blocks):
        one(w, w, w * one.rows)
    if between is not None:
        between()

    def body(w, carry):
        one(None, w, pl.multiple_of(w * one.rows, one.rows))
        return carry

    lax.fori_loop(prompt_blocks, blocks, body, 0)


def masked_scores(score, mask, side, rows):
    if mask == "causal":
        key = lax.broadcasted_iota(jnp.int32, (rows, rows), 0)
        query = lax.broadcasted_iota(jnp.int32, (rows, rows), 1)
        return jnp.where(key <= query, score, NEGATIVE)
    if mask == "side":
        return jnp.where(side == 1, score, NEGATIVE)
    return score


def row_sums(values):
    total = values[:, :HD]
    for first in range(HD, values.shape[1], HD):
        total = total + values[:, first : first + HD]
    return jnp.sum(total.T, 0, keepdims=True)


def turn(values, cosine, sine):
    return values * cosine + pltpu.roll(values, HD // 2, 1) * sine


def inverse_norms(sums_ref, at):
    inverse = lax.rsqrt(sums_ref[:, at].T / D + EPSILON)
    return inverse[:, 0:1], inverse[:, 1:2]


def peer_copies(size, src, dst, send, recv, grp, wide, narrow):
    return [
        remote(src, dst.at[k - 1], send.at[k - 1], recv.at[k - 1], (grp, lax.rem(wide + k, size), narrow))
        for k in range(1, size)
    ]


def attend_kernel(
    rows, prompt_blocks, paired, shared, carried, raw_ref, gains_ref, cos_ref, sin_ref, *refs
):
    carry_in, refs = refs[:carried], refs[carried:]
    q_ref, k_ref, v_ref, ko_ref, vo_ref, o_ref, own_ref, lse_ref, sums_ref = refs[:9]
    carry_out, refs = refs[9 : 9 + carried], refs[9 + carried :]
    vt_ref, vto_ref, came_ref, sum_send, sum_recv, pair_send, pair_recv, out_send, out_recv = refs[:9]
    gather = Gather(carry_in, carry_out, *refs[9:]) if carried else None
    half, columns = q_ref.shape
    size = half // rows
    heads = columns // HD
    grp, wide, narrow = (lax.axis_index(a) for a in ("grp", "wide", "narrow"))
    partner = (grp, wide, 1 - narrow)
    greet([((grp, lax.rem(wide + k, size), narrow), None) for k in range(1, size)] + [(partner, None)])
    if carried:
        gather.start()
    pairs = [
        remote(src.at[pl.ds(0, shared)], dst, pair_send.at[i], pair_recv.at[i], partner)
        for i, (src, dst) in enumerate(((k_ref, ko_ref), (v_ref, vo_ref)))
    ]
    v_ref[...] = raw_ref[:, 2 * columns :].astype(jnp.bfloat16)
    pairs[1].start()
    sums_ref[...] = jnp.zeros_like(sums_ref)

    def squares(b, carry):
        at = pl.ds(pl.multiple_of(b * rows, rows), rows)
        for i in range(2):
            part = raw_ref[at, i * columns : (i + 1) * columns]
            sums_ref[i : i + 1, at] = row_sums(part * part)
        return carry

    lax.fori_loop(0, size, squares, 0)
    copies = peer_copies(size, sums_ref, came_ref, sum_send, sum_recv, grp, wide, narrow)
    for copy in copies:
        copy.start()
    for h in range(heads):
        hs = slice(h * HD, (h + 1) * HD)
        vt_ref[hs, :] = v_ref[:, hs].T
    for copy in copies:
        copy.wait()
    total = sums_ref[...]
    for k in range(size - 1):
        total = total + came_ref[k]
    sums_ref[...] = total

    def prepare(i, ref):
        def body(b, carry):
            at = pl.ds(pl.multiple_of(b * rows, rows), rows)
            inverse = inverse_norms(sums_ref, at)[i]
            for h in range(heads):
                hs = slice(h * HD, (h + 1) * HD)
                values = raw_ref[at, i * columns + h * HD : i * columns + (h + 1) * HD]
                values = values * inverse * gains_ref[i : i + 1, hs]
                ref[at, hs] = turn(values, cos_ref[at], sin_ref[at]).astype(jnp.bfloat16)
            return carry

        return body

    lax.fori_loop(0, shared // rows, prepare(1, k_ref), 0)
    pairs[0].start()
    lax.fori_loop(shared // rows, size, prepare(1, k_ref), 0)
    lax.fori_loop(0, size, prepare(0, q_ref), 0)
    if carried:
        gather.forward(1)
    pairs[1].wait()
    for h in range(heads):
        hs = slice(h * HD, (h + 1) * HD)
        vto_ref[hs, :] = vo_ref[:, hs].T
    pairs[0].wait()

    def mine():
        return pl.ds(pl.multiple_of(wide * columns, columns), columns)

    def hand_out(w):
        return remote(
            o_ref.at[pl.ds(pl.multiple_of(w * rows, rows), rows)],
            own_ref.at[:, mine()],
            out_send.at[w],
            out_recv.at[wide],
            (grp, w, narrow),
        )

    def one(w, w_index, start):
        block = pl.ds(start, rows)
        for h in range(heads):
            hs = slice(h * HD, (h + 1) * HD)
            query = q_ref[block, hs]
            scores = []
            for plane in range(2):
                for first, count, mask in key_parts(w, plane, rows, prompt_blocks, paired):
                    at = pl.ds(start if first is None else first, count)
                    key = (k_ref, ko_ref)[plane][at, hs]
                    score = lax.dot_general(key, query, NT, preferred_element_type=jnp.float32)
                    score = score * (HD**-0.5 * LOG2E)
                    scores.append((plane, at, masked_scores(score, mask, narrow, rows)))
            largest = functools.reduce(
                jnp.maximum, [jnp.max(score, 0, keepdims=True) for _, _, score in scores]
            )
            total = jnp.zeros((1, rows), jnp.float32)
            mixed = jnp.zeros((HD, rows), jnp.float32)
            for plane, at, score in scores:
                weight = jnp.exp2(score - largest)
                total = total + jnp.sum(weight, 0, keepdims=True)
                mixed = mixed + dot((vt_ref, vto_ref)[plane][hs, at], weight.astype(jnp.bfloat16))
            o_ref[block, hs] = (mixed / total).T.astype(jnp.bfloat16)
            lse_ref[h : h + 1, block] = largest + jnp.log(total) * LOG2E

        @pl.when(w_index != wide)
        def _():
            hand_out(w_index).start()

    one.rows = rows
    for_blocks(size, prompt_blocks, one, (lambda: gather.forward(2)) if carried else None)
    if carried:
        gather.forward(3)
    own_ref[:, mine()] = o_ref[pl.ds(pl.multiple_of(wide * rows, rows), rows)]

    def finish(w, carry):
        @pl.when(w != wide)
        def _():
            hand_out(w).wait_send()
            remote(
                o_ref.at[pl.ds(0, rows)], own_ref.at[:, mine()], out_send.at[w], out_recv.at[w], (grp, w, narrow)
            ).wait_recv()

        return carry

    lax.fori_loop(0, size, finish, 0)
    if carried:
        gather.finish()


def attend_back_kernel(
    rows, prompt_blocks, paired, shared, carried, raw_ref, gains_ref, cos_ref, sin_ref, sums_ref,
    q_ref, k_ref, v_ref, ko_ref, vo_ref, grad_ref, o_ref, lse_ref, *refs
):
    carry_in, refs = refs[:carried], refs[carried:]
    joined_ref, gain_ref = refs[:2]
    carry_out, refs = refs[2 : 2 + carried], refs[2 + carried :]
    do_ref, dq_ref, dk_ref, dv_ref, dko_ref, dvo_ref, dkb_ref, dvb_ref, dkr_ref, dvr_ref, kt_ref, kto_ref = refs[:12]
    dots_ref, came_ref, sum_send, sum_recv, pair_send, pair_recv, in_send, in_recv = refs[12:20]
    gather = Gather(carry_in, carry_out, *refs[20:]) if carried else None
    half, columns = q_ref.shape
    size = half // rows
    heads = columns // HD
    grp, wide, narrow = (lax.axis_index(a) for a in ("grp", "wide", "narrow"))
    partner = (grp, wide, 1 - narrow)
    greet([((grp, lax.rem(wide + k, size), narrow), None) for k in range(1, size)] + [(partner, None)])
    my_rows = pl.ds(pl.multiple_of(wide * rows, rows), rows)

    def part_of(w):
        return pl.ds(pl.multiple_of(w * columns, columns), columns)

    def hand_in(w):
        return remote(
            grad_ref.at[:, part_of(w)], do_ref.at[my_rows], in_send.at[w], in_recv.at[wide], (grp, w, narrow)
        )

    def each_peer(act):
        def body(w, carry):
            pl.when(w != wide)(lambda: act(w))
            return carry

        lax.fori_loop(0, size, body, 0)

    each_peer(lambda w: hand_in(w).start())
    if carried:
        gather.start()
    do_ref[my_rows, :] = grad_ref[:, part_of(wide)]
    for ref in (dk_ref, dv_ref, dko_ref, dvo_ref, dots_ref, gain_ref):
        ref[...] = jnp.zeros_like(ref)
    for h in range(heads):
        hs = slice(h * HD, (h + 1) * HD)
        kt_ref[hs, :] = k_ref[:, hs].T
        kto_ref[hs, :] = ko_ref[:, hs].T
    each_peer(
        lambda w: remote(
            grad_ref.at[:, part_of(w)], do_ref.at[my_rows], in_send.at[w], in_recv.at[w], (grp, w, narrow)
        ).wait_recv()
    )

    def sweep(plane):
        keys, values = ((k_ref, v_ref), (ko_ref, vo_ref))[plane]
        dk, dv = ((dk_ref, dv_ref), (dko_ref, dvo_ref))[plane]
        flipped = (kt_ref, kto_ref)[plane]

        def one(w, w_index, start):
            block = pl.ds(start, rows)
            for h in range(heads):
                hs = slice(h * HD, (h + 1) * HD)
                query = q_ref[block, hs]
                grad = do_ref[block, hs]
                delta = row_sums(grad.astype(jnp.float32) * o_ref[block, hs].astype(jnp.float32))
                lse = lse_ref[h : h + 1, block]
                back = jnp.zeros((HD, rows), jnp.float32)
                for first, count, mask in key_parts(w, plane, rows, prompt_blocks, paired):
                    at = pl.ds(start if first is None else first, count)
                    score = lax.dot_general(keys[at, hs], query, NT, preferred_element_type=jnp.float32)
                    score = masked_scores(score * (HD**-0.5 * LOG2E), mask, narrow, rows)
                    weight = jnp.exp2(score - lse)
                    grad_weight = lax.dot_general(values[at, hs], grad, NT, preferred_element_type=jnp.float32)
                    grad_score = (weight * (grad_weight - delta)).astype(jnp.bfloat16)
                    dv[at, hs] += dot(weight.astype(jnp.bfloat16), grad)
                    dk[at, hs] += dot(grad_score, query) * HD**-0.5
                    back = back + dot(flipped[hs, at], grad_score)
                back = back.T * HD**-0.5
                dq_ref[block, hs] = back if plane == 1 else dq_ref[block, hs] + back

        one.rows = rows
        for_blocks(size, prompt_blocks, one, (lambda: gather.forward(2 - plane)) if carried else None)

    sweep(1)
    dkb_ref[...] = dko_ref[...].astype(jnp.bfloat16)
    dvb_ref[...] = dvo_ref[...].astype(jnp.bfloat16)
    pairs = [
        remote(src, dst, pair_send.at[i], pair_recv.at[i], partner)
        for i, (src, dst) in enumerate(((dkb_ref, dkr_ref), (dvb_ref, dvr_ref)))
    ]
    for copy in pairs:
        copy.start()
    sweep(0)

    def turn_back(i, ref):
        def body(b, carry):
            at = pl.ds(pl.multiple_of(b * rows, rows), rows)
            inverse = inverse_norms(sums_ref, at)[i]
            products = []
            for h in range(heads):
                hs = slice(h * HD, (h + 1) * HD)
                grad = turn(ref[at, hs], cos_ref[at], -sin_ref[at])
                ref[at, hs] = grad
                product = grad * raw_ref[at, i * columns + h * HD : i * columns + (h + 1) * HD]
                gain_ref[i : i + 1, hs] += jnp.sum(product * inverse, 0, keepdims=True)
                products.append(product * gains_ref[i : i + 1, hs])
            dots_ref[i : i + 1, at] = row_sums(sum(products[1:], products[0]))
            return carry

        lax.fori_loop(0, size, body, 0)

    turn_back(0, dq_ref)
    if carried:
        gather.forward(3)
    for copy in pairs:
        copy.wait()
    dk_ref[0:shared, :] += dkr_ref[...].astype(jnp.float32)
    turn_back(1, dk_ref)
    copies = peer_copies(size, dots_ref, came_ref, sum_send, sum_recv, grp, wide, narrow)
    for copy in copies:
        copy.start()
    joined_ref[0:shared, 2 * columns :] = (dv_ref[0:shared] + dvr_ref[...].astype(jnp.float32)).astype(jnp.bfloat16)
    if shared < half:
        joined_ref[shared:, 2 * columns :] = dv_ref[shared:].astype(jnp.bfloat16)
    for copy in copies:
        copy.wait()
    total = dots_ref[...]
    for k in range(size - 1):
        total = total + came_ref[k]
    dots_ref[...] = total

    def finish(b, carry):
        at = pl.ds(pl.multiple_of(b * rows, rows), rows)
        inverses = inverse_norms(sums_ref, at)
        products = dots_ref[:, at].T / D
        for i, ref in enumerate((dq_ref, dk_ref)):
            inverse = inverses[i]
            cubed = inverse * inverse * inverse * products[:, i : i + 1]
            for h in range(heads):
                hs = slice(h * HD, (h + 1) * HD)
                there = slice(i * columns + h * HD, i * columns + (h + 1) * HD)
                value = inverse * gains_ref[i : i + 1, hs] * ref[at, hs] - raw_ref[at, there] * cubed
                joined_ref[at, there] = value.astype(jnp.bfloat16)
        return carry

    lax.fori_loop(0, size, finish, 0)
    each_peer(lambda w: hand_in(w).wait_send())
    if carried:
        gather.finish()


def attention_calls(rows, half, shared, columns, prompt_blocks, paired, ids):
    heads = columns // HD
    size = half // rows
    bf16, f32 = jnp.bfloat16, jnp.float32
    shape = lambda dtype, *dims: jax.ShapeDtypeStruct(dims, dtype)
    sems = pltpu.SemaphoreType.DMA
    peers = [sems((size - 1,)), sems((size - 1,)), sems((2,)), sems((2,)), sems((size,)), sems((size,))]

    def params(k):
        return pltpu.CompilerParams(vmem_limit_bytes=60 * 2**20, collective_id=ids[k], has_side_effects=True)

    carried = 1 if size == 2 * LINE else 0
    forward_call = pl.pallas_call(
        functools.partial(attend_kernel, rows, prompt_blocks, paired, shared, carried),
        out_shape=[shape(bf16, half, columns)] * 3
        + [shape(bf16, shared, columns)] * 2
        + [shape(bf16, half, columns), shape(bf16, rows, size * columns), shape(f32, heads, half), shape(f32, 8, half)]
        + [shape(bf16, size, rows, D)] * carried,
        in_specs=[VMEM] * 4 + [ANY] * carried,
        out_specs=[VMEM] * 9 + [ANY] * carried,
        scratch_shapes=[
            pltpu.VMEM((columns, half), bf16),
            pltpu.VMEM((columns, shared), bf16),
            pltpu.VMEM((size - 1, 8, half), f32),
        ]
        + peers
        + gather_sems(carried) * carried,
        compiler_params=params(0),
        cost_estimate=pl.CostEstimate(flops=0, bytes_accessed=300_000_000, transcendentals=0),
    )

    def forward(raw, gains, cosine, sine, carry):
        if carried:
            return forward_call(raw, gains, cosine, sine, carry)
        return [*forward_call(raw, gains, cosine, sine), lax.all_gather(carry, "wide", axis=0)]

    backward_call = pl.pallas_call(
        functools.partial(attend_back_kernel, rows, prompt_blocks, paired, shared, carried),
        out_shape=[shape(bf16, half, 3 * columns), shape(f32, 8, columns)]
        + [shape(bf16, size, rows, D)] * carried,
        in_specs=[VMEM] * 13 + [ANY] * carried,
        out_specs=[VMEM] * 2 + [ANY] * carried,
        scratch_shapes=[pltpu.VMEM((half, columns), bf16)]
        + [pltpu.VMEM((half, columns), f32)] * 3
        + [pltpu.VMEM((shared, columns), f32)] * 2
        + [pltpu.VMEM((shared, columns), bf16)] * 4
        + [
            pltpu.VMEM((columns, half), bf16),
            pltpu.VMEM((columns, shared), bf16),
            pltpu.VMEM((8, half), f32),
            pltpu.VMEM((size - 1, 8, half), f32),
        ]
        + peers
        + gather_sems(carried) * carried,
        compiler_params=params(1),
        cost_estimate=pl.CostEstimate(flops=0, bytes_accessed=300_000_000, transcendentals=0),
    )
    def backward(*args):
        if carried:
            return backward_call(*args)
        return [*backward_call(*args[:-1]), lax.all_gather(args[-1], "wide", axis=0)]

    return forward, backward


def dot(a, b):
    return jnp.dot(a, b, preferred_element_type=jnp.float32)


def dot_nt(a, b):
    return lax.dot_general(a, b, NT, preferred_element_type=jnp.float32)


def dot_tn(a, b):
    return lax.dot_general(a, b, (((0,), (0,)), ((), ())), preferred_element_type=jnp.float32)


def start_kernel(count, swaps, *refs):
    ins, given = refs[:count], refs[count : count + swaps]
    outs = refs[count + swaps : 2 * count + swaps]
    got = refs[2 * count + swaps : 2 * (count + swaps)]
    send, recv, local, swap_send, swap_recv, twin_send, twin_recv = refs[2 * (count + swaps) :]
    grp, wide, narrow, line, cross = position()
    partner = (grp, wide, 1 - narrow)
    twin = (1 - grp, wide, narrow)

    def half(ref, which):
        size = ref.shape[0] // 2
        return ref.at[pl.ds(pl.multiple_of(which * size, size), size)]

    def swap(i):
        return remote(half(given[i], grp), half(got[i], grp), swap_send.at[i], swap_recv.at[i], partner)

    def share(i, which):
        return remote(half(got[i], which), half(got[i], which), twin_send.at[i], twin_recv.at[i], twin)

    def begin():
        for i in range(swaps):
            swap(i).start()

    def finish():
        for i in range(swaps):
            swap(i).wait_recv()
            share(i, grp).start()
        for i in range(swaps):
            swap(i).wait_send()
            share(i, grp).wait_send()
            share(i, 1 - grp).wait_recv()

    gather_body(count, ins, outs, send, recv, local, [(partner, None), (twin, None)], begin, finish)


def start_exchange(arrays, weights, collective_id):
    size = lax.axis_size("wide")
    if size != 2 * LINE or lax.axis_size("grp") != 2:
        swap = [(0, 1), (1, 0)]
        return [lax.all_gather(a, "wide", axis=0) for a in arrays], [lax.ppermute(w, "narrow", swap) for w in weights]
    count, swaps = len(arrays), len(weights)
    out = pl.pallas_call(
        functools.partial(start_kernel, count, swaps),
        out_shape=[jax.ShapeDtypeStruct((size, *a.shape), a.dtype) for a in arrays]
        + [jax.ShapeDtypeStruct(w.shape, w.dtype) for w in weights],
        in_specs=[ANY] * (count + swaps),
        out_specs=[ANY] * (count + swaps),
        scratch_shapes=[
            pltpu.SemaphoreType.DMA((count, 3, LINE)),
            pltpu.SemaphoreType.DMA((count, size)),
            pltpu.SemaphoreType.DMA((count,)),
        ]
        + [pltpu.SemaphoreType.DMA((swaps,))] * 4,
        compiler_params=pltpu.CompilerParams(collective_id=collective_id, has_side_effects=True),
        cost_estimate=lasts(150),
    )(*arrays, *weights)
    return out[:count], out[count:]


def expert_grad_kernel(
    part_ref, *refs
):
    operands = refs[0:5]
    out_ref, gate_out, up_out, down_out = refs[5:9]
    held, from_across, from_line, x_buf, g_buf, inner_buf, gate_buf, up_buf, stage = refs[9:18]
    load, send, recv_a, recv_l, fetch, put = refs[18:]
    grp, wide, narrow, line, cross = position()
    across = (grp, line * 2 + 1 - cross, narrow)
    above = (grp, wide + 2, narrow)
    below = (grp, wide - 2, narrow)
    has_above, has_below = line < LINE - 1, line > 0
    f32, bf16 = jnp.float32, jnp.bfloat16
    greet([(across, None), (above, has_above), (below, has_below)])
    order = [(distance, sign) for distance in range(LINE - 1, 0, -1) for sign in (1, -1)]

    def valid(owner):
        return (owner >= 0) & (owner < LINE)

    def across_copy(owner):
        return remote(
            part_ref.at[owner * 2 + 1 - cross], from_across.at[owner], send.at[0, owner], recv_a.at[owner], across
        )

    def load_copy(owner):
        return pltpu.make_async_copy(part_ref.at[owner * 2 + cross], held.at[owner], load.at[owner])

    def line_copy(owner, up):
        slot = 0 if up else 1
        return remote(
            held.at[owner], from_line.at[slot, owner], send.at[1, owner], recv_l.at[slot, owner], above if up else below
        )

    for distance, sign in order + [(0, 1)]:
        owner = line + sign * distance

        @pl.when(valid(owner))
        def _(owner=owner):
            across_copy(owner).start()
            load_copy(owner).start()

    bufs = (x_buf, g_buf, inner_buf, gate_buf, up_buf)

    fetches = [pltpu.make_async_copy(src, dst, fetch.at[i]) for i, (src, dst) in enumerate(zip(operands, bufs))]
    for copy in fetches:
        copy.start()

    tiles = stage.shape[0]
    width = gate_buf.shape[1] // tiles

    def tile(n, size):
        return pl.ds(pl.multiple_of(n * size, size), size)

    def column_job(values, result):
        def put_copy(n):
            return pltpu.make_async_copy(stage.at[n], result.at[:, tile(n, width)], put.at[n])

        def run():
            @pl.loop(0, tiles)
            def _(n):
                stage[n] = dot_tn(x_buf[...], values[:, tile(n, width)]).astype(bf16)
                put_copy(n).start()

            @pl.loop(0, tiles)
            def _(n):
                put_copy(n).wait()

        return run

    def down_job(result):
        units = inner_buf.shape[1] // tiles

        def run():
            for n in range(tiles):
                at = slice(n * units, (n + 1) * units)
                product = dot_tn(inner_buf[:, at], g_buf[...]).astype(bf16)
                for c in range(product.shape[1] // width):
                    stage[n, c * units : (c + 1) * units, :] = product[:, c * width : (c + 1) * width]
            copies = [
                pltpu.make_async_copy(
                    stage.at[n, pl.ds(c * units, units)],
                    result.at[pl.ds(n * units, units), pl.ds(c * width, width)],
                    put.at[n * (g_buf.shape[1] // width) + c],
                )
                for n in range(tiles)
                for c in range(g_buf.shape[1] // width)
            ]
            for copy in copies:
                copy.start()
            for copy in copies:
                copy.wait()

        return run

    def first_job():
        for copy in fetches:
            copy.wait()
        column_job(gate_buf, gate_out)()

    jobs = [first_job, None, column_job(up_buf, up_out), None, down_job(down_out), None]
    for job, (distance, sign) in zip(jobs, order):
        if job is not None:
            job()
        owner = line + sign * distance

        @pl.when(valid(owner))
        def _(owner=owner, sign=sign):
            load_copy(owner).wait()
            across_copy(owner).wait_recv()
            up = sign > 0
            came = has_below if up else has_above
            total = held[owner].astype(f32) + from_across[owner].astype(f32)

            @pl.when(came)
            def _():
                line_copy(owner, up).wait_recv()
                held[owner] = (total + from_line[0 if up else 1, owner].astype(f32)).astype(held.dtype)

            @pl.when(jnp.logical_not(came))
            def _():
                held[owner] = total.astype(held.dtype)

            line_copy(owner, up).start()

    load_copy(line).wait()
    across_copy(line).wait_recv()
    out_ref[...] = held[line].astype(f32) + from_across[line].astype(f32)

    @pl.when(has_below)
    def _():
        line_copy(line, True).wait_recv()
        out_ref[...] += from_line[0, line].astype(f32)

    @pl.when(has_above)
    def _():
        line_copy(line, False).wait_recv()
        out_ref[...] += from_line[1, line].astype(f32)

    for owner in range(LINE):
        across_copy(owner).wait_send()

        @pl.when(owner > line)
        def _(owner=owner):
            line_copy(owner, True).wait_send()

        @pl.when(owner < line)
        def _(owner=owner):
            line_copy(owner, False).wait_send()


def plain_grads(x, g, inner, gate, up):
    return [dot_tn(a, b).astype(jnp.bfloat16) for a, b in ((x, gate), (x, up), (inner, g))]


def expert_grad(part, own, collective_id):
    size, rows, columns = part.shape
    f32, bf16 = jnp.float32, jnp.bfloat16
    if size != 2 * LINE:
        return lax.psum_scatter(part, "wide", scatter_dimension=0, tiled=False).astype(f32), *plain_grads(*own)
    count, units = own[2].shape
    tiles = 4
    block = (LINE, rows, columns)
    gate = jax.ShapeDtypeStruct((D, units), bf16)
    down = jax.ShapeDtypeStruct((units, D), bf16)
    dma = pltpu.SemaphoreType.DMA
    return pl.pallas_call(
        expert_grad_kernel,
        out_shape=[jax.ShapeDtypeStruct((rows, columns), f32), gate, gate, down],
        in_specs=[ANY] * 6,
        out_specs=[VMEM] + [ANY] * 3,
        scratch_shapes=[
            pltpu.VMEM(block, bf16),
            pltpu.VMEM(block, bf16),
            pltpu.VMEM((2, *block), bf16),
            pltpu.VMEM((count, D), bf16),
            pltpu.VMEM((count, D), bf16),
            pltpu.VMEM((count, units), bf16),
            pltpu.VMEM((count, units), bf16),
            pltpu.VMEM((count, units), bf16),
            pltpu.VMEM((tiles, D, units // tiles), bf16),
            dma((LINE,)),
            dma((2, LINE)),
            dma((LINE,)),
            dma((2, LINE)),
            dma((5,)),
            dma((tiles * D // (units // tiles),)),
        ],
        compiler_params=pltpu.CompilerParams(
            collective_id=collective_id, has_side_effects=True, vmem_limit_bytes=60 * 2**20
        ),
        cost_estimate=lasts(1),
    )(part, *own)


class SmallSum:
    def __init__(self, x_ref, o_ref, parts, total, send, recv, send_back, recv_back):
        self.refs = x_ref, o_ref, parts, total, send, recv, send_back, recv_back
        grp, wide, narrow, _, _ = position()
        self.size, _, self.width = parts.shape
        self.me = wide * 2 + narrow
        self.ranks = [lax.rem(self.me + k, self.size) for k in range(self.size)]
        self.devices = [(grp, rank // 2, lax.rem(rank, 2)) for rank in self.ranks]
        self.targets = [(device, None) for device in self.devices[1:]]

    def columns(self, rank):
        return pl.ds(pl.multiple_of(rank * self.width, self.width), self.width)

    def run(self):
        x_ref, o_ref, parts, total, send, recv, send_back, recv_back = self.refs
        devices, size, mine = self.devices, self.size, self.columns(self.me)
        out = [
            remote(x_ref.at[:, self.columns(self.ranks[k])], parts.at[k], send.at[k], recv.at[k], devices[k])
            for k in range(1, size)
        ]
        for copy in out:
            copy.start()
        total[...] = x_ref[:, mine]
        for k, copy in enumerate(out):
            copy.wait()
            total[...] += parts[k + 1]
        back = [
            remote(total, o_ref.at[:, mine], send_back.at[k], recv_back.at[k], devices[k]) for k in range(1, size)
        ]
        for copy in back:
            copy.start()
        o_ref[:, mine] = total[...]
        for copy in back:
            copy.wait_send()
        for k in range(1, size):
            rank = lax.rem(self.me - k + size, size)
            remote(total, o_ref.at[:, self.columns(rank)], send_back.at[k], recv_back.at[k], devices[k]).wait_recv()


def input_grad_kernel(
    gain_row, joined_ref, weights_ref, tokens_ref, hidden_ref, gain_ref, small_ref, out_ref, sums_ref,
    held, from_across, from_line, x_ref, parts, total_ref, send, recv_a, recv_l, *small_sems
):
    rows = tokens_ref.shape[0]
    f32 = jnp.float32
    small = SmallSum(x_ref, sums_ref, parts, total_ref, *small_sems)
    grp, wide, narrow, line, cross = position()
    across = (grp, line * 2 + 1 - cross, narrow)
    above = (grp, wide + 2, narrow)
    below = (grp, wide - 2, narrow)
    has_above, has_below = line < LINE - 1, line > 0
    greet(small.targets)
    order = [(distance, sign) for distance in range(LINE - 1, 0, -1) for sign in (1, -1)] + [(0, 1)]

    def valid(owner):
        return (owner >= 0) & (owner < LINE)

    def part(owner, column):
        at = pl.ds(pl.multiple_of((owner * 2 + column) * rows, rows), rows)
        return dot_nt(joined_ref[at], weights_ref[...])

    def across_copy(owner):
        return remote(held.at[0, owner], from_across.at[owner], send.at[0, owner], recv_a.at[owner], across)

    def line_copy(owner, up):
        slot = 0 if up else 1
        return remote(
            held.at[1, owner], from_line.at[slot, owner], send.at[1, owner], recv_l.at[slot, owner], above if up else below
        )

    for distance, sign in order:
        owner = line + sign * distance

        @pl.when(valid(owner))
        def _(owner=owner):
            held[0, owner] = part(owner, 1 - cross).astype(held.dtype)
            across_copy(owner).start()

    for distance, sign in order[:-1]:
        owner = line + sign * distance

        @pl.when(valid(owner))
        def _(owner=owner, sign=sign):
            up = sign > 0
            came = has_below if up else has_above
            total = part(owner, cross)
            across_copy(owner).wait_recv()
            total = total + from_across[owner].astype(f32)

            @pl.when(came)
            def _():
                line_copy(owner, up).wait_recv()
                held[1, owner] = (total + from_line[0 if up else 1, owner].astype(f32)).astype(held.dtype)

            @pl.when(jnp.logical_not(came))
            def _():
                held[1, owner] = total.astype(held.dtype)

            line_copy(owner, up).start()

    out_ref[...] = part(line, cross)
    across_copy(line).wait_recv()
    out_ref[...] += from_across[line].astype(f32)

    @pl.when(has_below)
    def _():
        line_copy(line, True).wait_recv()
        out_ref[...] += from_line[0, line].astype(f32)

    @pl.when(has_above)
    def _():
        line_copy(line, False).wait_recv()
        out_ref[...] += from_line[1, line].astype(f32)

    x_ref[...] = small_ref[...]
    x_ref[gain_row : gain_row + 1, :] = jnp.zeros((1, D), f32)
    chunk = min(rows, 64)

    def finish(i, carry):
        at = pl.ds(pl.multiple_of(i * chunk, chunk), chunk)
        grad = out_ref[at]
        stream = tokens_ref[at].astype(f32)
        inverse = lax.rsqrt(jnp.mean(stream * stream, -1, keepdims=True) + EPSILON)
        product = grad * stream
        x_ref[gain_row : gain_row + 1, :] += jnp.sum(product * inverse, 0, keepdims=True)
        slope = inverse * inverse * inverse * jnp.sum(product * gain_ref[...], -1, keepdims=True) / D
        out_ref[at] = hidden_ref[at] + inverse * gain_ref[...] * grad - stream * slope
        return carry

    lax.fori_loop(0, rows // chunk, finish, 0)
    small.run()

    for owner in range(LINE):
        across_copy(owner).wait_send()

        @pl.when(owner > line)
        def _(owner=owner):
            line_copy(owner, True).wait_send()

        @pl.when(owner < line)
        def _(owner=owner):
            line_copy(owner, False).wait_send()


def input_grad(joined, weights, tokens, grad_hidden, gain, small, gain_row, ids):
    size = lax.axis_size("wide")
    rows = tokens.shape[0]
    f32, bf16 = jnp.float32, jnp.bfloat16
    if size != 2 * LINE:
        part = dot_nt(joined, weights).astype(bf16).reshape(size, rows, D)
        grad = lax.psum_scatter(part, "wide", scatter_dimension=0, tiled=False).astype(f32)
        stream = tokens.astype(f32)
        inverse = lax.rsqrt(jnp.mean(stream * stream, -1, keepdims=True) + EPSILON)
        small = small.at[gain_row].set(jnp.sum(grad * stream * inverse, 0))
        slope = inverse**3 * jnp.sum(grad * gain * stream, -1, keepdims=True) / D
        return grad_hidden + inverse * gain * grad - stream * slope, lax.psum(small, ("wide", "narrow"))
    devices = 4 * LINE
    block = (LINE, rows, D)
    dma = pltpu.SemaphoreType.DMA
    return pl.pallas_call(
        functools.partial(input_grad_kernel, gain_row),
        out_shape=[jax.ShapeDtypeStruct((rows, D), f32), jax.ShapeDtypeStruct(small.shape, f32)],
        in_specs=[VMEM] * 6,
        out_specs=[VMEM] * 2,
        scratch_shapes=[
            pltpu.VMEM((2, *block), bf16),
            pltpu.VMEM(block, bf16),
            pltpu.VMEM((2, *block), bf16),
            pltpu.VMEM(small.shape, f32),
            pltpu.VMEM((devices, small.shape[0], D // devices), f32),
            pltpu.VMEM((small.shape[0], D // devices), f32),
            dma((2, LINE)),
            dma((LINE,)),
            dma((2, LINE)),
        ]
        + [dma((devices,))] * 4,
        compiler_params=pltpu.CompilerParams(
            collective_id=ids, has_side_effects=True, vmem_limit_bytes=56 * 2**20
        ),
        cost_estimate=lasts(100),
    )(joined, weights, tokens, grad_hidden, gain, small)


def expert_kernel(
    tiles, capacity, experts, first, id_ref, slot_ref, tokens_ref, grads_ref, router_ref, gate_ref, up_ref, down_ref, *refs
):
    if not first:
        moe_in_ref, part_in_ref, router_in_ref = refs[:3]
        refs = refs[3:]
    (
        moe_ref, part_ref, x_ref, g_ref, inner_ref, grad_gate_ref, grad_up_ref, router_grad_ref,
        x_all, g_all, picks, moe_all, part_all, probs_all, scores_all, router_sum,
    ) = refs
    f32, bf16 = jnp.float32, jnp.bfloat16
    group, step = pl.program_id(0), pl.program_id(1)
    blocks = picks.shape[0]
    expert = id_ref[0]
    lane = lax.broadcasted_iota(jnp.int32, (1, 128), 1)

    @pl.when(step < blocks)
    def _():
        rows = tokens_ref.shape[1]
        row = lax.broadcasted_iota(jnp.int32, (capacity, rows), 0)
        pick = jnp.where(row == slot_ref[0], 1.0, 0.0).astype(bf16)
        picks[step] = pick
        here = pl.ds(pl.multiple_of(step * capacity, capacity), capacity)
        x = dot(pick, tokens_ref[0]).astype(bf16)
        g = dot(pick, grads_ref[0]).astype(bf16)
        x_all[here], x_ref[...] = x, x
        g_all[here], g_ref[...] = g, g

    @pl.when(step == blocks)
    def _():
        logits = jnp.where(lane < experts, dot(x_all[...], router_ref[...]), NEGATIVE)
        weight = jnp.exp(logits - jnp.max(logits, -1, keepdims=True))
        probs_all[...] = weight / jnp.sum(weight, -1, keepdims=True)
        moe_all[...] = jnp.zeros_like(moe_all)
        part_all[...] = jnp.zeros_like(part_all)
        scores_all[...] = jnp.zeros_like(scores_all)

    @pl.when((step >= blocks) & (step < blocks + tiles))
    def _():
        x, g = x_all[...], g_all[...]
        gate = jnp.sum(jnp.where(lane == expert, probs_all[...], 0.0), -1, keepdims=True)
        gate_pre = dot(x, gate_ref[...])
        up_pre = dot(x, up_ref[...])
        back = dot_nt(g, down_ref[...])
        sigmoid = 1.0 / (1.0 + jnp.exp(-gate_pre))
        silu = gate_pre * sigmoid
        inner = silu * up_pre
        scores_all[...] += jnp.sum(inner * back, -1, keepdims=True)
        inner_gated = (gate * inner).astype(bf16)
        back = gate * back
        grad_gate_pre = (back * up_pre * sigmoid * (1.0 + gate_pre * (1.0 - sigmoid))).astype(bf16)
        grad_up_pre = (back * silu).astype(bf16)
        inner_ref[...] = inner_gated
        grad_gate_ref[...] = grad_gate_pre
        grad_up_ref[...] = grad_up_pre
        moe_all[...] += dot(inner_gated, down_ref[...])
        part_all[...] += dot_nt(grad_gate_pre, gate_ref[...]) + dot_nt(grad_up_pre, up_ref[...])

    @pl.when(step == blocks + tiles)
    def _():
        probs = probs_all[...]
        here = jnp.where(lane == expert, 1.0, 0.0)
        gate = jnp.sum(probs * here, -1, keepdims=True)
        mixing = (gate * scores_all[...] * (here - probs)).astype(bf16)
        part_all[...] += dot_nt(mixing, router_ref[...])
        grad = dot_tn(mixing, x_all[...])

        @pl.when(group == 0)
        def _():
            router_sum[...] = grad if first else grad + router_in_ref[...]

        @pl.when(group > 0)
        def _():
            router_sum[...] += grad

        router_grad_ref[...] = router_sum[...]

    @pl.when(step >= blocks + tiles)
    def _():
        block = step - blocks - tiles
        pick = picks[block]
        here = pl.ds(pl.multiple_of(block * capacity, capacity), capacity)
        moe = dot_tn(pick, moe_all[here].astype(bf16))
        part = dot_tn(pick, part_all[here].astype(bf16))
        if not first:
            moe = moe + moe_in_ref[0].astype(f32)
            part = part + part_in_ref[0].astype(f32)
        moe_ref[0] = moe.astype(bf16)
        part_ref[0] = part.astype(bf16)


def expert_call(expert, slots, tokens, grads, router, weights, capacity, experts, before=None):
    wide, rows, _ = tokens.shape
    units = weights[0].shape[1]
    groups = 2 if wide * capacity > 1024 else 1
    blocks, tile = wide // groups, 256
    tiles = units // tile
    last = blocks + tiles
    first = before is None
    bf16, f32 = jnp.bfloat16, jnp.float32

    def picked(g, i):
        return g * blocks + jnp.minimum(i, blocks - 1)

    def tiled(i):
        return jnp.clip(i - blocks, 0, tiles - 1)

    def spread(g, i):
        return g * blocks + jnp.clip(i - last, 0, blocks - 1)

    whole = pl.BlockSpec((1, rows, D), lambda g, i: (picked(g, i), 0, 0))
    back = pl.BlockSpec((1, rows, D), lambda g, i: (spread(g, i), 0, 0))
    row = pl.BlockSpec((capacity, D), lambda g, i: (picked(g, i), 0))
    column = pl.BlockSpec((D, tile), lambda g, i: (0, tiled(i)))
    unit = pl.BlockSpec((blocks * capacity, tile), lambda g, i: (g, tiled(i)))
    fixed = pl.BlockSpec((128, D), lambda g, i: (0, 0))
    in_specs = [
        pl.BlockSpec(memory_space=pltpu.SMEM),
        pl.BlockSpec((1, 1, rows), lambda g, i: (picked(g, i), 0, 0)),
        whole,
        whole,
        pl.BlockSpec((D, 128), lambda g, i: (0, 0)),
        column,
        column,
        pl.BlockSpec((tile, D), lambda g, i: (tiled(i), 0)),
    ] + ([] if first else [back, back, fixed])
    count = wide * capacity
    compact = jax.ShapeDtypeStruct((count, D), bf16)
    narrow = jax.ShapeDtypeStruct((count, units), bf16)
    held = blocks * capacity
    return pl.pallas_call(
        functools.partial(expert_kernel, tiles, capacity, experts, first),
        grid=(groups, last + blocks),
        in_specs=in_specs,
        out_specs=[back, back, row, row, unit, unit, unit, fixed],
        out_shape=[jax.ShapeDtypeStruct((wide, rows, D), bf16)] * 2
        + [compact] * 2
        + [narrow] * 3
        + [jax.ShapeDtypeStruct((128, D), f32)],
        scratch_shapes=[
            pltpu.VMEM((held, D), bf16),
            pltpu.VMEM((held, D), bf16),
            pltpu.VMEM((blocks, capacity, rows), bf16),
            pltpu.VMEM((held, D), f32),
            pltpu.VMEM((held, D), f32),
            pltpu.VMEM((held, 128), f32),
            pltpu.VMEM((held, 1), f32),
            pltpu.VMEM((128, D), f32),
        ],
        compiler_params=pltpu.CompilerParams(vmem_limit_bytes=60 * 2**20),
        cost_estimate=pl.CostEstimate(
            flops=0, bytes_accessed=250_000_000, transcendentals=0
        ),
    )(expert.astype(jnp.int32).reshape(1), slots, tokens, grads, router, *weights, *(before or ()))


def positions(token_ids):
    local = token_ids % (PROMPT + NCONT * CONT)
    return jnp.where(local < PROMPT, local, PROMPT + (local - PROMPT) % CONT)


def rotation(place):
    frequency = THETA ** (-2.0 * jnp.arange(HD // 2, dtype=jnp.float32) / HD)
    angle = place.astype(jnp.float32)[:, None] * frequency[None, :]
    cosine, sine = jnp.cos(angle), jnp.sin(angle)
    return jnp.concatenate([cosine, cosine], 1), jnp.concatenate([-sine, sine], 1)


def shards(
    tokens,
    cotangent,
    valid,
    routes,
    w_query,
    w_key,
    w_value,
    w_out,
    norm_attn,
    norm_query,
    norm_key,
    norm_moe,
    w_router,
    w_gate,
    w_up,
    w_down,
):
    bf16, f32 = jnp.bfloat16, jnp.float32
    wide_count = lax.axis_size("wide")
    narrow_count = lax.axis_size("narrow")
    rows = tokens.shape[0]
    half = rows * wide_count
    columns = w_query.shape[1]
    experts = w_router.shape[1]
    hidden_units = w_gate.shape[2]
    capacity = min(max(rows * TOP * 5 // (4 * experts), 2), rows)
    assert narrow_count == 2 and CONT in (rows, 2 * rows)
    paired = CONT == 2 * rows
    side = lax.axis_index("narrow")
    place = lax.axis_index("wide")
    group = lax.axis_index("grp")
    swap = [(0, 1), (1, 0)]
    twins = lax.axis_size("grp") == 2
    prompt_blocks = PROMPT // (rows * narrow_count)
    shared = half if paired else prompt_blocks * rows
    attend, attend_back = attention_calls(rows, half, shared, columns, prompt_blocks, paired, (1, 2))
    barrier = lax.optimization_barrier

    def exchange(value):
        return lax.ppermute(value, "narrow", swap)

    stream = tokens.astype(f32)
    inv_one = lax.rsqrt(jnp.mean(stream * stream, -1, keepdims=True) + EPSILON)
    gain_one = norm_attn.astype(f32)
    normed = (stream * inv_one * gain_one).astype(bf16)
    mask = valid.astype(f32)[:, None]
    grad_final = cotangent.astype(f32) * mask
    pieces = 2 * narrow_count if twins else 1
    piece_width = D // pieces
    piece_id = group * narrow_count + side if twins else 0
    piece = lax.dynamic_slice_in_dim(w_out, piece_id * piece_width, piece_width, 1)
    (routes_plane, normed_plane, out_piece), (other_up,) = start_exchange([routes.T, normed, piece], [w_up[0]], 0)
    normed_plane = normed_plane.reshape(half, D)
    out_pieces = [out_piece.reshape(D, piece_width)]
    if twins:
        out_pieces.append(exchange(out_pieces[0]))
        out_pieces += [lax.ppermute(p, "grp", swap) for p in out_pieces]

    def ordered(parts):
        if not twins:
            return parts
        parts = [jnp.where(side == 0, parts[k], parts[k ^ 1]) for k in range(4)]
        return [jnp.where(group == 0, parts[k], parts[k ^ 2]) for k in range(4)]

    def unordered(whole):
        return ordered([whole[:, k * piece_width : (k + 1) * piece_width] for k in range(pieces)])

    joined = jnp.concatenate([w_query, w_key, w_value], 1)
    raw = dot(normed_plane, joined)
    gains = jnp.pad(jnp.stack([norm_query, norm_key]).astype(f32), ((0, 6), (0, 0)))
    plane_ids = (
        (jnp.arange(wide_count, dtype=jnp.int32)[:, None] * narrow_count + side) * rows
        + jnp.arange(rows, dtype=jnp.int32)[None, :]
    ).reshape(half)
    cosine, sine = rotation(positions(plane_ids))
    kept = attend(raw, gains, cosine, sine, grad_final.astype(bf16))
    attended, attended_own, lse, sums, grads_in = kept[5:]

    branch = jnp.concatenate(ordered([dot(attended_own, p) for p in out_pieces]), 1)
    hidden = stream + branch
    inv_two = lax.rsqrt(jnp.mean(hidden * hidden, -1, keepdims=True) + EPSILON)
    gain_two = norm_moe.astype(f32)
    moe_in = (hidden * inv_two * gain_two).astype(bf16)
    (tokens_in,), (other_gate, other_down) = start_exchange([moe_in], [w_gate[0], w_down[0]], 6)

    earlier = (jnp.arange(rows)[:, None] < jnp.arange(rows)[None, :]).astype(bf16)

    def slots_of(expert):
        chosen = jnp.any(routes_plane == expert, 1)
        rank = dot(chosen.astype(bf16), earlier).astype(jnp.int32)
        return jnp.where(chosen, rank, -1).reshape(wide_count, 1, rows)

    router = jnp.pad(w_router, ((0, 0), (0, 128 - experts)))

    def run_expert(expert, weights, before):
        return expert_call(
            expert, slots_of(expert), tokens_in, grads_in, router, weights, capacity, experts, before
        )

    other = run_expert(place * narrow_count + 1 - side, (other_gate, other_up, other_down), None)
    partner_grads = plain_grads(*other[2:7])
    came = [exchange(g) for g in partner_grads[:2]]
    before, partner_grads = barrier(((other[0], other[1], other[7]), partner_grads))
    own = run_expert(place * narrow_count + side, (w_gate[0], w_up[0], w_down[0]), before)
    moe_part, grad_part, grad_router = own[0], own[1], own[7][:experts]
    moe = lax.psum_scatter(moe_part.reshape(half, D), "wide", scatter_dimension=0, tiled=True).astype(f32)
    grad_moe_in, *own_grads = expert_grad(grad_part, own[2:7], 5)
    grad_moe_in, moe, down_grad = barrier((grad_moe_in, moe, partner_grads[2]))
    came.append(exchange(down_grad))

    grad_gain_two = jnp.sum(grad_moe_in * hidden * inv_two, 0)
    grad_hidden = (
        grad_final
        + inv_two * gain_two * grad_moe_in
        - hidden * inv_two**3 * jnp.sum(grad_moe_in * gain_two * hidden, -1, keepdims=True) / D
    )
    grad_branch = grad_hidden.astype(bf16)
    grad_attended_own = sum(dot_nt(g, p) for g, p in zip(unordered(grad_branch), out_pieces)).astype(bf16)
    grad_attended_own, came[0], came[1] = barrier((grad_attended_own, came[0], came[1]))
    grads_joined, gain_grads, branch_plane = attend_back(
        raw, gains, cosine, sine, sums, *kept[:5], grad_attended_own, attended, lse, grad_branch
    )
    grads_joined, came[2] = barrier((grads_joined, came[2]))
    grad_out = barrier(dot_tn(attended, branch_plane.reshape(half, D)).astype(bf16))
    grad_weights = barrier(dot_tn(normed_plane, grads_joined).astype(bf16))
    weights_came = exchange(grad_weights)
    out_came = exchange(grad_out)
    stats = jnp.stack([jnp.sum(v * v * mask) for v in (stream, branch, hidden, moe, hidden + moe)] + [jnp.sum(mask)])
    here = jnp.repeat(jnp.arange(wide_count) == place, columns)
    spots = [jnp.where(here, jnp.tile(g, wide_count), 0.0) for g in gain_grads[:2]]
    zeros = jnp.zeros((D,), f32)
    small = jnp.stack([zeros, grad_gain_two, *spots, jnp.pad(stats, (0, D - stats.shape[0]))])
    small = jnp.concatenate([grad_router, small, jnp.zeros((-(experts + 5) % 8, D), f32)], 0)
    small, _, _ = barrier((small, grad_weights, grad_out))
    grad_input, small = input_grad(
        grads_joined, joined, tokens, grad_hidden, gain_one.reshape(1, D), small, experts, 3
    )
    grad_weights = grad_weights.astype(f32) + weights_came.astype(f32)
    grad_out = grad_out.astype(f32) + out_came.astype(f32)
    grad_query_w, grad_key_w, grad_value_w = (
        grad_weights[:, i * columns : (i + 1) * columns] for i in range(3)
    )
    final = hidden + moe
    output = final.astype(bf16)
    grad_gate_w, grad_up_w, grad_down_w = (
        (own.astype(f32) + other.astype(f32))[None] for own, other in zip(own_grads, came)
    )

    spots = lax.dynamic_slice_in_dim(small[experts + 2 : experts + 4], place * columns, columns, 1)
    stats = small[experts + 4, :6]
    rms = jnp.sqrt(stats[:5] / (jnp.maximum(stats[5], 1.0) * D))
    return (
        output,
        grad_input,
        grad_query_w,
        grad_key_w,
        grad_value_w,
        grad_out,
        small[experts],
        spots[0],
        spots[1],
        small[experts + 1],
        small[:experts].T,
        grad_gate_w,
        grad_up_w,
        grad_down_w,
        rms,
    )


def solution(mesh):
    return jax.shard_map(
        shards,
        mesh=mesh,
        in_specs=(
            P(("grp", "wide", "narrow"), None),
            P(("grp", "wide", "narrow"), None),
            P(("grp", "wide", "narrow")),
            P(("grp", "wide", "narrow"), None),
            P(None, "wide"),
            P(None, "wide"),
            P(None, "wide"),
            P("wide", None),
            P(),
            P("wide"),
            P("wide"),
            P(),
            P(),
            P(("wide", "narrow"), None, None),
            P(("wide", "narrow"), None, None),
            P(("wide", "narrow"), None, None),
        ),
        out_specs=(
            P(("grp", "wide", "narrow"), None),
            P(("grp", "wide", "narrow"), None),
            P("grp", "wide"),
            P("grp", "wide"),
            P("grp", "wide"),
            P(("grp", "wide"), None),
            P("grp"),
            P(("grp", "wide")),
            P(("grp", "wide")),
            P("grp"),
            P("grp", None),
            P(("grp", "wide", "narrow"), None, None),
            P(("grp", "wide", "narrow"), None, None),
            P(("grp", "wide", "narrow"), None, None),
            P("grp"),
        ),
        check_vma=False,
    )
```

```python
import functools

import jax
import jax.numpy as jnp
from jax import lax
from jax.experimental import pallas as pl
from jax.experimental.pallas import tpu as pltpu
from jax.sharding import PartitionSpec as P

D = 2048
HD = 128
TOP = 8
PROMPT = 2048
CONT = 256
NCONT = 8

EPSILON = 1e-05
THETA = 10000.0
NEGATIVE = -1e30


MESH_ID = pl.DeviceIdType.MESH
ANY = pl.BlockSpec(memory_space=pl.ANY)
VMEM = pl.BlockSpec(memory_space=pltpu.VMEM)
LINE = 4


def lasts(microseconds):
    return pl.CostEstimate(flops=0, bytes_accessed=microseconds * 3_000_000, transcendentals=0)


def position():
    grp, wide, narrow = (lax.axis_index(a) for a in ("grp", "wide", "narrow"))
    return grp, wide, narrow, wide // 2, lax.rem(wide, 2)


def greet(targets):
    barrier = pltpu.get_barrier_semaphore()
    for device, when in targets:
        def signal(device=device):
            pl.semaphore_signal(barrier, inc=1, device_id=device, device_id_type=MESH_ID)

        if when is None:
            signal()
        else:
            pl.when(when)(signal)
    peers = sum(1 if when is None else when.astype(jnp.int32) for _, when in targets)
    pl.semaphore_wait(barrier, peers)


def remote(src, dst, send, recv, device):
    return pltpu.make_async_remote_copy(
        src_ref=src, dst_ref=dst, send_sem=send, recv_sem=recv, device_id=device, device_id_type=MESH_ID
    )


def gather_kernel(count, *refs):
    ins, outs = refs[:count], refs[count : 2 * count]
    gather_body(count, ins, outs, *refs[2 * count :])


class Gather:
    def __init__(self, ins, outs, send, recv, local):
        self.ins, self.outs, self.send, self.recv, self.local = ins, outs, send, recv, local
        grp, wide, narrow, self.line, self.cross = position()
        self.wide = wide
        self.across = (grp, self.line * 2 + 1 - self.cross, narrow)
        self.above = (grp, wide + 2, narrow)
        self.below = (grp, wide - 2, narrow)
        self.has_above, self.has_below = self.line < LINE - 1, self.line > 0
        self.targets = [(self.across, None), (self.above, self.has_above), (self.below, self.has_below)]
        self.arrived = lambda i, slot: None

    def copy(self, i, source_line, way, device):
        slot = source_line * 2 + self.cross
        out = self.outs[i].at[slot]
        return remote(out, out, self.send.at[i, way, source_line], self.recv.at[i, slot], device)

    def own(self, i, way, device):
        return remote(
            self.ins[i], self.outs[i].at[self.wide], self.send.at[i, way, self.line], self.recv.at[i, self.wide], device
        )

    def mine(self, i):
        return pltpu.make_async_copy(self.ins[i], self.outs[i].at[self.wide], self.local.at[i])

    def start(self):
        for i in range(len(self.ins)):
            pl.when(self.has_above)(self.own(i, 1, self.above).start)
            pl.when(self.has_below)(self.own(i, 2, self.below).start)
            self.own(i, 0, self.across).start()
            self.mine(i).start()
            self.arrived(i, None)

    def forward(self, distance, only=None):
        for i in range(len(self.ins)) if only is None else (only,):
            for sign in (-1, 1):
                source = self.line + sign * distance

                @pl.when((source >= 0) & (source < LINE))
                def _(i=i, source=source, sign=sign):
                    self.copy(i, source, 0, self.across).wait_recv()
                    onward = self.above if sign < 0 else self.below

                    @pl.when(self.has_above if sign < 0 else self.has_below)
                    def _():
                        self.copy(i, source, 1 if sign < 0 else 2, onward).start()

                    self.copy(i, source, 0, self.across).start()
                    self.arrived(i, source * 2 + self.cross)

    def finish(self):
        for i in range(len(self.ins)):
            send, recv, src, out = self.send, self.recv, self.ins[i], self.outs[i]
            for source in range(LINE):
                other = source * 2 + 1 - self.cross
                remote(src, out.at[other], send.at[i, 0, 0], recv.at[i, other], self.across).wait_recv()
                self.arrived(i, other)
            for source in range(LINE):
                remote(src, out.at[0], send.at[i, 0, source], recv.at[i, 0], self.across).wait_send()

                @pl.when(self.has_above & (source <= self.line))
                def _(source=source):
                    remote(src, out.at[0], send.at[i, 1, source], recv.at[i, 0], self.above).wait_send()

                @pl.when(self.has_below & (source >= self.line))
                def _(source=source):
                    remote(src, out.at[0], send.at[i, 2, source], recv.at[i, 0], self.below).wait_send()

            self.mine(i).wait()


def gather_sems(count):
    return [
        pltpu.SemaphoreType.DMA((count, 3, LINE)),
        pltpu.SemaphoreType.DMA((count, 2 * LINE)),
        pltpu.SemaphoreType.DMA((count,)),
    ]


def gather_body(count, ins, outs, send, recv, local, more=(), begin=None, finish=None, arrived=None):
    gather = Gather(ins, outs, send, recv, local)
    if arrived is not None:
        gather.arrived = arrived
    greet([*gather.targets, *more])
    gather.start()
    if begin is not None:
        begin()
    for i in range(count):
        for distance in range(1, LINE):
            gather.forward(distance, i)
    gather.finish()
    if finish is not None:
        finish()


def gather_wide(arrays, collective_id):
    count = len(arrays)
    size = lax.axis_size("wide")
    if size != 2 * LINE:
        return [lax.all_gather(a, "wide", axis=0) for a in arrays]
    return pl.pallas_call(
        functools.partial(gather_kernel, count),
        out_shape=[jax.ShapeDtypeStruct((size, *a.shape), a.dtype) for a in arrays],
        in_specs=[ANY] * count,
        out_specs=[ANY] * count,
        scratch_shapes=[
            pltpu.SemaphoreType.DMA((count, 3, LINE)),
            pltpu.SemaphoreType.DMA((count, size)),
            pltpu.SemaphoreType.DMA((count,)),
        ],
        compiler_params=pltpu.CompilerParams(collective_id=collective_id, has_side_effects=True),
        cost_estimate=lasts(100),
    )(*arrays)


def scatter_kernel(part_ref, out_ref, held, from_across, from_line, load, send, recv_a, recv_l):
    grp, wide, narrow, line, cross = position()
    across = (grp, line * 2 + 1 - cross, narrow)
    above = (grp, wide + 2, narrow)
    below = (grp, wide - 2, narrow)
    has_above, has_below = line < LINE - 1, line > 0
    f32 = jnp.float32
    greet([(across, None), (above, has_above), (below, has_below)])

    order = []
    for distance in range(LINE - 1, 0, -1):
        for sign in (1, -1):
            order.append((distance, sign))

    def valid(owner):
        return (owner >= 0) & (owner < LINE)

    def across_copy(owner):
        return remote(
            part_ref.at[owner * 2 + 1 - cross], from_across.at[owner], send.at[0, owner], recv_a.at[owner], across
        )

    def load_copy(owner):
        return pltpu.make_async_copy(part_ref.at[owner * 2 + cross], held.at[owner], load.at[owner])

    def line_copy(owner, up):
        return remote(
            held.at[owner],
            from_line.at[0 if up else 1, owner],
            send.at[1, owner],
            recv_l.at[0 if up else 1, owner],
            above if up else below,
        )

    for distance, sign in order + [(0, 1)]:
        owner = line + sign * distance

        @pl.when(valid(owner))
        def _(owner=owner):
            across_copy(owner).start()
            load_copy(owner).start()

    for distance, sign in order:
        owner = line + sign * distance

        @pl.when(valid(owner))
        def _(owner=owner, sign=sign):
            load_copy(owner).wait()
            across_copy(owner).wait_recv()
            up = sign > 0
            came = has_below if up else has_above
            total = held[owner].astype(f32) + from_across[owner].astype(f32)

            @pl.when(came)
            def _():
                line_copy(owner, up).wait_recv()
                held[owner] = (total + from_line[0 if up else 1, owner].astype(f32)).astype(held.dtype)

            @pl.when(jnp.logical_not(came))
            def _():
                held[owner] = total.astype(held.dtype)

            line_copy(owner, up).start()

    load_copy(line).wait()
    across_copy(line).wait_recv()
    out_ref[...] = held[line].astype(f32) + from_across[line].astype(f32)

    @pl.when(has_below)
    def _():
        line_copy(line, True).wait_recv()
        out_ref[...] += from_line[0, line].astype(f32)

    @pl.when(has_above)
    def _():
        line_copy(line, False).wait_recv()
        out_ref[...] += from_line[1, line].astype(f32)

    for owner in range(LINE):
        across_copy(owner).wait_send()

        @pl.when(owner > line)
        def _(owner=owner):
            line_copy(owner, True).wait_send()

        @pl.when(owner < line)
        def _(owner=owner):
            line_copy(owner, False).wait_send()


def scatter_wide(part, collective_id):
    size, rows, columns = part.shape
    if size != 2 * LINE:
        return lax.psum_scatter(part, "wide", scatter_dimension=0, tiled=False).astype(jnp.float32)
    block = (LINE, rows, columns)
    return pl.pallas_call(
        scatter_kernel,
        out_shape=jax.ShapeDtypeStruct((rows, columns), jnp.float32),
        in_specs=[ANY],
        out_specs=VMEM,
        scratch_shapes=[
            pltpu.VMEM(block, part.dtype),
            pltpu.VMEM(block, part.dtype),
            pltpu.VMEM((2, *block), part.dtype),
            pltpu.SemaphoreType.DMA((LINE,)),
            pltpu.SemaphoreType.DMA((2, LINE)),
            pltpu.SemaphoreType.DMA((LINE,)),
            pltpu.SemaphoreType.DMA((2, LINE)),
        ],
        compiler_params=pltpu.CompilerParams(
            collective_id=collective_id, has_side_effects=True, vmem_limit_bytes=48 * 2**20
        ),
        cost_estimate=lasts(95),
    )(part)


def sum_kernel(x_ref, o_ref, held, send, recv):
    grp, wide, narrow, _, _ = position()
    size = held.shape[0] + 1
    others = [(grp, lax.rem(wide + k, size), narrow) for k in range(1, size)]
    greet([(device, None) for device in others])
    copies = [
        remote(x_ref, held.at[k], send.at[k], recv.at[k], device) for k, device in enumerate(others)
    ]
    for copy in copies:
        copy.start()
    for copy in copies:
        copy.wait()
    total = x_ref[...]
    for k in range(size - 1):
        total = total + held[k]
    o_ref[...] = total


def sum_wide(x, collective_id):
    size = lax.axis_size("wide")
    if size != 2 * LINE:
        return lax.psum(x, "wide")
    return pl.pallas_call(
        sum_kernel,
        out_shape=jax.ShapeDtypeStruct(x.shape, x.dtype),
        in_specs=[VMEM],
        out_specs=VMEM,
        scratch_shapes=[
            pltpu.VMEM((size - 1, *x.shape), x.dtype),
            pltpu.SemaphoreType.DMA((size - 1,)),
            pltpu.SemaphoreType.DMA((size - 1,)),
        ],
        compiler_params=pltpu.CompilerParams(collective_id=collective_id, has_side_effects=True),
        cost_estimate=lasts(8),
    )(x)


LOG2E = 1.4426950408889634
NT = (((1,), (1,)), ((), ()))


def key_parts(w, plane, rows, prompt_blocks, paired, limit=512):
    count = (prompt_blocks if w is None else w) * rows
    parts = [(first, min(limit, count - first), None) for first in range(0, count, limit)]
    own = None if w is None else w * rows
    if plane == 0:
        parts.append((own, rows, "causal"))
    elif w is not None or paired:
        parts.append((own, rows, "side"))
    return parts


def for_blocks(blocks, prompt_blocks, one, between=None):
    for w in range(prompt_blocks):
        one(w, w, w * one.rows)
    if between is not None:
        between()

    def body(w, carry):
        one(None, w, pl.multiple_of(w * one.rows, one.rows))
        return carry

    lax.fori_loop(prompt_blocks, blocks, body, 0)


def masked_scores(score, mask, side, rows):
    if mask == "causal":
        key = lax.broadcasted_iota(jnp.int32, (rows, rows), 0)
        query = lax.broadcasted_iota(jnp.int32, (rows, rows), 1)
        return jnp.where(key <= query, score, NEGATIVE)
    if mask == "side":
        return jnp.where(side == 1, score, NEGATIVE)
    return score


def row_sums(values):
    total = values[:, :HD]
    for first in range(HD, values.shape[1], HD):
        total = total + values[:, first : first + HD]
    return jnp.sum(total.T, 0, keepdims=True)


def turn(values, cosine, sine):
    return values * cosine + pltpu.roll(values, HD // 2, 1) * sine


def inverse_norms(sums_ref, at):
    inverse = lax.rsqrt(sums_ref[:, at].T / D + EPSILON)
    return inverse[:, 0:1], inverse[:, 1:2]


def peer_copies(size, src, dst, send, recv, grp, wide, narrow):
    return [
        remote(src, dst.at[k - 1], send.at[k - 1], recv.at[k - 1], (grp, lax.rem(wide + k, size), narrow))
        for k in range(1, size)
    ]


def attend_kernel(
    rows, prompt_blocks, paired, shared, carried, raw_ref, gains_ref, cos_ref, sin_ref, *refs
):
    carry_in, refs = refs[:carried], refs[carried:]
    q_ref, k_ref, v_ref, ko_ref, vo_ref, o_ref, own_ref, lse_ref, sums_ref = refs[:9]
    carry_out, refs = refs[9 : 9 + carried], refs[9 + carried :]
    vt_ref, vto_ref, came_ref, sum_send, sum_recv, pair_send, pair_recv, out_send, out_recv = refs[:9]
    gather = Gather(carry_in, carry_out, *refs[9:]) if carried else None
    half, columns = q_ref.shape
    size = half // rows
    heads = columns // HD
    grp, wide, narrow = (lax.axis_index(a) for a in ("grp", "wide", "narrow"))
    partner = (grp, wide, 1 - narrow)
    greet([((grp, lax.rem(wide + k, size), narrow), None) for k in range(1, size)] + [(partner, None)])
    if carried:
        gather.start()
    pairs = [
        remote(src.at[pl.ds(0, shared)], dst, pair_send.at[i], pair_recv.at[i], partner)
        for i, (src, dst) in enumerate(((k_ref, ko_ref), (v_ref, vo_ref)))
    ]
    v_ref[...] = raw_ref[:, 2 * columns :].astype(jnp.bfloat16)
    pairs[1].start()
    sums_ref[...] = jnp.zeros_like(sums_ref)

    def squares(b, carry):
        at = pl.ds(pl.multiple_of(b * rows, rows), rows)
        for i in range(2):
            part = raw_ref[at, i * columns : (i + 1) * columns]
            sums_ref[i : i + 1, at] = row_sums(part * part)
        return carry

    lax.fori_loop(0, size, squares, 0)
    copies = peer_copies(size, sums_ref, came_ref, sum_send, sum_recv, grp, wide, narrow)
    for copy in copies:
        copy.start()
    for h in range(heads):
        hs = slice(h * HD, (h + 1) * HD)
        vt_ref[hs, :] = v_ref[:, hs].T
    for copy in copies:
        copy.wait()
    total = sums_ref[...]
    for k in range(size - 1):
        total = total + came_ref[k]
    sums_ref[...] = total

    def prepare(i, ref):
        def body(b, carry):
            at = pl.ds(pl.multiple_of(b * rows, rows), rows)
            inverse = inverse_norms(sums_ref, at)[i]
            for h in range(heads):
                hs = slice(h * HD, (h + 1) * HD)
                values = raw_ref[at, i * columns + h * HD : i * columns + (h + 1) * HD]
                values = values * inverse * gains_ref[i : i + 1, hs]
                ref[at, hs] = turn(values, cos_ref[at], sin_ref[at]).astype(jnp.bfloat16)
            return carry

        return body

    lax.fori_loop(0, shared // rows, prepare(1, k_ref), 0)
    pairs[0].start()
    lax.fori_loop(shared // rows, size, prepare(1, k_ref), 0)
    lax.fori_loop(0, size, prepare(0, q_ref), 0)
    if carried:
        gather.forward(1)
    pairs[1].wait()
    for h in range(heads):
        hs = slice(h * HD, (h + 1) * HD)
        vto_ref[hs, :] = vo_ref[:, hs].T
    pairs[0].wait()

    def mine():
        return pl.ds(pl.multiple_of(wide * columns, columns), columns)

    def hand_out(w):
        return remote(
            o_ref.at[pl.ds(pl.multiple_of(w * rows, rows), rows)],
            own_ref.at[:, mine()],
            out_send.at[w],
            out_recv.at[wide],
            (grp, w, narrow),
        )

    def one(w, w_index, start):
        block = pl.ds(start, rows)
        for h in range(heads):
            hs = slice(h * HD, (h + 1) * HD)
            query = q_ref[block, hs]
            scores = []
            for plane in range(2):
                for first, count, mask in key_parts(w, plane, rows, prompt_blocks, paired):
                    at = pl.ds(start if first is None else first, count)
                    key = (k_ref, ko_ref)[plane][at, hs]
                    score = lax.dot_general(key, query, NT, preferred_element_type=jnp.float32)
                    score = score * (HD**-0.5 * LOG2E)
                    scores.append((plane, at, masked_scores(score, mask, narrow, rows)))
            largest = functools.reduce(
                jnp.maximum, [jnp.max(score, 0, keepdims=True) for _, _, score in scores]
            )
            total = jnp.zeros((1, rows), jnp.float32)
            mixed = jnp.zeros((HD, rows), jnp.float32)
            for plane, at, score in scores:
                weight = jnp.exp2(score - largest)
                total = total + jnp.sum(weight, 0, keepdims=True)
                mixed = mixed + dot((vt_ref, vto_ref)[plane][hs, at], weight.astype(jnp.bfloat16))
            o_ref[block, hs] = (mixed / total).T.astype(jnp.bfloat16)
            lse_ref[h : h + 1, block] = largest + jnp.log(total) * LOG2E

        @pl.when(w_index != wide)
        def _():
            hand_out(w_index).start()

    one.rows = rows
    for_blocks(size, prompt_blocks, one, (lambda: gather.forward(2)) if carried else None)
    if carried:
        gather.forward(3)
    own_ref[:, mine()] = o_ref[pl.ds(pl.multiple_of(wide * rows, rows), rows)]

    def finish(w, carry):
        @pl.when(w != wide)
        def _():
            hand_out(w).wait_send()
            remote(
                o_ref.at[pl.ds(0, rows)], own_ref.at[:, mine()], out_send.at[w], out_recv.at[w], (grp, w, narrow)
            ).wait_recv()

        return carry

    lax.fori_loop(0, size, finish, 0)
    if carried:
        gather.finish()


def attend_back_kernel(
    rows, prompt_blocks, paired, shared, carried, raw_ref, gains_ref, cos_ref, sin_ref, sums_ref,
    q_ref, k_ref, v_ref, ko_ref, vo_ref, grad_ref, o_ref, lse_ref, *refs
):
    carry_in, refs = refs[:carried], refs[carried:]
    joined_ref, gain_ref = refs[:2]
    carry_out, refs = refs[2 : 2 + carried], refs[2 + carried :]
    do_ref, dq_ref, dk_ref, dv_ref, dko_ref, dvo_ref, dkb_ref, dvb_ref, dkr_ref, dvr_ref, kt_ref, kto_ref = refs[:12]
    dots_ref, came_ref, sum_send, sum_recv, pair_send, pair_recv, in_send, in_recv = refs[12:20]
    gather = Gather(carry_in, carry_out, *refs[20:]) if carried else None
    half, columns = q_ref.shape
    size = half // rows
    heads = columns // HD
    grp, wide, narrow = (lax.axis_index(a) for a in ("grp", "wide", "narrow"))
    partner = (grp, wide, 1 - narrow)
    greet([((grp, lax.rem(wide + k, size), narrow), None) for k in range(1, size)] + [(partner, None)])
    my_rows = pl.ds(pl.multiple_of(wide * rows, rows), rows)

    def part_of(w):
        return pl.ds(pl.multiple_of(w * columns, columns), columns)

    def hand_in(w):
        return remote(
            grad_ref.at[:, part_of(w)], do_ref.at[my_rows], in_send.at[w], in_recv.at[wide], (grp, w, narrow)
        )

    def each_peer(act):
        def body(w, carry):
            pl.when(w != wide)(lambda: act(w))
            return carry

        lax.fori_loop(0, size, body, 0)

    each_peer(lambda w: hand_in(w).start())
    if carried:
        gather.start()
    do_ref[my_rows, :] = grad_ref[:, part_of(wide)]
    for ref in (dk_ref, dv_ref, dko_ref, dvo_ref, dots_ref, gain_ref):
        ref[...] = jnp.zeros_like(ref)
    for h in range(heads):
        hs = slice(h * HD, (h + 1) * HD)
        kt_ref[hs, :] = k_ref[:, hs].T
        kto_ref[hs, :] = ko_ref[:, hs].T
    each_peer(
        lambda w: remote(
            grad_ref.at[:, part_of(w)], do_ref.at[my_rows], in_send.at[w], in_recv.at[w], (grp, w, narrow)
        ).wait_recv()
    )

    def sweep(plane):
        keys, values = ((k_ref, v_ref), (ko_ref, vo_ref))[plane]
        dk, dv = ((dk_ref, dv_ref), (dko_ref, dvo_ref))[plane]
        flipped = (kt_ref, kto_ref)[plane]

        def one(w, w_index, start):
            block = pl.ds(start, rows)
            for h in range(heads):
                hs = slice(h * HD, (h + 1) * HD)
                query = q_ref[block, hs]
                grad = do_ref[block, hs]
                delta = row_sums(grad.astype(jnp.float32) * o_ref[block, hs].astype(jnp.float32))
                lse = lse_ref[h : h + 1, block]
                back = jnp.zeros((HD, rows), jnp.float32)
                for first, count, mask in key_parts(w, plane, rows, prompt_blocks, paired):
                    at = pl.ds(start if first is None else first, count)
                    score = lax.dot_general(keys[at, hs], query, NT, preferred_element_type=jnp.float32)
                    score = masked_scores(score * (HD**-0.5 * LOG2E), mask, narrow, rows)
                    weight = jnp.exp2(score - lse)
                    grad_weight = lax.dot_general(values[at, hs], grad, NT, preferred_element_type=jnp.float32)
                    grad_score = (weight * (grad_weight - delta)).astype(jnp.bfloat16)
                    dv[at, hs] += dot(weight.astype(jnp.bfloat16), grad)
                    dk[at, hs] += dot(grad_score, query) * HD**-0.5
                    back = back + dot(flipped[hs, at], grad_score)
                back = back.T * HD**-0.5
                dq_ref[block, hs] = back if plane == 1 else dq_ref[block, hs] + back

        one.rows = rows
        for_blocks(size, prompt_blocks, one, (lambda: gather.forward(2 - plane)) if carried else None)

    sweep(1)
    dkb_ref[...] = dko_ref[...].astype(jnp.bfloat16)
    dvb_ref[...] = dvo_ref[...].astype(jnp.bfloat16)
    pairs = [
        remote(src, dst, pair_send.at[i], pair_recv.at[i], partner)
        for i, (src, dst) in enumerate(((dkb_ref, dkr_ref), (dvb_ref, dvr_ref)))
    ]
    for copy in pairs:
        copy.start()
    sweep(0)

    def turn_back(i, ref):
        def body(b, carry):
            at = pl.ds(pl.multiple_of(b * rows, rows), rows)
            inverse = inverse_norms(sums_ref, at)[i]
            products = []
            for h in range(heads):
                hs = slice(h * HD, (h + 1) * HD)
                grad = turn(ref[at, hs], cos_ref[at], -sin_ref[at])
                ref[at, hs] = grad
                product = grad * raw_ref[at, i * columns + h * HD : i * columns + (h + 1) * HD]
                gain_ref[i : i + 1, hs] += jnp.sum(product * inverse, 0, keepdims=True)
                products.append(product * gains_ref[i : i + 1, hs])
            dots_ref[i : i + 1, at] = row_sums(sum(products[1:], products[0]))
            return carry

        lax.fori_loop(0, size, body, 0)

    turn_back(0, dq_ref)
    if carried:
        gather.forward(3)
    for copy in pairs:
        copy.wait()
    dk_ref[0:shared, :] += dkr_ref[...].astype(jnp.float32)
    turn_back(1, dk_ref)
    copies = peer_copies(size, dots_ref, came_ref, sum_send, sum_recv, grp, wide, narrow)
    for copy in copies:
        copy.start()
    joined_ref[0:shared, 2 * columns :] = (dv_ref[0:shared] + dvr_ref[...].astype(jnp.float32)).astype(jnp.bfloat16)
    if shared < half:
        joined_ref[shared:, 2 * columns :] = dv_ref[shared:].astype(jnp.bfloat16)
    for copy in copies:
        copy.wait()
    total = dots_ref[...]
    for k in range(size - 1):
        total = total + came_ref[k]
    dots_ref[...] = total

    def finish(b, carry):
        at = pl.ds(pl.multiple_of(b * rows, rows), rows)
        inverses = inverse_norms(sums_ref, at)
        products = dots_ref[:, at].T / D
        for i, ref in enumerate((dq_ref, dk_ref)):
            inverse = inverses[i]
            cubed = inverse * inverse * inverse * products[:, i : i + 1]
            for h in range(heads):
                hs = slice(h * HD, (h + 1) * HD)
                there = slice(i * columns + h * HD, i * columns + (h + 1) * HD)
                value = inverse * gains_ref[i : i + 1, hs] * ref[at, hs] - raw_ref[at, there] * cubed
                joined_ref[at, there] = value.astype(jnp.bfloat16)
        return carry

    lax.fori_loop(0, size, finish, 0)
    each_peer(lambda w: hand_in(w).wait_send())
    if carried:
        gather.finish()


def attention_calls(rows, half, shared, columns, prompt_blocks, paired, ids):
    heads = columns // HD
    size = half // rows
    bf16, f32 = jnp.bfloat16, jnp.float32
    shape = lambda dtype, *dims: jax.ShapeDtypeStruct(dims, dtype)
    sems = pltpu.SemaphoreType.DMA
    peers = [sems((size - 1,)), sems((size - 1,)), sems((2,)), sems((2,)), sems((size,)), sems((size,))]

    def params(k):
        return pltpu.CompilerParams(vmem_limit_bytes=60 * 2**20, collective_id=ids[k], has_side_effects=True)

    carried = 1 if size == 2 * LINE else 0
    forward = pl.pallas_call(
        functools.partial(attend_kernel, rows, prompt_blocks, paired, shared, 0),
        out_shape=[shape(bf16, half, columns)] * 3
        + [shape(bf16, shared, columns)] * 2
        + [shape(bf16, half, columns), shape(bf16, rows, size * columns), shape(f32, heads, half), shape(f32, 8, half)],
        in_specs=[VMEM] * 4,
        out_specs=[VMEM] * 9,
        scratch_shapes=[
            pltpu.VMEM((columns, half), bf16),
            pltpu.VMEM((columns, shared), bf16),
            pltpu.VMEM((size - 1, 8, half), f32),
        ]
        + peers,
        compiler_params=params(0),
        cost_estimate=pl.CostEstimate(flops=0, bytes_accessed=300_000_000, transcendentals=0),
    )

    backward_call = pl.pallas_call(
        functools.partial(attend_back_kernel, rows, prompt_blocks, paired, shared, carried),
        out_shape=[shape(bf16, half, 3 * columns), shape(f32, 8, columns)]
        + [shape(bf16, size, rows, D)] * carried,
        in_specs=[VMEM] * 13 + [ANY] * carried,
        out_specs=[VMEM] * 2 + [ANY] * carried,
        scratch_shapes=[pltpu.VMEM((half, columns), bf16)]
        + [pltpu.VMEM((half, columns), f32)] * 3
        + [pltpu.VMEM((shared, columns), f32)] * 2
        + [pltpu.VMEM((shared, columns), bf16)] * 4
        + [
            pltpu.VMEM((columns, half), bf16),
            pltpu.VMEM((columns, shared), bf16),
            pltpu.VMEM((8, half), f32),
            pltpu.VMEM((size - 1, 8, half), f32),
        ]
        + peers
        + gather_sems(carried) * carried,
        compiler_params=params(1),
        cost_estimate=pl.CostEstimate(flops=0, bytes_accessed=300_000_000, transcendentals=0),
    )
    def backward(*args):
        if carried:
            return backward_call(*args)
        return [*backward_call(*args[:-1]), lax.all_gather(args[-1], "wide", axis=0)]

    return forward, backward


def dot(a, b):
    return jnp.dot(a, b, preferred_element_type=jnp.float32)


def dot_nt(a, b):
    return lax.dot_general(a, b, NT, preferred_element_type=jnp.float32)


def dot_tn(a, b):
    return lax.dot_general(a, b, (((0,), (0,)), ((), ())), preferred_element_type=jnp.float32)


def start_kernel(count, swaps, spread, *refs):
    ins, given = refs[:count], refs[count : count + swaps]
    refs = refs[count + swaps :]
    outs, got, pieces = refs[:count], refs[count : count + swaps], refs[count + swaps : count + swaps + 3 * spread]
    refs = refs[count + swaps + 3 * spread :]
    send, recv, local, swap_send, swap_recv, twin_send, twin_recv = refs[:7]
    grp, wide, narrow, line, cross = position()
    partner = (grp, wide, 1 - narrow)
    twin = (1 - grp, wide, narrow)
    size = 2 * LINE

    def half(ref, which):
        size = ref.shape[0] // 2
        return ref.at[pl.ds(pl.multiple_of(which * size, size), size)]

    def swap(i):
        return remote(half(given[i], grp), half(got[i], grp), swap_send.at[i], swap_recv.at[i], partner)

    def share(i, which):
        return remote(half(got[i], which), half(got[i], which), twin_send.at[i], twin_recv.at[i], twin)

    def piece(k, slot):
        piece_send, piece_recv = refs[7:]
        src = pieces[0] if k == 2 else outs[-1]
        device = twin if k else partner
        return remote(src.at[slot], pieces[k].at[slot], piece_send.at[k, slot], piece_recv.at[k, slot], device)

    def own_piece(k):
        piece_send, piece_recv = refs[7:]
        device = twin if k else partner
        return remote(ins[-1], pieces[k].at[wide], piece_send.at[k, wide], piece_recv.at[k, wide], device)

    def arrived(i, slot):
        if i == count - 1:
            for k in range(2):
                if slot is None:
                    own_piece(k).start()
                else:
                    piece(k, slot).start()

    def begin():
        for i in range(swaps):
            swap(i).start()

    def finish():
        if spread:
            for slot in range(size):
                piece(0, slot).wait_recv()
                piece(2, slot).start()
        for i in range(swaps):
            swap(i).wait_recv()
            share(i, grp).start()
        for i in range(swaps):
            swap(i).wait_send()
            share(i, grp).wait_send()
            share(i, 1 - grp).wait_recv()
        if spread:
            for slot in range(size):
                piece(0, slot).wait_send()
                piece(1, slot).wait()
                piece(2, slot).wait()

    more = [(partner, None), (twin, None)]
    gather_body(count, ins, outs, send, recv, local, more, begin, finish, arrived if spread else None)


def start_exchange(arrays, weights, collective_id, spread=False):
    size = lax.axis_size("wide")
    swap = [(0, 1), (1, 0)]
    if size != 2 * LINE or lax.axis_size("grp") != 2:
        return [lax.all_gather(a, "wide", axis=0) for a in arrays], [lax.ppermute(w, "narrow", swap) for w in weights], []
    count, swaps, spread = len(arrays), len(weights), int(spread)
    gathered = [jax.ShapeDtypeStruct((size, *a.shape), a.dtype) for a in arrays]
    dma = pltpu.SemaphoreType.DMA
    out = pl.pallas_call(
        functools.partial(start_kernel, count, swaps, spread),
        out_shape=gathered + [jax.ShapeDtypeStruct(w.shape, w.dtype) for w in weights] + gathered[-1:] * 3 * spread,
        in_specs=[ANY] * (count + swaps),
        out_specs=[ANY] * (count + swaps + 3 * spread),
        scratch_shapes=gather_sems(count) + [dma((swaps,))] * 4 + [dma((3, size))] * 2 * spread,
        compiler_params=pltpu.CompilerParams(collective_id=collective_id, has_side_effects=True),
        cost_estimate=lasts(120),
    )(*arrays, *weights)
    return out[:count], out[count : count + swaps], out[count + swaps :]


def expert_grad_kernel(
    part_ref, *refs
):
    operands = refs[0:5]
    out_ref, gate_out, up_out, down_out = refs[5:9]
    held, from_across, from_line, x_buf, g_buf, inner_buf, gate_buf, up_buf, stage = refs[9:18]
    load, send, recv_a, recv_l, fetch, put = refs[18:]
    grp, wide, narrow, line, cross = position()
    across = (grp, line * 2 + 1 - cross, narrow)
    above = (grp, wide + 2, narrow)
    below = (grp, wide - 2, narrow)
    has_above, has_below = line < LINE - 1, line > 0
    f32, bf16 = jnp.float32, jnp.bfloat16
    greet([(across, None), (above, has_above), (below, has_below)])
    order = [(distance, sign) for distance in range(LINE - 1, 0, -1) for sign in (1, -1)]

    def valid(owner):
        return (owner >= 0) & (owner < LINE)

    def across_copy(owner):
        return remote(
            part_ref.at[owner * 2 + 1 - cross], from_across.at[owner], send.at[0, owner], recv_a.at[owner], across
        )

    def load_copy(owner):
        return pltpu.make_async_copy(part_ref.at[owner * 2 + cross], held.at[owner], load.at[owner])

    def line_copy(owner, up):
        slot = 0 if up else 1
        return remote(
            held.at[owner], from_line.at[slot, owner], send.at[1, owner], recv_l.at[slot, owner], above if up else below
        )

    for distance, sign in order + [(0, 1)]:
        owner = line + sign * distance

        @pl.when(valid(owner))
        def _(owner=owner):
            across_copy(owner).start()
            load_copy(owner).start()

    bufs = (x_buf, g_buf, inner_buf, gate_buf, up_buf)

    fetches = [pltpu.make_async_copy(src, dst, fetch.at[i]) for i, (src, dst) in enumerate(zip(operands, bufs))]
    for copy in fetches:
        copy.start()

    tiles = stage.shape[0]
    width = gate_buf.shape[1] // tiles

    def tile(n, size):
        return pl.ds(pl.multiple_of(n * size, size), size)

    def column_job(values, result):
        def put_copy(n):
            return pltpu.make_async_copy(stage.at[n], result.at[:, tile(n, width)], put.at[n])

        def run():
            @pl.loop(0, tiles)
            def _(n):
                stage[n] = dot_tn(x_buf[...], values[:, tile(n, width)]).astype(bf16)
                put_copy(n).start()

            @pl.loop(0, tiles)
            def _(n):
                put_copy(n).wait()

        return run

    def down_job(result):
        units = inner_buf.shape[1] // tiles

        def run():
            for n in range(tiles):
                at = slice(n * units, (n + 1) * units)
                product = dot_tn(inner_buf[:, at], g_buf[...]).astype(bf16)
                for c in range(product.shape[1] // width):
                    stage[n, c * units : (c + 1) * units, :] = product[:, c * width : (c + 1) * width]
            copies = [
                pltpu.make_async_copy(
                    stage.at[n, pl.ds(c * units, units)],
                    result.at[pl.ds(n * units, units), pl.ds(c * width, width)],
                    put.at[n * (g_buf.shape[1] // width) + c],
                )
                for n in range(tiles)
                for c in range(g_buf.shape[1] // width)
            ]
            for copy in copies:
                copy.start()
            for copy in copies:
                copy.wait()

        return run

    def first_job():
        for copy in fetches:
            copy.wait()
        column_job(gate_buf, gate_out)()

    jobs = [first_job, None, column_job(up_buf, up_out), None, down_job(down_out), None]
    for job, (distance, sign) in zip(jobs, order):
        if job is not None:
            job()
        owner = line + sign * distance

        @pl.when(valid(owner))
        def _(owner=owner, sign=sign):
            load_copy(owner).wait()
            across_copy(owner).wait_recv()
            up = sign > 0
            came = has_below if up else has_above
            total = held[owner].astype(f32) + from_across[owner].astype(f32)

            @pl.when(came)
            def _():
                line_copy(owner, up).wait_recv()
                held[owner] = (total + from_line[0 if up else 1, owner].astype(f32)).astype(held.dtype)

            @pl.when(jnp.logical_not(came))
            def _():
                held[owner] = total.astype(held.dtype)

            line_copy(owner, up).start()

    load_copy(line).wait()
    across_copy(line).wait_recv()
    out_ref[...] = held[line].astype(f32) + from_across[line].astype(f32)

    @pl.when(has_below)
    def _():
        line_copy(line, True).wait_recv()
        out_ref[...] += from_line[0, line].astype(f32)

    @pl.when(has_above)
    def _():
        line_copy(line, False).wait_recv()
        out_ref[...] += from_line[1, line].astype(f32)

    for owner in range(LINE):
        across_copy(owner).wait_send()

        @pl.when(owner > line)
        def _(owner=owner):
            line_copy(owner, True).wait_send()

        @pl.when(owner < line)
        def _(owner=owner):
            line_copy(owner, False).wait_send()


def plain_grads(x, g, inner, gate, up):
    return [dot_tn(a, b).astype(jnp.bfloat16) for a, b in ((x, gate), (x, up), (inner, g))]


def expert_grad(part, own, collective_id):
    size, rows, columns = part.shape
    f32, bf16 = jnp.float32, jnp.bfloat16
    if size != 2 * LINE:
        return lax.psum_scatter(part, "wide", scatter_dimension=0, tiled=False).astype(f32), *plain_grads(*own)
    count, units = own[2].shape
    tiles = 4
    block = (LINE, rows, columns)
    gate = jax.ShapeDtypeStruct((D, units), bf16)
    down = jax.ShapeDtypeStruct((units, D), bf16)
    dma = pltpu.SemaphoreType.DMA
    return pl.pallas_call(
        expert_grad_kernel,
        out_shape=[jax.ShapeDtypeStruct((rows, columns), f32), gate, gate, down],
        in_specs=[ANY] * 6,
        out_specs=[VMEM] + [ANY] * 3,
        scratch_shapes=[
            pltpu.VMEM(block, bf16),
            pltpu.VMEM(block, bf16),
            pltpu.VMEM((2, *block), bf16),
            pltpu.VMEM((count, D), bf16),
            pltpu.VMEM((count, D), bf16),
            pltpu.VMEM((count, units), bf16),
            pltpu.VMEM((count, units), bf16),
            pltpu.VMEM((count, units), bf16),
            pltpu.VMEM((tiles, D, units // tiles), bf16),
            dma((LINE,)),
            dma((2, LINE)),
            dma((LINE,)),
            dma((2, LINE)),
            dma((5,)),
            dma((tiles * D // (units // tiles),)),
        ],
        compiler_params=pltpu.CompilerParams(
            collective_id=collective_id, has_side_effects=True, vmem_limit_bytes=60 * 2**20
        ),
        cost_estimate=lasts(1),
    )(part, *own)


class SmallSum:
    def __init__(self, x_ref, o_ref, parts, total, send, recv, send_back, recv_back):
        self.refs = x_ref, o_ref, parts, total, send, recv, send_back, recv_back
        grp, wide, narrow, _, _ = position()
        self.size, _, self.width = parts.shape
        self.me = wide * 2 + narrow
        self.ranks = [lax.rem(self.me + k, self.size) for k in range(self.size)]
        self.devices = [(grp, rank // 2, lax.rem(rank, 2)) for rank in self.ranks]
        self.targets = [(device, None) for device in self.devices[1:]]

    def columns(self, rank):
        return pl.ds(pl.multiple_of(rank * self.width, self.width), self.width)

    def run(self):
        x_ref, o_ref, parts, total, send, recv, send_back, recv_back = self.refs
        devices, size, mine = self.devices, self.size, self.columns(self.me)
        out = [
            remote(x_ref.at[:, self.columns(self.ranks[k])], parts.at[k], send.at[k], recv.at[k], devices[k])
            for k in range(1, size)
        ]
        for copy in out:
            copy.start()
        total[...] = x_ref[:, mine]
        for k, copy in enumerate(out):
            copy.wait()
            total[...] += parts[k + 1]
        back = [
            remote(total, o_ref.at[:, mine], send_back.at[k], recv_back.at[k], devices[k]) for k in range(1, size)
        ]
        for copy in back:
            copy.start()
        o_ref[:, mine] = total[...]
        for copy in back:
            copy.wait_send()
        for k in range(1, size):
            rank = lax.rem(self.me - k + size, size)
            remote(total, o_ref.at[:, self.columns(rank)], send_back.at[k], recv_back.at[k], devices[k]).wait_recv()


def input_grad_kernel(
    gain_row, joined_ref, weights_ref, tokens_ref, hidden_ref, gain_ref, small_ref, out_ref, sums_ref,
    held, from_across, from_line, x_ref, parts, total_ref, send, recv_a, recv_l, *small_sems
):
    rows = tokens_ref.shape[0]
    f32 = jnp.float32
    small = SmallSum(x_ref, sums_ref, parts, total_ref, *small_sems)
    grp, wide, narrow, line, cross = position()
    across = (grp, line * 2 + 1 - cross, narrow)
    above = (grp, wide + 2, narrow)
    below = (grp, wide - 2, narrow)
    has_above, has_below = line < LINE - 1, line > 0
    greet(small.targets)
    order = [(distance, sign) for distance in range(LINE - 1, 0, -1) for sign in (1, -1)] + [(0, 1)]

    def valid(owner):
        return (owner >= 0) & (owner < LINE)

    def part(owner, column):
        at = pl.ds(pl.multiple_of((owner * 2 + column) * rows, rows), rows)
        return dot_nt(joined_ref[at], weights_ref[...])

    def across_copy(owner):
        return remote(held.at[0, owner], from_across.at[owner], send.at[0, owner], recv_a.at[owner], across)

    def line_copy(owner, up):
        slot = 0 if up else 1
        return remote(
            held.at[1, owner], from_line.at[slot, owner], send.at[1, owner], recv_l.at[slot, owner], above if up else below
        )

    for distance, sign in order:
        owner = line + sign * distance

        @pl.when(valid(owner))
        def _(owner=owner):
            held[0, owner] = part(owner, 1 - cross).astype(held.dtype)
            across_copy(owner).start()

    for distance, sign in order[:-1]:
        owner = line + sign * distance

        @pl.when(valid(owner))
        def _(owner=owner, sign=sign):
            up = sign > 0
            came = has_below if up else has_above
            total = part(owner, cross)
            across_copy(owner).wait_recv()
            total = total + from_across[owner].astype(f32)

            @pl.when(came)
            def _():
                line_copy(owner, up).wait_recv()
                held[1, owner] = (total + from_line[0 if up else 1, owner].astype(f32)).astype(held.dtype)

            @pl.when(jnp.logical_not(came))
            def _():
                held[1, owner] = total.astype(held.dtype)

            line_copy(owner, up).start()

    out_ref[...] = part(line, cross)
    across_copy(line).wait_recv()
    out_ref[...] += from_across[line].astype(f32)

    @pl.when(has_below)
    def _():
        line_copy(line, True).wait_recv()
        out_ref[...] += from_line[0, line].astype(f32)

    @pl.when(has_above)
    def _():
        line_copy(line, False).wait_recv()
        out_ref[...] += from_line[1, line].astype(f32)

    x_ref[...] = small_ref[...]
    x_ref[gain_row : gain_row + 1, :] = jnp.zeros((1, D), f32)
    chunk = min(rows, 64)

    def finish(i, carry):
        at = pl.ds(pl.multiple_of(i * chunk, chunk), chunk)
        grad = out_ref[at]
        stream = tokens_ref[at].astype(f32)
        inverse = lax.rsqrt(jnp.mean(stream * stream, -1, keepdims=True) + EPSILON)
        product = grad * stream
        x_ref[gain_row : gain_row + 1, :] += jnp.sum(product * inverse, 0, keepdims=True)
        slope = inverse * inverse * inverse * jnp.sum(product * gain_ref[...], -1, keepdims=True) / D
        out_ref[at] = hidden_ref[at] + inverse * gain_ref[...] * grad - stream * slope
        return carry

    lax.fori_loop(0, rows // chunk, finish, 0)
    small.run()

    for owner in range(LINE):
        across_copy(owner).wait_send()

        @pl.when(owner > line)
        def _(owner=owner):
            line_copy(owner, True).wait_send()

        @pl.when(owner < line)
        def _(owner=owner):
            line_copy(owner, False).wait_send()


def input_grad(joined, weights, tokens, grad_hidden, gain, small, gain_row, ids):
    size = lax.axis_size("wide")
    rows = tokens.shape[0]
    f32, bf16 = jnp.float32, jnp.bfloat16
    if size != 2 * LINE:
        part = dot_nt(joined, weights).astype(bf16).reshape(size, rows, D)
        grad = lax.psum_scatter(part, "wide", scatter_dimension=0, tiled=False).astype(f32)
        stream = tokens.astype(f32)
        inverse = lax.rsqrt(jnp.mean(stream * stream, -1, keepdims=True) + EPSILON)
        small = small.at[gain_row].set(jnp.sum(grad * stream * inverse, 0))
        slope = inverse**3 * jnp.sum(grad * gain * stream, -1, keepdims=True) / D
        return grad_hidden + inverse * gain * grad - stream * slope, lax.psum(small, ("wide", "narrow"))
    devices = 4 * LINE
    block = (LINE, rows, D)
    dma = pltpu.SemaphoreType.DMA
    return pl.pallas_call(
        functools.partial(input_grad_kernel, gain_row),
        out_shape=[jax.ShapeDtypeStruct((rows, D), f32), jax.ShapeDtypeStruct(small.shape, f32)],
        in_specs=[VMEM] * 6,
        out_specs=[VMEM] * 2,
        scratch_shapes=[
            pltpu.VMEM((2, *block), bf16),
            pltpu.VMEM(block, bf16),
            pltpu.VMEM((2, *block), bf16),
            pltpu.VMEM(small.shape, f32),
            pltpu.VMEM((devices, small.shape[0], D // devices), f32),
            pltpu.VMEM((small.shape[0], D // devices), f32),
            dma((2, LINE)),
            dma((LINE,)),
            dma((2, LINE)),
        ]
        + [dma((devices,))] * 4,
        compiler_params=pltpu.CompilerParams(
            collective_id=ids, has_side_effects=True, vmem_limit_bytes=56 * 2**20
        ),
        cost_estimate=lasts(100),
    )(joined, weights, tokens, grad_hidden, gain, small)


def pick_rows(step, capacity, slot_ref, source_ref, picks, held, out_ref):
    row = lax.broadcasted_iota(jnp.int32, (capacity, source_ref.shape[1]), 0)
    pick = jnp.where(row == slot_ref[0], 1.0, 0.0).astype(jnp.bfloat16)
    picks[step] = pick
    values = dot(pick, source_ref[0]).astype(jnp.bfloat16)
    held[pl.ds(pl.multiple_of(step * capacity, capacity), capacity)] = values
    out_ref[...] = values


def spread_rows(block, capacity, picks, total, before_ref, out_ref):
    here = pl.ds(pl.multiple_of(block * capacity, capacity), capacity)
    values = dot_tn(picks[block], total[here].astype(jnp.bfloat16))
    if before_ref is not None:
        values = values + before_ref[0].astype(jnp.float32)
    out_ref[0] = values.astype(jnp.bfloat16)


def expert_forward_kernel(
    tiles, capacity, experts, first, id_ref, slot_ref, tokens_ref, router_ref, gate_ref, up_ref, down_ref, *refs
):
    before_ref = None if first else refs[0]
    moe_ref, x_ref, inner_ref, gate_pre_ref, up_pre_ref, probs_ref, x_all, picks, moe_all = refs[0 if first else 1 :]
    step = pl.program_id(1)
    blocks = picks.shape[0]
    lane = lax.broadcasted_iota(jnp.int32, (1, 128), 1)

    @pl.when(step < blocks)
    def _():
        pick_rows(step, capacity, slot_ref, tokens_ref, picks, x_all, x_ref)

    @pl.when(step == blocks)
    def _():
        logits = jnp.where(lane < experts, dot(x_all[...], router_ref[...]), NEGATIVE)
        weight = jnp.exp(logits - jnp.max(logits, -1, keepdims=True))
        probs_ref[...] = weight / jnp.sum(weight, -1, keepdims=True)
        moe_all[...] = jnp.zeros_like(moe_all)

    @pl.when((step >= blocks) & (step < blocks + tiles))
    def _():
        x = x_all[...]
        gate = jnp.sum(jnp.where(lane == id_ref[0], probs_ref[...], 0.0), -1, keepdims=True)
        gate_pre = dot(x, gate_ref[...])
        up_pre = dot(x, up_ref[...])
        gate_pre_ref[...] = gate_pre
        up_pre_ref[...] = up_pre
        inner_gated = (gate * (gate_pre / (1.0 + jnp.exp(-gate_pre))) * up_pre).astype(jnp.bfloat16)
        inner_ref[...] = inner_gated
        moe_all[...] += dot(inner_gated, down_ref[...])

    @pl.when(step >= blocks + tiles)
    def _():
        spread_rows(step - blocks - tiles, capacity, picks, moe_all, before_ref, moe_ref)


def expert_backward_kernel(
    tiles, capacity, first, id_ref, slot_ref, grads_ref, x_ref, probs_ref, gate_pre_ref, up_pre_ref,
    router_ref, gate_ref, up_ref, down_ref, *refs
):
    before_ref, router_in_ref = (None, None) if first else refs[:2]
    (
        part_ref, g_ref, grad_gate_ref, grad_up_ref, router_grad_ref,
        g_all, picks, part_all, scores_all, router_sum,
    ) = refs[0 if first else 2 :]
    bf16 = jnp.bfloat16
    group, step = pl.program_id(0), pl.program_id(1)
    blocks = picks.shape[0]
    lane = lax.broadcasted_iota(jnp.int32, (1, 128), 1)
    here = jnp.where(lane == id_ref[0], 1.0, 0.0)

    @pl.when(step < blocks)
    def _():
        pick_rows(step, capacity, slot_ref, grads_ref, picks, g_all, g_ref)

    @pl.when(step == blocks)
    def _():
        part_all[...] = jnp.zeros_like(part_all)
        scores_all[...] = jnp.zeros_like(scores_all)

    @pl.when((step >= blocks) & (step < blocks + tiles))
    def _():
        gate = jnp.sum(probs_ref[...] * here, -1, keepdims=True)
        gate_pre, up_pre = gate_pre_ref[...], up_pre_ref[...]
        back = dot_nt(g_all[...], down_ref[...])
        sigmoid = 1.0 / (1.0 + jnp.exp(-gate_pre))
        silu = gate_pre * sigmoid
        scores_all[...] += jnp.sum(silu * up_pre * back, -1, keepdims=True)
        back = gate * back
        grad_gate_pre = (back * up_pre * sigmoid * (1.0 + gate_pre * (1.0 - sigmoid))).astype(bf16)
        grad_up_pre = (back * silu).astype(bf16)
        grad_gate_ref[...] = grad_gate_pre
        grad_up_ref[...] = grad_up_pre
        part_all[...] += dot_nt(grad_gate_pre, gate_ref[...]) + dot_nt(grad_up_pre, up_ref[...])

    @pl.when(step == blocks + tiles)
    def _():
        probs = probs_ref[...]
        gate = jnp.sum(probs * here, -1, keepdims=True)
        mixing = (gate * scores_all[...] * (here - probs)).astype(bf16)
        part_all[...] += dot_nt(mixing, router_ref[...])
        grad = dot_tn(mixing, x_ref[...])

        @pl.when(group == 0)
        def _():
            router_sum[...] = grad if first else grad + router_in_ref[...]

        @pl.when(group > 0)
        def _():
            router_sum[...] += grad

        router_grad_ref[...] = router_sum[...]

    @pl.when(step >= blocks + tiles)
    def _():
        spread_rows(step - blocks - tiles, capacity, picks, part_all, before_ref, part_ref)


class Expert:
    def __init__(self, expert, slots, router, weights, capacity, experts):
        self.scalars = expert.astype(jnp.int32).reshape(1), slots
        self.router, self.weights, self.capacity, self.experts = router, weights, capacity, experts
        wide, _, rows = slots.shape
        units = weights[0].shape[1]
        groups = 2 if wide * capacity > 1024 else 1
        blocks, tile = wide // groups, 256
        tiles = units // tile
        last = blocks + tiles
        self.tiles, self.grid = tiles, (groups, last + blocks)
        self.held, self.blocks, self.rows = blocks * capacity, blocks, rows
        count = wide * capacity

        def picked(g, i):
            return g * blocks + jnp.minimum(i, blocks - 1)

        def tiled(i):
            return jnp.clip(i - blocks, 0, tiles - 1)

        self.whole = pl.BlockSpec((1, rows, D), lambda g, i: (picked(g, i), 0, 0))
        self.back = pl.BlockSpec((1, rows, D), lambda g, i: (g * blocks + jnp.clip(i - last, 0, blocks - 1), 0, 0))
        self.row = pl.BlockSpec((capacity, D), lambda g, i: (picked(g, i), 0))
        column = pl.BlockSpec((D, tile), lambda g, i: (0, tiled(i)))
        self.unit = pl.BlockSpec((self.held, tile), lambda g, i: (g, tiled(i)))
        self.fixed = pl.BlockSpec((128, D), lambda g, i: (0, 0))
        self.rows_all = pl.BlockSpec((self.held, D), lambda g, i: (g, 0))
        self.probs = pl.BlockSpec((self.held, 128), lambda g, i: (g, 0))
        self.heads = [
            pl.BlockSpec(memory_space=pltpu.SMEM), pl.BlockSpec((1, 1, rows), lambda g, i: (picked(g, i), 0, 0))
        ]
        self.weight_specs = [
            pl.BlockSpec((D, 128), lambda g, i: (0, 0)), column, column,
            pl.BlockSpec((tile, D), lambda g, i: (tiled(i), 0)),
        ]
        shape = jax.ShapeDtypeStruct
        self.blocks_shape = shape((wide, rows, D), jnp.bfloat16)
        self.compact = shape((count, D), jnp.bfloat16)
        self.narrow = shape((count, units), jnp.bfloat16)
        self.narrow32 = shape((count, units), jnp.float32)
        self.probs_shape = shape((count, 128), jnp.float32)
        self.common = dict(
            grid=self.grid,
            compiler_params=pltpu.CompilerParams(vmem_limit_bytes=60 * 2**20),
            cost_estimate=pl.CostEstimate(flops=0, bytes_accessed=120_000_000, transcendentals=0),
        )

    def forward(self, tokens, before):
        first = before is None
        f32, bf16 = jnp.float32, jnp.bfloat16
        return pl.pallas_call(
            functools.partial(expert_forward_kernel, self.tiles, self.capacity, self.experts, first),
            in_specs=self.heads + [self.whole] + self.weight_specs + ([] if first else [self.back]),
            out_specs=[self.back, self.row, self.unit, self.unit, self.unit, self.probs],
            out_shape=[
                self.blocks_shape, self.compact, self.narrow, self.narrow32, self.narrow32, self.probs_shape
            ],
            scratch_shapes=[
                pltpu.VMEM((self.held, D), bf16),
                pltpu.VMEM((self.blocks, self.capacity, self.rows), bf16),
                pltpu.VMEM((self.held, D), f32),
            ],
            **self.common,
        )(*self.scalars, tokens, self.router, *self.weights, *(() if first else (before,)))

    def backward(self, grads, kept, before):
        first = before is None
        f32, bf16 = jnp.float32, jnp.bfloat16
        _, x, _, gate_pre, up_pre, probs = kept
        return pl.pallas_call(
            functools.partial(expert_backward_kernel, self.tiles, self.capacity, first),
            in_specs=self.heads
            + [self.whole, self.rows_all, self.probs, self.unit, self.unit]
            + self.weight_specs
            + ([] if first else [self.back, self.fixed]),
            out_specs=[self.back, self.row, self.unit, self.unit, self.fixed],
            out_shape=[
                self.blocks_shape, self.compact, self.narrow, self.narrow, jax.ShapeDtypeStruct((128, D), f32)
            ],
            scratch_shapes=[
                pltpu.VMEM((self.held, D), bf16),
                pltpu.VMEM((self.blocks, self.capacity, self.rows), bf16),
                pltpu.VMEM((self.held, D), f32),
                pltpu.VMEM((self.held, 1), f32),
                pltpu.VMEM((128, D), f32),
            ],
            **self.common,
        )(*self.scalars, grads, x, probs, gate_pre, up_pre, self.router, *self.weights, *(before or ()))


def positions(token_ids):
    local = token_ids % (PROMPT + NCONT * CONT)
    return jnp.where(local < PROMPT, local, PROMPT + (local - PROMPT) % CONT)


def rotation(place):
    frequency = THETA ** (-2.0 * jnp.arange(HD // 2, dtype=jnp.float32) / HD)
    angle = place.astype(jnp.float32)[:, None] * frequency[None, :]
    cosine, sine = jnp.cos(angle), jnp.sin(angle)
    return jnp.concatenate([cosine, cosine], 1), jnp.concatenate([-sine, sine], 1)


def shards(
    tokens,
    cotangent,
    valid,
    routes,
    w_query,
    w_key,
    w_value,
    w_out,
    norm_attn,
    norm_query,
    norm_key,
    norm_moe,
    w_router,
    w_gate,
    w_up,
    w_down,
):
    bf16, f32 = jnp.bfloat16, jnp.float32
    wide_count = lax.axis_size("wide")
    narrow_count = lax.axis_size("narrow")
    rows = tokens.shape[0]
    half = rows * wide_count
    columns = w_query.shape[1]
    experts = w_router.shape[1]
    hidden_units = w_gate.shape[2]
    capacity = min(max(rows * TOP * 5 // (4 * experts), 2), rows)
    assert narrow_count == 2 and CONT in (rows, 2 * rows)
    paired = CONT == 2 * rows
    side = lax.axis_index("narrow")
    place = lax.axis_index("wide")
    group = lax.axis_index("grp")
    swap = [(0, 1), (1, 0)]
    twins = lax.axis_size("grp") == 2
    prompt_blocks = PROMPT // (rows * narrow_count)
    shared = half if paired else prompt_blocks * rows
    attend, attend_back = attention_calls(rows, half, shared, columns, prompt_blocks, paired, (1, 2))
    barrier = lax.optimization_barrier

    def exchange(value):
        return lax.ppermute(value, "narrow", swap)

    stream = tokens.astype(f32)
    inv_one = lax.rsqrt(jnp.mean(stream * stream, -1, keepdims=True) + EPSILON)
    gain_one = norm_attn.astype(f32)
    normed = (stream * inv_one * gain_one).astype(bf16)
    mask = valid.astype(f32)[:, None]
    grad_final = cotangent.astype(f32) * mask
    pieces = 2 * narrow_count if twins else 1
    piece_width = D // pieces
    piece_id = group * narrow_count + side if twins else 0
    piece = lax.dynamic_slice_in_dim(w_out, piece_id * piece_width, piece_width, 1)
    (routes_plane, normed_plane, out_piece), (other_up,), others = start_exchange(
        [routes.T, normed, piece], [w_up[0]], 0, twins
    )
    normed_plane = normed_plane.reshape(half, D)
    out_pieces = [p.reshape(D, piece_width) for p in (out_piece, *others)]

    def ordered(parts):
        if not twins:
            return parts
        parts = [jnp.where(side == 0, parts[k], parts[k ^ 1]) for k in range(4)]
        return [jnp.where(group == 0, parts[k], parts[k ^ 2]) for k in range(4)]

    def unordered(whole):
        return ordered([whole[:, k * piece_width : (k + 1) * piece_width] for k in range(pieces)])

    grad_final_b, _ = barrier((grad_final.astype(bf16), normed_plane))
    grads_in = lax.all_gather(grad_final_b, "wide", axis=0, tiled=True).reshape(wide_count, rows, D)
    joined = jnp.concatenate([w_query, w_key, w_value], 1)
    raw = dot(normed_plane, joined)
    gains = jnp.pad(jnp.stack([norm_query, norm_key]).astype(f32), ((0, 6), (0, 0)))
    plane_ids = (
        (jnp.arange(wide_count, dtype=jnp.int32)[:, None] * narrow_count + side) * rows
        + jnp.arange(rows, dtype=jnp.int32)[None, :]
    ).reshape(half)
    cosine, sine = rotation(positions(plane_ids))
    kept = attend(raw, gains, cosine, sine)
    attended, attended_own, lse, sums = kept[5:]

    branch = jnp.concatenate(ordered([dot(attended_own, p) for p in out_pieces]), 1)
    hidden = stream + branch
    inv_two = lax.rsqrt(jnp.mean(hidden * hidden, -1, keepdims=True) + EPSILON)
    gain_two = norm_moe.astype(f32)
    moe_in = (hidden * inv_two * gain_two).astype(bf16)
    (tokens_in,), (other_gate, other_down), _ = start_exchange([moe_in], [w_gate[0], w_down[0]], 6)

    earlier = (jnp.arange(rows)[:, None] < jnp.arange(rows)[None, :]).astype(bf16)

    def slots_of(expert):
        chosen = jnp.any(routes_plane == expert, 1)
        rank = dot(chosen.astype(bf16), earlier).astype(jnp.int32)
        return jnp.where(chosen, rank, -1).reshape(wide_count, 1, rows)

    router = jnp.pad(w_router, ((0, 0), (0, 128 - experts)))

    own, other = (
        Expert(e, slots_of(e), router, w, capacity, experts)
        for e, w in (
            (place * narrow_count + side, (w_gate[0], w_up[0], w_down[0])),
            (place * narrow_count + 1 - side, (other_gate, other_up, other_down)),
        )
    )
    kept_own = own.forward(tokens_in, None)
    kept_other = other.forward(tokens_in, kept_own[0])
    moe_part = kept_other[0]
    moe = lax.psum_scatter(moe_part.reshape(half, D), "wide", scatter_dimension=0, tiled=True).astype(f32)
    kept_other, grads_in, _ = barrier((kept_other, grads_in, moe_part))
    back_other = other.backward(grads_in, kept_other, None)
    partner_grads = plain_grads(kept_other[1], back_other[1], kept_other[2], back_other[2], back_other[3])
    came = [exchange(g) for g in partner_grads[:2]]
    before, partner_grads = barrier(((back_other[0], back_other[4]), partner_grads))
    back_own = own.backward(grads_in, kept_own, before)
    grad_part, grad_router = back_own[0], back_own[4][:experts]
    own_operands = (kept_own[1], back_own[1], kept_own[2], back_own[2], back_own[3])
    grad_moe_in, *own_grads = expert_grad(grad_part, own_operands, 5)
    grad_moe_in, moe, came[0], down_grad = barrier((grad_moe_in, moe, came[0], partner_grads[2]))
    came.append(exchange(down_grad))

    grad_gain_two = jnp.sum(grad_moe_in * hidden * inv_two, 0)
    grad_hidden = (
        grad_final
        + inv_two * gain_two * grad_moe_in
        - hidden * inv_two**3 * jnp.sum(grad_moe_in * gain_two * hidden, -1, keepdims=True) / D
    )
    grad_branch = grad_hidden.astype(bf16)
    grad_attended_own = sum(dot_nt(g, p) for g, p in zip(unordered(grad_branch), out_pieces)).astype(bf16)
    grads_joined, gain_grads, branch_plane = attend_back(
        raw, gains, cosine, sine, sums, *kept[:5], grad_attended_own, attended, lse, grad_branch
    )
    grads_joined, came[1], came[2] = barrier((grads_joined, came[1], came[2]))
    grad_out = barrier(dot_tn(attended, branch_plane.reshape(half, D)).astype(bf16))
    grad_weights = barrier(dot_tn(normed_plane, grads_joined).astype(bf16))
    weights_came = exchange(grad_weights)
    out_came = exchange(grad_out)
    stats = jnp.stack([jnp.sum(v * v * mask) for v in (stream, branch, hidden, moe, hidden + moe)] + [jnp.sum(mask)])
    here = jnp.repeat(jnp.arange(wide_count) == place, columns)
    spots = [jnp.where(here, jnp.tile(g, wide_count), 0.0) for g in gain_grads[:2]]
    zeros = jnp.zeros((D,), f32)
    small = jnp.stack([zeros, grad_gain_two, *spots, jnp.pad(stats, (0, D - stats.shape[0]))])
    small = jnp.concatenate([grad_router, small, jnp.zeros((-(experts + 5) % 8, D), f32)], 0)
    small, _, _ = barrier((small, grad_weights, grad_out))
    grad_input, small = input_grad(
        grads_joined, joined, tokens, grad_hidden, gain_one.reshape(1, D), small, experts, 3
    )
    grad_weights = grad_weights.astype(f32) + weights_came.astype(f32)
    grad_out = grad_out.astype(f32) + out_came.astype(f32)
    grad_query_w, grad_key_w, grad_value_w = (
        grad_weights[:, i * columns : (i + 1) * columns] for i in range(3)
    )
    final = hidden + moe
    output = final.astype(bf16)
    grad_gate_w, grad_up_w, grad_down_w = (
        (own.astype(f32) + other.astype(f32))[None] for own, other in zip(own_grads, came)
    )

    spots = lax.dynamic_slice_in_dim(small[experts + 2 : experts + 4], place * columns, columns, 1)
    stats = small[experts + 4, :6]
    rms = jnp.sqrt(stats[:5] / (jnp.maximum(stats[5], 1.0) * D))
    return (
        output,
        grad_input,
        grad_query_w,
        grad_key_w,
        grad_value_w,
        grad_out,
        small[experts],
        spots[0],
        spots[1],
        small[experts + 1],
        small[:experts].T,
        grad_gate_w,
        grad_up_w,
        grad_down_w,
        rms,
    )


def solution(mesh):
    return jax.shard_map(
        shards,
        mesh=mesh,
        in_specs=(
            P(("grp", "wide", "narrow"), None),
            P(("grp", "wide", "narrow"), None),
            P(("grp", "wide", "narrow")),
            P(("grp", "wide", "narrow"), None),
            P(None, "wide"),
            P(None, "wide"),
            P(None, "wide"),
            P("wide", None),
            P(),
            P("wide"),
            P("wide"),
            P(),
            P(),
            P(("wide", "narrow"), None, None),
            P(("wide", "narrow"), None, None),
            P(("wide", "narrow"), None, None),
        ),
        out_specs=(
            P(("grp", "wide", "narrow"), None),
            P(("grp", "wide", "narrow"), None),
            P("grp", "wide"),
            P("grp", "wide"),
            P("grp", "wide"),
            P(("grp", "wide"), None),
            P("grp"),
            P(("grp", "wide")),
            P(("grp", "wide")),
            P("grp"),
            P("grp", None),
            P(("grp", "wide", "narrow"), None, None),
            P(("grp", "wide", "narrow"), None, None),
            P(("grp", "wide", "narrow"), None, None),
            P("grp"),
        ),
        check_vma=False,
    )
```

```python
import functools

import jax
import jax.numpy as jnp
from jax import lax
from jax.experimental import pallas as pl
from jax.experimental.pallas import tpu as pltpu
from jax.sharding import PartitionSpec as P

D = 2048
HD = 128
TOP = 8
PROMPT = 2048
CONT = 256
NCONT = 8

EPSILON = 1e-05
THETA = 10000.0
NEGATIVE = -1e30


MESH_ID = pl.DeviceIdType.MESH
ANY = pl.BlockSpec(memory_space=pl.ANY)
VMEM = pl.BlockSpec(memory_space=pltpu.VMEM)
LINE = 4


def lasts(microseconds):
    return pl.CostEstimate(flops=0, bytes_accessed=microseconds * 3_000_000, transcendentals=0)


def position():
    grp, wide, narrow = (lax.axis_index(a) for a in ("grp", "wide", "narrow"))
    return grp, wide, narrow, wide // 2, lax.rem(wide, 2)


def greet(targets):
    barrier = pltpu.get_barrier_semaphore()
    for device, when in targets:
        def signal(device=device):
            pl.semaphore_signal(barrier, inc=1, device_id=device, device_id_type=MESH_ID)

        if when is None:
            signal()
        else:
            pl.when(when)(signal)
    peers = sum(1 if when is None else when.astype(jnp.int32) for _, when in targets)
    pl.semaphore_wait(barrier, peers)


def remote(src, dst, send, recv, device):
    return pltpu.make_async_remote_copy(
        src_ref=src, dst_ref=dst, send_sem=send, recv_sem=recv, device_id=device, device_id_type=MESH_ID
    )


def gather_kernel(count, *refs):
    ins, outs = refs[:count], refs[count : 2 * count]
    gather_body(count, ins, outs, *refs[2 * count :])


class Gather:
    def __init__(self, ins, outs, send, recv, local):
        self.ins, self.outs, self.send, self.recv, self.local = ins, outs, send, recv, local
        grp, wide, narrow, self.line, self.cross = position()
        self.wide = wide
        self.across = (grp, self.line * 2 + 1 - self.cross, narrow)
        self.above = (grp, wide + 2, narrow)
        self.below = (grp, wide - 2, narrow)
        self.has_above, self.has_below = self.line < LINE - 1, self.line > 0
        self.targets = [(self.across, None), (self.above, self.has_above), (self.below, self.has_below)]
        self.arrived = lambda i, slot: None

    def copy(self, i, source_line, way, device):
        slot = source_line * 2 + self.cross
        out = self.outs[i].at[slot]
        return remote(out, out, self.send.at[i, way, source_line], self.recv.at[i, slot], device)

    def own(self, i, way, device):
        return remote(
            self.ins[i], self.outs[i].at[self.wide], self.send.at[i, way, self.line], self.recv.at[i, self.wide], device
        )

    def mine(self, i):
        return pltpu.make_async_copy(self.ins[i], self.outs[i].at[self.wide], self.local.at[i])

    def start(self):
        for i in range(len(self.ins)):
            pl.when(self.has_above)(self.own(i, 1, self.above).start)
            pl.when(self.has_below)(self.own(i, 2, self.below).start)
            self.own(i, 0, self.across).start()
            self.mine(i).start()
            self.arrived(i, None)

    def forward(self, distance, only=None):
        for i in range(len(self.ins)) if only is None else (only,):
            for sign in (-1, 1):
                source = self.line + sign * distance

                @pl.when((source >= 0) & (source < LINE))
                def _(i=i, source=source, sign=sign):
                    self.copy(i, source, 0, self.across).wait_recv()
                    onward = self.above if sign < 0 else self.below

                    @pl.when(self.has_above if sign < 0 else self.has_below)
                    def _():
                        self.copy(i, source, 1 if sign < 0 else 2, onward).start()

                    self.copy(i, source, 0, self.across).start()
                    self.arrived(i, source * 2 + self.cross)

    def finish(self):
        for i in range(len(self.ins)):
            send, recv, src, out = self.send, self.recv, self.ins[i], self.outs[i]
            for source in range(LINE):
                other = source * 2 + 1 - self.cross
                remote(src, out.at[other], send.at[i, 0, 0], recv.at[i, other], self.across).wait_recv()
                self.arrived(i, other)
            for source in range(LINE):
                remote(src, out.at[0], send.at[i, 0, source], recv.at[i, 0], self.across).wait_send()

                @pl.when(self.has_above & (source <= self.line))
                def _(source=source):
                    remote(src, out.at[0], send.at[i, 1, source], recv.at[i, 0], self.above).wait_send()

                @pl.when(self.has_below & (source >= self.line))
                def _(source=source):
                    remote(src, out.at[0], send.at[i, 2, source], recv.at[i, 0], self.below).wait_send()

            self.mine(i).wait()


def gather_sems(count):
    return [
        pltpu.SemaphoreType.DMA((count, 3, LINE)),
        pltpu.SemaphoreType.DMA((count, 2 * LINE)),
        pltpu.SemaphoreType.DMA((count,)),
    ]


def gather_body(count, ins, outs, send, recv, local, more=(), begin=None, finish=None, arrived=None):
    gather = Gather(ins, outs, send, recv, local)
    if arrived is not None:
        gather.arrived = arrived
    greet([*gather.targets, *more])
    gather.start()
    if begin is not None:
        begin()
    for i in range(count):
        for distance in range(1, LINE):
            gather.forward(distance, i)
    gather.finish()
    if finish is not None:
        finish()


def gather_wide(arrays, collective_id):
    count = len(arrays)
    size = lax.axis_size("wide")
    if size != 2 * LINE:
        return [lax.all_gather(a, "wide", axis=0) for a in arrays]
    return pl.pallas_call(
        functools.partial(gather_kernel, count),
        out_shape=[jax.ShapeDtypeStruct((size, *a.shape), a.dtype) for a in arrays],
        in_specs=[ANY] * count,
        out_specs=[ANY] * count,
        scratch_shapes=[
            pltpu.SemaphoreType.DMA((count, 3, LINE)),
            pltpu.SemaphoreType.DMA((count, size)),
            pltpu.SemaphoreType.DMA((count,)),
        ],
        compiler_params=pltpu.CompilerParams(collective_id=collective_id, has_side_effects=True),
        cost_estimate=lasts(100),
    )(*arrays)


def scatter_kernel(part_ref, out_ref, held, from_across, from_line, load, send, recv_a, recv_l):
    grp, wide, narrow, line, cross = position()
    across = (grp, line * 2 + 1 - cross, narrow)
    above = (grp, wide + 2, narrow)
    below = (grp, wide - 2, narrow)
    has_above, has_below = line < LINE - 1, line > 0
    f32 = jnp.float32
    greet([(across, None), (above, has_above), (below, has_below)])

    order = []
    for distance in range(LINE - 1, 0, -1):
        for sign in (1, -1):
            order.append((distance, sign))

    def valid(owner):
        return (owner >= 0) & (owner < LINE)

    def across_copy(owner):
        return remote(
            part_ref.at[owner * 2 + 1 - cross], from_across.at[owner], send.at[0, owner], recv_a.at[owner], across
        )

    def load_copy(owner):
        return pltpu.make_async_copy(part_ref.at[owner * 2 + cross], held.at[owner], load.at[owner])

    def line_copy(owner, up):
        return remote(
            held.at[owner],
            from_line.at[0 if up else 1, owner],
            send.at[1, owner],
            recv_l.at[0 if up else 1, owner],
            above if up else below,
        )

    for distance, sign in order + [(0, 1)]:
        owner = line + sign * distance

        @pl.when(valid(owner))
        def _(owner=owner):
            across_copy(owner).start()
            load_copy(owner).start()

    for distance, sign in order:
        owner = line + sign * distance

        @pl.when(valid(owner))
        def _(owner=owner, sign=sign):
            load_copy(owner).wait()
            across_copy(owner).wait_recv()
            up = sign > 0
            came = has_below if up else has_above
            total = held[owner].astype(f32) + from_across[owner].astype(f32)

            @pl.when(came)
            def _():
                line_copy(owner, up).wait_recv()
                held[owner] = (total + from_line[0 if up else 1, owner].astype(f32)).astype(held.dtype)

            @pl.when(jnp.logical_not(came))
            def _():
                held[owner] = total.astype(held.dtype)

            line_copy(owner, up).start()

    load_copy(line).wait()
    across_copy(line).wait_recv()
    out_ref[...] = held[line].astype(f32) + from_across[line].astype(f32)

    @pl.when(has_below)
    def _():
        line_copy(line, True).wait_recv()
        out_ref[...] += from_line[0, line].astype(f32)

    @pl.when(has_above)
    def _():
        line_copy(line, False).wait_recv()
        out_ref[...] += from_line[1, line].astype(f32)

    for owner in range(LINE):
        across_copy(owner).wait_send()

        @pl.when(owner > line)
        def _(owner=owner):
            line_copy(owner, True).wait_send()

        @pl.when(owner < line)
        def _(owner=owner):
            line_copy(owner, False).wait_send()


def scatter_wide(part, collective_id):
    size, rows, columns = part.shape
    if size != 2 * LINE:
        return lax.psum_scatter(part, "wide", scatter_dimension=0, tiled=False).astype(jnp.float32)
    block = (LINE, rows, columns)
    return pl.pallas_call(
        scatter_kernel,
        out_shape=jax.ShapeDtypeStruct((rows, columns), jnp.float32),
        in_specs=[ANY],
        out_specs=VMEM,
        scratch_shapes=[
            pltpu.VMEM(block, part.dtype),
            pltpu.VMEM(block, part.dtype),
            pltpu.VMEM((2, *block), part.dtype),
            pltpu.SemaphoreType.DMA((LINE,)),
            pltpu.SemaphoreType.DMA((2, LINE)),
            pltpu.SemaphoreType.DMA((LINE,)),
            pltpu.SemaphoreType.DMA((2, LINE)),
        ],
        compiler_params=pltpu.CompilerParams(
            collective_id=collective_id, has_side_effects=True, vmem_limit_bytes=48 * 2**20
        ),
        cost_estimate=lasts(95),
    )(part)


def sum_kernel(x_ref, o_ref, held, send, recv):
    grp, wide, narrow, _, _ = position()
    size = held.shape[0] + 1
    others = [(grp, lax.rem(wide + k, size), narrow) for k in range(1, size)]
    greet([(device, None) for device in others])
    copies = [
        remote(x_ref, held.at[k], send.at[k], recv.at[k], device) for k, device in enumerate(others)
    ]
    for copy in copies:
        copy.start()
    for copy in copies:
        copy.wait()
    total = x_ref[...]
    for k in range(size - 1):
        total = total + held[k]
    o_ref[...] = total


def sum_wide(x, collective_id):
    size = lax.axis_size("wide")
    if size != 2 * LINE:
        return lax.psum(x, "wide")
    return pl.pallas_call(
        sum_kernel,
        out_shape=jax.ShapeDtypeStruct(x.shape, x.dtype),
        in_specs=[VMEM],
        out_specs=VMEM,
        scratch_shapes=[
            pltpu.VMEM((size - 1, *x.shape), x.dtype),
            pltpu.SemaphoreType.DMA((size - 1,)),
            pltpu.SemaphoreType.DMA((size - 1,)),
        ],
        compiler_params=pltpu.CompilerParams(collective_id=collective_id, has_side_effects=True),
        cost_estimate=lasts(8),
    )(x)


LOG2E = 1.4426950408889634
NT = (((1,), (1,)), ((), ()))


def key_parts(w, plane, rows, prompt_blocks, paired, limit=512):
    count = (prompt_blocks if w is None else w) * rows
    parts = [(first, min(limit, count - first), None) for first in range(0, count, limit)]
    own = None if w is None else w * rows
    if plane == 0:
        parts.append((own, rows, "causal"))
    elif w is not None or paired:
        parts.append((own, rows, "side"))
    return parts


def for_blocks(blocks, prompt_blocks, one, between=None, first=0):
    for w in range(prompt_blocks):
        one(w, w, w * one.rows)
    if between is not None:
        between()

    def body(i, carry):
        w = prompt_blocks + lax.rem(i - prompt_blocks + first, blocks - prompt_blocks)
        one(None, w, pl.multiple_of(w * one.rows, one.rows))
        return carry

    lax.fori_loop(prompt_blocks, blocks, body, 0)


def masked_scores(score, mask, side, rows):
    if mask == "causal":
        key = lax.broadcasted_iota(jnp.int32, (rows, rows), 0)
        query = lax.broadcasted_iota(jnp.int32, (rows, rows), 1)
        return jnp.where(key <= query, score, NEGATIVE)
    if mask == "side":
        return jnp.where(side == 1, score, NEGATIVE)
    return score


def row_sums(values):
    total = values[:, :HD]
    for first in range(HD, values.shape[1], HD):
        total = total + values[:, first : first + HD]
    return jnp.sum(total.T, 0, keepdims=True)


def turn(values, cosine, sine):
    return values * cosine + pltpu.roll(values, HD // 2, 1) * sine


def inverse_norms(sums_ref, at):
    inverse = lax.rsqrt(sums_ref[:, at].T / D + EPSILON)
    return inverse[:, 0:1], inverse[:, 1:2]


def peer_copies(size, src, dst, send, recv, grp, wide, narrow):
    return [
        remote(src, dst.at[k - 1], send.at[k - 1], recv.at[k - 1], (grp, lax.rem(wide + k, size), narrow))
        for k in range(1, size)
    ]


def attend_kernel(
    rows, prompt_blocks, paired, shared, carried, raw_ref, gains_ref, cos_ref, sin_ref, *refs
):
    carry_in, refs = refs[:carried], refs[carried:]
    q_ref, k_ref, v_ref, ko_ref, vo_ref, o_ref, own_ref, lse_ref, sums_ref = refs[:9]
    carry_out, refs = refs[9 : 9 + carried], refs[9 + carried :]
    vt_ref, vto_ref, came_ref, sum_send, sum_recv, pair_send, pair_recv, out_send, out_recv = refs[:9]
    gather = Gather(carry_in, carry_out, *refs[9:]) if carried else None
    half, columns = q_ref.shape
    size = half // rows
    heads = columns // HD
    grp, wide, narrow = (lax.axis_index(a) for a in ("grp", "wide", "narrow"))
    partner = (grp, wide, 1 - narrow)
    greet([((grp, lax.rem(wide + k, size), narrow), None) for k in range(1, size)] + [(partner, None)])
    if carried:
        gather.start()
    pairs = [
        remote(src.at[pl.ds(0, shared)], dst, pair_send.at[i], pair_recv.at[i], partner)
        for i, (src, dst) in enumerate(((k_ref, ko_ref), (v_ref, vo_ref)))
    ]
    v_ref[...] = raw_ref[:, 2 * columns :].astype(jnp.bfloat16)
    pairs[1].start()
    sums_ref[...] = jnp.zeros_like(sums_ref)

    def squares(b, carry):
        at = pl.ds(pl.multiple_of(b * rows, rows), rows)
        for i in range(2):
            part = raw_ref[at, i * columns : (i + 1) * columns]
            sums_ref[i : i + 1, at] = row_sums(part * part)
        return carry

    lax.fori_loop(0, size, squares, 0)
    copies = peer_copies(size, sums_ref, came_ref, sum_send, sum_recv, grp, wide, narrow)
    for copy in copies:
        copy.start()
    for h in range(heads):
        hs = slice(h * HD, (h + 1) * HD)
        vt_ref[hs, :] = v_ref[:, hs].T
    for copy in copies:
        copy.wait()
    total = sums_ref[...]
    for k in range(size - 1):
        total = total + came_ref[k]
    sums_ref[...] = total

    def prepare(i, ref):
        def body(b, carry):
            at = pl.ds(pl.multiple_of(b * rows, rows), rows)
            inverse = inverse_norms(sums_ref, at)[i]
            for h in range(heads):
                hs = slice(h * HD, (h + 1) * HD)
                values = raw_ref[at, i * columns + h * HD : i * columns + (h + 1) * HD]
                values = values * inverse * gains_ref[i : i + 1, hs]
                ref[at, hs] = turn(values, cos_ref[at], sin_ref[at]).astype(jnp.bfloat16)
            return carry

        return body

    lax.fori_loop(0, shared // rows, prepare(1, k_ref), 0)
    pairs[0].start()
    lax.fori_loop(shared // rows, size, prepare(1, k_ref), 0)
    lax.fori_loop(0, size, prepare(0, q_ref), 0)
    if carried:
        gather.forward(1)
    pairs[1].wait()
    for h in range(heads):
        hs = slice(h * HD, (h + 1) * HD)
        vto_ref[hs, :] = vo_ref[:, hs].T
    pairs[0].wait()

    def mine():
        return pl.ds(pl.multiple_of(wide * columns, columns), columns)

    def hand_out(w):
        return remote(
            o_ref.at[pl.ds(pl.multiple_of(w * rows, rows), rows)],
            own_ref.at[:, mine()],
            out_send.at[w],
            out_recv.at[wide],
            (grp, w, narrow),
        )

    def one(w, w_index, start):
        block = pl.ds(start, rows)
        for h in range(heads):
            hs = slice(h * HD, (h + 1) * HD)
            query = q_ref[block, hs]
            scores = []
            for plane in range(2):
                for first, count, mask in key_parts(w, plane, rows, prompt_blocks, paired):
                    at = pl.ds(start if first is None else first, count)
                    key = (k_ref, ko_ref)[plane][at, hs]
                    score = lax.dot_general(key, query, NT, preferred_element_type=jnp.float32)
                    score = score * (HD**-0.5 * LOG2E)
                    scores.append((plane, at, masked_scores(score, mask, narrow, rows)))
            largest = functools.reduce(
                jnp.maximum, [jnp.max(score, 0, keepdims=True) for _, _, score in scores]
            )
            total = jnp.zeros((1, rows), jnp.float32)
            mixed = jnp.zeros((HD, rows), jnp.float32)
            for plane, at, score in scores:
                weight = jnp.exp2(score - largest)
                total = total + jnp.sum(weight, 0, keepdims=True)
                mixed = mixed + dot((vt_ref, vto_ref)[plane][hs, at], weight.astype(jnp.bfloat16))
            o_ref[block, hs] = (mixed / total).T.astype(jnp.bfloat16)
            lse_ref[h : h + 1, block] = largest + jnp.log(total) * LOG2E

        @pl.when(w_index != wide)
        def _():
            hand_out(w_index).start()

    one.rows = rows
    for_blocks(size, prompt_blocks, one, (lambda: gather.forward(2)) if carried else None, wide)
    if carried:
        gather.forward(3)
    own_ref[:, mine()] = o_ref[pl.ds(pl.multiple_of(wide * rows, rows), rows)]

    def finish(w, carry):
        @pl.when(w != wide)
        def _():
            hand_out(w).wait_send()
            remote(
                o_ref.at[pl.ds(0, rows)], own_ref.at[:, mine()], out_send.at[w], out_recv.at[w], (grp, w, narrow)
            ).wait_recv()

        return carry

    lax.fori_loop(0, size, finish, 0)
    if carried:
        gather.finish()


def attend_back_kernel(
    rows, prompt_blocks, paired, shared, carried, raw_ref, gains_ref, cos_ref, sin_ref, sums_ref,
    q_ref, k_ref, v_ref, ko_ref, vo_ref, grad_ref, o_ref, lse_ref, *refs
):
    carry_in, refs = refs[:carried], refs[carried:]
    joined_ref, gain_ref = refs[:2]
    carry_out, refs = refs[2 : 2 + carried], refs[2 + carried :]
    do_ref, dq_ref, dk_ref, dv_ref, dko_ref, dvo_ref, dkb_ref, dvb_ref, dkr_ref, dvr_ref, kt_ref, kto_ref = refs[:12]
    dots_ref, came_ref, sum_send, sum_recv, pair_send, pair_recv, in_send, in_recv = refs[12:20]
    gather = Gather(carry_in, carry_out, *refs[20:]) if carried else None
    half, columns = q_ref.shape
    size = half // rows
    heads = columns // HD
    grp, wide, narrow = (lax.axis_index(a) for a in ("grp", "wide", "narrow"))
    partner = (grp, wide, 1 - narrow)
    greet([((grp, lax.rem(wide + k, size), narrow), None) for k in range(1, size)] + [(partner, None)])
    my_rows = pl.ds(pl.multiple_of(wide * rows, rows), rows)

    def part_of(w):
        return pl.ds(pl.multiple_of(w * columns, columns), columns)

    def hand_in(w):
        return remote(
            grad_ref.at[:, part_of(w)], do_ref.at[my_rows], in_send.at[w], in_recv.at[wide], (grp, w, narrow)
        )

    def each_peer(act):
        def body(w, carry):
            pl.when(w != wide)(lambda: act(w))
            return carry

        lax.fori_loop(0, size, body, 0)

    each_peer(lambda w: hand_in(w).start())
    do_ref[my_rows, :] = grad_ref[:, part_of(wide)]
    for ref in (dk_ref, dv_ref, dko_ref, dvo_ref, dots_ref, gain_ref):
        ref[...] = jnp.zeros_like(ref)
    for h in range(heads):
        hs = slice(h * HD, (h + 1) * HD)
        kt_ref[hs, :] = k_ref[:, hs].T
        kto_ref[hs, :] = ko_ref[:, hs].T
    each_peer(
        lambda w: remote(
            grad_ref.at[:, part_of(w)], do_ref.at[my_rows], in_send.at[w], in_recv.at[w], (grp, w, narrow)
        ).wait_recv()
    )
    if carried:
        gather.start()

    def sweep(plane):
        keys, values = ((k_ref, v_ref), (ko_ref, vo_ref))[plane]
        dk, dv = ((dk_ref, dv_ref), (dko_ref, dvo_ref))[plane]
        flipped = (kt_ref, kto_ref)[plane]

        def one(w, w_index, start):
            block = pl.ds(start, rows)
            for h in range(heads):
                hs = slice(h * HD, (h + 1) * HD)
                query = q_ref[block, hs]
                grad = do_ref[block, hs]
                delta = row_sums(grad.astype(jnp.float32) * o_ref[block, hs].astype(jnp.float32))
                lse = lse_ref[h : h + 1, block]
                back = jnp.zeros((HD, rows), jnp.float32)
                for first, count, mask in key_parts(w, plane, rows, prompt_blocks, paired):
                    at = pl.ds(start if first is None else first, count)
                    score = lax.dot_general(keys[at, hs], query, NT, preferred_element_type=jnp.float32)
                    score = masked_scores(score * (HD**-0.5 * LOG2E), mask, narrow, rows)
                    weight = jnp.exp2(score - lse)
                    grad_weight = lax.dot_general(values[at, hs], grad, NT, preferred_element_type=jnp.float32)
                    grad_score = (weight * (grad_weight - delta)).astype(jnp.bfloat16)
                    dv[at, hs] += dot(weight.astype(jnp.bfloat16), grad)
                    dk[at, hs] += dot(grad_score, query) * HD**-0.5
                    back = back + dot(flipped[hs, at], grad_score)
                back = back.T * HD**-0.5
                dq_ref[block, hs] = back if plane == 1 else dq_ref[block, hs] + back

        one.rows = rows
        for_blocks(size, prompt_blocks, one, (lambda: gather.forward(2 - plane)) if carried else None)

    sweep(1)
    dkb_ref[...] = dko_ref[...].astype(jnp.bfloat16)
    dvb_ref[...] = dvo_ref[...].astype(jnp.bfloat16)
    pairs = [
        remote(src, dst, pair_send.at[i], pair_recv.at[i], partner)
        for i, (src, dst) in enumerate(((dkb_ref, dkr_ref), (dvb_ref, dvr_ref)))
    ]
    for copy in pairs:
        copy.start()
    sweep(0)

    def turn_back(i, ref):
        def body(b, carry):
            at = pl.ds(pl.multiple_of(b * rows, rows), rows)
            inverse = inverse_norms(sums_ref, at)[i]
            products = []
            for h in range(heads):
                hs = slice(h * HD, (h + 1) * HD)
                grad = turn(ref[at, hs], cos_ref[at], -sin_ref[at])
                ref[at, hs] = grad
                product = grad * raw_ref[at, i * columns + h * HD : i * columns + (h + 1) * HD]
                gain_ref[i : i + 1, hs] += jnp.sum(product * inverse, 0, keepdims=True)
                products.append(product * gains_ref[i : i + 1, hs])
            dots_ref[i : i + 1, at] = row_sums(sum(products[1:], products[0]))
            return carry

        lax.fori_loop(0, size, body, 0)

    turn_back(0, dq_ref)
    if carried:
        gather.forward(3)
    for copy in pairs:
        copy.wait()
    dk_ref[0:shared, :] += dkr_ref[...].astype(jnp.float32)
    turn_back(1, dk_ref)
    copies = peer_copies(size, dots_ref, came_ref, sum_send, sum_recv, grp, wide, narrow)
    for copy in copies:
        copy.start()
    joined_ref[0:shared, 2 * columns :] = (dv_ref[0:shared] + dvr_ref[...].astype(jnp.float32)).astype(jnp.bfloat16)
    if shared < half:
        joined_ref[shared:, 2 * columns :] = dv_ref[shared:].astype(jnp.bfloat16)
    for copy in copies:
        copy.wait()
    total = dots_ref[...]
    for k in range(size - 1):
        total = total + came_ref[k]
    dots_ref[...] = total

    def finish(b, carry):
        at = pl.ds(pl.multiple_of(b * rows, rows), rows)
        inverses = inverse_norms(sums_ref, at)
        products = dots_ref[:, at].T / D
        for i, ref in enumerate((dq_ref, dk_ref)):
            inverse = inverses[i]
            cubed = inverse * inverse * inverse * products[:, i : i + 1]
            for h in range(heads):
                hs = slice(h * HD, (h + 1) * HD)
                there = slice(i * columns + h * HD, i * columns + (h + 1) * HD)
                value = inverse * gains_ref[i : i + 1, hs] * ref[at, hs] - raw_ref[at, there] * cubed
                joined_ref[at, there] = value.astype(jnp.bfloat16)
        return carry

    lax.fori_loop(0, size, finish, 0)
    each_peer(lambda w: hand_in(w).wait_send())
    if carried:
        gather.finish()


def attention_calls(rows, half, shared, columns, prompt_blocks, paired, ids):
    heads = columns // HD
    size = half // rows
    bf16, f32 = jnp.bfloat16, jnp.float32
    shape = lambda dtype, *dims: jax.ShapeDtypeStruct(dims, dtype)
    sems = pltpu.SemaphoreType.DMA
    peers = [sems((size - 1,)), sems((size - 1,)), sems((2,)), sems((2,)), sems((size,)), sems((size,))]

    def params(k):
        return pltpu.CompilerParams(vmem_limit_bytes=60 * 2**20, collective_id=ids[k], has_side_effects=True)

    carried = 1 if size == 2 * LINE else 0
    forward = pl.pallas_call(
        functools.partial(attend_kernel, rows, prompt_blocks, paired, shared, 0),
        out_shape=[shape(bf16, half, columns)] * 3
        + [shape(bf16, shared, columns)] * 2
        + [shape(bf16, half, columns), shape(bf16, rows, size * columns), shape(f32, heads, half), shape(f32, 8, half)],
        in_specs=[VMEM] * 4,
        out_specs=[VMEM] * 9,
        scratch_shapes=[
            pltpu.VMEM((columns, half), bf16),
            pltpu.VMEM((columns, shared), bf16),
            pltpu.VMEM((size - 1, 8, half), f32),
        ]
        + peers,
        compiler_params=params(0),
        cost_estimate=pl.CostEstimate(flops=0, bytes_accessed=300_000_000, transcendentals=0),
    )

    backward_call = pl.pallas_call(
        functools.partial(attend_back_kernel, rows, prompt_blocks, paired, shared, carried),
        out_shape=[shape(bf16, half, 3 * columns), shape(f32, 8, columns)]
        + [shape(bf16, size, rows, D)] * carried,
        in_specs=[VMEM] * 13 + [ANY] * carried,
        out_specs=[VMEM] * 2 + [ANY] * carried,
        scratch_shapes=[pltpu.VMEM((half, columns), bf16)]
        + [pltpu.VMEM((half, columns), f32)] * 3
        + [pltpu.VMEM((shared, columns), f32)] * 2
        + [pltpu.VMEM((shared, columns), bf16)] * 4
        + [
            pltpu.VMEM((columns, half), bf16),
            pltpu.VMEM((columns, shared), bf16),
            pltpu.VMEM((8, half), f32),
            pltpu.VMEM((size - 1, 8, half), f32),
        ]
        + peers
        + gather_sems(carried) * carried,
        compiler_params=params(1),
        cost_estimate=pl.CostEstimate(flops=0, bytes_accessed=300_000_000, transcendentals=0),
    )
    def backward(*args):
        if carried:
            return backward_call(*args)
        return [*backward_call(*args[:-1]), lax.all_gather(args[-1], "wide", axis=0)]

    return forward, backward


def dot(a, b):
    return jnp.dot(a, b, preferred_element_type=jnp.float32)


def dot_nt(a, b):
    return lax.dot_general(a, b, NT, preferred_element_type=jnp.float32)


def dot_tn(a, b):
    return lax.dot_general(a, b, (((0,), (0,)), ((), ())), preferred_element_type=jnp.float32)


def start_kernel(count, swaps, spread, *refs):
    ins, given = refs[:count], refs[count : count + swaps]
    refs = refs[count + swaps :]
    outs, got, pieces = refs[:count], refs[count : count + swaps], refs[count + swaps : count + swaps + 3 * spread]
    refs = refs[count + swaps + 3 * spread :]
    send, recv, local, swap_send, swap_recv, twin_send, twin_recv = refs[:7]
    grp, wide, narrow, line, cross = position()
    partner = (grp, wide, 1 - narrow)
    twin = (1 - grp, wide, narrow)
    size = 2 * LINE

    def half(ref, which):
        size = ref.shape[0] // 2
        return ref.at[pl.ds(pl.multiple_of(which * size, size), size)]

    def swap(i):
        return remote(half(given[i], grp), half(got[i], grp), swap_send.at[i], swap_recv.at[i], partner)

    def share(i, which):
        return remote(half(got[i], which), half(got[i], which), twin_send.at[i], twin_recv.at[i], twin)

    def piece(k, slot):
        piece_send, piece_recv = refs[7:]
        src = pieces[0] if k == 2 else outs[-1]
        device = twin if k else partner
        return remote(src.at[slot], pieces[k].at[slot], piece_send.at[k, slot], piece_recv.at[k, slot], device)

    def own_piece(k):
        piece_send, piece_recv = refs[7:]
        device = twin if k else partner
        return remote(ins[-1], pieces[k].at[wide], piece_send.at[k, wide], piece_recv.at[k, wide], device)

    def arrived(i, slot):
        if i == count - 1:
            for k in range(2):
                if slot is None:
                    own_piece(k).start()
                else:
                    piece(k, slot).start()

    def begin():
        for i in range(swaps):
            swap(i).start()

    def finish():
        if spread:
            for slot in range(size):
                piece(0, slot).wait_recv()
                piece(2, slot).start()
        for i in range(swaps):
            swap(i).wait_recv()
            share(i, grp).start()
        for i in range(swaps):
            swap(i).wait_send()
            share(i, grp).wait_send()
            share(i, 1 - grp).wait_recv()
        if spread:
            for slot in range(size):
                piece(0, slot).wait_send()
                piece(1, slot).wait()
                piece(2, slot).wait()

    more = [(partner, None), (twin, None)]
    gather_body(count, ins, outs, send, recv, local, more, begin, finish, arrived if spread else None)


def start_exchange(arrays, weights, collective_id, spread=False):
    size = lax.axis_size("wide")
    swap = [(0, 1), (1, 0)]
    if size != 2 * LINE or lax.axis_size("grp") != 2:
        return [lax.all_gather(a, "wide", axis=0) for a in arrays], [lax.ppermute(w, "narrow", swap) for w in weights], []
    count, swaps, spread = len(arrays), len(weights), int(spread)
    gathered = [jax.ShapeDtypeStruct((size, *a.shape), a.dtype) for a in arrays]
    dma = pltpu.SemaphoreType.DMA
    out = pl.pallas_call(
        functools.partial(start_kernel, count, swaps, spread),
        out_shape=gathered + [jax.ShapeDtypeStruct(w.shape, w.dtype) for w in weights] + gathered[-1:] * 3 * spread,
        in_specs=[ANY] * (count + swaps),
        out_specs=[ANY] * (count + swaps + 3 * spread),
        scratch_shapes=gather_sems(count) + [dma((swaps,))] * 4 + [dma((3, size))] * 2 * spread,
        compiler_params=pltpu.CompilerParams(collective_id=collective_id, has_side_effects=True),
        cost_estimate=lasts(120),
    )(*arrays, *weights)
    return out[:count], out[count : count + swaps], out[count + swaps :]


def expert_grad_kernel(
    part_ref, *refs
):
    operands = refs[0:5]
    out_ref, gate_out, up_out, down_out = refs[5:9]
    held, from_across, from_line, x_buf, g_buf, inner_buf, gate_buf, up_buf, stage = refs[9:18]
    load, send, recv_a, recv_l, fetch, put = refs[18:]
    grp, wide, narrow, line, cross = position()
    across = (grp, line * 2 + 1 - cross, narrow)
    above = (grp, wide + 2, narrow)
    below = (grp, wide - 2, narrow)
    has_above, has_below = line < LINE - 1, line > 0
    f32, bf16 = jnp.float32, jnp.bfloat16
    greet([(across, None), (above, has_above), (below, has_below)])
    order = [(distance, sign) for distance in range(LINE - 1, 0, -1) for sign in (1, -1)]

    def valid(owner):
        return (owner >= 0) & (owner < LINE)

    def across_copy(owner):
        return remote(
            part_ref.at[owner * 2 + 1 - cross], from_across.at[owner], send.at[0, owner], recv_a.at[owner], across
        )

    def load_copy(owner):
        return pltpu.make_async_copy(part_ref.at[owner * 2 + cross], held.at[owner], load.at[owner])

    def line_copy(owner, up):
        slot = 0 if up else 1
        return remote(
            held.at[owner], from_line.at[slot, owner], send.at[1, owner], recv_l.at[slot, owner], above if up else below
        )

    for distance, sign in order + [(0, 1)]:
        owner = line + sign * distance

        @pl.when(valid(owner))
        def _(owner=owner):
            across_copy(owner).start()
            load_copy(owner).start()

    bufs = (x_buf, g_buf, inner_buf, gate_buf, up_buf)

    fetches = [pltpu.make_async_copy(src, dst, fetch.at[i]) for i, (src, dst) in enumerate(zip(operands, bufs))]
    for copy in fetches:
        copy.start()

    tiles = stage.shape[0]
    width = gate_buf.shape[1] // tiles

    def tile(n, size):
        return pl.ds(pl.multiple_of(n * size, size), size)

    def column_job(values, result):
        def put_copy(n):
            return pltpu.make_async_copy(stage.at[n], result.at[:, tile(n, width)], put.at[n])

        def run():
            @pl.loop(0, tiles)
            def _(n):
                stage[n] = dot_tn(x_buf[...], values[:, tile(n, width)]).astype(bf16)
                put_copy(n).start()

            @pl.loop(0, tiles)
            def _(n):
                put_copy(n).wait()

        return run

    def down_job(result):
        units = inner_buf.shape[1] // tiles

        def run():
            for n in range(tiles):
                at = slice(n * units, (n + 1) * units)
                product = dot_tn(inner_buf[:, at], g_buf[...]).astype(bf16)
                for c in range(product.shape[1] // width):
                    stage[n, c * units : (c + 1) * units, :] = product[:, c * width : (c + 1) * width]
            copies = [
                pltpu.make_async_copy(
                    stage.at[n, pl.ds(c * units, units)],
                    result.at[pl.ds(n * units, units), pl.ds(c * width, width)],
                    put.at[n * (g_buf.shape[1] // width) + c],
                )
                for n in range(tiles)
                for c in range(g_buf.shape[1] // width)
            ]
            for copy in copies:
                copy.start()
            for copy in copies:
                copy.wait()

        return run

    def first_job():
        for copy in fetches:
            copy.wait()
        column_job(gate_buf, gate_out)()

    jobs = [first_job, None, column_job(up_buf, up_out), None, down_job(down_out), None]
    for job, (distance, sign) in zip(jobs, order):
        if job is not None:
            job()
        owner = line + sign * distance

        @pl.when(valid(owner))
        def _(owner=owner, sign=sign):
            load_copy(owner).wait()
            across_copy(owner).wait_recv()
            up = sign > 0
            came = has_below if up else has_above
            total = held[owner].astype(f32) + from_across[owner].astype(f32)

            @pl.when(came)
            def _():
                line_copy(owner, up).wait_recv()
                held[owner] = (total + from_line[0 if up else 1, owner].astype(f32)).astype(held.dtype)

            @pl.when(jnp.logical_not(came))
            def _():
                held[owner] = total.astype(held.dtype)

            line_copy(owner, up).start()

    load_copy(line).wait()
    across_copy(line).wait_recv()
    out_ref[...] = held[line].astype(f32) + from_across[line].astype(f32)

    @pl.when(has_below)
    def _():
        line_copy(line, True).wait_recv()
        out_ref[...] += from_line[0, line].astype(f32)

    @pl.when(has_above)
    def _():
        line_copy(line, False).wait_recv()
        out_ref[...] += from_line[1, line].astype(f32)

    for owner in range(LINE):
        across_copy(owner).wait_send()

        @pl.when(owner > line)
        def _(owner=owner):
            line_copy(owner, True).wait_send()

        @pl.when(owner < line)
        def _(owner=owner):
            line_copy(owner, False).wait_send()


def plain_grads(x, g, inner, gate, up):
    return [dot_tn(a, b).astype(jnp.bfloat16) for a, b in ((x, gate), (x, up), (inner, g))]


def expert_grad(part, own, collective_id):
    size, rows, columns = part.shape
    f32, bf16 = jnp.float32, jnp.bfloat16
    if size != 2 * LINE:
        return lax.psum_scatter(part, "wide", scatter_dimension=0, tiled=False).astype(f32), *plain_grads(*own)
    count, units = own[2].shape
    tiles = 4
    block = (LINE, rows, columns)
    gate = jax.ShapeDtypeStruct((D, units), bf16)
    down = jax.ShapeDtypeStruct((units, D), bf16)
    dma = pltpu.SemaphoreType.DMA
    return pl.pallas_call(
        expert_grad_kernel,
        out_shape=[jax.ShapeDtypeStruct((rows, columns), f32), gate, gate, down],
        in_specs=[ANY] * 6,
        out_specs=[VMEM] + [ANY] * 3,
        scratch_shapes=[
            pltpu.VMEM(block, bf16),
            pltpu.VMEM(block, bf16),
            pltpu.VMEM((2, *block), bf16),
            pltpu.VMEM((count, D), bf16),
            pltpu.VMEM((count, D), bf16),
            pltpu.VMEM((count, units), bf16),
            pltpu.VMEM((count, units), bf16),
            pltpu.VMEM((count, units), bf16),
            pltpu.VMEM((tiles, D, units // tiles), bf16),
            dma((LINE,)),
            dma((2, LINE)),
            dma((LINE,)),
            dma((2, LINE)),
            dma((5,)),
            dma((tiles * D // (units // tiles),)),
        ],
        compiler_params=pltpu.CompilerParams(
            collective_id=collective_id, has_side_effects=True, vmem_limit_bytes=60 * 2**20
        ),
        cost_estimate=lasts(1),
    )(part, *own)


class SmallSum:
    def __init__(self, x_ref, o_ref, parts, total, send, recv, send_back, recv_back):
        self.refs = x_ref, o_ref, parts, total, send, recv, send_back, recv_back
        grp, wide, narrow, _, _ = position()
        self.size, _, self.width = parts.shape
        self.me = wide * 2 + narrow
        self.ranks = [lax.rem(self.me + k, self.size) for k in range(self.size)]
        self.devices = [(grp, rank // 2, lax.rem(rank, 2)) for rank in self.ranks]
        self.targets = [(device, None) for device in self.devices[1:]]

    def columns(self, rank):
        return pl.ds(pl.multiple_of(rank * self.width, self.width), self.width)

    def run(self):
        x_ref, o_ref, parts, total, send, recv, send_back, recv_back = self.refs
        devices, size, mine = self.devices, self.size, self.columns(self.me)
        out = [
            remote(x_ref.at[:, self.columns(self.ranks[k])], parts.at[k], send.at[k], recv.at[k], devices[k])
            for k in range(1, size)
        ]
        for copy in out:
            copy.start()
        total[...] = x_ref[:, mine]
        for k, copy in enumerate(out):
            copy.wait()
            total[...] += parts[k + 1]
        back = [
            remote(total, o_ref.at[:, mine], send_back.at[k], recv_back.at[k], devices[k]) for k in range(1, size)
        ]
        for copy in back:
            copy.start()
        o_ref[:, mine] = total[...]
        for copy in back:
            copy.wait_send()
        for k in range(1, size):
            rank = lax.rem(self.me - k + size, size)
            remote(total, o_ref.at[:, self.columns(rank)], send_back.at[k], recv_back.at[k], devices[k]).wait_recv()


def input_grad_kernel(
    gain_row, joined_ref, weights_ref, tokens_ref, hidden_ref, gain_ref, small_ref, out_ref, sums_ref,
    held, from_across, from_line, x_ref, parts, total_ref, send, recv_a, recv_l, *small_sems
):
    rows = tokens_ref.shape[0]
    f32 = jnp.float32
    small = SmallSum(x_ref, sums_ref, parts, total_ref, *small_sems)
    grp, wide, narrow, line, cross = position()
    across = (grp, line * 2 + 1 - cross, narrow)
    above = (grp, wide + 2, narrow)
    below = (grp, wide - 2, narrow)
    has_above, has_below = line < LINE - 1, line > 0
    greet(small.targets)
    order = [(distance, sign) for distance in range(LINE - 1, 0, -1) for sign in (1, -1)] + [(0, 1)]

    def valid(owner):
        return (owner >= 0) & (owner < LINE)

    def part(owner, column):
        at = pl.ds(pl.multiple_of((owner * 2 + column) * rows, rows), rows)
        return dot_nt(joined_ref[at], weights_ref[...])

    def across_copy(owner):
        return remote(held.at[0, owner], from_across.at[owner], send.at[0, owner], recv_a.at[owner], across)

    def line_copy(owner, up):
        slot = 0 if up else 1
        return remote(
            held.at[1, owner], from_line.at[slot, owner], send.at[1, owner], recv_l.at[slot, owner], above if up else below
        )

    for distance, sign in order:
        owner = line + sign * distance

        @pl.when(valid(owner))
        def _(owner=owner):
            held[0, owner] = part(owner, 1 - cross).astype(held.dtype)
            across_copy(owner).start()

    for distance, sign in order[:-1]:
        owner = line + sign * distance

        @pl.when(valid(owner))
        def _(owner=owner, sign=sign):
            up = sign > 0
            came = has_below if up else has_above
            total = part(owner, cross)
            across_copy(owner).wait_recv()
            total = total + from_across[owner].astype(f32)

            @pl.when(came)
            def _():
                line_copy(owner, up).wait_recv()
                held[1, owner] = (total + from_line[0 if up else 1, owner].astype(f32)).astype(held.dtype)

            @pl.when(jnp.logical_not(came))
            def _():
                held[1, owner] = total.astype(held.dtype)

            line_copy(owner, up).start()

    out_ref[...] = part(line, cross)
    across_copy(line).wait_recv()
    out_ref[...] += from_across[line].astype(f32)

    @pl.when(has_below)
    def _():
        line_copy(line, True).wait_recv()
        out_ref[...] += from_line[0, line].astype(f32)

    @pl.when(has_above)
    def _():
        line_copy(line, False).wait_recv()
        out_ref[...] += from_line[1, line].astype(f32)

    x_ref[...] = small_ref[...]
    x_ref[gain_row : gain_row + 1, :] = jnp.zeros((1, D), f32)
    chunk = min(rows, 64)

    def finish(i, carry):
        at = pl.ds(pl.multiple_of(i * chunk, chunk), chunk)
        grad = out_ref[at]
        stream = tokens_ref[at].astype(f32)
        inverse = lax.rsqrt(jnp.mean(stream * stream, -1, keepdims=True) + EPSILON)
        product = grad * stream
        x_ref[gain_row : gain_row + 1, :] += jnp.sum(product * inverse, 0, keepdims=True)
        slope = inverse * inverse * inverse * jnp.sum(product * gain_ref[...], -1, keepdims=True) / D
        out_ref[at] = hidden_ref[at] + inverse * gain_ref[...] * grad - stream * slope
        return carry

    lax.fori_loop(0, rows // chunk, finish, 0)
    small.run()

    for owner in range(LINE):
        across_copy(owner).wait_send()

        @pl.when(owner > line)
        def _(owner=owner):
            line_copy(owner, True).wait_send()

        @pl.when(owner < line)
        def _(owner=owner):
            line_copy(owner, False).wait_send()


def input_grad(joined, weights, tokens, grad_hidden, gain, small, gain_row, ids):
    size = lax.axis_size("wide")
    rows = tokens.shape[0]
    f32, bf16 = jnp.float32, jnp.bfloat16
    if size != 2 * LINE:
        part = dot_nt(joined, weights).astype(bf16).reshape(size, rows, D)
        grad = lax.psum_scatter(part, "wide", scatter_dimension=0, tiled=False).astype(f32)
        stream = tokens.astype(f32)
        inverse = lax.rsqrt(jnp.mean(stream * stream, -1, keepdims=True) + EPSILON)
        small = small.at[gain_row].set(jnp.sum(grad * stream * inverse, 0))
        slope = inverse**3 * jnp.sum(grad * gain * stream, -1, keepdims=True) / D
        return grad_hidden + inverse * gain * grad - stream * slope, lax.psum(small, ("wide", "narrow"))
    devices = 4 * LINE
    block = (LINE, rows, D)
    dma = pltpu.SemaphoreType.DMA
    return pl.pallas_call(
        functools.partial(input_grad_kernel, gain_row),
        out_shape=[jax.ShapeDtypeStruct((rows, D), f32), jax.ShapeDtypeStruct(small.shape, f32)],
        in_specs=[VMEM] * 6,
        out_specs=[VMEM] * 2,
        scratch_shapes=[
            pltpu.VMEM((2, *block), bf16),
            pltpu.VMEM(block, bf16),
            pltpu.VMEM((2, *block), bf16),
            pltpu.VMEM(small.shape, f32),
            pltpu.VMEM((devices, small.shape[0], D // devices), f32),
            pltpu.VMEM((small.shape[0], D // devices), f32),
            dma((2, LINE)),
            dma((LINE,)),
            dma((2, LINE)),
        ]
        + [dma((devices,))] * 4,
        compiler_params=pltpu.CompilerParams(
            collective_id=ids, has_side_effects=True, vmem_limit_bytes=56 * 2**20
        ),
        cost_estimate=lasts(100),
    )(joined, weights, tokens, grad_hidden, gain, small)


def pick_rows(step, capacity, slot_ref, source_refs, picks, held, out_ref):
    row = lax.broadcasted_iota(jnp.int32, (capacity, slot_ref.shape[2]), 0)
    pick = jnp.where(row == slot_ref[0], 1.0, 0.0).astype(jnp.bfloat16)
    picks[step] = pick
    part = pick.shape[1] // len(source_refs)
    values = sum(dot(pick[:, k * part : (k + 1) * part], ref[0]) for k, ref in enumerate(source_refs))
    values = values.astype(jnp.bfloat16)
    held[pl.ds(pl.multiple_of(step * capacity, capacity), capacity)] = values
    out_ref[...] = values


def spread_rows(block, capacity, picks, total, before_ref, out_ref):
    here = pl.ds(pl.multiple_of(block * capacity, capacity), capacity)
    values = dot_tn(picks[block], total[here].astype(jnp.bfloat16))
    if before_ref is not None:
        values = values + before_ref[0].astype(jnp.float32)
    out_ref[0] = values.astype(jnp.bfloat16)


def expert_forward_kernel(
    tiles, capacity, experts, first, id_ref, slot_ref, tokens_ref, router_ref, gate_ref, up_ref, down_ref, *refs
):
    before_ref = None if first else refs[0]
    moe_ref, x_ref, inner_ref, gate_pre_ref, up_pre_ref, probs_ref, x_all, picks, moe_all = refs[0 if first else 1 :]
    step = pl.program_id(1)
    blocks = picks.shape[0]
    lane = lax.broadcasted_iota(jnp.int32, (1, 128), 1)

    @pl.when(step < blocks)
    def _():
        pick_rows(step, capacity, slot_ref, [tokens_ref], picks, x_all, x_ref)

    @pl.when(step == blocks)
    def _():
        logits = jnp.where(lane < experts, dot(x_all[...], router_ref[...]), NEGATIVE)
        weight = jnp.exp(logits - jnp.max(logits, -1, keepdims=True))
        probs_ref[...] = weight / jnp.sum(weight, -1, keepdims=True)
        moe_all[...] = jnp.zeros_like(moe_all)

    @pl.when((step >= blocks) & (step < blocks + tiles))
    def _():
        x = x_all[...]
        gate = jnp.sum(jnp.where(lane == id_ref[0], probs_ref[...], 0.0), -1, keepdims=True)
        gate_pre = dot(x, gate_ref[...])
        up_pre = dot(x, up_ref[...])
        gate_pre_ref[...] = gate_pre
        up_pre_ref[...] = up_pre
        inner_gated = (gate * (gate_pre / (1.0 + jnp.exp(-gate_pre))) * up_pre).astype(jnp.bfloat16)
        inner_ref[...] = inner_gated
        moe_all[...] += dot(inner_gated, down_ref[...])

    @pl.when(step >= blocks + tiles)
    def _():
        spread_rows(step - blocks - tiles, capacity, picks, moe_all, before_ref, moe_ref)


def expert_backward_kernel(
    tiles, capacity, first, id_ref, slot_ref, low_ref, high_ref, x_ref, probs_ref, gate_pre_ref, up_pre_ref,
    router_ref, gate_ref, up_ref, down_ref, *refs
):
    before_ref, router_in_ref = (None, None) if first else refs[:2]
    (
        part_ref, g_ref, grad_gate_ref, grad_up_ref, router_grad_ref,
        g_all, picks, part_all, scores_all, router_sum,
    ) = refs[0 if first else 2 :]
    bf16 = jnp.bfloat16
    group, step = pl.program_id(0), pl.program_id(1)
    blocks = picks.shape[0]
    lane = lax.broadcasted_iota(jnp.int32, (1, 128), 1)
    here = jnp.where(lane == id_ref[0], 1.0, 0.0)

    @pl.when(step < blocks)
    def _():
        pick_rows(step, capacity, slot_ref, [low_ref, high_ref], picks, g_all, g_ref)

    @pl.when(step == blocks)
    def _():
        part_all[...] = jnp.zeros_like(part_all)
        scores_all[...] = jnp.zeros_like(scores_all)

    @pl.when((step >= blocks) & (step < blocks + tiles))
    def _():
        gate = jnp.sum(probs_ref[...] * here, -1, keepdims=True)
        gate_pre, up_pre = gate_pre_ref[...], up_pre_ref[...]
        back = dot_nt(g_all[...], down_ref[...])
        sigmoid = 1.0 / (1.0 + jnp.exp(-gate_pre))
        silu = gate_pre * sigmoid
        scores_all[...] += jnp.sum(silu * up_pre * back, -1, keepdims=True)
        back = gate * back
        grad_gate_pre = (back * up_pre * sigmoid * (1.0 + gate_pre * (1.0 - sigmoid))).astype(bf16)
        grad_up_pre = (back * silu).astype(bf16)
        grad_gate_ref[...] = grad_gate_pre
        grad_up_ref[...] = grad_up_pre
        part_all[...] += dot_nt(grad_gate_pre, gate_ref[...]) + dot_nt(grad_up_pre, up_ref[...])

    @pl.when(step == blocks + tiles)
    def _():
        probs = probs_ref[...]
        gate = jnp.sum(probs * here, -1, keepdims=True)
        mixing = (gate * scores_all[...] * (here - probs)).astype(bf16)
        part_all[...] += dot_nt(mixing, router_ref[...])
        grad = dot_tn(mixing, x_ref[...])

        @pl.when(group == 0)
        def _():
            router_sum[...] = grad if first else grad + router_in_ref[...]

        @pl.when(group > 0)
        def _():
            router_sum[...] += grad

        router_grad_ref[...] = router_sum[...]

    @pl.when(step >= blocks + tiles)
    def _():
        spread_rows(step - blocks - tiles, capacity, picks, part_all, before_ref, part_ref)


class Expert:
    def __init__(self, expert, slots, router, weights, capacity, experts):
        self.scalars = expert.astype(jnp.int32).reshape(1), slots
        self.router, self.weights, self.capacity, self.experts = router, weights, capacity, experts
        wide, _, rows = slots.shape
        units = weights[0].shape[1]
        groups = 2 if wide * capacity > 1024 else 1
        blocks, tile = wide // groups, 256
        tiles = units // tile
        last = blocks + tiles
        self.tiles, self.grid = tiles, (groups, last + blocks)
        self.held, self.blocks, self.rows = blocks * capacity, blocks, rows
        count = wide * capacity

        def picked(g, i):
            return g * blocks + jnp.minimum(i, blocks - 1)

        def tiled(i):
            return jnp.clip(i - blocks, 0, tiles - 1)

        self.whole = pl.BlockSpec((1, rows, D), lambda g, i: (picked(g, i), 0, 0))
        self.part = pl.BlockSpec((1, rows // 2, D), lambda g, i: (picked(g, i), 0, 0))
        self.back = pl.BlockSpec((1, rows, D), lambda g, i: (g * blocks + jnp.clip(i - last, 0, blocks - 1), 0, 0))
        self.row = pl.BlockSpec((capacity, D), lambda g, i: (picked(g, i), 0))
        column = pl.BlockSpec((D, tile), lambda g, i: (0, tiled(i)))
        self.unit = pl.BlockSpec((self.held, tile), lambda g, i: (g, tiled(i)))
        self.fixed = pl.BlockSpec((128, D), lambda g, i: (0, 0))
        self.rows_all = pl.BlockSpec((self.held, D), lambda g, i: (g, 0))
        self.probs = pl.BlockSpec((self.held, 128), lambda g, i: (g, 0))
        self.heads = [
            pl.BlockSpec(memory_space=pltpu.SMEM), pl.BlockSpec((1, 1, rows), lambda g, i: (picked(g, i), 0, 0))
        ]
        self.weight_specs = [
            pl.BlockSpec((D, 128), lambda g, i: (0, 0)), column, column,
            pl.BlockSpec((tile, D), lambda g, i: (tiled(i), 0)),
        ]
        shape = jax.ShapeDtypeStruct
        self.blocks_shape = shape((wide, rows, D), jnp.bfloat16)
        self.compact = shape((count, D), jnp.bfloat16)
        self.narrow = shape((count, units), jnp.bfloat16)
        self.narrow32 = shape((count, units), jnp.float32)
        self.probs_shape = shape((count, 128), jnp.float32)
        self.common = dict(
            grid=self.grid,
            compiler_params=pltpu.CompilerParams(vmem_limit_bytes=60 * 2**20),
            cost_estimate=pl.CostEstimate(flops=0, bytes_accessed=120_000_000, transcendentals=0),
        )

    def forward(self, tokens, before):
        first = before is None
        f32, bf16 = jnp.float32, jnp.bfloat16
        return pl.pallas_call(
            functools.partial(expert_forward_kernel, self.tiles, self.capacity, self.experts, first),
            in_specs=self.heads + [self.whole] + self.weight_specs + ([] if first else [self.back]),
            out_specs=[self.back, self.row, self.unit, self.unit, self.unit, self.probs],
            out_shape=[
                self.blocks_shape, self.compact, self.narrow, self.narrow32, self.narrow32, self.probs_shape
            ],
            scratch_shapes=[
                pltpu.VMEM((self.held, D), bf16),
                pltpu.VMEM((self.blocks, self.capacity, self.rows), bf16),
                pltpu.VMEM((self.held, D), f32),
            ],
            **self.common,
        )(*self.scalars, tokens, self.router, *self.weights, *(() if first else (before,)))

    def backward(self, grads, kept, before):
        first = before is None
        f32, bf16 = jnp.float32, jnp.bfloat16
        _, x, _, gate_pre, up_pre, probs = kept
        return pl.pallas_call(
            functools.partial(expert_backward_kernel, self.tiles, self.capacity, first),
            in_specs=self.heads
            + [self.part, self.part, self.rows_all, self.probs, self.unit, self.unit]
            + self.weight_specs
            + ([] if first else [self.back, self.fixed]),
            out_specs=[self.back, self.row, self.unit, self.unit, self.fixed],
            out_shape=[
                self.blocks_shape, self.compact, self.narrow, self.narrow, jax.ShapeDtypeStruct((128, D), f32)
            ],
            scratch_shapes=[
                pltpu.VMEM((self.held, D), bf16),
                pltpu.VMEM((self.blocks, self.capacity, self.rows), bf16),
                pltpu.VMEM((self.held, D), f32),
                pltpu.VMEM((self.held, 1), f32),
                pltpu.VMEM((128, D), f32),
            ],
            **self.common,
        )(*self.scalars, *grads, x, probs, gate_pre, up_pre, self.router, *self.weights, *(before or ()))


def positions(token_ids):
    local = token_ids % (PROMPT + NCONT * CONT)
    return jnp.where(local < PROMPT, local, PROMPT + (local - PROMPT) % CONT)


def rotation(place):
    frequency = THETA ** (-2.0 * jnp.arange(HD // 2, dtype=jnp.float32) / HD)
    angle = place.astype(jnp.float32)[:, None] * frequency[None, :]
    cosine, sine = jnp.cos(angle), jnp.sin(angle)
    return jnp.concatenate([cosine, cosine], 1), jnp.concatenate([-sine, sine], 1)


def shards(
    tokens,
    cotangent,
    valid,
    routes,
    w_query,
    w_key,
    w_value,
    w_out,
    norm_attn,
    norm_query,
    norm_key,
    norm_moe,
    w_router,
    w_gate,
    w_up,
    w_down,
):
    bf16, f32 = jnp.bfloat16, jnp.float32
    wide_count = lax.axis_size("wide")
    narrow_count = lax.axis_size("narrow")
    rows = tokens.shape[0]
    half = rows * wide_count
    columns = w_query.shape[1]
    experts = w_router.shape[1]
    hidden_units = w_gate.shape[2]
    capacity = min(max(rows * TOP * 5 // (4 * experts), 2), rows)
    assert narrow_count == 2 and CONT in (rows, 2 * rows)
    paired = CONT == 2 * rows
    side = lax.axis_index("narrow")
    place = lax.axis_index("wide")
    group = lax.axis_index("grp")
    swap = [(0, 1), (1, 0)]
    twins = lax.axis_size("grp") == 2
    prompt_blocks = PROMPT // (rows * narrow_count)
    shared = half if paired else prompt_blocks * rows
    attend, attend_back = attention_calls(rows, half, shared, columns, prompt_blocks, paired, (1, 2))
    barrier = lax.optimization_barrier

    def exchange(value):
        return lax.ppermute(value, "narrow", swap)

    stream = tokens.astype(f32)
    inv_one = lax.rsqrt(jnp.mean(stream * stream, -1, keepdims=True) + EPSILON)
    gain_one = norm_attn.astype(f32)
    normed = (stream * inv_one * gain_one).astype(bf16)
    mask = valid.astype(f32)[:, None]
    grad_final = cotangent.astype(f32) * mask
    pieces = 2 * narrow_count if twins else 1
    piece_width = D // pieces
    piece_id = group * narrow_count + side if twins else 0
    piece = lax.dynamic_slice_in_dim(w_out, piece_id * piece_width, piece_width, 1)
    (routes_plane, normed_plane, out_piece), (other_up,), others = start_exchange(
        [routes.T, normed, piece], [w_up[0]], 0, twins
    )
    normed_plane = normed_plane.reshape(half, D)
    out_pieces = [p.reshape(D, piece_width) for p in (out_piece, *others)]

    def ordered(parts):
        if not twins:
            return parts
        parts = [jnp.where(side == 0, parts[k], parts[k ^ 1]) for k in range(4)]
        return [jnp.where(group == 0, parts[k], parts[k ^ 2]) for k in range(4)]

    def unordered(whole):
        return ordered([whole[:, k * piece_width : (k + 1) * piece_width] for k in range(pieces)])

    grad_final_b = grad_final.astype(bf16)
    low, _ = barrier((grad_final_b[: rows // 2], normed_plane))
    grads_low = lax.all_gather(low, "wide", axis=0, tiled=True).reshape(wide_count, rows // 2, D)
    joined = jnp.concatenate([w_query, w_key, w_value], 1)
    raw = dot(normed_plane, joined)
    gains = jnp.pad(jnp.stack([norm_query, norm_key]).astype(f32), ((0, 6), (0, 0)))
    plane_ids = (
        (jnp.arange(wide_count, dtype=jnp.int32)[:, None] * narrow_count + side) * rows
        + jnp.arange(rows, dtype=jnp.int32)[None, :]
    ).reshape(half)
    cosine, sine = rotation(positions(plane_ids))
    kept = attend(raw, gains, cosine, sine)
    attended, attended_own, lse, sums = kept[5:]

    branch = jnp.concatenate(ordered([dot(attended_own, p) for p in out_pieces]), 1)
    hidden = stream + branch
    inv_two = lax.rsqrt(jnp.mean(hidden * hidden, -1, keepdims=True) + EPSILON)
    gain_two = norm_moe.astype(f32)
    moe_in = (hidden * inv_two * gain_two).astype(bf16)
    (tokens_in,), (other_gate, other_down), _ = start_exchange([moe_in], [w_gate[0], w_down[0]], 6)

    high, tokens_in, grads_low = barrier((grad_final_b[rows // 2 :], tokens_in, grads_low))
    grads_high = lax.all_gather(high, "wide", axis=0, tiled=True).reshape(wide_count, rows // 2, D)

    earlier = (jnp.arange(rows)[:, None] < jnp.arange(rows)[None, :]).astype(bf16)

    def slots_of(expert):
        chosen = jnp.any(routes_plane == expert, 1)
        rank = dot(chosen.astype(bf16), earlier).astype(jnp.int32)
        return jnp.where(chosen, rank, -1).reshape(wide_count, 1, rows)

    router = jnp.pad(w_router, ((0, 0), (0, 128 - experts)))

    own, other = (
        Expert(e, slots_of(e), router, w, capacity, experts)
        for e, w in (
            (place * narrow_count + side, (w_gate[0], w_up[0], w_down[0])),
            (place * narrow_count + 1 - side, (other_gate, other_up, other_down)),
        )
    )
    kept_own = own.forward(tokens_in, None)
    kept_other = other.forward(tokens_in, kept_own[0])
    moe_part = kept_other[0]
    moe = lax.psum_scatter(moe_part.reshape(half, D), "wide", scatter_dimension=0, tiled=True).astype(f32)
    kept_other, grads_high, _ = barrier((kept_other, grads_high, moe_part))
    grads_in = (grads_low, grads_high)
    back_other = other.backward(grads_in, kept_other, None)
    partner_grads = plain_grads(kept_other[1], back_other[1], kept_other[2], back_other[2], back_other[3])
    came = [exchange(g) for g in partner_grads[:2]]
    before, partner_grads = barrier(((back_other[0], back_other[4]), partner_grads))
    back_own = own.backward(grads_in, kept_own, before)
    grad_part, grad_router = back_own[0], back_own[4][:experts]
    own_operands = (kept_own[1], back_own[1], kept_own[2], back_own[2], back_own[3])
    grad_moe_in, *own_grads = expert_grad(grad_part, own_operands, 5)
    grad_moe_in, moe, came[0], down_grad = barrier((grad_moe_in, moe, came[0], partner_grads[2]))
    came.append(exchange(down_grad))

    grad_gain_two = jnp.sum(grad_moe_in * hidden * inv_two, 0)
    grad_hidden = (
        grad_final
        + inv_two * gain_two * grad_moe_in
        - hidden * inv_two**3 * jnp.sum(grad_moe_in * gain_two * hidden, -1, keepdims=True) / D
    )
    grad_branch = grad_hidden.astype(bf16)
    grad_attended_own = sum(dot_nt(g, p) for g, p in zip(unordered(grad_branch), out_pieces)).astype(bf16)
    grads_joined, gain_grads, branch_plane = attend_back(
        raw, gains, cosine, sine, sums, *kept[:5], grad_attended_own, attended, lse, grad_branch
    )
    grads_joined, came[1], came[2] = barrier((grads_joined, came[1], came[2]))
    grad_out = barrier(dot_tn(attended, branch_plane.reshape(half, D)).astype(bf16))
    grad_weights = barrier(dot_tn(normed_plane, grads_joined).astype(bf16))
    weights_came = exchange(grad_weights)
    out_came = exchange(grad_out)
    stats = jnp.stack([jnp.sum(v * v * mask) for v in (stream, branch, hidden, moe, hidden + moe)] + [jnp.sum(mask)])
    here = jnp.repeat(jnp.arange(wide_count) == place, columns)
    spots = [jnp.where(here, jnp.tile(g, wide_count), 0.0) for g in gain_grads[:2]]
    zeros = jnp.zeros((D,), f32)
    small = jnp.stack([zeros, grad_gain_two, *spots, jnp.pad(stats, (0, D - stats.shape[0]))])
    small = jnp.concatenate([grad_router, small, jnp.zeros((-(experts + 5) % 8, D), f32)], 0)
    small, _, _ = barrier((small, grad_weights, grad_out))
    grad_input, small = input_grad(
        grads_joined, joined, tokens, grad_hidden, gain_one.reshape(1, D), small, experts, 3
    )
    grad_weights = grad_weights.astype(f32) + weights_came.astype(f32)
    grad_out = grad_out.astype(f32) + out_came.astype(f32)
    grad_query_w, grad_key_w, grad_value_w = (
        grad_weights[:, i * columns : (i + 1) * columns] for i in range(3)
    )
    final = hidden + moe
    output = final.astype(bf16)
    grad_gate_w, grad_up_w, grad_down_w = (
        (own.astype(f32) + other.astype(f32))[None] for own, other in zip(own_grads, came)
    )

    spots = lax.dynamic_slice_in_dim(small[experts + 2 : experts + 4], place * columns, columns, 1)
    stats = small[experts + 4, :6]
    rms = jnp.sqrt(stats[:5] / (jnp.maximum(stats[5], 1.0) * D))
    return (
        output,
        grad_input,
        grad_query_w,
        grad_key_w,
        grad_value_w,
        grad_out,
        small[experts],
        spots[0],
        spots[1],
        small[experts + 1],
        small[:experts].T,
        grad_gate_w,
        grad_up_w,
        grad_down_w,
        rms,
    )


def solution(mesh):
    return jax.shard_map(
        shards,
        mesh=mesh,
        in_specs=(
            P(("grp", "wide", "narrow"), None),
            P(("grp", "wide", "narrow"), None),
            P(("grp", "wide", "narrow")),
            P(("grp", "wide", "narrow"), None),
            P(None, "wide"),
            P(None, "wide"),
            P(None, "wide"),
            P("wide", None),
            P(),
            P("wide"),
            P("wide"),
            P(),
            P(),
            P(("wide", "narrow"), None, None),
            P(("wide", "narrow"), None, None),
            P(("wide", "narrow"), None, None),
        ),
        out_specs=(
            P(("grp", "wide", "narrow"), None),
            P(("grp", "wide", "narrow"), None),
            P("grp", "wide"),
            P("grp", "wide"),
            P("grp", "wide"),
            P(("grp", "wide"), None),
            P("grp"),
            P(("grp", "wide")),
            P(("grp", "wide")),
            P("grp"),
            P("grp", None),
            P(("grp", "wide", "narrow"), None, None),
            P(("grp", "wide", "narrow"), None, None),
            P(("grp", "wide", "narrow"), None, None),
            P("grp"),
        ),
        check_vma=False,
    )
```

```python
import functools

import jax
import jax.numpy as jnp
from jax import lax
from jax.experimental import pallas as pl
from jax.experimental.pallas import tpu as pltpu
from jax.sharding import PartitionSpec as P

D = 2048
HD = 128
TOP = 8
PROMPT = 2048
CONT = 256
NCONT = 8

EPSILON = 1e-05
THETA = 10000.0
NEGATIVE = -1e30


MESH_ID = pl.DeviceIdType.MESH
ANY = pl.BlockSpec(memory_space=pl.ANY)
VMEM = pl.BlockSpec(memory_space=pltpu.VMEM)
LINE = 4


def lasts(microseconds):
    return pl.CostEstimate(flops=0, bytes_accessed=microseconds * 3_000_000, transcendentals=0)


def position():
    grp, wide, narrow = (lax.axis_index(a) for a in ("grp", "wide", "narrow"))
    return grp, wide, narrow, wide // 2, lax.rem(wide, 2)


def greet(targets):
    barrier = pltpu.get_barrier_semaphore()
    for device, when in targets:
        def signal(device=device):
            pl.semaphore_signal(barrier, inc=1, device_id=device, device_id_type=MESH_ID)

        if when is None:
            signal()
        else:
            pl.when(when)(signal)
    peers = sum(1 if when is None else when.astype(jnp.int32) for _, when in targets)
    pl.semaphore_wait(barrier, peers)


def remote(src, dst, send, recv, device):
    return pltpu.make_async_remote_copy(
        src_ref=src, dst_ref=dst, send_sem=send, recv_sem=recv, device_id=device, device_id_type=MESH_ID
    )


def gather_kernel(count, *refs):
    ins, outs = refs[:count], refs[count : 2 * count]
    gather_body(count, ins, outs, *refs[2 * count :])


class Gather:
    def __init__(self, ins, outs, send, recv, local):
        self.ins, self.outs, self.send, self.recv, self.local = ins, outs, send, recv, local
        grp, wide, narrow, self.line, self.cross = position()
        self.wide = wide
        self.across = (grp, self.line * 2 + 1 - self.cross, narrow)
        self.above = (grp, wide + 2, narrow)
        self.below = (grp, wide - 2, narrow)
        self.has_above, self.has_below = self.line < LINE - 1, self.line > 0
        self.targets = [(self.across, None), (self.above, self.has_above), (self.below, self.has_below)]
        self.arrived = lambda i, slot: None

    def copy(self, i, source_line, way, device):
        slot = source_line * 2 + self.cross
        out = self.outs[i].at[slot]
        return remote(out, out, self.send.at[i, way, source_line], self.recv.at[i, slot], device)

    def own(self, i, way, device):
        return remote(
            self.ins[i], self.outs[i].at[self.wide], self.send.at[i, way, self.line], self.recv.at[i, self.wide], device
        )

    def mine(self, i):
        return pltpu.make_async_copy(self.ins[i], self.outs[i].at[self.wide], self.local.at[i])

    def start(self):
        for i in range(len(self.ins)):
            pl.when(self.has_above)(self.own(i, 1, self.above).start)
            pl.when(self.has_below)(self.own(i, 2, self.below).start)
            self.own(i, 0, self.across).start()
            self.mine(i).start()
            self.arrived(i, None)

    def forward(self, distance, only=None):
        for i in range(len(self.ins)) if only is None else (only,):
            for sign in (-1, 1):
                source = self.line + sign * distance

                @pl.when((source >= 0) & (source < LINE))
                def _(i=i, source=source, sign=sign):
                    self.copy(i, source, 0, self.across).wait_recv()
                    onward = self.above if sign < 0 else self.below

                    @pl.when(self.has_above if sign < 0 else self.has_below)
                    def _():
                        self.copy(i, source, 1 if sign < 0 else 2, onward).start()

                    self.copy(i, source, 0, self.across).start()
                    self.arrived(i, source * 2 + self.cross)

    def finish(self):
        for i in range(len(self.ins)):
            send, recv, src, out = self.send, self.recv, self.ins[i], self.outs[i]
            for source in range(LINE):
                other = source * 2 + 1 - self.cross
                remote(src, out.at[other], send.at[i, 0, 0], recv.at[i, other], self.across).wait_recv()
                self.arrived(i, other)
            for source in range(LINE):
                remote(src, out.at[0], send.at[i, 0, source], recv.at[i, 0], self.across).wait_send()

                @pl.when(self.has_above & (source <= self.line))
                def _(source=source):
                    remote(src, out.at[0], send.at[i, 1, source], recv.at[i, 0], self.above).wait_send()

                @pl.when(self.has_below & (source >= self.line))
                def _(source=source):
                    remote(src, out.at[0], send.at[i, 2, source], recv.at[i, 0], self.below).wait_send()

            self.mine(i).wait()


def gather_sems(count):
    return [
        pltpu.SemaphoreType.DMA((count, 3, LINE)),
        pltpu.SemaphoreType.DMA((count, 2 * LINE)),
        pltpu.SemaphoreType.DMA((count,)),
    ]


def gather_body(count, ins, outs, send, recv, local, more=(), begin=None, finish=None, arrived=None):
    gather = Gather(ins, outs, send, recv, local)
    if arrived is not None:
        gather.arrived = arrived
    greet([*gather.targets, *more])
    gather.start()
    if begin is not None:
        begin()
    for i in range(count):
        for distance in range(1, LINE):
            gather.forward(distance, i)
    gather.finish()
    if finish is not None:
        finish()


def gather_wide(arrays, collective_id):
    count = len(arrays)
    size = lax.axis_size("wide")
    if size != 2 * LINE:
        return [lax.all_gather(a, "wide", axis=0) for a in arrays]
    return pl.pallas_call(
        functools.partial(gather_kernel, count),
        out_shape=[jax.ShapeDtypeStruct((size, *a.shape), a.dtype) for a in arrays],
        in_specs=[ANY] * count,
        out_specs=[ANY] * count,
        scratch_shapes=[
            pltpu.SemaphoreType.DMA((count, 3, LINE)),
            pltpu.SemaphoreType.DMA((count, size)),
            pltpu.SemaphoreType.DMA((count,)),
        ],
        compiler_params=pltpu.CompilerParams(collective_id=collective_id, has_side_effects=True),
        cost_estimate=lasts(100),
    )(*arrays)


def scatter_kernel(part_ref, out_ref, held, from_across, from_line, load, send, recv_a, recv_l):
    grp, wide, narrow, line, cross = position()
    across = (grp, line * 2 + 1 - cross, narrow)
    above = (grp, wide + 2, narrow)
    below = (grp, wide - 2, narrow)
    has_above, has_below = line < LINE - 1, line > 0
    f32 = jnp.float32
    greet([(across, None), (above, has_above), (below, has_below)])

    order = []
    for distance in range(LINE - 1, 0, -1):
        for sign in (1, -1):
            order.append((distance, sign))

    def valid(owner):
        return (owner >= 0) & (owner < LINE)

    def across_copy(owner):
        return remote(
            part_ref.at[owner * 2 + 1 - cross], from_across.at[owner], send.at[0, owner], recv_a.at[owner], across
        )

    def load_copy(owner):
        return pltpu.make_async_copy(part_ref.at[owner * 2 + cross], held.at[owner], load.at[owner])

    def line_copy(owner, up):
        return remote(
            held.at[owner],
            from_line.at[0 if up else 1, owner],
            send.at[1, owner],
            recv_l.at[0 if up else 1, owner],
            above if up else below,
        )

    for distance, sign in order + [(0, 1)]:
        owner = line + sign * distance

        @pl.when(valid(owner))
        def _(owner=owner):
            across_copy(owner).start()
            load_copy(owner).start()

    for distance, sign in order:
        owner = line + sign * distance

        @pl.when(valid(owner))
        def _(owner=owner, sign=sign):
            load_copy(owner).wait()
            across_copy(owner).wait_recv()
            up = sign > 0
            came = has_below if up else has_above
            total = held[owner].astype(f32) + from_across[owner].astype(f32)

            @pl.when(came)
            def _():
                line_copy(owner, up).wait_recv()
                held[owner] = (total + from_line[0 if up else 1, owner].astype(f32)).astype(held.dtype)

            @pl.when(jnp.logical_not(came))
            def _():
                held[owner] = total.astype(held.dtype)

            line_copy(owner, up).start()

    load_copy(line).wait()
    across_copy(line).wait_recv()
    out_ref[...] = held[line].astype(f32) + from_across[line].astype(f32)

    @pl.when(has_below)
    def _():
        line_copy(line, True).wait_recv()
        out_ref[...] += from_line[0, line].astype(f32)

    @pl.when(has_above)
    def _():
        line_copy(line, False).wait_recv()
        out_ref[...] += from_line[1, line].astype(f32)

    for owner in range(LINE):
        across_copy(owner).wait_send()

        @pl.when(owner > line)
        def _(owner=owner):
            line_copy(owner, True).wait_send()

        @pl.when(owner < line)
        def _(owner=owner):
            line_copy(owner, False).wait_send()


def scatter_wide(part, collective_id):
    size, rows, columns = part.shape
    if size != 2 * LINE:
        return lax.psum_scatter(part, "wide", scatter_dimension=0, tiled=False).astype(jnp.float32)
    block = (LINE, rows, columns)
    return pl.pallas_call(
        scatter_kernel,
        out_shape=jax.ShapeDtypeStruct((rows, columns), jnp.float32),
        in_specs=[ANY],
        out_specs=VMEM,
        scratch_shapes=[
            pltpu.VMEM(block, part.dtype),
            pltpu.VMEM(block, part.dtype),
            pltpu.VMEM((2, *block), part.dtype),
            pltpu.SemaphoreType.DMA((LINE,)),
            pltpu.SemaphoreType.DMA((2, LINE)),
            pltpu.SemaphoreType.DMA((LINE,)),
            pltpu.SemaphoreType.DMA((2, LINE)),
        ],
        compiler_params=pltpu.CompilerParams(
            collective_id=collective_id, has_side_effects=True, vmem_limit_bytes=48 * 2**20
        ),
        cost_estimate=lasts(95),
    )(part)


def sum_kernel(x_ref, o_ref, held, send, recv):
    grp, wide, narrow, _, _ = position()
    size = held.shape[0] + 1
    others = [(grp, lax.rem(wide + k, size), narrow) for k in range(1, size)]
    greet([(device, None) for device in others])
    copies = [
        remote(x_ref, held.at[k], send.at[k], recv.at[k], device) for k, device in enumerate(others)
    ]
    for copy in copies:
        copy.start()
    for copy in copies:
        copy.wait()
    total = x_ref[...]
    for k in range(size - 1):
        total = total + held[k]
    o_ref[...] = total


def sum_wide(x, collective_id):
    size = lax.axis_size("wide")
    if size != 2 * LINE:
        return lax.psum(x, "wide")
    return pl.pallas_call(
        sum_kernel,
        out_shape=jax.ShapeDtypeStruct(x.shape, x.dtype),
        in_specs=[VMEM],
        out_specs=VMEM,
        scratch_shapes=[
            pltpu.VMEM((size - 1, *x.shape), x.dtype),
            pltpu.SemaphoreType.DMA((size - 1,)),
            pltpu.SemaphoreType.DMA((size - 1,)),
        ],
        compiler_params=pltpu.CompilerParams(collective_id=collective_id, has_side_effects=True),
        cost_estimate=lasts(8),
    )(x)


LOG2E = 1.4426950408889634
NT = (((1,), (1,)), ((), ()))


def key_parts(w, plane, rows, prompt_blocks, paired, limit=512):
    count = (prompt_blocks if w is None else w) * rows
    parts = [(first, min(limit, count - first), None) for first in range(0, count, limit)]
    own = None if w is None else w * rows
    if plane == 0:
        parts.append((own, rows, "causal"))
    elif w is not None or paired:
        parts.append((own, rows, "side"))
    return parts


def for_blocks(blocks, prompt_blocks, one, between=None, first=0):
    for w in range(prompt_blocks):
        one(w, w, w * one.rows)
    if between is not None:
        between()

    def body(i, carry):
        w = prompt_blocks + lax.rem(i - prompt_blocks + first, blocks - prompt_blocks)
        one(None, w, pl.multiple_of(w * one.rows, one.rows))
        return carry

    lax.fori_loop(prompt_blocks, blocks, body, 0)


def masked_scores(score, mask, side, rows):
    if mask == "causal":
        key = lax.broadcasted_iota(jnp.int32, (rows, rows), 0)
        query = lax.broadcasted_iota(jnp.int32, (rows, rows), 1)
        return jnp.where(key <= query, score, NEGATIVE)
    if mask == "side":
        return jnp.where(side == 1, score, NEGATIVE)
    return score


def row_sums(values):
    total = values[:, :HD]
    for first in range(HD, values.shape[1], HD):
        total = total + values[:, first : first + HD]
    return jnp.sum(total.T, 0, keepdims=True)


def turn(values, cosine, sine):
    return values * cosine + pltpu.roll(values, HD // 2, 1) * sine


def inverse_norms(sums_ref, at):
    inverse = lax.rsqrt(sums_ref[:, at].T / D + EPSILON)
    return inverse[:, 0:1], inverse[:, 1:2]


def peer_copies(size, src, dst, send, recv, grp, wide, narrow):
    return [
        remote(src, dst.at[k - 1], send.at[k - 1], recv.at[k - 1], (grp, lax.rem(wide + k, size), narrow))
        for k in range(1, size)
    ]


def attend_kernel(
    rows, prompt_blocks, paired, shared, carried, raw_ref, gains_ref, cos_ref, sin_ref, *refs
):
    carry_in, refs = refs[:carried], refs[carried:]
    q_ref, k_ref, v_ref, ko_ref, vo_ref, o_ref, own_ref, lse_ref, sums_ref = refs[:9]
    carry_out, refs = refs[9 : 9 + carried], refs[9 + carried :]
    vt_ref, vto_ref, came_ref, sum_send, sum_recv, pair_send, pair_recv, out_send, out_recv = refs[:9]
    gather = Gather(carry_in, carry_out, *refs[9:]) if carried else None
    half, columns = q_ref.shape
    size = half // rows
    heads = columns // HD
    grp, wide, narrow = (lax.axis_index(a) for a in ("grp", "wide", "narrow"))
    partner = (grp, wide, 1 - narrow)
    greet([((grp, lax.rem(wide + k, size), narrow), None) for k in range(1, size)] + [(partner, None)])
    if carried:
        gather.start()
    pairs = [
        remote(src.at[pl.ds(0, shared)], dst, pair_send.at[i], pair_recv.at[i], partner)
        for i, (src, dst) in enumerate(((k_ref, ko_ref), (v_ref, vo_ref)))
    ]
    v_ref[...] = raw_ref[:, 2 * columns :].astype(jnp.bfloat16)
    pairs[1].start()
    sums_ref[...] = jnp.zeros_like(sums_ref)

    def squares(b, carry):
        at = pl.ds(pl.multiple_of(b * rows, rows), rows)
        for i in range(2):
            part = raw_ref[at, i * columns : (i + 1) * columns]
            sums_ref[i : i + 1, at] = row_sums(part * part)
        return carry

    lax.fori_loop(0, size, squares, 0)
    copies = peer_copies(size, sums_ref, came_ref, sum_send, sum_recv, grp, wide, narrow)
    for copy in copies:
        copy.start()
    for h in range(heads):
        hs = slice(h * HD, (h + 1) * HD)
        vt_ref[hs, :] = v_ref[:, hs].T
    for copy in copies:
        copy.wait()
    total = sums_ref[...]
    for k in range(size - 1):
        total = total + came_ref[k]
    sums_ref[...] = total

    def prepare(i, ref):
        def body(b, carry):
            at = pl.ds(pl.multiple_of(b * rows, rows), rows)
            inverse = inverse_norms(sums_ref, at)[i]
            for h in range(heads):
                hs = slice(h * HD, (h + 1) * HD)
                values = raw_ref[at, i * columns + h * HD : i * columns + (h + 1) * HD]
                values = values * inverse * gains_ref[i : i + 1, hs]
                ref[at, hs] = turn(values, cos_ref[at], sin_ref[at]).astype(jnp.bfloat16)
            return carry

        return body

    lax.fori_loop(0, shared // rows, prepare(1, k_ref), 0)
    pairs[0].start()
    lax.fori_loop(shared // rows, size, prepare(1, k_ref), 0)
    lax.fori_loop(0, size, prepare(0, q_ref), 0)
    if carried:
        gather.forward(1)
    pairs[1].wait()
    for h in range(heads):
        hs = slice(h * HD, (h + 1) * HD)
        vto_ref[hs, :] = vo_ref[:, hs].T
    pairs[0].wait()

    def mine():
        return pl.ds(pl.multiple_of(wide * columns, columns), columns)

    def hand_out(w):
        return remote(
            o_ref.at[pl.ds(pl.multiple_of(w * rows, rows), rows)],
            own_ref.at[:, mine()],
            out_send.at[w],
            out_recv.at[wide],
            (grp, w, narrow),
        )

    def one(w, w_index, start):
        block = pl.ds(start, rows)
        for h in range(heads):
            hs = slice(h * HD, (h + 1) * HD)
            query = q_ref[block, hs]
            scores = []
            for plane in range(2):
                for first, count, mask in key_parts(w, plane, rows, prompt_blocks, paired):
                    at = pl.ds(start if first is None else first, count)
                    key = (k_ref, ko_ref)[plane][at, hs]
                    score = lax.dot_general(key, query, NT, preferred_element_type=jnp.float32)
                    score = score * (HD**-0.5 * LOG2E)
                    scores.append((plane, at, masked_scores(score, mask, narrow, rows)))
            largest = functools.reduce(
                jnp.maximum, [jnp.max(score, 0, keepdims=True) for _, _, score in scores]
            )
            total = jnp.zeros((1, rows), jnp.float32)
            mixed = jnp.zeros((HD, rows), jnp.float32)
            for plane, at, score in scores:
                weight = jnp.exp2(score - largest)
                total = total + jnp.sum(weight, 0, keepdims=True)
                mixed = mixed + dot((vt_ref, vto_ref)[plane][hs, at], weight.astype(jnp.bfloat16))
            o_ref[block, hs] = (mixed / total).T.astype(jnp.bfloat16)
            lse_ref[h : h + 1, block] = largest + jnp.log(total) * LOG2E

        @pl.when(w_index != wide)
        def _():
            hand_out(w_index).start()

    one.rows = rows
    for_blocks(size, prompt_blocks, one, (lambda: gather.forward(2)) if carried else None, wide)
    if carried:
        gather.forward(3)
    own_ref[:, mine()] = o_ref[pl.ds(pl.multiple_of(wide * rows, rows), rows)]

    def finish(w, carry):
        @pl.when(w != wide)
        def _():
            hand_out(w).wait_send()
            remote(
                o_ref.at[pl.ds(0, rows)], own_ref.at[:, mine()], out_send.at[w], out_recv.at[w], (grp, w, narrow)
            ).wait_recv()

        return carry

    lax.fori_loop(0, size, finish, 0)
    if carried:
        gather.finish()


def attend_back_kernel(
    rows, prompt_blocks, paired, shared, carried, raw_ref, gains_ref, cos_ref, sin_ref, sums_ref,
    q_ref, k_ref, v_ref, ko_ref, vo_ref, grad_ref, o_ref, lse_ref, *refs
):
    carry_in, refs = refs[:carried], refs[carried:]
    joined_ref, gain_ref = refs[:2]
    carry_out, refs = refs[2 : 2 + carried], refs[2 + carried :]
    do_ref, dq_ref, dk_ref, dv_ref, dko_ref, dvo_ref, dkb_ref, dvb_ref, dkr_ref, dvr_ref, kt_ref, kto_ref = refs[:12]
    dots_ref, came_ref, sum_send, sum_recv, pair_send, pair_recv, in_send, in_recv = refs[12:20]
    gather = Gather(carry_in, carry_out, *refs[20:]) if carried else None
    half, columns = q_ref.shape
    size = half // rows
    heads = columns // HD
    grp, wide, narrow = (lax.axis_index(a) for a in ("grp", "wide", "narrow"))
    partner = (grp, wide, 1 - narrow)
    greet([((grp, lax.rem(wide + k, size), narrow), None) for k in range(1, size)] + [(partner, None)])
    my_rows = pl.ds(pl.multiple_of(wide * rows, rows), rows)

    def part_of(w):
        return pl.ds(pl.multiple_of(w * columns, columns), columns)

    def hand_in(w):
        return remote(
            grad_ref.at[:, part_of(w)], do_ref.at[my_rows], in_send.at[w], in_recv.at[wide], (grp, w, narrow)
        )

    def each_peer(act):
        def body(w, carry):
            pl.when(w != wide)(lambda: act(w))
            return carry

        lax.fori_loop(0, size, body, 0)

    each_peer(lambda w: hand_in(w).start())
    do_ref[my_rows, :] = grad_ref[:, part_of(wide)]
    for ref in (dk_ref, dv_ref, dko_ref, dvo_ref, dots_ref, gain_ref):
        ref[...] = jnp.zeros_like(ref)
    for h in range(heads):
        hs = slice(h * HD, (h + 1) * HD)
        kt_ref[hs, :] = k_ref[:, hs].T
        kto_ref[hs, :] = ko_ref[:, hs].T
    each_peer(
        lambda w: remote(
            grad_ref.at[:, part_of(w)], do_ref.at[my_rows], in_send.at[w], in_recv.at[w], (grp, w, narrow)
        ).wait_recv()
    )
    if carried:
        gather.start()

    def sweep(plane):
        keys, values = ((k_ref, v_ref), (ko_ref, vo_ref))[plane]
        dk, dv = ((dk_ref, dv_ref), (dko_ref, dvo_ref))[plane]
        flipped = (kt_ref, kto_ref)[plane]

        def one(w, w_index, start):
            block = pl.ds(start, rows)
            for h in range(heads):
                hs = slice(h * HD, (h + 1) * HD)
                query = q_ref[block, hs]
                grad = do_ref[block, hs]
                delta = row_sums(grad.astype(jnp.float32) * o_ref[block, hs].astype(jnp.float32))
                lse = lse_ref[h : h + 1, block]
                back = jnp.zeros((HD, rows), jnp.float32)
                for first, count, mask in key_parts(w, plane, rows, prompt_blocks, paired):
                    at = pl.ds(start if first is None else first, count)
                    score = lax.dot_general(keys[at, hs], query, NT, preferred_element_type=jnp.float32)
                    score = masked_scores(score * (HD**-0.5 * LOG2E), mask, narrow, rows)
                    weight = jnp.exp2(score - lse)
                    grad_weight = lax.dot_general(values[at, hs], grad, NT, preferred_element_type=jnp.float32)
                    grad_score = (weight * (grad_weight - delta)).astype(jnp.bfloat16)
                    dv[at, hs] += dot(weight.astype(jnp.bfloat16), grad)
                    dk[at, hs] += dot(grad_score, query) * HD**-0.5
                    back = back + dot(flipped[hs, at], grad_score)
                back = back.T * HD**-0.5
                dq_ref[block, hs] = back if plane == 1 else dq_ref[block, hs] + back

        one.rows = rows
        for_blocks(size, prompt_blocks, one, (lambda: gather.forward(2 - plane)) if carried else None)

    sweep(1)
    dkb_ref[...] = dko_ref[...].astype(jnp.bfloat16)
    dvb_ref[...] = dvo_ref[...].astype(jnp.bfloat16)
    pairs = [
        remote(src, dst, pair_send.at[i], pair_recv.at[i], partner)
        for i, (src, dst) in enumerate(((dkb_ref, dkr_ref), (dvb_ref, dvr_ref)))
    ]
    for copy in pairs:
        copy.start()
    sweep(0)

    def turn_back(i, ref):
        def body(b, carry):
            at = pl.ds(pl.multiple_of(b * rows, rows), rows)
            inverse = inverse_norms(sums_ref, at)[i]
            products = []
            for h in range(heads):
                hs = slice(h * HD, (h + 1) * HD)
                grad = turn(ref[at, hs], cos_ref[at], -sin_ref[at])
                ref[at, hs] = grad
                product = grad * raw_ref[at, i * columns + h * HD : i * columns + (h + 1) * HD]
                gain_ref[i : i + 1, hs] += jnp.sum(product * inverse, 0, keepdims=True)
                products.append(product * gains_ref[i : i + 1, hs])
            dots_ref[i : i + 1, at] = row_sums(sum(products[1:], products[0]))
            return carry

        lax.fori_loop(0, size, body, 0)

    turn_back(0, dq_ref)
    if carried:
        gather.forward(3)
    for copy in pairs:
        copy.wait()
    dk_ref[0:shared, :] += dkr_ref[...].astype(jnp.float32)
    turn_back(1, dk_ref)
    copies = peer_copies(size, dots_ref, came_ref, sum_send, sum_recv, grp, wide, narrow)
    for copy in copies:
        copy.start()
    joined_ref[0:shared, 2 * columns :] = (dv_ref[0:shared] + dvr_ref[...].astype(jnp.float32)).astype(jnp.bfloat16)
    if shared < half:
        joined_ref[shared:, 2 * columns :] = dv_ref[shared:].astype(jnp.bfloat16)
    for copy in copies:
        copy.wait()
    total = dots_ref[...]
    for k in range(size - 1):
        total = total + came_ref[k]
    dots_ref[...] = total

    def finish(b, carry):
        at = pl.ds(pl.multiple_of(b * rows, rows), rows)
        inverses = inverse_norms(sums_ref, at)
        products = dots_ref[:, at].T / D
        for i, ref in enumerate((dq_ref, dk_ref)):
            inverse = inverses[i]
            cubed = inverse * inverse * inverse * products[:, i : i + 1]
            for h in range(heads):
                hs = slice(h * HD, (h + 1) * HD)
                there = slice(i * columns + h * HD, i * columns + (h + 1) * HD)
                value = inverse * gains_ref[i : i + 1, hs] * ref[at, hs] - raw_ref[at, there] * cubed
                joined_ref[at, there] = value.astype(jnp.bfloat16)
        return carry

    lax.fori_loop(0, size, finish, 0)
    each_peer(lambda w: hand_in(w).wait_send())
    if carried:
        gather.finish()


def attention_calls(rows, half, shared, columns, prompt_blocks, paired, ids):
    heads = columns // HD
    size = half // rows
    bf16, f32 = jnp.bfloat16, jnp.float32
    shape = lambda dtype, *dims: jax.ShapeDtypeStruct(dims, dtype)
    sems = pltpu.SemaphoreType.DMA
    peers = [sems((size - 1,)), sems((size - 1,)), sems((2,)), sems((2,)), sems((size,)), sems((size,))]

    def params(k):
        return pltpu.CompilerParams(vmem_limit_bytes=60 * 2**20, collective_id=ids[k], has_side_effects=True)

    carried = 0
    forward = pl.pallas_call(
        functools.partial(attend_kernel, rows, prompt_blocks, paired, shared, 0),
        out_shape=[shape(bf16, half, columns)] * 3
        + [shape(bf16, shared, columns)] * 2
        + [shape(bf16, half, columns), shape(bf16, rows, size * columns), shape(f32, heads, half), shape(f32, 8, half)],
        in_specs=[VMEM] * 4,
        out_specs=[VMEM] * 9,
        scratch_shapes=[
            pltpu.VMEM((columns, half), bf16),
            pltpu.VMEM((columns, shared), bf16),
            pltpu.VMEM((size - 1, 8, half), f32),
        ]
        + peers,
        compiler_params=params(0),
        cost_estimate=pl.CostEstimate(flops=0, bytes_accessed=300_000_000, transcendentals=0),
    )

    backward = pl.pallas_call(
        functools.partial(attend_back_kernel, rows, prompt_blocks, paired, shared, carried),
        out_shape=[shape(bf16, half, 3 * columns), shape(f32, 8, columns)]
        + [shape(bf16, size, rows, D)] * carried,
        in_specs=[VMEM] * 13 + [ANY] * carried,
        out_specs=[VMEM] * 2 + [ANY] * carried,
        scratch_shapes=[pltpu.VMEM((half, columns), bf16)]
        + [pltpu.VMEM((half, columns), f32)] * 3
        + [pltpu.VMEM((shared, columns), f32)] * 2
        + [pltpu.VMEM((shared, columns), bf16)] * 4
        + [
            pltpu.VMEM((columns, half), bf16),
            pltpu.VMEM((columns, shared), bf16),
            pltpu.VMEM((8, half), f32),
            pltpu.VMEM((size - 1, 8, half), f32),
        ]
        + peers
        + gather_sems(carried) * carried,
        compiler_params=params(1),
        cost_estimate=pl.CostEstimate(flops=0, bytes_accessed=300_000_000, transcendentals=0),
    )
    return forward, backward


def dot(a, b):
    return jnp.dot(a, b, preferred_element_type=jnp.float32)


def dot_nt(a, b):
    return lax.dot_general(a, b, NT, preferred_element_type=jnp.float32)


def dot_tn(a, b):
    return lax.dot_general(a, b, (((0,), (0,)), ((), ())), preferred_element_type=jnp.float32)


def start_kernel(count, swaps, spread, *refs):
    ins, given = refs[:count], refs[count : count + swaps]
    refs = refs[count + swaps :]
    outs, got, pieces = refs[:count], refs[count : count + swaps], refs[count + swaps : count + swaps + 3 * spread]
    refs = refs[count + swaps + 3 * spread :]
    send, recv, local, swap_send, swap_recv, twin_send, twin_recv = refs[:7]
    grp, wide, narrow, line, cross = position()
    partner = (grp, wide, 1 - narrow)
    twin = (1 - grp, wide, narrow)
    size = 2 * LINE

    def half(ref, which):
        size = ref.shape[0] // 2
        return ref.at[pl.ds(pl.multiple_of(which * size, size), size)]

    def swap(i):
        return remote(half(given[i], grp), half(got[i], grp), swap_send.at[i], swap_recv.at[i], partner)

    def share(i, which):
        return remote(half(got[i], which), half(got[i], which), twin_send.at[i], twin_recv.at[i], twin)

    def piece(k, slot):
        piece_send, piece_recv = refs[7:]
        src = pieces[0] if k == 2 else outs[-1]
        device = twin if k else partner
        return remote(src.at[slot], pieces[k].at[slot], piece_send.at[k, slot], piece_recv.at[k, slot], device)

    def own_piece(k):
        piece_send, piece_recv = refs[7:]
        device = twin if k else partner
        return remote(ins[-1], pieces[k].at[wide], piece_send.at[k, wide], piece_recv.at[k, wide], device)

    def arrived(i, slot):
        if i == count - 1:
            for k in range(2):
                if slot is None:
                    own_piece(k).start()
                else:
                    piece(k, slot).start()

    def begin():
        for i in range(swaps):
            swap(i).start()

    def finish():
        if spread:
            for slot in range(size):
                piece(0, slot).wait_recv()
                piece(2, slot).start()
        for i in range(swaps):
            swap(i).wait_recv()
            share(i, grp).start()
        for i in range(swaps):
            swap(i).wait_send()
            share(i, grp).wait_send()
            share(i, 1 - grp).wait_recv()
        if spread:
            for slot in range(size):
                piece(0, slot).wait_send()
                piece(1, slot).wait()
                piece(2, slot).wait()

    more = [(partner, None), (twin, None)]
    gather_body(count, ins, outs, send, recv, local, more, begin, finish, arrived if spread else None)


def start_exchange(arrays, weights, collective_id, spread=False):
    size = lax.axis_size("wide")
    swap = [(0, 1), (1, 0)]
    if size != 2 * LINE or lax.axis_size("grp") != 2:
        return [lax.all_gather(a, "wide", axis=0) for a in arrays], [lax.ppermute(w, "narrow", swap) for w in weights], []
    count, swaps, spread = len(arrays), len(weights), int(spread)
    gathered = [jax.ShapeDtypeStruct((size, *a.shape), a.dtype) for a in arrays]
    dma = pltpu.SemaphoreType.DMA
    out = pl.pallas_call(
        functools.partial(start_kernel, count, swaps, spread),
        out_shape=gathered + [jax.ShapeDtypeStruct(w.shape, w.dtype) for w in weights] + gathered[-1:] * 3 * spread,
        in_specs=[ANY] * (count + swaps),
        out_specs=[ANY] * (count + swaps + 3 * spread),
        scratch_shapes=gather_sems(count) + [dma((swaps,))] * 4 + [dma((3, size))] * 2 * spread,
        compiler_params=pltpu.CompilerParams(collective_id=collective_id, has_side_effects=True),
        cost_estimate=lasts(120),
    )(*arrays, *weights)
    return out[:count], out[count : count + swaps], out[count + swaps :]


def expert_grad_kernel(
    part_ref, *refs
):
    operands = refs[0:5]
    out_ref, gate_out, up_out, down_out = refs[5:9]
    held, from_across, from_line, x_buf, g_buf, inner_buf, gate_buf, up_buf, stage = refs[9:18]
    load, send, recv_a, recv_l, fetch, put = refs[18:]
    grp, wide, narrow, line, cross = position()
    across = (grp, line * 2 + 1 - cross, narrow)
    above = (grp, wide + 2, narrow)
    below = (grp, wide - 2, narrow)
    has_above, has_below = line < LINE - 1, line > 0
    f32, bf16 = jnp.float32, jnp.bfloat16
    greet([(across, None), (above, has_above), (below, has_below)])
    order = [(distance, sign) for distance in range(LINE - 1, 0, -1) for sign in (1, -1)]

    def valid(owner):
        return (owner >= 0) & (owner < LINE)

    def across_copy(owner):
        return remote(
            part_ref.at[owner * 2 + 1 - cross], from_across.at[owner], send.at[0, owner], recv_a.at[owner], across
        )

    def load_copy(owner):
        return pltpu.make_async_copy(part_ref.at[owner * 2 + cross], held.at[owner], load.at[owner])

    def line_copy(owner, up):
        slot = 0 if up else 1
        return remote(
            held.at[owner], from_line.at[slot, owner], send.at[1, owner], recv_l.at[slot, owner], above if up else below
        )

    for distance, sign in order + [(0, 1)]:
        owner = line + sign * distance

        @pl.when(valid(owner))
        def _(owner=owner):
            across_copy(owner).start()
            load_copy(owner).start()

    bufs = (x_buf, g_buf, inner_buf, gate_buf, up_buf)

    fetches = [pltpu.make_async_copy(src, dst, fetch.at[i]) for i, (src, dst) in enumerate(zip(operands, bufs))]
    for copy in fetches:
        copy.start()

    tiles = stage.shape[0]
    width = gate_buf.shape[1] // tiles

    def tile(n, size):
        return pl.ds(pl.multiple_of(n * size, size), size)

    def column_job(values, result):
        def put_copy(n):
            return pltpu.make_async_copy(stage.at[n], result.at[:, tile(n, width)], put.at[n])

        def run():
            @pl.loop(0, tiles)
            def _(n):
                stage[n] = dot_tn(x_buf[...], values[:, tile(n, width)]).astype(bf16)
                put_copy(n).start()

            @pl.loop(0, tiles)
            def _(n):
                put_copy(n).wait()

        return run

    def down_job(result):
        units = inner_buf.shape[1] // tiles

        def run():
            for n in range(tiles):
                at = slice(n * units, (n + 1) * units)
                product = dot_tn(inner_buf[:, at], g_buf[...]).astype(bf16)
                for c in range(product.shape[1] // width):
                    stage[n, c * units : (c + 1) * units, :] = product[:, c * width : (c + 1) * width]
            copies = [
                pltpu.make_async_copy(
                    stage.at[n, pl.ds(c * units, units)],
                    result.at[pl.ds(n * units, units), pl.ds(c * width, width)],
                    put.at[n * (g_buf.shape[1] // width) + c],
                )
                for n in range(tiles)
                for c in range(g_buf.shape[1] // width)
            ]
            for copy in copies:
                copy.start()
            for copy in copies:
                copy.wait()

        return run

    def first_job():
        for copy in fetches:
            copy.wait()
        column_job(gate_buf, gate_out)()

    jobs = [first_job, None, column_job(up_buf, up_out), None, down_job(down_out), None]
    for job, (distance, sign) in zip(jobs, order):
        if job is not None:
            job()
        owner = line + sign * distance

        @pl.when(valid(owner))
        def _(owner=owner, sign=sign):
            load_copy(owner).wait()
            across_copy(owner).wait_recv()
            up = sign > 0
            came = has_below if up else has_above
            total = held[owner].astype(f32) + from_across[owner].astype(f32)

            @pl.when(came)
            def _():
                line_copy(owner, up).wait_recv()
                held[owner] = (total + from_line[0 if up else 1, owner].astype(f32)).astype(held.dtype)

            @pl.when(jnp.logical_not(came))
            def _():
                held[owner] = total.astype(held.dtype)

            line_copy(owner, up).start()

    load_copy(line).wait()
    across_copy(line).wait_recv()
    out_ref[...] = held[line].astype(f32) + from_across[line].astype(f32)

    @pl.when(has_below)
    def _():
        line_copy(line, True).wait_recv()
        out_ref[...] += from_line[0, line].astype(f32)

    @pl.when(has_above)
    def _():
        line_copy(line, False).wait_recv()
        out_ref[...] += from_line[1, line].astype(f32)

    for owner in range(LINE):
        across_copy(owner).wait_send()

        @pl.when(owner > line)
        def _(owner=owner):
            line_copy(owner, True).wait_send()

        @pl.when(owner < line)
        def _(owner=owner):
            line_copy(owner, False).wait_send()


def plain_grads(x, g, inner, gate, up):
    return [dot_tn(a, b).astype(jnp.bfloat16) for a, b in ((x, gate), (x, up), (inner, g))]


def expert_grad(part, own, collective_id):
    size, rows, columns = part.shape
    f32, bf16 = jnp.float32, jnp.bfloat16
    if size != 2 * LINE:
        return lax.psum_scatter(part, "wide", scatter_dimension=0, tiled=False).astype(f32), *plain_grads(*own)
    count, units = own[2].shape
    tiles = 4
    block = (LINE, rows, columns)
    gate = jax.ShapeDtypeStruct((D, units), bf16)
    down = jax.ShapeDtypeStruct((units, D), bf16)
    dma = pltpu.SemaphoreType.DMA
    return pl.pallas_call(
        expert_grad_kernel,
        out_shape=[jax.ShapeDtypeStruct((rows, columns), f32), gate, gate, down],
        in_specs=[ANY] * 6,
        out_specs=[VMEM] + [ANY] * 3,
        scratch_shapes=[
            pltpu.VMEM(block, bf16),
            pltpu.VMEM(block, bf16),
            pltpu.VMEM((2, *block), bf16),
            pltpu.VMEM((count, D), bf16),
            pltpu.VMEM((count, D), bf16),
            pltpu.VMEM((count, units), bf16),
            pltpu.VMEM((count, units), bf16),
            pltpu.VMEM((count, units), bf16),
            pltpu.VMEM((tiles, D, units // tiles), bf16),
            dma((LINE,)),
            dma((2, LINE)),
            dma((LINE,)),
            dma((2, LINE)),
            dma((5,)),
            dma((tiles * D // (units // tiles),)),
        ],
        compiler_params=pltpu.CompilerParams(
            collective_id=collective_id, has_side_effects=True, vmem_limit_bytes=60 * 2**20
        ),
        cost_estimate=lasts(1),
    )(part, *own)


class SmallSum:
    def __init__(self, x_ref, o_ref, parts, total, send, recv, send_back, recv_back):
        self.refs = x_ref, o_ref, parts, total, send, recv, send_back, recv_back
        grp, wide, narrow, _, _ = position()
        self.size, _, self.width = parts.shape
        self.me = wide * 2 + narrow
        self.ranks = [lax.rem(self.me + k, self.size) for k in range(self.size)]
        self.devices = [(grp, rank // 2, lax.rem(rank, 2)) for rank in self.ranks]
        self.targets = [(device, None) for device in self.devices[1:]]

    def columns(self, rank):
        return pl.ds(pl.multiple_of(rank * self.width, self.width), self.width)

    def run(self):
        x_ref, o_ref, parts, total, send, recv, send_back, recv_back = self.refs
        devices, size, mine = self.devices, self.size, self.columns(self.me)
        out = [
            remote(x_ref.at[:, self.columns(self.ranks[k])], parts.at[k], send.at[k], recv.at[k], devices[k])
            for k in range(1, size)
        ]
        for copy in out:
            copy.start()
        total[...] = x_ref[:, mine]
        for k, copy in enumerate(out):
            copy.wait()
            total[...] += parts[k + 1]
        back = [
            remote(total, o_ref.at[:, mine], send_back.at[k], recv_back.at[k], devices[k]) for k in range(1, size)
        ]
        for copy in back:
            copy.start()
        o_ref[:, mine] = total[...]
        for copy in back:
            copy.wait_send()
        for k in range(1, size):
            rank = lax.rem(self.me - k + size, size)
            remote(total, o_ref.at[:, self.columns(rank)], send_back.at[k], recv_back.at[k], devices[k]).wait_recv()


def input_grad_kernel(
    gain_row, joined_ref, weights_ref, tokens_ref, hidden_ref, gain_ref, small_ref, out_ref, sums_ref,
    held, from_across, from_line, x_ref, parts, total_ref, send, recv_a, recv_l, *small_sems
):
    rows = tokens_ref.shape[0]
    f32 = jnp.float32
    small = SmallSum(x_ref, sums_ref, parts, total_ref, *small_sems)
    grp, wide, narrow, line, cross = position()
    across = (grp, line * 2 + 1 - cross, narrow)
    above = (grp, wide + 2, narrow)
    below = (grp, wide - 2, narrow)
    has_above, has_below = line < LINE - 1, line > 0
    greet(small.targets)
    order = [(distance, sign) for distance in range(LINE - 1, 0, -1) for sign in (1, -1)] + [(0, 1)]

    def valid(owner):
        return (owner >= 0) & (owner < LINE)

    def part(owner, column):
        at = pl.ds(pl.multiple_of((owner * 2 + column) * rows, rows), rows)
        return dot_nt(joined_ref[at], weights_ref[...])

    def across_copy(owner):
        return remote(held.at[0, owner], from_across.at[owner], send.at[0, owner], recv_a.at[owner], across)

    def line_copy(owner, up):
        slot = 0 if up else 1
        return remote(
            held.at[1, owner], from_line.at[slot, owner], send.at[1, owner], recv_l.at[slot, owner], above if up else below
        )

    for distance, sign in order:
        owner = line + sign * distance

        @pl.when(valid(owner))
        def _(owner=owner):
            held[0, owner] = part(owner, 1 - cross).astype(held.dtype)
            across_copy(owner).start()

    for distance, sign in order[:-1]:
        owner = line + sign * distance

        @pl.when(valid(owner))
        def _(owner=owner, sign=sign):
            up = sign > 0
            came = has_below if up else has_above
            total = part(owner, cross)
            across_copy(owner).wait_recv()
            total = total + from_across[owner].astype(f32)

            @pl.when(came)
            def _():
                line_copy(owner, up).wait_recv()
                held[1, owner] = (total + from_line[0 if up else 1, owner].astype(f32)).astype(held.dtype)

            @pl.when(jnp.logical_not(came))
            def _():
                held[1, owner] = total.astype(held.dtype)

            line_copy(owner, up).start()

    out_ref[...] = part(line, cross)
    across_copy(line).wait_recv()
    out_ref[...] += from_across[line].astype(f32)

    @pl.when(has_below)
    def _():
        line_copy(line, True).wait_recv()
        out_ref[...] += from_line[0, line].astype(f32)

    @pl.when(has_above)
    def _():
        line_copy(line, False).wait_recv()
        out_ref[...] += from_line[1, line].astype(f32)

    x_ref[...] = small_ref[...]
    x_ref[gain_row : gain_row + 1, :] = jnp.zeros((1, D), f32)
    chunk = min(rows, 64)

    def finish(i, carry):
        at = pl.ds(pl.multiple_of(i * chunk, chunk), chunk)
        grad = out_ref[at]
        stream = tokens_ref[at].astype(f32)
        inverse = lax.rsqrt(jnp.mean(stream * stream, -1, keepdims=True) + EPSILON)
        product = grad * stream
        x_ref[gain_row : gain_row + 1, :] += jnp.sum(product * inverse, 0, keepdims=True)
        slope = inverse * inverse * inverse * jnp.sum(product * gain_ref[...], -1, keepdims=True) / D
        out_ref[at] = hidden_ref[at] + inverse * gain_ref[...] * grad - stream * slope
        return carry

    lax.fori_loop(0, rows // chunk, finish, 0)
    small.run()

    for owner in range(LINE):
        across_copy(owner).wait_send()

        @pl.when(owner > line)
        def _(owner=owner):
            line_copy(owner, True).wait_send()

        @pl.when(owner < line)
        def _(owner=owner):
            line_copy(owner, False).wait_send()


def input_grad(joined, weights, tokens, grad_hidden, gain, small, gain_row, ids):
    size = lax.axis_size("wide")
    rows = tokens.shape[0]
    f32, bf16 = jnp.float32, jnp.bfloat16
    if size != 2 * LINE:
        part = dot_nt(joined, weights).astype(bf16).reshape(size, rows, D)
        grad = lax.psum_scatter(part, "wide", scatter_dimension=0, tiled=False).astype(f32)
        stream = tokens.astype(f32)
        inverse = lax.rsqrt(jnp.mean(stream * stream, -1, keepdims=True) + EPSILON)
        small = small.at[gain_row].set(jnp.sum(grad * stream * inverse, 0))
        slope = inverse**3 * jnp.sum(grad * gain * stream, -1, keepdims=True) / D
        return grad_hidden + inverse * gain * grad - stream * slope, lax.psum(small, ("wide", "narrow"))
    devices = 4 * LINE
    block = (LINE, rows, D)
    dma = pltpu.SemaphoreType.DMA
    return pl.pallas_call(
        functools.partial(input_grad_kernel, gain_row),
        out_shape=[jax.ShapeDtypeStruct((rows, D), f32), jax.ShapeDtypeStruct(small.shape, f32)],
        in_specs=[VMEM] * 6,
        out_specs=[VMEM] * 2,
        scratch_shapes=[
            pltpu.VMEM((2, *block), bf16),
            pltpu.VMEM(block, bf16),
            pltpu.VMEM((2, *block), bf16),
            pltpu.VMEM(small.shape, f32),
            pltpu.VMEM((devices, small.shape[0], D // devices), f32),
            pltpu.VMEM((small.shape[0], D // devices), f32),
            dma((2, LINE)),
            dma((LINE,)),
            dma((2, LINE)),
        ]
        + [dma((devices,))] * 4,
        compiler_params=pltpu.CompilerParams(
            collective_id=ids, has_side_effects=True, vmem_limit_bytes=56 * 2**20
        ),
        cost_estimate=lasts(100),
    )(joined, weights, tokens, grad_hidden, gain, small)


def pick_rows(step, capacity, slot_ref, source_refs, picks, held, out_ref):
    row = lax.broadcasted_iota(jnp.int32, (capacity, slot_ref.shape[2]), 0)
    pick = jnp.where(row == slot_ref[0], 1.0, 0.0).astype(jnp.bfloat16)
    picks[step] = pick
    part = pick.shape[1] // len(source_refs)
    values = sum(dot(pick[:, k * part : (k + 1) * part], ref[0]) for k, ref in enumerate(source_refs))
    values = values.astype(jnp.bfloat16)
    held[pl.ds(pl.multiple_of(step * capacity, capacity), capacity)] = values
    out_ref[...] = values


def spread_rows(block, capacity, picks, total, before_ref, out_ref):
    here = pl.ds(pl.multiple_of(block * capacity, capacity), capacity)
    values = dot_tn(picks[block], total[here].astype(jnp.bfloat16))
    if before_ref is not None:
        values = values + before_ref[0].astype(jnp.float32)
    out_ref[0] = values.astype(jnp.bfloat16)


def expert_forward_kernel(
    tiles, capacity, experts, first, id_ref, slot_ref, tokens_ref, router_ref, gate_ref, up_ref, down_ref, *refs
):
    before_ref = None if first else refs[0]
    moe_ref, x_ref, inner_ref, gate_pre_ref, up_pre_ref, probs_ref, x_all, picks, moe_all = refs[0 if first else 1 :]
    step = pl.program_id(1)
    blocks = picks.shape[0]
    lane = lax.broadcasted_iota(jnp.int32, (1, 128), 1)

    @pl.when(step < blocks)
    def _():
        pick_rows(step, capacity, slot_ref, [tokens_ref], picks, x_all, x_ref)

    @pl.when(step == blocks)
    def _():
        logits = jnp.where(lane < experts, dot(x_all[...], router_ref[...]), NEGATIVE)
        weight = jnp.exp(logits - jnp.max(logits, -1, keepdims=True))
        probs_ref[...] = weight / jnp.sum(weight, -1, keepdims=True)
        moe_all[...] = jnp.zeros_like(moe_all)

    @pl.when((step >= blocks) & (step < blocks + tiles))
    def _():
        x = x_all[...]
        gate = jnp.sum(jnp.where(lane == id_ref[0], probs_ref[...], 0.0), -1, keepdims=True)
        gate_pre = dot(x, gate_ref[...])
        up_pre = dot(x, up_ref[...])
        gate_pre_ref[...] = gate_pre
        up_pre_ref[...] = up_pre
        inner_gated = (gate * (gate_pre / (1.0 + jnp.exp(-gate_pre))) * up_pre).astype(jnp.bfloat16)
        inner_ref[...] = inner_gated
        moe_all[...] += dot(inner_gated, down_ref[...])

    @pl.when(step >= blocks + tiles)
    def _():
        spread_rows(step - blocks - tiles, capacity, picks, moe_all, before_ref, moe_ref)


def expert_backward_kernel(
    tiles, capacity, first, id_ref, slot_ref, low_ref, high_ref, x_ref, probs_ref, gate_pre_ref, up_pre_ref,
    router_ref, gate_ref, up_ref, down_ref, *refs
):
    before_ref, router_in_ref = (None, None) if first else refs[:2]
    (
        part_ref, g_ref, grad_gate_ref, grad_up_ref, router_grad_ref,
        g_all, picks, part_all, scores_all, router_sum,
    ) = refs[0 if first else 2 :]
    bf16 = jnp.bfloat16
    group, step = pl.program_id(0), pl.program_id(1)
    blocks = picks.shape[0]
    lane = lax.broadcasted_iota(jnp.int32, (1, 128), 1)
    here = jnp.where(lane == id_ref[0], 1.0, 0.0)

    @pl.when(step < blocks)
    def _():
        pick_rows(step, capacity, slot_ref, [low_ref, high_ref], picks, g_all, g_ref)

    @pl.when(step == blocks)
    def _():
        part_all[...] = jnp.zeros_like(part_all)
        scores_all[...] = jnp.zeros_like(scores_all)

    @pl.when((step >= blocks) & (step < blocks + tiles))
    def _():
        gate = jnp.sum(probs_ref[...] * here, -1, keepdims=True)
        gate_pre, up_pre = gate_pre_ref[...], up_pre_ref[...]
        back = dot_nt(g_all[...], down_ref[...])
        sigmoid = 1.0 / (1.0 + jnp.exp(-gate_pre))
        silu = gate_pre * sigmoid
        scores_all[...] += jnp.sum(silu * up_pre * back, -1, keepdims=True)
        back = gate * back
        grad_gate_pre = (back * up_pre * sigmoid * (1.0 + gate_pre * (1.0 - sigmoid))).astype(bf16)
        grad_up_pre = (back * silu).astype(bf16)
        grad_gate_ref[...] = grad_gate_pre
        grad_up_ref[...] = grad_up_pre
        part_all[...] += dot_nt(grad_gate_pre, gate_ref[...]) + dot_nt(grad_up_pre, up_ref[...])

    @pl.when(step == blocks + tiles)
    def _():
        probs = probs_ref[...]
        gate = jnp.sum(probs * here, -1, keepdims=True)
        mixing = (gate * scores_all[...] * (here - probs)).astype(bf16)
        part_all[...] += dot_nt(mixing, router_ref[...])
        grad = dot_tn(mixing, x_ref[...])

        @pl.when(group == 0)
        def _():
            router_sum[...] = grad if first else grad + router_in_ref[...]

        @pl.when(group > 0)
        def _():
            router_sum[...] += grad

        router_grad_ref[...] = router_sum[...]

    @pl.when(step >= blocks + tiles)
    def _():
        spread_rows(step - blocks - tiles, capacity, picks, part_all, before_ref, part_ref)


class Expert:
    def __init__(self, expert, slots, router, weights, capacity, experts):
        self.scalars = expert.astype(jnp.int32).reshape(1), slots
        self.router, self.weights, self.capacity, self.experts = router, weights, capacity, experts
        wide, _, rows = slots.shape
        units = weights[0].shape[1]
        groups = 1 if wide * capacity <= 1280 else 2
        blocks, tile = wide // groups, 256
        tiles = units // tile
        last = blocks + tiles
        self.tiles, self.grid = tiles, (groups, last + blocks)
        self.held, self.blocks, self.rows = blocks * capacity, blocks, rows
        count = wide * capacity

        def picked(g, i):
            return g * blocks + jnp.minimum(i, blocks - 1)

        def tiled(i):
            return jnp.clip(i - blocks, 0, tiles - 1)

        self.whole = pl.BlockSpec((1, rows, D), lambda g, i: (picked(g, i), 0, 0))
        self.part = pl.BlockSpec((1, rows // 2, D), lambda g, i: (picked(g, i), 0, 0))
        self.back = pl.BlockSpec((1, rows, D), lambda g, i: (g * blocks + jnp.clip(i - last, 0, blocks - 1), 0, 0))
        self.row = pl.BlockSpec((capacity, D), lambda g, i: (picked(g, i), 0))
        column = pl.BlockSpec((D, tile), lambda g, i: (0, tiled(i)))
        self.unit = pl.BlockSpec((self.held, tile), lambda g, i: (g, tiled(i)))
        self.fixed = pl.BlockSpec((128, D), lambda g, i: (0, 0))
        self.rows_all = pl.BlockSpec((self.held, D), lambda g, i: (g, 0))
        self.probs = pl.BlockSpec((self.held, 128), lambda g, i: (g, 0))
        self.heads = [
            pl.BlockSpec(memory_space=pltpu.SMEM), pl.BlockSpec((1, 1, rows), lambda g, i: (picked(g, i), 0, 0))
        ]
        self.weight_specs = [
            pl.BlockSpec((D, 128), lambda g, i: (0, 0)), column, column,
            pl.BlockSpec((tile, D), lambda g, i: (tiled(i), 0)),
        ]
        shape = jax.ShapeDtypeStruct
        self.blocks_shape = shape((wide, rows, D), jnp.bfloat16)
        self.compact = shape((count, D), jnp.bfloat16)
        self.narrow = shape((count, units), jnp.bfloat16)
        self.narrow32 = shape((count, units), jnp.float32)
        self.probs_shape = shape((count, 128), jnp.float32)
        self.common = dict(
            grid=self.grid,
            compiler_params=pltpu.CompilerParams(vmem_limit_bytes=60 * 2**20),
            cost_estimate=pl.CostEstimate(flops=0, bytes_accessed=120_000_000, transcendentals=0),
        )

    def forward(self, tokens, before):
        first = before is None
        f32, bf16 = jnp.float32, jnp.bfloat16
        return pl.pallas_call(
            functools.partial(expert_forward_kernel, self.tiles, self.capacity, self.experts, first),
            in_specs=self.heads + [self.whole] + self.weight_specs + ([] if first else [self.back]),
            out_specs=[self.back, self.row, self.unit, self.unit, self.unit, self.probs],
            out_shape=[
                self.blocks_shape, self.compact, self.narrow, self.narrow32, self.narrow32, self.probs_shape
            ],
            scratch_shapes=[
                pltpu.VMEM((self.held, D), bf16),
                pltpu.VMEM((self.blocks, self.capacity, self.rows), bf16),
                pltpu.VMEM((self.held, D), f32),
            ],
            **self.common,
        )(*self.scalars, tokens, self.router, *self.weights, *(() if first else (before,)))

    def backward(self, grads, kept, before):
        first = before is None
        f32, bf16 = jnp.float32, jnp.bfloat16
        _, x, _, gate_pre, up_pre, probs = kept
        return pl.pallas_call(
            functools.partial(expert_backward_kernel, self.tiles, self.capacity, first),
            in_specs=self.heads
            + [self.part, self.part, self.rows_all, self.probs, self.unit, self.unit]
            + self.weight_specs
            + ([] if first else [self.back, self.fixed]),
            out_specs=[self.back, self.row, self.unit, self.unit, self.fixed],
            out_shape=[
                self.blocks_shape, self.compact, self.narrow, self.narrow, jax.ShapeDtypeStruct((128, D), f32)
            ],
            scratch_shapes=[
                pltpu.VMEM((self.held, D), bf16),
                pltpu.VMEM((self.blocks, self.capacity, self.rows), bf16),
                pltpu.VMEM((self.held, D), f32),
                pltpu.VMEM((self.held, 1), f32),
                pltpu.VMEM((128, D), f32),
            ],
            **self.common,
        )(*self.scalars, *grads, x, probs, gate_pre, up_pre, self.router, *self.weights, *(before or ()))


def positions(token_ids):
    local = token_ids % (PROMPT + NCONT * CONT)
    return jnp.where(local < PROMPT, local, PROMPT + (local - PROMPT) % CONT)


def rotation(place):
    frequency = THETA ** (-2.0 * jnp.arange(HD // 2, dtype=jnp.float32) / HD)
    angle = place.astype(jnp.float32)[:, None] * frequency[None, :]
    cosine, sine = jnp.cos(angle), jnp.sin(angle)
    return jnp.concatenate([cosine, cosine], 1), jnp.concatenate([-sine, sine], 1)


def shards(
    tokens,
    cotangent,
    valid,
    routes,
    w_query,
    w_key,
    w_value,
    w_out,
    norm_attn,
    norm_query,
    norm_key,
    norm_moe,
    w_router,
    w_gate,
    w_up,
    w_down,
):
    bf16, f32 = jnp.bfloat16, jnp.float32
    wide_count = lax.axis_size("wide")
    narrow_count = lax.axis_size("narrow")
    rows = tokens.shape[0]
    half = rows * wide_count
    columns = w_query.shape[1]
    experts = w_router.shape[1]
    hidden_units = w_gate.shape[2]
    capacity = min(max(rows * TOP * 5 // (4 * experts), 2), rows)
    assert narrow_count == 2 and CONT in (rows, 2 * rows)
    paired = CONT == 2 * rows
    side = lax.axis_index("narrow")
    place = lax.axis_index("wide")
    group = lax.axis_index("grp")
    swap = [(0, 1), (1, 0)]
    twins = lax.axis_size("grp") == 2
    prompt_blocks = PROMPT // (rows * narrow_count)
    shared = half if paired else prompt_blocks * rows
    attend, attend_back = attention_calls(rows, half, shared, columns, prompt_blocks, paired, (1, 2))
    barrier = lax.optimization_barrier

    def exchange(value):
        return lax.ppermute(value, "narrow", swap)

    stream = tokens.astype(f32)
    inv_one = lax.rsqrt(jnp.mean(stream * stream, -1, keepdims=True) + EPSILON)
    gain_one = norm_attn.astype(f32)
    normed = (stream * inv_one * gain_one).astype(bf16)
    mask = valid.astype(f32)[:, None]
    grad_final = cotangent.astype(f32) * mask
    pieces = 2 * narrow_count if twins else 1
    piece_width = D // pieces
    piece_id = group * narrow_count + side if twins else 0
    piece = lax.dynamic_slice_in_dim(w_out, piece_id * piece_width, piece_width, 1)
    (routes_plane, normed_plane, out_piece), (other_up,), others = start_exchange(
        [routes.T, normed, piece], [w_up[0]], 0, twins
    )
    normed_plane = normed_plane.reshape(half, D)
    out_pieces = [p.reshape(D, piece_width) for p in (out_piece, *others)]

    def ordered(parts):
        if not twins:
            return parts
        parts = [jnp.where(side == 0, parts[k], parts[k ^ 1]) for k in range(4)]
        return [jnp.where(group == 0, parts[k], parts[k ^ 2]) for k in range(4)]

    def unordered(whole):
        return ordered([whole[:, k * piece_width : (k + 1) * piece_width] for k in range(pieces)])

    grad_final_b = grad_final.astype(bf16)
    low, _ = barrier((grad_final_b[: rows // 2], normed_plane))
    grads_low = lax.all_gather(low, "wide", axis=0, tiled=True).reshape(wide_count, rows // 2, D)
    joined = jnp.concatenate([w_query, w_key, w_value], 1)
    raw = dot(normed_plane, joined)
    gains = jnp.pad(jnp.stack([norm_query, norm_key]).astype(f32), ((0, 6), (0, 0)))
    plane_ids = (
        (jnp.arange(wide_count, dtype=jnp.int32)[:, None] * narrow_count + side) * rows
        + jnp.arange(rows, dtype=jnp.int32)[None, :]
    ).reshape(half)
    cosine, sine = rotation(positions(plane_ids))
    kept = attend(raw, gains, cosine, sine)
    attended, attended_own, lse, sums = kept[5:]

    branch = jnp.concatenate(ordered([dot(attended_own, p) for p in out_pieces]), 1)
    hidden = stream + branch
    inv_two = lax.rsqrt(jnp.mean(hidden * hidden, -1, keepdims=True) + EPSILON)
    gain_two = norm_moe.astype(f32)
    moe_in = (hidden * inv_two * gain_two).astype(bf16)
    (tokens_in,), (other_gate, other_down), _ = start_exchange([moe_in], [w_gate[0], w_down[0]], 6)

    high, tokens_in, grads_low = barrier((grad_final_b[rows // 2 :], tokens_in, grads_low))
    grads_high = lax.all_gather(high, "wide", axis=0, tiled=True).reshape(wide_count, rows // 2, D)

    earlier = (jnp.arange(rows)[:, None] < jnp.arange(rows)[None, :]).astype(bf16)

    def slots_of(expert):
        chosen = jnp.any(routes_plane == expert, 1)
        rank = dot(chosen.astype(bf16), earlier).astype(jnp.int32)
        return jnp.where(chosen, rank, -1).reshape(wide_count, 1, rows)

    router = jnp.pad(w_router, ((0, 0), (0, 128 - experts)))

    own, other = (
        Expert(e, slots_of(e), router, w, capacity, experts)
        for e, w in (
            (place * narrow_count + side, (w_gate[0], w_up[0], w_down[0])),
            (place * narrow_count + 1 - side, (other_gate, other_up, other_down)),
        )
    )
    kept_own = own.forward(tokens_in, None)
    kept_other = other.forward(tokens_in, kept_own[0])
    moe_part = kept_other[0]
    moe = lax.psum_scatter(moe_part.reshape(half, D), "wide", scatter_dimension=0, tiled=True).astype(f32)
    kept_other, grads_high, _ = barrier((kept_other, grads_high, moe_part))
    grads_in = (grads_low, grads_high)
    back_other = other.backward(grads_in, kept_other, None)
    partner_grads = plain_grads(kept_other[1], back_other[1], kept_other[2], back_other[2], back_other[3])
    came = [exchange(g) for g in partner_grads[:2]]
    before, partner_grads = barrier(((back_other[0], back_other[4]), partner_grads))
    back_own = own.backward(grads_in, kept_own, before)
    grad_part, grad_router = back_own[0], back_own[4][:experts]
    own_operands = (kept_own[1], back_own[1], kept_own[2], back_own[2], back_own[3])
    grad_moe_in, *own_grads = expert_grad(grad_part, own_operands, 5)
    grad_moe_in, moe, came[0], came[1], down_grad = barrier((grad_moe_in, moe, *came, partner_grads[2]))
    came.append(exchange(down_grad))

    grad_gain_two = jnp.sum(grad_moe_in * hidden * inv_two, 0)
    grad_hidden = (
        grad_final
        + inv_two * gain_two * grad_moe_in
        - hidden * inv_two**3 * jnp.sum(grad_moe_in * gain_two * hidden, -1, keepdims=True) / D
    )
    grad_branch = grad_hidden.astype(bf16)
    grad_attended_own = sum(dot_nt(g, p) for g, p in zip(unordered(grad_branch), out_pieces)).astype(bf16)
    branch_plane = lax.all_gather(grad_branch, "wide", axis=0, tiled=True)
    grads_joined, gain_grads = attend_back(
        raw, gains, cosine, sine, sums, *kept[:5], grad_attended_own, attended, lse
    )
    grads_joined, came[2] = barrier((grads_joined, came[2]))
    grad_out = barrier(dot_tn(attended, branch_plane).astype(bf16))
    grad_weights = barrier(dot_tn(normed_plane, grads_joined).astype(bf16))
    weights_came = exchange(grad_weights)
    out_came = exchange(grad_out)
    stats = jnp.stack([jnp.sum(v * v * mask) for v in (stream, branch, hidden, moe, hidden + moe)] + [jnp.sum(mask)])
    here = jnp.repeat(jnp.arange(wide_count) == place, columns)
    spots = [jnp.where(here, jnp.tile(g, wide_count), 0.0) for g in gain_grads[:2]]
    zeros = jnp.zeros((D,), f32)
    small = jnp.stack([zeros, grad_gain_two, *spots, jnp.pad(stats, (0, D - stats.shape[0]))])
    small = jnp.concatenate([grad_router, small, jnp.zeros((-(experts + 5) % 8, D), f32)], 0)
    small, _ = barrier((small, grad_weights))
    grad_input, small = input_grad(
        grads_joined, joined, tokens, grad_hidden, gain_one.reshape(1, D), small, experts, 3
    )
    grad_weights = grad_weights.astype(f32) + weights_came.astype(f32)
    grad_out = grad_out.astype(f32) + out_came.astype(f32)
    grad_query_w, grad_key_w, grad_value_w = (
        grad_weights[:, i * columns : (i + 1) * columns] for i in range(3)
    )
    final = hidden + moe
    output = final.astype(bf16)
    grad_gate_w, grad_up_w, grad_down_w = (
        (own.astype(f32) + other.astype(f32))[None] for own, other in zip(own_grads, came)
    )

    spots = lax.dynamic_slice_in_dim(small[experts + 2 : experts + 4], place * columns, columns, 1)
    stats = small[experts + 4, :6]
    rms = jnp.sqrt(stats[:5] / (jnp.maximum(stats[5], 1.0) * D))
    return (
        output,
        grad_input,
        grad_query_w,
        grad_key_w,
        grad_value_w,
        grad_out,
        small[experts],
        spots[0],
        spots[1],
        small[experts + 1],
        small[:experts].T,
        grad_gate_w,
        grad_up_w,
        grad_down_w,
        rms,
    )


def solution(mesh):
    return jax.shard_map(
        shards,
        mesh=mesh,
        in_specs=(
            P(("grp", "wide", "narrow"), None),
            P(("grp", "wide", "narrow"), None),
            P(("grp", "wide", "narrow")),
            P(("grp", "wide", "narrow"), None),
            P(None, "wide"),
            P(None, "wide"),
            P(None, "wide"),
            P("wide", None),
            P(),
            P("wide"),
            P("wide"),
            P(),
            P(),
            P(("wide", "narrow"), None, None),
            P(("wide", "narrow"), None, None),
            P(("wide", "narrow"), None, None),
        ),
        out_specs=(
            P(("grp", "wide", "narrow"), None),
            P(("grp", "wide", "narrow"), None),
            P("grp", "wide"),
            P("grp", "wide"),
            P("grp", "wide"),
            P(("grp", "wide"), None),
            P("grp"),
            P(("grp", "wide")),
            P(("grp", "wide")),
            P("grp"),
            P("grp", None),
            P(("grp", "wide", "narrow"), None, None),
            P(("grp", "wide", "narrow"), None, None),
            P(("grp", "wide", "narrow"), None, None),
            P("grp"),
        ),
        check_vma=False,
    )
```

```python
import functools

import jax
import jax.numpy as jnp
from jax import lax
from jax.experimental import pallas as pl
from jax.experimental.pallas import tpu as pltpu
from jax.sharding import PartitionSpec as P

D = 2048
HD = 128
TOP = 8
PROMPT = 2048
CONT = 256
NCONT = 8

EPSILON = 1e-05
THETA = 10000.0
NEGATIVE = -1e30


MESH_ID = pl.DeviceIdType.MESH
ANY = pl.BlockSpec(memory_space=pl.ANY)
VMEM = pl.BlockSpec(memory_space=pltpu.VMEM)
LINE = 4


def lasts(microseconds):
    return pl.CostEstimate(flops=0, bytes_accessed=microseconds * 3_000_000, transcendentals=0)


def position():
    grp, wide, narrow = (lax.axis_index(a) for a in ("grp", "wide", "narrow"))
    return grp, wide, narrow, wide // 2, lax.rem(wide, 2)


def greet(targets):
    barrier = pltpu.get_barrier_semaphore()
    for device, when in targets:
        def signal(device=device):
            pl.semaphore_signal(barrier, inc=1, device_id=device, device_id_type=MESH_ID)

        if when is None:
            signal()
        else:
            pl.when(when)(signal)
    peers = sum(1 if when is None else when.astype(jnp.int32) for _, when in targets)
    pl.semaphore_wait(barrier, peers)


def remote(src, dst, send, recv, device):
    return pltpu.make_async_remote_copy(
        src_ref=src, dst_ref=dst, send_sem=send, recv_sem=recv, device_id=device, device_id_type=MESH_ID
    )


def gather_kernel(count, *refs):
    ins, outs = refs[:count], refs[count : 2 * count]
    gather_body(count, ins, outs, *refs[2 * count :])


class Gather:
    def __init__(self, ins, outs, send, recv, local):
        self.ins, self.outs, self.send, self.recv, self.local = ins, outs, send, recv, local
        grp, wide, narrow, self.line, self.cross = position()
        self.wide = wide
        self.across = (grp, self.line * 2 + 1 - self.cross, narrow)
        self.above = (grp, wide + 2, narrow)
        self.below = (grp, wide - 2, narrow)
        self.has_above, self.has_below = self.line < LINE - 1, self.line > 0
        self.targets = [(self.across, None), (self.above, self.has_above), (self.below, self.has_below)]
        self.arrived = lambda i, slot: None

    def copy(self, i, source_line, way, device):
        slot = source_line * 2 + self.cross
        out = self.outs[i].at[slot]
        return remote(out, out, self.send.at[i, way, source_line], self.recv.at[i, slot], device)

    def own(self, i, way, device):
        return remote(
            self.ins[i], self.outs[i].at[self.wide], self.send.at[i, way, self.line], self.recv.at[i, self.wide], device
        )

    def mine(self, i):
        return pltpu.make_async_copy(self.ins[i], self.outs[i].at[self.wide], self.local.at[i])

    def start(self):
        for i in range(len(self.ins)):
            pl.when(self.has_above)(self.own(i, 1, self.above).start)
            pl.when(self.has_below)(self.own(i, 2, self.below).start)
            self.own(i, 0, self.across).start()
            self.mine(i).start()
            self.arrived(i, None)

    def forward(self, distance, only=None):
        for i in range(len(self.ins)) if only is None else (only,):
            for sign in (-1, 1):
                source = self.line + sign * distance

                @pl.when((source >= 0) & (source < LINE))
                def _(i=i, source=source, sign=sign):
                    self.copy(i, source, 0, self.across).wait_recv()
                    onward = self.above if sign < 0 else self.below

                    @pl.when(self.has_above if sign < 0 else self.has_below)
                    def _():
                        self.copy(i, source, 1 if sign < 0 else 2, onward).start()

                    self.copy(i, source, 0, self.across).start()
                    self.arrived(i, source * 2 + self.cross)

    def finish(self):
        for i in range(len(self.ins)):
            send, recv, src, out = self.send, self.recv, self.ins[i], self.outs[i]
            for source in range(LINE):
                other = source * 2 + 1 - self.cross
                remote(src, out.at[other], send.at[i, 0, 0], recv.at[i, other], self.across).wait_recv()
                self.arrived(i, other)
            for source in range(LINE):
                remote(src, out.at[0], send.at[i, 0, source], recv.at[i, 0], self.across).wait_send()

                @pl.when(self.has_above & (source <= self.line))
                def _(source=source):
                    remote(src, out.at[0], send.at[i, 1, source], recv.at[i, 0], self.above).wait_send()

                @pl.when(self.has_below & (source >= self.line))
                def _(source=source):
                    remote(src, out.at[0], send.at[i, 2, source], recv.at[i, 0], self.below).wait_send()

            self.mine(i).wait()


def gather_sems(count):
    return [
        pltpu.SemaphoreType.DMA((count, 3, LINE)),
        pltpu.SemaphoreType.DMA((count, 2 * LINE)),
        pltpu.SemaphoreType.DMA((count,)),
    ]


def gather_body(count, ins, outs, send, recv, local, more=(), begin=None, finish=None, arrived=None):
    gather = Gather(ins, outs, send, recv, local)
    if arrived is not None:
        gather.arrived = arrived
    greet([*gather.targets, *more])
    gather.start()
    if begin is not None:
        begin()
    for i in range(count):
        for distance in range(1, LINE):
            gather.forward(distance, i)
    gather.finish()
    if finish is not None:
        finish()


def gather_wide(arrays, collective_id):
    count = len(arrays)
    size = lax.axis_size("wide")
    if size != 2 * LINE:
        return [lax.all_gather(a, "wide", axis=0) for a in arrays]
    return pl.pallas_call(
        functools.partial(gather_kernel, count),
        out_shape=[jax.ShapeDtypeStruct((size, *a.shape), a.dtype) for a in arrays],
        in_specs=[ANY] * count,
        out_specs=[ANY] * count,
        scratch_shapes=[
            pltpu.SemaphoreType.DMA((count, 3, LINE)),
            pltpu.SemaphoreType.DMA((count, size)),
            pltpu.SemaphoreType.DMA((count,)),
        ],
        compiler_params=pltpu.CompilerParams(collective_id=collective_id, has_side_effects=True),
        cost_estimate=lasts(100),
    )(*arrays)


def scatter_kernel(part_ref, out_ref, held, from_across, from_line, load, send, recv_a, recv_l):
    grp, wide, narrow, line, cross = position()
    across = (grp, line * 2 + 1 - cross, narrow)
    above = (grp, wide + 2, narrow)
    below = (grp, wide - 2, narrow)
    has_above, has_below = line < LINE - 1, line > 0
    f32 = jnp.float32
    greet([(across, None), (above, has_above), (below, has_below)])

    order = []
    for distance in range(LINE - 1, 0, -1):
        for sign in (1, -1):
            order.append((distance, sign))

    def valid(owner):
        return (owner >= 0) & (owner < LINE)

    def across_copy(owner):
        return remote(
            part_ref.at[owner * 2 + 1 - cross], from_across.at[owner], send.at[0, owner], recv_a.at[owner], across
        )

    def load_copy(owner):
        return pltpu.make_async_copy(part_ref.at[owner * 2 + cross], held.at[owner], load.at[owner])

    def line_copy(owner, up):
        return remote(
            held.at[owner],
            from_line.at[0 if up else 1, owner],
            send.at[1, owner],
            recv_l.at[0 if up else 1, owner],
            above if up else below,
        )

    for distance, sign in order + [(0, 1)]:
        owner = line + sign * distance

        @pl.when(valid(owner))
        def _(owner=owner):
            across_copy(owner).start()
            load_copy(owner).start()

    for distance, sign in order:
        owner = line + sign * distance

        @pl.when(valid(owner))
        def _(owner=owner, sign=sign):
            load_copy(owner).wait()
            across_copy(owner).wait_recv()
            up = sign > 0
            came = has_below if up else has_above
            total = held[owner].astype(f32) + from_across[owner].astype(f32)

            @pl.when(came)
            def _():
                line_copy(owner, up).wait_recv()
                held[owner] = (total + from_line[0 if up else 1, owner].astype(f32)).astype(held.dtype)

            @pl.when(jnp.logical_not(came))
            def _():
                held[owner] = total.astype(held.dtype)

            line_copy(owner, up).start()

    load_copy(line).wait()
    across_copy(line).wait_recv()
    out_ref[...] = held[line].astype(f32) + from_across[line].astype(f32)

    @pl.when(has_below)
    def _():
        line_copy(line, True).wait_recv()
        out_ref[...] += from_line[0, line].astype(f32)

    @pl.when(has_above)
    def _():
        line_copy(line, False).wait_recv()
        out_ref[...] += from_line[1, line].astype(f32)

    for owner in range(LINE):
        across_copy(owner).wait_send()

        @pl.when(owner > line)
        def _(owner=owner):
            line_copy(owner, True).wait_send()

        @pl.when(owner < line)
        def _(owner=owner):
            line_copy(owner, False).wait_send()


def scatter_wide(part, collective_id):
    size, rows, columns = part.shape
    if size != 2 * LINE:
        return lax.psum_scatter(part, "wide", scatter_dimension=0, tiled=False).astype(jnp.float32)
    block = (LINE, rows, columns)
    return pl.pallas_call(
        scatter_kernel,
        out_shape=jax.ShapeDtypeStruct((rows, columns), jnp.float32),
        in_specs=[ANY],
        out_specs=VMEM,
        scratch_shapes=[
            pltpu.VMEM(block, part.dtype),
            pltpu.VMEM(block, part.dtype),
            pltpu.VMEM((2, *block), part.dtype),
            pltpu.SemaphoreType.DMA((LINE,)),
            pltpu.SemaphoreType.DMA((2, LINE)),
            pltpu.SemaphoreType.DMA((LINE,)),
            pltpu.SemaphoreType.DMA((2, LINE)),
        ],
        compiler_params=pltpu.CompilerParams(
            collective_id=collective_id, has_side_effects=True, vmem_limit_bytes=48 * 2**20
        ),
        cost_estimate=lasts(95),
    )(part)


def sum_kernel(x_ref, o_ref, held, send, recv):
    grp, wide, narrow, _, _ = position()
    size = held.shape[0] + 1
    others = [(grp, lax.rem(wide + k, size), narrow) for k in range(1, size)]
    greet([(device, None) for device in others])
    copies = [
        remote(x_ref, held.at[k], send.at[k], recv.at[k], device) for k, device in enumerate(others)
    ]
    for copy in copies:
        copy.start()
    for copy in copies:
        copy.wait()
    total = x_ref[...]
    for k in range(size - 1):
        total = total + held[k]
    o_ref[...] = total


def sum_wide(x, collective_id):
    size = lax.axis_size("wide")
    if size != 2 * LINE:
        return lax.psum(x, "wide")
    return pl.pallas_call(
        sum_kernel,
        out_shape=jax.ShapeDtypeStruct(x.shape, x.dtype),
        in_specs=[VMEM],
        out_specs=VMEM,
        scratch_shapes=[
            pltpu.VMEM((size - 1, *x.shape), x.dtype),
            pltpu.SemaphoreType.DMA((size - 1,)),
            pltpu.SemaphoreType.DMA((size - 1,)),
        ],
        compiler_params=pltpu.CompilerParams(collective_id=collective_id, has_side_effects=True),
        cost_estimate=lasts(8),
    )(x)


LOG2E = 1.4426950408889634
NT = (((1,), (1,)), ((), ()))


def key_parts(w, plane, rows, prompt_blocks, paired, limit=512):
    count = (prompt_blocks if w is None else w) * rows
    parts = [(first, min(limit, count - first), None) for first in range(0, count, limit)]
    own = None if w is None else w * rows
    if plane == 0:
        parts.append((own, rows, "causal"))
    elif w is not None or paired:
        parts.append((own, rows, "side"))
    return parts


def for_blocks(blocks, prompt_blocks, one, between=None, first=0):
    for w in range(prompt_blocks):
        one(w, w, w * one.rows)
    if between is not None:
        between()

    def body(i, carry):
        w = prompt_blocks + lax.rem(i - prompt_blocks + first, blocks - prompt_blocks)
        one(None, w, pl.multiple_of(w * one.rows, one.rows))
        return carry

    lax.fori_loop(prompt_blocks, blocks, body, 0)


def masked_scores(score, mask, side, rows):
    if mask == "causal":
        key = lax.broadcasted_iota(jnp.int32, (rows, rows), 0)
        query = lax.broadcasted_iota(jnp.int32, (rows, rows), 1)
        return jnp.where(key <= query, score, NEGATIVE)
    if mask == "side":
        return jnp.where(side == 1, score, NEGATIVE)
    return score


def row_sums(values):
    total = values[:, :HD]
    for first in range(HD, values.shape[1], HD):
        total = total + values[:, first : first + HD]
    return jnp.sum(total.T, 0, keepdims=True)


def turn(values, cosine, sine):
    return values * cosine + pltpu.roll(values, HD // 2, 1) * sine


def inverse_norms(sums_ref, at):
    inverse = lax.rsqrt(sums_ref[:, at].T / D + EPSILON)
    return inverse[:, 0:1], inverse[:, 1:2]


def peer_copies(size, src, dst, send, recv, grp, wide, narrow):
    return [
        remote(src, dst.at[k - 1], send.at[k - 1], recv.at[k - 1], (grp, lax.rem(wide + k, size), narrow))
        for k in range(1, size)
    ]


def attend_kernel(
    rows, prompt_blocks, paired, shared, carried, raw_ref, gains_ref, cos_ref, sin_ref, *refs
):
    carry_in, refs = refs[:carried], refs[carried:]
    q_ref, k_ref, v_ref, ko_ref, vo_ref, o_ref, own_ref, lse_ref, sums_ref = refs[:9]
    carry_out, refs = refs[9 : 9 + carried], refs[9 + carried :]
    vt_ref, vto_ref, came_ref, sum_send, sum_recv, pair_send, pair_recv, out_send, out_recv = refs[:9]
    gather = Gather(carry_in, carry_out, *refs[9:]) if carried else None
    half, columns = q_ref.shape
    size = half // rows
    heads = columns // HD
    grp, wide, narrow = (lax.axis_index(a) for a in ("grp", "wide", "narrow"))
    partner = (grp, wide, 1 - narrow)
    greet([((grp, lax.rem(wide + k, size), narrow), None) for k in range(1, size)] + [(partner, None)])
    if carried:
        gather.start()
    pairs = [
        remote(src.at[pl.ds(0, shared)], dst, pair_send.at[i], pair_recv.at[i], partner)
        for i, (src, dst) in enumerate(((k_ref, ko_ref), (v_ref, vo_ref)))
    ]
    v_ref[...] = raw_ref[:, 2 * columns :].astype(jnp.bfloat16)
    pairs[1].start()
    sums_ref[...] = jnp.zeros_like(sums_ref)

    def squares(b, carry):
        at = pl.ds(pl.multiple_of(b * rows, rows), rows)
        for i in range(2):
            part = raw_ref[at, i * columns : (i + 1) * columns]
            sums_ref[i : i + 1, at] = row_sums(part * part)
        return carry

    lax.fori_loop(0, size, squares, 0)
    copies = peer_copies(size, sums_ref, came_ref, sum_send, sum_recv, grp, wide, narrow)
    for copy in copies:
        copy.start()
    for h in range(heads):
        hs = slice(h * HD, (h + 1) * HD)
        vt_ref[hs, :] = v_ref[:, hs].T
    for copy in copies:
        copy.wait()
    total = sums_ref[...]
    for k in range(size - 1):
        total = total + came_ref[k]
    sums_ref[...] = total

    def prepare(i, ref):
        def body(b, carry):
            at = pl.ds(pl.multiple_of(b * rows, rows), rows)
            inverse = inverse_norms(sums_ref, at)[i]
            for h in range(heads):
                hs = slice(h * HD, (h + 1) * HD)
                values = raw_ref[at, i * columns + h * HD : i * columns + (h + 1) * HD]
                values = values * inverse * gains_ref[i : i + 1, hs]
                ref[at, hs] = turn(values, cos_ref[at], sin_ref[at]).astype(jnp.bfloat16)
            return carry

        return body

    lax.fori_loop(0, shared // rows, prepare(1, k_ref), 0)
    pairs[0].start()
    lax.fori_loop(shared // rows, size, prepare(1, k_ref), 0)
    lax.fori_loop(0, size, prepare(0, q_ref), 0)
    if carried:
        gather.forward(1)
    pairs[1].wait()
    for h in range(heads):
        hs = slice(h * HD, (h + 1) * HD)
        vto_ref[hs, :] = vo_ref[:, hs].T
    pairs[0].wait()

    def mine():
        return pl.ds(pl.multiple_of(wide * columns, columns), columns)

    def hand_out(w):
        return remote(
            o_ref.at[pl.ds(pl.multiple_of(w * rows, rows), rows)],
            own_ref.at[:, mine()],
            out_send.at[w],
            out_recv.at[wide],
            (grp, w, narrow),
        )

    def one(w, w_index, start):
        block = pl.ds(start, rows)
        for h in range(heads):
            hs = slice(h * HD, (h + 1) * HD)
            query = q_ref[block, hs]
            scores = []
            for plane in range(2):
                for first, count, mask in key_parts(w, plane, rows, prompt_blocks, paired):
                    at = pl.ds(start if first is None else first, count)
                    key = (k_ref, ko_ref)[plane][at, hs]
                    score = lax.dot_general(key, query, NT, preferred_element_type=jnp.float32)
                    score = score * (HD**-0.5 * LOG2E)
                    scores.append((plane, at, masked_scores(score, mask, narrow, rows)))
            largest = functools.reduce(
                jnp.maximum, [jnp.max(score, 0, keepdims=True) for _, _, score in scores]
            )
            total = jnp.zeros((1, rows), jnp.float32)
            mixed = jnp.zeros((HD, rows), jnp.float32)
            for plane, at, score in scores:
                weight = jnp.exp2(score - largest)
                total = total + jnp.sum(weight, 0, keepdims=True)
                mixed = mixed + dot((vt_ref, vto_ref)[plane][hs, at], weight.astype(jnp.bfloat16))
            o_ref[block, hs] = (mixed / total).T.astype(jnp.bfloat16)
            lse_ref[h : h + 1, block] = largest + jnp.log(total) * LOG2E

        @pl.when(w_index != wide)
        def _():
            hand_out(w_index).start()

    one.rows = rows
    for_blocks(size, prompt_blocks, one, (lambda: gather.forward(2)) if carried else None, wide)
    if carried:
        gather.forward(3)
    own_ref[:, mine()] = o_ref[pl.ds(pl.multiple_of(wide * rows, rows), rows)]

    def finish(w, carry):
        @pl.when(w != wide)
        def _():
            hand_out(w).wait_send()
            remote(
                o_ref.at[pl.ds(0, rows)], own_ref.at[:, mine()], out_send.at[w], out_recv.at[w], (grp, w, narrow)
            ).wait_recv()

        return carry

    lax.fori_loop(0, size, finish, 0)
    if carried:
        gather.finish()


def attend_back_kernel(
    rows, prompt_blocks, paired, shared, carried, raw_ref, gains_ref, cos_ref, sin_ref, sums_ref,
    q_ref, k_ref, v_ref, ko_ref, vo_ref, grad_ref, o_ref, lse_ref, *refs
):
    carry_in, refs = refs[:carried], refs[carried:]
    joined_ref, gain_ref = refs[:2]
    carry_out, refs = refs[2 : 2 + carried], refs[2 + carried :]
    do_ref, dq_ref, dk_ref, dv_ref, dko_ref, dvo_ref, dkb_ref, dvb_ref, dkr_ref, dvr_ref, kt_ref, kto_ref = refs[:12]
    dots_ref, came_ref, sum_send, sum_recv, pair_send, pair_recv, in_send, in_recv = refs[12:20]
    gather = Gather(carry_in, carry_out, *refs[20:]) if carried else None
    half, columns = q_ref.shape
    size = half // rows
    heads = columns // HD
    grp, wide, narrow = (lax.axis_index(a) for a in ("grp", "wide", "narrow"))
    partner = (grp, wide, 1 - narrow)
    greet([((grp, lax.rem(wide + k, size), narrow), None) for k in range(1, size)] + [(partner, None)])
    my_rows = pl.ds(pl.multiple_of(wide * rows, rows), rows)

    def part_of(w):
        return pl.ds(pl.multiple_of(w * columns, columns), columns)

    def hand_in(w):
        return remote(
            grad_ref.at[:, part_of(w)], do_ref.at[my_rows], in_send.at[w], in_recv.at[wide], (grp, w, narrow)
        )

    def each_peer(act):
        def body(w, carry):
            pl.when(w != wide)(lambda: act(w))
            return carry

        lax.fori_loop(0, size, body, 0)

    each_peer(lambda w: hand_in(w).start())
    do_ref[my_rows, :] = grad_ref[:, part_of(wide)]
    for ref in (dk_ref, dv_ref, dko_ref, dvo_ref, dots_ref, gain_ref):
        ref[...] = jnp.zeros_like(ref)
    for h in range(heads):
        hs = slice(h * HD, (h + 1) * HD)
        kt_ref[hs, :] = k_ref[:, hs].T
        kto_ref[hs, :] = ko_ref[:, hs].T
    each_peer(
        lambda w: remote(
            grad_ref.at[:, part_of(w)], do_ref.at[my_rows], in_send.at[w], in_recv.at[w], (grp, w, narrow)
        ).wait_recv()
    )
    if carried:
        gather.start()

    def sweep(plane):
        keys, values = ((k_ref, v_ref), (ko_ref, vo_ref))[plane]
        dk, dv = ((dk_ref, dv_ref), (dko_ref, dvo_ref))[plane]
        flipped = (kt_ref, kto_ref)[plane]

        def one(w, w_index, start):
            block = pl.ds(start, rows)
            for h in range(heads):
                hs = slice(h * HD, (h + 1) * HD)
                query = q_ref[block, hs]
                grad = do_ref[block, hs]
                delta = row_sums(grad.astype(jnp.float32) * o_ref[block, hs].astype(jnp.float32))
                lse = lse_ref[h : h + 1, block]
                back = jnp.zeros((HD, rows), jnp.float32)
                for first, count, mask in key_parts(w, plane, rows, prompt_blocks, paired):
                    at = pl.ds(start if first is None else first, count)
                    score = lax.dot_general(keys[at, hs], query, NT, preferred_element_type=jnp.float32)
                    score = masked_scores(score * (HD**-0.5 * LOG2E), mask, narrow, rows)
                    weight = jnp.exp2(score - lse)
                    grad_weight = lax.dot_general(values[at, hs], grad, NT, preferred_element_type=jnp.float32)
                    grad_score = (weight * (grad_weight - delta)).astype(jnp.bfloat16)
                    dv[at, hs] += dot(weight.astype(jnp.bfloat16), grad)
                    dk[at, hs] += dot(grad_score, query) * HD**-0.5
                    back = back + dot(flipped[hs, at], grad_score)
                back = back.T * HD**-0.5
                dq_ref[block, hs] = back if plane == 1 else dq_ref[block, hs] + back

        one.rows = rows
        for_blocks(size, prompt_blocks, one, (lambda: gather.forward(2 - plane)) if carried else None)

    sweep(1)
    dkb_ref[...] = dko_ref[...].astype(jnp.bfloat16)
    dvb_ref[...] = dvo_ref[...].astype(jnp.bfloat16)
    pairs = [
        remote(src, dst, pair_send.at[i], pair_recv.at[i], partner)
        for i, (src, dst) in enumerate(((dkb_ref, dkr_ref), (dvb_ref, dvr_ref)))
    ]
    for copy in pairs:
        copy.start()
    sweep(0)

    def turn_back(i, ref):
        def body(b, carry):
            at = pl.ds(pl.multiple_of(b * rows, rows), rows)
            inverse = inverse_norms(sums_ref, at)[i]
            products = []
            for h in range(heads):
                hs = slice(h * HD, (h + 1) * HD)
                grad = turn(ref[at, hs], cos_ref[at], -sin_ref[at])
                ref[at, hs] = grad
                product = grad * raw_ref[at, i * columns + h * HD : i * columns + (h + 1) * HD]
                gain_ref[i : i + 1, hs] += jnp.sum(product * inverse, 0, keepdims=True)
                products.append(product * gains_ref[i : i + 1, hs])
            dots_ref[i : i + 1, at] = row_sums(sum(products[1:], products[0]))
            return carry

        lax.fori_loop(0, size, body, 0)

    turn_back(0, dq_ref)
    if carried:
        gather.forward(3)
    for copy in pairs:
        copy.wait()
    dk_ref[0:shared, :] += dkr_ref[...].astype(jnp.float32)
    turn_back(1, dk_ref)
    copies = peer_copies(size, dots_ref, came_ref, sum_send, sum_recv, grp, wide, narrow)
    for copy in copies:
        copy.start()
    joined_ref[0:shared, 2 * columns :] = (dv_ref[0:shared] + dvr_ref[...].astype(jnp.float32)).astype(jnp.bfloat16)
    if shared < half:
        joined_ref[shared:, 2 * columns :] = dv_ref[shared:].astype(jnp.bfloat16)
    for copy in copies:
        copy.wait()
    total = dots_ref[...]
    for k in range(size - 1):
        total = total + came_ref[k]
    dots_ref[...] = total

    def finish(b, carry):
        at = pl.ds(pl.multiple_of(b * rows, rows), rows)
        inverses = inverse_norms(sums_ref, at)
        products = dots_ref[:, at].T / D
        for i, ref in enumerate((dq_ref, dk_ref)):
            inverse = inverses[i]
            cubed = inverse * inverse * inverse * products[:, i : i + 1]
            for h in range(heads):
                hs = slice(h * HD, (h + 1) * HD)
                there = slice(i * columns + h * HD, i * columns + (h + 1) * HD)
                value = inverse * gains_ref[i : i + 1, hs] * ref[at, hs] - raw_ref[at, there] * cubed
                joined_ref[at, there] = value.astype(jnp.bfloat16)
        return carry

    lax.fori_loop(0, size, finish, 0)
    each_peer(lambda w: hand_in(w).wait_send())
    if carried:
        gather.finish()


def attention_calls(rows, half, shared, columns, prompt_blocks, paired, ids):
    heads = columns // HD
    size = half // rows
    bf16, f32 = jnp.bfloat16, jnp.float32
    shape = lambda dtype, *dims: jax.ShapeDtypeStruct(dims, dtype)
    sems = pltpu.SemaphoreType.DMA
    peers = [sems((size - 1,)), sems((size - 1,)), sems((2,)), sems((2,)), sems((size,)), sems((size,))]

    def params(k):
        return pltpu.CompilerParams(vmem_limit_bytes=60 * 2**20, collective_id=ids[k], has_side_effects=True)

    carried = 1 if size == 2 * LINE else 0
    forward = pl.pallas_call(
        functools.partial(attend_kernel, rows, prompt_blocks, paired, shared, 0),
        out_shape=[shape(bf16, half, columns)] * 3
        + [shape(bf16, shared, columns)] * 2
        + [shape(bf16, half, columns), shape(bf16, rows, size * columns), shape(f32, heads, half), shape(f32, 8, half)],
        in_specs=[VMEM] * 4,
        out_specs=[VMEM] * 9,
        scratch_shapes=[
            pltpu.VMEM((columns, half), bf16),
            pltpu.VMEM((columns, shared), bf16),
            pltpu.VMEM((size - 1, 8, half), f32),
        ]
        + peers,
        compiler_params=params(0),
        cost_estimate=pl.CostEstimate(flops=0, bytes_accessed=300_000_000, transcendentals=0),
    )

    backward_call = pl.pallas_call(
        functools.partial(attend_back_kernel, rows, prompt_blocks, paired, shared, carried),
        out_shape=[shape(bf16, half, 3 * columns), shape(f32, 8, columns)]
        + [shape(bf16, size, rows, D)] * carried,
        in_specs=[VMEM] * 13 + [ANY] * carried,
        out_specs=[VMEM] * 2 + [ANY] * carried,
        scratch_shapes=[pltpu.VMEM((half, columns), bf16)]
        + [pltpu.VMEM((half, columns), f32)] * 3
        + [pltpu.VMEM((shared, columns), f32)] * 2
        + [pltpu.VMEM((shared, columns), bf16)] * 4
        + [
            pltpu.VMEM((columns, half), bf16),
            pltpu.VMEM((columns, shared), bf16),
            pltpu.VMEM((8, half), f32),
            pltpu.VMEM((size - 1, 8, half), f32),
        ]
        + peers
        + gather_sems(carried) * carried,
        compiler_params=params(1),
        cost_estimate=pl.CostEstimate(flops=0, bytes_accessed=300_000_000, transcendentals=0),
    )
    def backward(*args):
        if carried:
            return backward_call(*args)
        return [*backward_call(*args[:-1]), lax.all_gather(args[-1], "wide", axis=0)]

    return forward, backward


def dot(a, b):
    return jnp.dot(a, b, preferred_element_type=jnp.float32)


def dot_nt(a, b):
    return lax.dot_general(a, b, NT, preferred_element_type=jnp.float32)


def dot_tn(a, b):
    return lax.dot_general(a, b, (((0,), (0,)), ((), ())), preferred_element_type=jnp.float32)


def start_kernel(count, swaps, spread, *refs):
    ins, given = refs[:count], refs[count : count + swaps]
    refs = refs[count + swaps :]
    outs, got, pieces = refs[:count], refs[count : count + swaps], refs[count + swaps : count + swaps + 3 * spread]
    refs = refs[count + swaps + 3 * spread :]
    send, recv, local, swap_send, swap_recv, twin_send, twin_recv = refs[:7]
    grp, wide, narrow, line, cross = position()
    partner = (grp, wide, 1 - narrow)
    twin = (1 - grp, wide, narrow)
    size = 2 * LINE

    def half(ref, which):
        size = ref.shape[0] // 2
        return ref.at[pl.ds(pl.multiple_of(which * size, size), size)]

    def swap(i):
        return remote(half(given[i], grp), half(got[i], grp), swap_send.at[i], swap_recv.at[i], partner)

    def share(i, which):
        return remote(half(got[i], which), half(got[i], which), twin_send.at[i], twin_recv.at[i], twin)

    def piece(k, slot):
        piece_send, piece_recv = refs[7:]
        src = pieces[0] if k == 2 else outs[-1]
        device = twin if k else partner
        return remote(src.at[slot], pieces[k].at[slot], piece_send.at[k, slot], piece_recv.at[k, slot], device)

    def own_piece(k):
        piece_send, piece_recv = refs[7:]
        device = twin if k else partner
        return remote(ins[-1], pieces[k].at[wide], piece_send.at[k, wide], piece_recv.at[k, wide], device)

    def arrived(i, slot):
        if i == count - 1:
            for k in range(2):
                if slot is None:
                    own_piece(k).start()
                else:
                    piece(k, slot).start()

    def begin():
        for i in range(swaps):
            swap(i).start()

    def finish():
        if spread:
            for slot in range(size):
                piece(0, slot).wait_recv()
                piece(2, slot).start()
        for i in range(swaps):
            swap(i).wait_recv()
            share(i, grp).start()
        for i in range(swaps):
            swap(i).wait_send()
            share(i, grp).wait_send()
            share(i, 1 - grp).wait_recv()
        if spread:
            for slot in range(size):
                piece(0, slot).wait_send()
                piece(1, slot).wait()
                piece(2, slot).wait()

    more = [(partner, None), (twin, None)]
    gather_body(count, ins, outs, send, recv, local, more, begin, finish, arrived if spread else None)


def start_exchange(arrays, weights, collective_id, spread=False):
    size = lax.axis_size("wide")
    swap = [(0, 1), (1, 0)]
    if size != 2 * LINE or lax.axis_size("grp") != 2:
        return [lax.all_gather(a, "wide", axis=0) for a in arrays], [lax.ppermute(w, "narrow", swap) for w in weights], []
    count, swaps, spread = len(arrays), len(weights), int(spread)
    gathered = [jax.ShapeDtypeStruct((size, *a.shape), a.dtype) for a in arrays]
    dma = pltpu.SemaphoreType.DMA
    out = pl.pallas_call(
        functools.partial(start_kernel, count, swaps, spread),
        out_shape=gathered + [jax.ShapeDtypeStruct(w.shape, w.dtype) for w in weights] + gathered[-1:] * 3 * spread,
        in_specs=[ANY] * (count + swaps),
        out_specs=[ANY] * (count + swaps + 3 * spread),
        scratch_shapes=gather_sems(count) + [dma((swaps,))] * 4 + [dma((3, size))] * 2 * spread,
        compiler_params=pltpu.CompilerParams(collective_id=collective_id, has_side_effects=True),
        cost_estimate=lasts(120),
    )(*arrays, *weights)
    return out[:count], out[count : count + swaps], out[count + swaps :]


def expert_grad_kernel(
    part_ref, *refs
):
    operands = refs[0:5]
    out_ref, gate_out, up_out, down_out = refs[5:9]
    held, from_across, from_line, x_buf, g_buf, inner_buf, gate_buf, up_buf, stage = refs[9:18]
    load, send, recv_a, recv_l, fetch, put = refs[18:]
    grp, wide, narrow, line, cross = position()
    across = (grp, line * 2 + 1 - cross, narrow)
    above = (grp, wide + 2, narrow)
    below = (grp, wide - 2, narrow)
    has_above, has_below = line < LINE - 1, line > 0
    f32, bf16 = jnp.float32, jnp.bfloat16
    greet([(across, None), (above, has_above), (below, has_below)])
    order = [(distance, sign) for distance in range(LINE - 1, 0, -1) for sign in (1, -1)]

    def valid(owner):
        return (owner >= 0) & (owner < LINE)

    def across_copy(owner):
        return remote(
            part_ref.at[owner * 2 + 1 - cross], from_across.at[owner], send.at[0, owner], recv_a.at[owner], across
        )

    def load_copy(owner):
        return pltpu.make_async_copy(part_ref.at[owner * 2 + cross], held.at[owner], load.at[owner])

    def line_copy(owner, up):
        slot = 0 if up else 1
        return remote(
            held.at[owner], from_line.at[slot, owner], send.at[1, owner], recv_l.at[slot, owner], above if up else below
        )

    for distance, sign in order + [(0, 1)]:
        owner = line + sign * distance

        @pl.when(valid(owner))
        def _(owner=owner):
            across_copy(owner).start()
            load_copy(owner).start()

    bufs = (x_buf, g_buf, inner_buf, gate_buf, up_buf)

    fetches = [pltpu.make_async_copy(src, dst, fetch.at[i]) for i, (src, dst) in enumerate(zip(operands, bufs))]
    for copy in fetches:
        copy.start()

    tiles = stage.shape[0]
    width = gate_buf.shape[1] // tiles

    def tile(n, size):
        return pl.ds(pl.multiple_of(n * size, size), size)

    def column_job(values, result):
        def put_copy(n):
            return pltpu.make_async_copy(stage.at[n], result.at[:, tile(n, width)], put.at[n])

        def run():
            @pl.loop(0, tiles)
            def _(n):
                stage[n] = dot_tn(x_buf[...], values[:, tile(n, width)]).astype(bf16)
                put_copy(n).start()

            @pl.loop(0, tiles)
            def _(n):
                put_copy(n).wait()

        return run

    def down_job(result):
        units = inner_buf.shape[1] // tiles

        def run():
            for n in range(tiles):
                at = slice(n * units, (n + 1) * units)
                product = dot_tn(inner_buf[:, at], g_buf[...]).astype(bf16)
                for c in range(product.shape[1] // width):
                    stage[n, c * units : (c + 1) * units, :] = product[:, c * width : (c + 1) * width]
            copies = [
                pltpu.make_async_copy(
                    stage.at[n, pl.ds(c * units, units)],
                    result.at[pl.ds(n * units, units), pl.ds(c * width, width)],
                    put.at[n * (g_buf.shape[1] // width) + c],
                )
                for n in range(tiles)
                for c in range(g_buf.shape[1] // width)
            ]
            for copy in copies:
                copy.start()
            for copy in copies:
                copy.wait()

        return run

    def first_job():
        for copy in fetches:
            copy.wait()
        column_job(gate_buf, gate_out)()

    jobs = [first_job, None, column_job(up_buf, up_out), None, down_job(down_out), None]
    for job, (distance, sign) in zip(jobs, order):
        if job is not None:
            job()
        owner = line + sign * distance

        @pl.when(valid(owner))
        def _(owner=owner, sign=sign):
            load_copy(owner).wait()
            across_copy(owner).wait_recv()
            up = sign > 0
            came = has_below if up else has_above
            total = held[owner].astype(f32) + from_across[owner].astype(f32)

            @pl.when(came)
            def _():
                line_copy(owner, up).wait_recv()
                held[owner] = (total + from_line[0 if up else 1, owner].astype(f32)).astype(held.dtype)

            @pl.when(jnp.logical_not(came))
            def _():
                held[owner] = total.astype(held.dtype)

            line_copy(owner, up).start()

    load_copy(line).wait()
    across_copy(line).wait_recv()
    out_ref[...] = held[line].astype(f32) + from_across[line].astype(f32)

    @pl.when(has_below)
    def _():
        line_copy(line, True).wait_recv()
        out_ref[...] += from_line[0, line].astype(f32)

    @pl.when(has_above)
    def _():
        line_copy(line, False).wait_recv()
        out_ref[...] += from_line[1, line].astype(f32)

    for owner in range(LINE):
        across_copy(owner).wait_send()

        @pl.when(owner > line)
        def _(owner=owner):
            line_copy(owner, True).wait_send()

        @pl.when(owner < line)
        def _(owner=owner):
            line_copy(owner, False).wait_send()


def plain_grads(x, g, inner, gate, up):
    return [dot_tn(a, b).astype(jnp.bfloat16) for a, b in ((x, gate), (x, up), (inner, g))]


def expert_grad(part, own, collective_id):
    size, rows, columns = part.shape
    f32, bf16 = jnp.float32, jnp.bfloat16
    if size != 2 * LINE:
        return lax.psum_scatter(part, "wide", scatter_dimension=0, tiled=False).astype(f32), *plain_grads(*own)
    count, units = own[2].shape
    tiles = 4
    block = (LINE, rows, columns)
    gate = jax.ShapeDtypeStruct((D, units), bf16)
    down = jax.ShapeDtypeStruct((units, D), bf16)
    dma = pltpu.SemaphoreType.DMA
    return pl.pallas_call(
        expert_grad_kernel,
        out_shape=[jax.ShapeDtypeStruct((rows, columns), f32), gate, gate, down],
        in_specs=[ANY] * 6,
        out_specs=[VMEM] + [ANY] * 3,
        scratch_shapes=[
            pltpu.VMEM(block, bf16),
            pltpu.VMEM(block, bf16),
            pltpu.VMEM((2, *block), bf16),
            pltpu.VMEM((count, D), bf16),
            pltpu.VMEM((count, D), bf16),
            pltpu.VMEM((count, units), bf16),
            pltpu.VMEM((count, units), bf16),
            pltpu.VMEM((count, units), bf16),
            pltpu.VMEM((tiles, D, units // tiles), bf16),
            dma((LINE,)),
            dma((2, LINE)),
            dma((LINE,)),
            dma((2, LINE)),
            dma((5,)),
            dma((tiles * D // (units // tiles),)),
        ],
        compiler_params=pltpu.CompilerParams(
            collective_id=collective_id, has_side_effects=True, vmem_limit_bytes=60 * 2**20
        ),
        cost_estimate=lasts(1),
    )(part, *own)


class SmallSum:
    def __init__(self, x_ref, o_ref, parts, total, send, recv, send_back, recv_back):
        self.refs = x_ref, o_ref, parts, total, send, recv, send_back, recv_back
        grp, wide, narrow, _, _ = position()
        self.size, _, self.width = parts.shape
        self.me = wide * 2 + narrow
        self.ranks = [lax.rem(self.me + k, self.size) for k in range(self.size)]
        self.devices = [(grp, rank // 2, lax.rem(rank, 2)) for rank in self.ranks]
        self.targets = [(device, None) for device in self.devices[1:]]

    def columns(self, rank):
        return pl.ds(pl.multiple_of(rank * self.width, self.width), self.width)

    def run(self):
        x_ref, o_ref, parts, total, send, recv, send_back, recv_back = self.refs
        devices, size, mine = self.devices, self.size, self.columns(self.me)
        out = [
            remote(x_ref.at[:, self.columns(self.ranks[k])], parts.at[k], send.at[k], recv.at[k], devices[k])
            for k in range(1, size)
        ]
        for copy in out:
            copy.start()
        total[...] = x_ref[:, mine]
        for k, copy in enumerate(out):
            copy.wait()
            total[...] += parts[k + 1]
        back = [
            remote(total, o_ref.at[:, mine], send_back.at[k], recv_back.at[k], devices[k]) for k in range(1, size)
        ]
        for copy in back:
            copy.start()
        o_ref[:, mine] = total[...]
        for copy in back:
            copy.wait_send()
        for k in range(1, size):
            rank = lax.rem(self.me - k + size, size)
            remote(total, o_ref.at[:, self.columns(rank)], send_back.at[k], recv_back.at[k], devices[k]).wait_recv()


def input_grad_kernel(
    gain_row, joined_ref, weights_ref, tokens_ref, hidden_ref, gain_ref, small_ref, out_ref, sums_ref,
    held, from_across, from_line, x_ref, parts, total_ref, send, recv_a, recv_l, *small_sems
):
    rows = tokens_ref.shape[0]
    f32 = jnp.float32
    small = SmallSum(x_ref, sums_ref, parts, total_ref, *small_sems)
    grp, wide, narrow, line, cross = position()
    across = (grp, line * 2 + 1 - cross, narrow)
    above = (grp, wide + 2, narrow)
    below = (grp, wide - 2, narrow)
    has_above, has_below = line < LINE - 1, line > 0
    greet(small.targets)
    order = [(distance, sign) for distance in range(LINE - 1, 0, -1) for sign in (1, -1)] + [(0, 1)]

    def valid(owner):
        return (owner >= 0) & (owner < LINE)

    def part(owner, column):
        at = pl.ds(pl.multiple_of((owner * 2 + column) * rows, rows), rows)
        return dot_nt(joined_ref[at], weights_ref[...])

    def across_copy(owner):
        return remote(held.at[0, owner], from_across.at[owner], send.at[0, owner], recv_a.at[owner], across)

    def line_copy(owner, up):
        slot = 0 if up else 1
        return remote(
            held.at[1, owner], from_line.at[slot, owner], send.at[1, owner], recv_l.at[slot, owner], above if up else below
        )

    for distance, sign in order:
        owner = line + sign * distance

        @pl.when(valid(owner))
        def _(owner=owner):
            held[0, owner] = part(owner, 1 - cross).astype(held.dtype)
            across_copy(owner).start()

    for distance, sign in order[:-1]:
        owner = line + sign * distance

        @pl.when(valid(owner))
        def _(owner=owner, sign=sign):
            up = sign > 0
            came = has_below if up else has_above
            total = part(owner, cross)
            across_copy(owner).wait_recv()
            total = total + from_across[owner].astype(f32)

            @pl.when(came)
            def _():
                line_copy(owner, up).wait_recv()
                held[1, owner] = (total + from_line[0 if up else 1, owner].astype(f32)).astype(held.dtype)

            @pl.when(jnp.logical_not(came))
            def _():
                held[1, owner] = total.astype(held.dtype)

            line_copy(owner, up).start()

    out_ref[...] = part(line, cross)
    across_copy(line).wait_recv()
    out_ref[...] += from_across[line].astype(f32)

    @pl.when(has_below)
    def _():
        line_copy(line, True).wait_recv()
        out_ref[...] += from_line[0, line].astype(f32)

    @pl.when(has_above)
    def _():
        line_copy(line, False).wait_recv()
        out_ref[...] += from_line[1, line].astype(f32)

    x_ref[...] = small_ref[...]
    x_ref[gain_row : gain_row + 1, :] = jnp.zeros((1, D), f32)
    chunk = min(rows, 64)

    def finish(i, carry):
        at = pl.ds(pl.multiple_of(i * chunk, chunk), chunk)
        grad = out_ref[at]
        stream = tokens_ref[at].astype(f32)
        inverse = lax.rsqrt(jnp.mean(stream * stream, -1, keepdims=True) + EPSILON)
        product = grad * stream
        x_ref[gain_row : gain_row + 1, :] += jnp.sum(product * inverse, 0, keepdims=True)
        slope = inverse * inverse * inverse * jnp.sum(product * gain_ref[...], -1, keepdims=True) / D
        out_ref[at] = hidden_ref[at] + inverse * gain_ref[...] * grad - stream * slope
        return carry

    lax.fori_loop(0, rows // chunk, finish, 0)
    small.run()

    for owner in range(LINE):
        across_copy(owner).wait_send()

        @pl.when(owner > line)
        def _(owner=owner):
            line_copy(owner, True).wait_send()

        @pl.when(owner < line)
        def _(owner=owner):
            line_copy(owner, False).wait_send()


def input_grad(joined, weights, tokens, grad_hidden, gain, small, gain_row, ids):
    size = lax.axis_size("wide")
    rows = tokens.shape[0]
    f32, bf16 = jnp.float32, jnp.bfloat16
    if size != 2 * LINE:
        part = dot_nt(joined, weights).astype(bf16).reshape(size, rows, D)
        grad = lax.psum_scatter(part, "wide", scatter_dimension=0, tiled=False).astype(f32)
        stream = tokens.astype(f32)
        inverse = lax.rsqrt(jnp.mean(stream * stream, -1, keepdims=True) + EPSILON)
        small = small.at[gain_row].set(jnp.sum(grad * stream * inverse, 0))
        slope = inverse**3 * jnp.sum(grad * gain * stream, -1, keepdims=True) / D
        return grad_hidden + inverse * gain * grad - stream * slope, lax.psum(small, ("wide", "narrow"))
    devices = 4 * LINE
    block = (LINE, rows, D)
    dma = pltpu.SemaphoreType.DMA
    return pl.pallas_call(
        functools.partial(input_grad_kernel, gain_row),
        out_shape=[jax.ShapeDtypeStruct((rows, D), f32), jax.ShapeDtypeStruct(small.shape, f32)],
        in_specs=[VMEM] * 6,
        out_specs=[VMEM] * 2,
        scratch_shapes=[
            pltpu.VMEM((2, *block), bf16),
            pltpu.VMEM(block, bf16),
            pltpu.VMEM((2, *block), bf16),
            pltpu.VMEM(small.shape, f32),
            pltpu.VMEM((devices, small.shape[0], D // devices), f32),
            pltpu.VMEM((small.shape[0], D // devices), f32),
            dma((2, LINE)),
            dma((LINE,)),
            dma((2, LINE)),
        ]
        + [dma((devices,))] * 4,
        compiler_params=pltpu.CompilerParams(
            collective_id=ids, has_side_effects=True, vmem_limit_bytes=56 * 2**20
        ),
        cost_estimate=lasts(100),
    )(joined, weights, tokens, grad_hidden, gain, small)


def pick_rows(step, capacity, slot_ref, source_refs, picks, held, out_ref):
    row = lax.broadcasted_iota(jnp.int32, (capacity, slot_ref.shape[2]), 0)
    pick = jnp.where(row == slot_ref[0], 1.0, 0.0).astype(jnp.bfloat16)
    picks[step] = pick
    part = pick.shape[1] // len(source_refs)
    values = sum(dot(pick[:, k * part : (k + 1) * part], ref[0]) for k, ref in enumerate(source_refs))
    values = values.astype(jnp.bfloat16)
    held[pl.ds(pl.multiple_of(step * capacity, capacity), capacity)] = values
    out_ref[...] = values


def spread_rows(block, capacity, picks, total, before_ref, out_ref):
    here = pl.ds(pl.multiple_of(block * capacity, capacity), capacity)
    values = dot_tn(picks[block], total[here].astype(jnp.bfloat16))
    if before_ref is not None:
        values = values + before_ref[0].astype(jnp.float32)
    out_ref[0] = values.astype(jnp.bfloat16)


def expert_forward_kernel(
    tiles, capacity, experts, first, id_ref, slot_ref, tokens_ref, router_ref, gate_ref, up_ref, down_ref, *refs
):
    before_ref = None if first else refs[0]
    moe_ref, x_ref, inner_ref, gate_pre_ref, up_pre_ref, probs_ref, x_all, picks, moe_all = refs[0 if first else 1 :]
    step = pl.program_id(1)
    blocks = picks.shape[0]
    lane = lax.broadcasted_iota(jnp.int32, (1, 128), 1)

    @pl.when(step < blocks)
    def _():
        pick_rows(step, capacity, slot_ref, [tokens_ref], picks, x_all, x_ref)

    @pl.when(step == blocks)
    def _():
        logits = jnp.where(lane < experts, dot(x_all[...], router_ref[...]), NEGATIVE)
        weight = jnp.exp(logits - jnp.max(logits, -1, keepdims=True))
        probs_ref[...] = weight / jnp.sum(weight, -1, keepdims=True)
        moe_all[...] = jnp.zeros_like(moe_all)

    @pl.when((step >= blocks) & (step < blocks + tiles))
    def _():
        x = x_all[...]
        gate = jnp.sum(jnp.where(lane == id_ref[0], probs_ref[...], 0.0), -1, keepdims=True)
        gate_pre = dot(x, gate_ref[...])
        up_pre = dot(x, up_ref[...])
        gate_pre_ref[...] = gate_pre
        up_pre_ref[...] = up_pre
        inner_gated = (gate * (gate_pre / (1.0 + jnp.exp(-gate_pre))) * up_pre).astype(jnp.bfloat16)
        inner_ref[...] = inner_gated
        moe_all[...] += dot(inner_gated, down_ref[...])

    @pl.when(step >= blocks + tiles)
    def _():
        spread_rows(step - blocks - tiles, capacity, picks, moe_all, before_ref, moe_ref)


def expert_backward_kernel(
    tiles, capacity, first, id_ref, slot_ref, low_ref, high_ref, x_ref, probs_ref, gate_pre_ref, up_pre_ref,
    router_ref, gate_ref, up_ref, down_ref, *refs
):
    before_ref, router_in_ref = (None, None) if first else refs[:2]
    (
        part_ref, g_ref, grad_gate_ref, grad_up_ref, router_grad_ref,
        g_all, picks, part_all, scores_all, router_sum,
    ) = refs[0 if first else 2 :]
    bf16 = jnp.bfloat16
    group, step = pl.program_id(0), pl.program_id(1)
    blocks = picks.shape[0]
    lane = lax.broadcasted_iota(jnp.int32, (1, 128), 1)
    here = jnp.where(lane == id_ref[0], 1.0, 0.0)

    @pl.when(step < blocks)
    def _():
        pick_rows(step, capacity, slot_ref, [low_ref, high_ref], picks, g_all, g_ref)

    @pl.when(step == blocks)
    def _():
        part_all[...] = jnp.zeros_like(part_all)
        scores_all[...] = jnp.zeros_like(scores_all)

    @pl.when((step >= blocks) & (step < blocks + tiles))
    def _():
        gate = jnp.sum(probs_ref[...] * here, -1, keepdims=True)
        gate_pre, up_pre = gate_pre_ref[...], up_pre_ref[...]
        back = dot_nt(g_all[...], down_ref[...])
        sigmoid = 1.0 / (1.0 + jnp.exp(-gate_pre))
        silu = gate_pre * sigmoid
        scores_all[...] += jnp.sum(silu * up_pre * back, -1, keepdims=True)
        back = gate * back
        grad_gate_pre = (back * up_pre * sigmoid * (1.0 + gate_pre * (1.0 - sigmoid))).astype(bf16)
        grad_up_pre = (back * silu).astype(bf16)
        grad_gate_ref[...] = grad_gate_pre
        grad_up_ref[...] = grad_up_pre
        part_all[...] += dot_nt(grad_gate_pre, gate_ref[...]) + dot_nt(grad_up_pre, up_ref[...])

    @pl.when(step == blocks + tiles)
    def _():
        probs = probs_ref[...]
        gate = jnp.sum(probs * here, -1, keepdims=True)
        mixing = (gate * scores_all[...] * (here - probs)).astype(bf16)
        part_all[...] += dot_nt(mixing, router_ref[...])
        grad = dot_tn(mixing, x_ref[...])

        @pl.when(group == 0)
        def _():
            router_sum[...] = grad if first else grad + router_in_ref[...]

        @pl.when(group > 0)
        def _():
            router_sum[...] += grad

        router_grad_ref[...] = router_sum[...]

    @pl.when(step >= blocks + tiles)
    def _():
        spread_rows(step - blocks - tiles, capacity, picks, part_all, before_ref, part_ref)


class Expert:
    def __init__(self, expert, slots, router, weights, capacity, experts):
        self.scalars = expert.astype(jnp.int32).reshape(1), slots
        self.router, self.weights, self.capacity, self.experts = router, weights, capacity, experts
        wide, _, rows = slots.shape
        units = weights[0].shape[1]
        groups = 1 if wide * capacity <= 1280 else 2
        blocks, tile = wide // groups, 256
        tiles = units // tile
        last = blocks + tiles
        self.tiles, self.grid = tiles, (groups, last + blocks)
        self.held, self.blocks, self.rows = blocks * capacity, blocks, rows
        count = wide * capacity

        def picked(g, i):
            return g * blocks + jnp.minimum(i, blocks - 1)

        def tiled(i):
            return jnp.clip(i - blocks, 0, tiles - 1)

        self.whole = pl.BlockSpec((1, rows, D), lambda g, i: (picked(g, i), 0, 0))
        self.part = pl.BlockSpec((1, rows // 2, D), lambda g, i: (picked(g, i), 0, 0))
        self.back = pl.BlockSpec((1, rows, D), lambda g, i: (g * blocks + jnp.clip(i - last, 0, blocks - 1), 0, 0))
        self.row = pl.BlockSpec((capacity, D), lambda g, i: (picked(g, i), 0))
        column = pl.BlockSpec((D, tile), lambda g, i: (0, tiled(i)))
        self.unit = pl.BlockSpec((self.held, tile), lambda g, i: (g, tiled(i)))
        self.fixed = pl.BlockSpec((128, D), lambda g, i: (0, 0))
        self.rows_all = pl.BlockSpec((self.held, D), lambda g, i: (g, 0))
        self.probs = pl.BlockSpec((self.held, 128), lambda g, i: (g, 0))
        self.heads = [
            pl.BlockSpec(memory_space=pltpu.SMEM), pl.BlockSpec((1, 1, rows), lambda g, i: (picked(g, i), 0, 0))
        ]
        self.weight_specs = [
            pl.BlockSpec((D, 128), lambda g, i: (0, 0)), column, column,
            pl.BlockSpec((tile, D), lambda g, i: (tiled(i), 0)),
        ]
        shape = jax.ShapeDtypeStruct
        self.blocks_shape = shape((wide, rows, D), jnp.bfloat16)
        self.compact = shape((count, D), jnp.bfloat16)
        self.narrow = shape((count, units), jnp.bfloat16)
        self.narrow32 = shape((count, units), jnp.float32)
        self.probs_shape = shape((count, 128), jnp.float32)
        self.common = dict(
            grid=self.grid,
            compiler_params=pltpu.CompilerParams(vmem_limit_bytes=60 * 2**20),
            cost_estimate=pl.CostEstimate(flops=0, bytes_accessed=120_000_000, transcendentals=0),
        )

    def forward(self, tokens, before):
        first = before is None
        f32, bf16 = jnp.float32, jnp.bfloat16
        return pl.pallas_call(
            functools.partial(expert_forward_kernel, self.tiles, self.capacity, self.experts, first),
            in_specs=self.heads + [self.whole] + self.weight_specs + ([] if first else [self.back]),
            out_specs=[self.back, self.row, self.unit, self.unit, self.unit, self.probs],
            out_shape=[
                self.blocks_shape, self.compact, self.narrow, self.narrow32, self.narrow32, self.probs_shape
            ],
            scratch_shapes=[
                pltpu.VMEM((self.held, D), bf16),
                pltpu.VMEM((self.blocks, self.capacity, self.rows), bf16),
                pltpu.VMEM((self.held, D), f32),
            ],
            **self.common,
        )(*self.scalars, tokens, self.router, *self.weights, *(() if first else (before,)))

    def backward(self, grads, kept, before):
        first = before is None
        f32, bf16 = jnp.float32, jnp.bfloat16
        _, x, _, gate_pre, up_pre, probs = kept
        return pl.pallas_call(
            functools.partial(expert_backward_kernel, self.tiles, self.capacity, first),
            in_specs=self.heads
            + [self.part, self.part, self.rows_all, self.probs, self.unit, self.unit]
            + self.weight_specs
            + ([] if first else [self.back, self.fixed]),
            out_specs=[self.back, self.row, self.unit, self.unit, self.fixed],
            out_shape=[
                self.blocks_shape, self.compact, self.narrow, self.narrow, jax.ShapeDtypeStruct((128, D), f32)
            ],
            scratch_shapes=[
                pltpu.VMEM((self.held, D), bf16),
                pltpu.VMEM((self.blocks, self.capacity, self.rows), bf16),
                pltpu.VMEM((self.held, D), f32),
                pltpu.VMEM((self.held, 1), f32),
                pltpu.VMEM((128, D), f32),
            ],
            **self.common,
        )(*self.scalars, *grads, x, probs, gate_pre, up_pre, self.router, *self.weights, *(before or ()))


def positions(token_ids):
    local = token_ids % (PROMPT + NCONT * CONT)
    return jnp.where(local < PROMPT, local, PROMPT + (local - PROMPT) % CONT)


def rotation(place):
    frequency = THETA ** (-2.0 * jnp.arange(HD // 2, dtype=jnp.float32) / HD)
    angle = place.astype(jnp.float32)[:, None] * frequency[None, :]
    cosine, sine = jnp.cos(angle), jnp.sin(angle)
    return jnp.concatenate([cosine, cosine], 1), jnp.concatenate([-sine, sine], 1)


def shards(
    tokens,
    cotangent,
    valid,
    routes,
    w_query,
    w_key,
    w_value,
    w_out,
    norm_attn,
    norm_query,
    norm_key,
    norm_moe,
    w_router,
    w_gate,
    w_up,
    w_down,
):
    bf16, f32 = jnp.bfloat16, jnp.float32
    wide_count = lax.axis_size("wide")
    narrow_count = lax.axis_size("narrow")
    rows = tokens.shape[0]
    half = rows * wide_count
    columns = w_query.shape[1]
    experts = w_router.shape[1]
    hidden_units = w_gate.shape[2]
    capacity = min(max(rows * TOP * 5 // (4 * experts), 2), rows)
    assert narrow_count == 2 and CONT in (rows, 2 * rows)
    paired = CONT == 2 * rows
    side = lax.axis_index("narrow")
    place = lax.axis_index("wide")
    group = lax.axis_index("grp")
    swap = [(0, 1), (1, 0)]
    twins = lax.axis_size("grp") == 2
    prompt_blocks = PROMPT // (rows * narrow_count)
    shared = half if paired else prompt_blocks * rows
    attend, attend_back = attention_calls(rows, half, shared, columns, prompt_blocks, paired, (1, 2))
    barrier = lax.optimization_barrier

    def exchange(value):
        return lax.ppermute(value, "narrow", swap)

    stream = tokens.astype(f32)
    inv_one = lax.rsqrt(jnp.mean(stream * stream, -1, keepdims=True) + EPSILON)
    gain_one = norm_attn.astype(f32)
    normed = (stream * inv_one * gain_one).astype(bf16)
    mask = valid.astype(f32)[:, None]
    grad_final = cotangent.astype(f32) * mask
    pieces = 2 * narrow_count if twins else 1
    piece_width = D // pieces
    piece_id = group * narrow_count + side if twins else 0
    piece = lax.dynamic_slice_in_dim(w_out, piece_id * piece_width, piece_width, 1)
    (routes_plane, normed_plane, out_piece), (other_up,), others = start_exchange(
        [routes.T, normed, piece], [w_up[0]], 0, twins
    )
    normed_plane = normed_plane.reshape(half, D)
    out_pieces = [p.reshape(D, piece_width) for p in (out_piece, *others)]

    def ordered(parts):
        if not twins:
            return parts
        parts = [jnp.where(side == 0, parts[k], parts[k ^ 1]) for k in range(4)]
        return [jnp.where(group == 0, parts[k], parts[k ^ 2]) for k in range(4)]

    def unordered(whole):
        return ordered([whole[:, k * piece_width : (k + 1) * piece_width] for k in range(pieces)])

    grad_final_b = grad_final.astype(bf16)
    low, _ = barrier((grad_final_b[: rows // 2], normed_plane))
    grads_low = lax.all_gather(low, "wide", axis=0, tiled=True).reshape(wide_count, rows // 2, D)
    joined = jnp.concatenate([w_query, w_key, w_value], 1)
    raw = dot(normed_plane, joined)
    gains = jnp.pad(jnp.stack([norm_query, norm_key]).astype(f32), ((0, 6), (0, 0)))
    plane_ids = (
        (jnp.arange(wide_count, dtype=jnp.int32)[:, None] * narrow_count + side) * rows
        + jnp.arange(rows, dtype=jnp.int32)[None, :]
    ).reshape(half)
    cosine, sine = rotation(positions(plane_ids))
    kept = attend(raw, gains, cosine, sine)
    attended, attended_own, lse, sums = kept[5:]

    branch = jnp.concatenate(ordered([dot(attended_own, p) for p in out_pieces]), 1)
    hidden = stream + branch
    inv_two = lax.rsqrt(jnp.mean(hidden * hidden, -1, keepdims=True) + EPSILON)
    gain_two = norm_moe.astype(f32)
    moe_in = (hidden * inv_two * gain_two).astype(bf16)
    (tokens_in,), (other_gate, other_down), _ = start_exchange([moe_in], [w_gate[0], w_down[0]], 6)

    high, tokens_in, grads_low = barrier((grad_final_b[rows // 2 :], tokens_in, grads_low))
    grads_high = lax.all_gather(high, "wide", axis=0, tiled=True).reshape(wide_count, rows // 2, D)

    earlier = (jnp.arange(rows)[:, None] < jnp.arange(rows)[None, :]).astype(bf16)

    def slots_of(expert):
        chosen = jnp.any(routes_plane == expert, 1)
        rank = dot(chosen.astype(bf16), earlier).astype(jnp.int32)
        return jnp.where(chosen, rank, -1).reshape(wide_count, 1, rows)

    router = jnp.pad(w_router, ((0, 0), (0, 128 - experts)))

    own, other = (
        Expert(e, slots_of(e), router, w, capacity, experts)
        for e, w in (
            (place * narrow_count + side, (w_gate[0], w_up[0], w_down[0])),
            (place * narrow_count + 1 - side, (other_gate, other_up, other_down)),
        )
    )
    kept_own = own.forward(tokens_in, None)
    kept_other = other.forward(tokens_in, kept_own[0])
    moe_part = kept_other[0]
    moe = lax.psum_scatter(moe_part.reshape(half, D), "wide", scatter_dimension=0, tiled=True).astype(f32)
    kept_other, grads_high, _ = barrier((kept_other, grads_high, moe_part))
    grads_in = (grads_low, grads_high)
    back_other = other.backward(grads_in, kept_other, None)
    partner_grads = plain_grads(kept_other[1], back_other[1], kept_other[2], back_other[2], back_other[3])
    came = [exchange(g) for g in partner_grads[:2]]
    before, partner_grads = barrier(((back_other[0], back_other[4]), partner_grads))
    back_own = own.backward(grads_in, kept_own, before)
    grad_part, grad_router = back_own[0], back_own[4][:experts]
    own_operands = (kept_own[1], back_own[1], kept_own[2], back_own[2], back_own[3])
    grad_moe_in, *own_grads = expert_grad(grad_part, own_operands, 5)
    grad_moe_in, moe, came[0], down_grad = barrier((grad_moe_in, moe, came[0], partner_grads[2]))
    came.append(exchange(down_grad))

    grad_gain_two = jnp.sum(grad_moe_in * hidden * inv_two, 0)
    grad_hidden = (
        grad_final
        + inv_two * gain_two * grad_moe_in
        - hidden * inv_two**3 * jnp.sum(grad_moe_in * gain_two * hidden, -1, keepdims=True) / D
    )
    grad_branch = grad_hidden.astype(bf16)
    grad_attended_own = sum(dot_nt(g, p) for g, p in zip(unordered(grad_branch), out_pieces)).astype(bf16)
    grads_joined, gain_grads, branch_plane = attend_back(
        raw, gains, cosine, sine, sums, *kept[:5], grad_attended_own, attended, lse, grad_branch
    )
    grads_joined, came[1], came[2] = barrier((grads_joined, came[1], came[2]))
    grad_out = barrier(dot_tn(attended, branch_plane.reshape(half, D)).astype(bf16))
    grad_weights = barrier(dot_tn(normed_plane, grads_joined).astype(bf16))
    weights_came = exchange(grad_weights)
    out_came = exchange(grad_out)
    stats = jnp.stack([jnp.sum(v * v * mask) for v in (stream, branch, hidden, moe, hidden + moe)] + [jnp.sum(mask)])
    here = jnp.repeat(jnp.arange(wide_count) == place, columns)
    spots = [jnp.where(here, jnp.tile(g, wide_count), 0.0) for g in gain_grads[:2]]
    zeros = jnp.zeros((D,), f32)
    small = jnp.stack([zeros, grad_gain_two, *spots, jnp.pad(stats, (0, D - stats.shape[0]))])
    small = jnp.concatenate([grad_router, small, jnp.zeros((-(experts + 5) % 8, D), f32)], 0)
    small, _, _ = barrier((small, grad_weights, grad_out))
    grad_input, small = input_grad(
        grads_joined, joined, tokens, grad_hidden, gain_one.reshape(1, D), small, experts, 3
    )
    grad_weights = grad_weights.astype(f32) + weights_came.astype(f32)
    grad_out = grad_out.astype(f32) + out_came.astype(f32)
    grad_query_w, grad_key_w, grad_value_w = (
        grad_weights[:, i * columns : (i + 1) * columns] for i in range(3)
    )
    final = hidden + moe
    output = final.astype(bf16)
    grad_gate_w, grad_up_w, grad_down_w = (
        (own.astype(f32) + other.astype(f32))[None] for own, other in zip(own_grads, came)
    )

    spots = lax.dynamic_slice_in_dim(small[experts + 2 : experts + 4], place * columns, columns, 1)
    stats = small[experts + 4, :6]
    rms = jnp.sqrt(stats[:5] / (jnp.maximum(stats[5], 1.0) * D))
    return (
        output,
        grad_input,
        grad_query_w,
        grad_key_w,
        grad_value_w,
        grad_out,
        small[experts],
        spots[0],
        spots[1],
        small[experts + 1],
        small[:experts].T,
        grad_gate_w,
        grad_up_w,
        grad_down_w,
        rms,
    )


def solution(mesh):
    return jax.shard_map(
        shards,
        mesh=mesh,
        in_specs=(
            P(("grp", "wide", "narrow"), None),
            P(("grp", "wide", "narrow"), None),
            P(("grp", "wide", "narrow")),
            P(("grp", "wide", "narrow"), None),
            P(None, "wide"),
            P(None, "wide"),
            P(None, "wide"),
            P("wide", None),
            P(),
            P("wide"),
            P("wide"),
            P(),
            P(),
            P(("wide", "narrow"), None, None),
            P(("wide", "narrow"), None, None),
            P(("wide", "narrow"), None, None),
        ),
        out_specs=(
            P(("grp", "wide", "narrow"), None),
            P(("grp", "wide", "narrow"), None),
            P("grp", "wide"),
            P("grp", "wide"),
            P("grp", "wide"),
            P(("grp", "wide"), None),
            P("grp"),
            P(("grp", "wide")),
            P(("grp", "wide")),
            P("grp"),
            P("grp", None),
            P(("grp", "wide", "narrow"), None, None),
            P(("grp", "wide", "narrow"), None, None),
            P(("grp", "wide", "narrow"), None, None),
            P("grp"),
        ),
        check_vma=False,
    )
```
